32 devices in a mesh: seq: 4 (over x, core), rep: 8 (over z, y).
Axes of the slice: x: 2, y: 2, z: 4, core: 2. Of those that a mesh axis runs over, the one named last changes fastest.
Arguments:
- x_words: float32 [8, 1024, 768], P('rep', 'seq'), may hold values from -6 to 6
- x_ents: float32 [8, 128, 768], P('rep', 'seq'), may hold values from -6 to 6
- spans: int32 [8, 128, 2], P('rep', 'seq'), may hold values from 0 to 1023, as said below
- word_mask: int32 [8, 1024], P('rep', 'seq'), may hold values 0 or 1
- ent_mask: int32 [8, 128], P('rep', 'seq'), may hold values 0 or 1
- cot_words: float32 [8, 1024, 768], P('rep', 'seq'), may hold values from -6 to 6
- cot_ents: float32 [8, 128, 768], P('rep', 'seq'), may hold values from -6 to 6
- attn_w: float32 [7, 768, 768], P(None, 'seq', 'rep')
- up_w: float32 [768, 3072], P('seq', 'rep'), may hold values from -0.21875 to 0.21875
- down_w: float32 [3072, 768], P('seq', 'rep'), may hold values from -0.109375 to 0.109375
- vecs: float32 [15, 768], replicated
- mom_attn: float32 [7, 768, 768], P(None, 'seq', 'rep'), may hold values from -1.75 to 1.75
- mom_up: float32 [768, 3072], P('seq', 'rep'), may hold values from -5 to 5
- mom_down: float32 [3072, 768], P('seq', 'rep'), may hold values from -5 to 5
- mom_vecs: float32 [15, 768], replicated, may hold values from -64 to 64
- err_attn: float32 [8, 7, 768, 768], P('rep', None, 'seq'), may hold values from -20 to 20
- err_up: float32 [8, 768, 3072], P('rep', 'seq'), may hold values from -64 to 64
- err_down: float32 [8, 3072, 768], P('rep', 'seq'), may hold values from -64 to 64
- attention_prior_right: float32 [7, 768, 8], replicated, may hold values from -6 to 6
- qf_up: float32 [3072, 8], replicated, may hold values from -6 to 6
- qf_down: float32 [768, 8], replicated, may hold values from -6 to 6
Outputs:
- out_words: float32 [8, 1024, 768], P('rep', 'seq')
- out_ents: float32 [8, 128, 768], P('rep', 'seq')
- grad_words: float32 [8, 1024, 768], P('rep', 'seq')
- grad_ents: float32 [8, 128, 768], P('rep', 'seq')
- new_attn: float32 [7, 768, 768], P(None, 'seq', 'rep')
- new_up: float32 [768, 3072], P('seq', 'rep')
- new_down: float32 [3072, 768], P('seq', 'rep')
- new_vecs: float32 [15, 768], replicated
- next_mom_attn: float32 [7, 768, 768], P(None, 'seq', 'rep')
- next_mom_up: float32 [768, 3072], P('seq', 'rep')
- next_mom_down: float32 [3072, 768], P('seq', 'rep')
- next_mom_vecs: float32 [15, 768], replicated
- next_err_attn: float32 [8, 7, 768, 768], P('rep', None, 'seq')
- next_err_up: float32 [8, 768, 3072], P('rep', 'seq')
- next_err_down: float32 [8, 3072, 768], P('rep', 'seq')
- p_attn: float32 [7, 768, 8], P(None, 'seq')
- p_up: float32 [768, 8], P('seq')
- p_down: float32 [3072, 8], P('seq')
- q_attn: float32 [7, 768, 8], replicated
- q_up: float32 [3072, 8], replicated
- q_down: float32 [768, 8], replicated
The draws below stay inside these ranges and needn't reach their ends.
Inputs may be any that keep to these rules, and one draw needn't show every extreme that they name: spans[b, e, 0] and spans[b, e, 1] are the first and last word of entity e of sequence b; a span holds 1 to 16 words.
All inputs are finite; a program needn't handle non-finite values. No bound on the sum of `word_mask` or of `ent_mask` on one device may be relied on, other than what follows from the above.
Results may differ from the reference program's by a relative error of at most 0.025.
The reference program's roundings to bfloat16 on the way count: a program that leaves them out, or rounds other values in their place, can miss the bound.
Values may be sent and summed in bfloat16 or wider, within the bound.
No kernel may reach another device: no remote copies, remote signals or barrier semaphores. Data moves between devices by JAX's collectives and lax.ppermute only.
A program may use at most 192 MiB of HBM per device.

```python
import math
import jax
import jax.numpy as jnp
from jax import lax

D = 768
HEADS = 12
FF = 3072
WORDS = 1024
ENTS = 128
SPAN = 16
RANK = 8
SEQS = 1
BATCH = 8
N_REP = 8


def draw_spans(key, part):
    first_key, second_key = jax.random.split(jax.random.fold_in(key, 7))
    lengths = jax.random.randint(first_key, (BATCH, ENTS), 1, SPAN + 1)
    starts = jax.random.randint(second_key, (BATCH, ENTS), 0, WORDS - SPAN + 1)
    starts = starts.at[0, 0].set(0).at[0, 1].set(WORDS - SPAN)
    lengths = lengths.at[0, 0].set(SPAN).at[0, 1].set(SPAN).at[0, 2].set(1)
    return jnp.stack([starts, starts + lengths - 1], -1).astype(jnp.int32)


def draw_attn_w(key, part):
    scales = jnp.array([1.5, 1.5, 1.5, 1.5, 1.0, 1.0, ((WORDS + ENTS) / 10.0) ** 0.5], jnp.float32) / D ** 0.5
    noise = jax.random.normal(key, (7, D, D), jnp.float32)
    return noise * scales[:, None, None]


def draw_vecs(key, part):
    noise = jax.random.normal(key, (15, D), jnp.float32)
    scales = jnp.array([0.3] * 7 + [0.1, 0.3, 0.1, 0.3] + [0.3] * 4, jnp.float32)
    shifts = jnp.array([0.0] * 7 + [1.0, 0.0, 1.0, 0.0] + [0.0] * 4, jnp.float32)
    return noise * scales[:, None] + shifts[:, None]


def with_ends(values, rng, low, largest):
    spot = [jax.random.randint(jax.random.fold_in(rng, axis), (), 0, length) for axis, length in enumerate(values.shape)]
    main_axis = values.shape.index(max(values.shape))
    next_to = spot[:main_axis] + [(spot[main_axis] + 1) % values.shape[main_axis]] + spot[main_axis + 1:]
    return values.at[tuple(spot)].set(low).at[tuple(next_to)].set(largest)


def block_levels(stream_key, shape, shards, low, high):
    factor_of, own = 1.0, jax.random.fold_in(stream_key, 6)
    for dim, parts in shards:
        heights = jnp.exp(jax.random.uniform(jax.random.fold_in(own, dim), (parts,), jnp.float32, low / len(shards), high / len(shards)))
        factor_of = factor_of * jnp.repeat(heights, shape[dim] // parts).reshape([-1 if axis == dim else 1 for axis in range(len(shape))])
    return factor_of


def centred(stream_key, dims, deviation, reach, cuts=(), kind=jnp.bfloat16):
    values = deviation * jax.random.normal(stream_key, dims, jnp.float32)
    if cuts:
        values = values * block_levels(stream_key, dims, cuts, -0.22, 0.18)
    return jnp.clip(values, -reach, reach).astype(kind)


def setup_inputs(seed: int = 0) -> dict:
    seeds = jax.random.split(jax.random.key(seed), 22)
    x_words = centred(seeds[0], (BATCH, WORDS, D), 1.0, 6.0, ((0, 8), (1, 4)), jnp.float32)
    x_ents = centred(seeds[1], (BATCH, ENTS, D), 1.0, 6.0, ((0, 8), (1, 4)), jnp.float32)
    spans = draw_spans(jax.random.fold_in(seeds[21], 71), 0)
    word_mask = with_ends((jax.random.randint(seeds[3], (BATCH, WORDS), 0, 8) < 7).astype(jnp.int32), jax.random.fold_in(seeds[3], 1), 0, 1)
    ent_mask = with_ends((jax.random.randint(seeds[4], (BATCH, ENTS), 0, 8) < 7).astype(jnp.int32), jax.random.fold_in(seeds[4], 1), 0, 1)
    cot_words = centred(seeds[5], (BATCH, WORDS, D), 1.0, 6.0, ((0, 8), (1, 4)), jnp.float32)
    cot_ents = centred(seeds[6], (BATCH, ENTS, D), 1.0, 6.0, ((0, 8), (1, 4)), jnp.float32)
    attn_w = draw_attn_w(jax.random.fold_in(seeds[21], 71), 0)
    up_w = centred(seeds[8], (D, FF), D ** -0.5, 0.21875, ((0, 4), (1, 8)), jnp.float32)
    down_w = centred(seeds[9], (FF, D), FF ** -0.5, 0.109375, ((0, 4), (1, 8)), jnp.float32)
    vecs = draw_vecs(jax.random.fold_in(seeds[21], 71), 0)
    mom_attn = centred(seeds[11], (7, D, D), (0.01 * (SEQS * (WORDS + ENTS)) ** 0.5 * N_REP ** -0.5), 1.75, ((1, 4), (2, 8)), jnp.float32)
    mom_up = centred(seeds[12], (D, FF), (0.03 * (SEQS * (WORDS + ENTS)) ** 0.5 * N_REP ** -0.5), 5.0, ((0, 4), (1, 8)), jnp.float32)
    mom_down = centred(seeds[13], (FF, D), (0.03 * (SEQS * (WORDS + ENTS)) ** 0.5 * N_REP ** -0.5), 5.0, ((0, 4), (1, 8)), jnp.float32)
    mom_vecs = centred(seeds[14], (15, D), ((SEQS * (WORDS + ENTS)) ** 0.5 * N_REP ** -0.5), 64.0, (), jnp.float32)
    err_attn = centred(seeds[15], (N_REP, 7, D, D), (0.1 * (SEQS * (WORDS + ENTS)) ** 0.5), 20.0, ((0, 8), (2, 4)), jnp.float32)
    err_up = centred(seeds[16], (N_REP, D, FF), (0.3 * (SEQS * (WORDS + ENTS)) ** 0.5), 64.0, ((0, 8), (1, 4)), jnp.float32)
    err_down = centred(seeds[17], (N_REP, FF, D), (0.3 * (SEQS * (WORDS + ENTS)) ** 0.5), 64.0, ((0, 8), (1, 4)), jnp.float32)
    attention_prior_right = centred(seeds[18], (7, D, RANK), 1.0, 6.0, (), jnp.float32)
    qf_up = centred(seeds[19], (FF, RANK), 1.0, 6.0, (), jnp.float32)
    qf_down = centred(seeds[20], (D, RANK), 1.0, 6.0, (), jnp.float32)
    return dict(x_words=x_words, x_ents=x_ents, spans=spans, word_mask=word_mask, ent_mask=ent_mask, cot_words=cot_words, cot_ents=cot_ents, attn_w=attn_w, up_w=up_w, down_w=down_w, vecs=vecs, mom_attn=mom_attn, mom_up=mom_up, mom_down=mom_down, mom_vecs=mom_vecs, err_attn=err_attn, err_up=err_up, err_down=err_down, attention_prior_right=attention_prior_right, qf_up=qf_up, qf_down=qf_down)


HIGH_PRECISION = lax.Precision.HIGHEST
EPS = 1e-05
MASK_FILL = 30000.0
MOMENTUM = 0.9

@jax.custom_vjp
def low(v):
    return lax.optimization_barrier(v.astype(jnp.bfloat16)).astype(jnp.float32)

@jax.custom_vjp
def low_back(v):
    return v

def low_keep(v):
    return (low(v), None)

def low_pass(kept, grad):
    return (grad,)

def back_keep(v):
    return (v, None)

def back_low(kept, grad):
    return (low(grad),)
low.defvjp(low_keep, low_pass)
low_back.defvjp(back_keep, back_low)

def span_mean(spans, model_width):
    starts = spans[..., 0]
    finals = spans[..., 1]
    lengths = (finals - starts + 1).astype(jnp.float32)
    offsets = jnp.arange(SPAN, dtype=jnp.int32)
    places = (starts[..., None] + offsets).astype(jnp.float32)
    shares = (offsets <= (finals - starts)[..., None]).astype(jnp.float32) / lengths[..., None]
    half_width = model_width // 2
    rates = jnp.exp(jnp.arange(half_width).astype(jnp.float32) * (-2.0 * math.log(10000.0) / model_width))
    angles = places[..., None] * rates
    table = jnp.concatenate([jnp.sin(angles), jnp.cos(angles)], -1)
    return lax.optimization_barrier(jnp.sum(table * shares[..., None], axis=-2))

def layer_norm(hidden, gain, shift):
    center = hidden - lax.optimization_barrier(jnp.mean(hidden, -1, keepdims=True))
    rstd = lax.rsqrt(lax.optimization_barrier(jnp.mean(center * center, -1, keepdims=True)) + EPS)
    return center * rstd * gain + shift

def dense(left, right):
    return jnp.dot(left, right, precision=HIGH_PRECISION)

def forward(attn_w, up_w, down_w, vecs, word_in, ent_in, span_in, word_live, ent_live):
    model_width = word_in.shape[-1]
    head_dim = model_width // HEADS
    input_arrays = jnp.concatenate([word_in, ent_in + span_mean(span_in, model_width)], 0)
    rows_all = input_arrays.shape[0]
    inputs_low = low(input_arrays)
    w_attn = low(attn_w)
    w_up = low(up_w)
    w_down = low(down_w)
    word_low = inputs_low[:WORDS]
    ent_low = inputs_low[WORDS:]
    word_bias = jnp.concatenate([jnp.broadcast_to(vecs[0], (WORDS, model_width)), jnp.broadcast_to(vecs[2], (ENTS, model_width))], 0)
    ent_bias = jnp.concatenate([jnp.broadcast_to(vecs[1], (WORDS, model_width)), jnp.broadcast_to(vecs[3], (ENTS, model_width))], 0)
    query_word = low(0.125 * (low_back(jnp.concatenate([dense(word_low, w_attn[0]), dense(ent_low, w_attn[2])], 0)) + word_bias))
    query_ent = low(0.125 * (low_back(jnp.concatenate([dense(word_low, w_attn[1]), dense(ent_low, w_attn[3])], 0)) + ent_bias))
    keys = low(low_back(dense(inputs_low, w_attn[4])))
    values = low(low_back(dense(inputs_low, w_attn[5])) + vecs[4])
    query_word = query_word.reshape(rows_all, HEADS, head_dim)
    query_ent = query_ent.reshape(rows_all, HEADS, head_dim)
    keys = keys.reshape(rows_all, HEADS, head_dim)
    values = values.reshape(rows_all, HEADS, head_dim)
    score_word = jnp.einsum('qhd,khd->hqk', query_word, keys[:WORDS], precision=HIGH_PRECISION)
    score_ent = jnp.einsum('qhd,khd->hqk', query_ent, keys[WORDS:], precision=HIGH_PRECISION)
    scores = low_back(jnp.concatenate([score_word, score_ent], -1))
    live = jnp.concatenate([word_live, ent_live], 0).astype(jnp.float32)
    scores = scores + (live - 1.0) * MASK_FILL
    row_top = lax.optimization_barrier(jnp.max(scores, -1, keepdims=True))
    weights = jnp.exp(scores - row_top)
    row_total = lax.optimization_barrier(jnp.sum(weights, -1))
    unnorm = low_back(jnp.einsum('hqk,khd->qhd', low(weights), values, precision=HIGH_PRECISION))
    attn = unnorm / jnp.transpose(row_total)[:, :, None]
    attn_low = low(attn.reshape(rows_all, model_width))
    branch = low_back(dense(attn_low, w_attn[6])) + vecs[5]
    mid = layer_norm(input_arrays + branch, vecs[7], vecs[8])
    pre = low_back(dense(low(mid), w_up)) + vecs[11:15].reshape(-1)
    act_low = low(jax.nn.gelu(pre, approximate=False))
    ffn = low_back(dense(act_low, w_down)) + vecs[6]
    return layer_norm(mid + ffn, vecs[9], vecs[10])

def orthonormal(left):
    gram = jnp.dot(left.T, left, precision=HIGH_PRECISION)
    lower = jnp.linalg.cholesky(gram)
    return jax.scipy.linalg.solve_triangular(lower, left.T, lower=True).T

def compress(gradient_list, errors, warm):
    full = gradient_list + errors
    left = lax.optimization_barrier(jnp.mean(jnp.einsum('wij,jr->wir', full, warm, precision=HIGH_PRECISION), 0))
    orth = orthonormal(left)
    right = lax.optimization_barrier(jnp.mean(jnp.einsum('wij,ir->wjr', full, orth, precision=HIGH_PRECISION), 0))
    approx = jnp.dot(orth, right.T, precision=HIGH_PRECISION)
    return (orth, right, approx, full - approx)

def reference(x_words, x_ents, spans, word_mask, ent_mask, cot_words, cot_ents, attn_w, up_w, down_w, vecs, mom_attn, mom_up, mom_down, mom_vecs, err_attn, err_up, err_down, attention_prior_right, qf_up, qf_down):

    def regroup(array):
        return array.reshape((N_REP, SEQS) + array.shape[1:])
    items = tuple((regroup(array) for array in (x_words, x_ents, spans, word_mask, ent_mask, cot_words, cot_ents)))

    def one_sequence(carry, item):
        word_in, ent_in, span_in, word_live, ent_live, word_cot, ent_cot = item

        def layer(arg_attn, arg_up, arg_down, arg_vecs, arg_words, arg_ents):
            return forward(arg_attn, arg_up, arg_down, arg_vecs, arg_words, arg_ents, span_in, word_live, ent_live)
        result, pullback = jax.vjp(layer, attn_w, up_w, down_w, vecs, word_in, ent_in)
        gradient_list = pullback(jnp.concatenate([word_cot, ent_cot], 0))
        carry = tuple((total + grad for total, grad in zip(carry, gradient_list[:4])))
        return (carry, (result[:WORDS], result[WORDS:], gradient_list[4], gradient_list[5]))

    def one_worker(item):
        start_sums = (jnp.zeros_like(attn_w), jnp.zeros_like(up_w), jnp.zeros_like(down_w), jnp.zeros_like(vecs))
        return lax.scan(one_sequence, start_sums, item)
    sums, outs = lax.map(one_worker, items)
    grad_attn, grad_up, grad_down, grad_vecs = sums

    def flatten(array):
        return array.reshape((N_REP * SEQS,) + array.shape[2:])
    out_words, out_ents, grad_words, grad_ents = (flatten(array) for array in outs)
    p_attn, q_attn, attention_estimate, next_err_attn = jax.vmap(compress, in_axes=(1, 1, 0), out_axes=(0, 0, 0, 1))(grad_attn, err_attn, attention_prior_right)
    p_up, q_up, approx_up, next_err_up = compress(grad_up, err_up, qf_up)
    p_down, q_down, approx_down, next_err_down = compress(grad_down, err_down, qf_down)
    lr_mat = 1.5 * math.sqrt(N_REP / (SEQS * (WORDS + ENTS)))
    lr_vec = 0.2 * math.sqrt(N_REP / (SEQS * (WORDS + ENTS)))
    next_mom_attn = MOMENTUM * mom_attn + attention_estimate
    next_mom_up = MOMENTUM * mom_up + approx_up
    next_mom_down = MOMENTUM * mom_down + approx_down
    next_mom_vecs = MOMENTUM * mom_vecs + lax.optimization_barrier(jnp.mean(grad_vecs, 0))
    new_attn = attn_w - lr_mat * next_mom_attn
    new_up = up_w - lr_mat * next_mom_up
    new_down = down_w - lr_mat * next_mom_down
    new_vecs = vecs - lr_vec * next_mom_vecs
    return (out_words, out_ents, grad_words, grad_ents, new_attn, new_up, new_down, new_vecs, next_mom_attn, next_mom_up, next_mom_down, next_mom_vecs, next_err_attn, next_err_up, next_err_down, p_attn, p_up, p_down, q_attn, q_up, q_down)
```

```python
import functools
import math

import jax
import jax.numpy as jnp
from jax import lax
from jax.experimental import pallas as pl
from jax.experimental.pallas import tpu as pltpu
from jax.sharding import PartitionSpec as P

HEADS = 12
WORDS = 1024
ENTS = 128
SPAN = 16
SEQS = 1


HIGH_PRECISION = lax.Precision.HIGHEST
EPS = 1e-05
MASK_FILL = 30000.0
MOMENTUM = 0.9


def span_mean(spans, model_width):
    starts = spans[..., 0]
    finals = spans[..., 1]
    lengths = (finals - starts + 1).astype(jnp.float32)
    offsets = jnp.arange(SPAN, dtype=jnp.int32)
    places = (starts[..., None] + offsets).astype(jnp.float32)
    shares = (offsets <= (finals - starts)[..., None]).astype(jnp.float32) / lengths[..., None]
    half_width = model_width // 2
    rates = jnp.exp(
        jnp.arange(half_width).astype(jnp.float32) * (-2.0 * math.log(10000.0) / model_width)
    )
    angles = places[..., None] * rates
    table = jnp.concatenate([jnp.sin(angles), jnp.cos(angles)], -1)
    return jnp.sum(table * shares[..., None], axis=-2)


def layer_norm(hidden, gain, shift):
    center = hidden - jnp.mean(hidden, -1, keepdims=True)
    rstd = lax.rsqrt(jnp.mean(center * center, -1, keepdims=True) + EPS)
    normed = center * rstd
    return (normed * gain + shift, normed, rstd)


def norm_back(grad, normed, rstd, gain):
    dnormed = grad * gain
    grad_in = rstd * (
        dnormed
        - jnp.mean(dnormed, -1, keepdims=True)
        - normed * jnp.mean(dnormed * normed, -1, keepdims=True)
    )
    return (grad_in, jnp.sum(grad * normed, axis=(0, 1)), jnp.sum(grad, axis=(0, 1)))


def gelu_exact(value):
    return jax.nn.gelu(value, approximate=False)


def project(row_entries, weight_matrix):
    return jnp.einsum("thq,qo->tho", row_entries, weight_matrix, preferred_element_type=jnp.float32)


def project_back(row_entries, weight_matrix):
    return jnp.einsum("hpf,zf->hpz", row_entries, weight_matrix, preferred_element_type=jnp.float32)


def weight_grad(input_arrays, gradient_list):
    return jnp.einsum(
        "cev,ceg->vg", input_arrays, gradient_list, preferred_element_type=jnp.float32
    )


def split_keys(pieces, words_dev, ents_dev, head_count):
    key_piece, live_piece = pieces
    batch_rows = key_piece.shape[0]
    both = key_piece.shape[2]
    model_width = both // 2
    head_dim = model_width // head_count
    rows_dev = words_dev + ents_dev
    blocks = key_piece.shape[1] // rows_dev
    grouped = key_piece.reshape(batch_rows, blocks, rows_dev, both)
    live_grouped = live_piece.reshape(batch_rows, blocks, rows_dev)
    word_part = grouped[:, :, :words_dev].reshape(batch_rows, blocks * words_dev, both)
    ent_part = grouped[:, :, words_dev:].reshape(batch_rows, blocks * ents_dev, both)
    keys_word = word_part[..., :model_width].reshape(batch_rows, -1, head_count, head_dim)
    keys_ent = ent_part[..., :model_width].reshape(batch_rows, -1, head_count, head_dim)
    values = jnp.concatenate(
        [word_part[..., model_width:], ent_part[..., model_width:]], 1
    ).reshape(batch_rows, -1, head_count, head_dim)
    live = jnp.concatenate(
        [
            live_grouped[:, :, :words_dev].reshape(batch_rows, -1),
            live_grouped[:, :, words_dev:].reshape(batch_rows, -1),
        ],
        1,
    )
    offsets = (live.astype(jnp.float32) - 1.0) * MASK_FILL
    return (keys_word, keys_ent, values, offsets, blocks)


def score_block(query_word, query_ent, keys_word, keys_ent, offsets):
    score_word = jnp.einsum(
        "sqhd,skhd->shqk", query_word, keys_word, preferred_element_type=jnp.float32
    )
    score_ent = jnp.einsum(
        "sqhd,skhd->shqk", query_ent, keys_ent, preferred_element_type=jnp.float32
    )
    return jnp.concatenate([score_word, score_ent], -1) + offsets[:, None, None, :]


def flat_heads(array):
    return array.reshape(array.shape[0], array.shape[1], -1)


def join_rows(grad_keys_word, grad_keys_ent, grad_values, blocks, words_dev, ents_dev):
    batch_rows = grad_keys_word.shape[0]
    word_count = grad_keys_word.shape[1]
    word_rows = jnp.concatenate(
        [flat_heads(grad_keys_word), flat_heads(grad_values[:, :word_count])], -1
    )
    ent_rows = jnp.concatenate(
        [flat_heads(grad_keys_ent), flat_heads(grad_values[:, word_count:])], -1
    )
    word_rows = word_rows.reshape(batch_rows, blocks, words_dev, -1)
    ent_rows = ent_rows.reshape(batch_rows, blocks, ents_dev, -1)
    return jnp.concatenate([word_rows, ent_rows], 2).reshape(
        batch_rows, blocks * (words_dev + ents_dev), -1
    )


def from_gram(left, gram):
    lower = jnp.linalg.cholesky(gram)
    return jax.scipy.linalg.solve_triangular(lower, left.T, lower=True).T


def orthonormal(left):
    return from_gram(left, jnp.dot(left.T, left, precision=HIGH_PRECISION))


def on_device(
    x_words,
    x_ents,
    spans,
    word_mask,
    ent_mask,
    cot_words,
    cot_ents,
    attn_w,
    up_w,
    down_w,
    vecs,
    mom_attn,
    mom_up,
    mom_down,
    mom_vecs,
    err_attn,
    err_up,
    err_down,
    attention_prior_right,
    qf_up,
    qf_down,
):
    batch_rows, words_dev, model_width = x_words.shape
    ents_dev = x_ents.shape[1]
    rows_dev = words_dev + ents_dev
    head_count = HEADS
    head_dim = model_width // head_count
    hidden_width = up_w.shape[1] * lax.axis_size("rep")
    seq_count = lax.axis_size("seq")
    rep_count = lax.axis_size("rep")
    seq_index = lax.axis_index("seq")
    rep_index = lax.axis_index("rep")
    lowered = jnp.bfloat16
    column_parts = (
        lax.all_gather(attn_w.astype(lowered), "rep", axis=2, tiled=True),
        lax.all_gather(up_w.astype(lowered), "rep", axis=1, tiled=True),
        lax.all_gather(down_w.astype(lowered), "rep", axis=1, tiled=True),
    )
    w_attn, w_up, w_down = (
        lax.all_gather(column_parts[0], "seq", axis=1, tiled=True),
        lax.all_gather(column_parts[1], "seq", axis=0, tiled=True),
        lax.all_gather(column_parts[2], "seq", axis=0, tiled=True),
    )
    input_arrays = jnp.concatenate([x_words, x_ents + span_mean(spans, model_width)], 1)
    inputs_low = input_arrays.astype(lowered)
    word_low = inputs_low[:, :words_dev]
    ent_low = inputs_low[:, words_dev:]
    query_word = (
        jnp.concatenate(
            [project(word_low, w_attn[0]) + vecs[0], project(ent_low, w_attn[2]) + vecs[2]], 1
        )
        * 0.125
    ).astype(lowered)
    query_ent = (
        jnp.concatenate(
            [project(word_low, w_attn[1]) + vecs[1], project(ent_low, w_attn[3]) + vecs[3]], 1
        )
        * 0.125
    ).astype(lowered)
    keys_low = project(inputs_low, w_attn[4]).astype(lowered)
    values_low = (project(inputs_low, w_attn[5]) + vecs[4]).astype(lowered)
    key_rows = jnp.concatenate([keys_low, values_low], -1)
    key_live = jnp.concatenate([word_mask, ent_mask], 1).astype(lowered)
    heads_word = query_word.reshape(batch_rows, rows_dev, head_count, head_dim)
    heads_ent = query_ent.reshape(batch_rows, rows_dev, head_count, head_dim)
    forward_row_top = jnp.full((batch_rows, head_count, rows_dev), -jnp.inf, jnp.float32)
    row_total = jnp.zeros((batch_rows, head_count, rows_dev), jnp.float32)
    weighted = jnp.zeros((batch_rows, rows_dev, head_count, head_dim), jnp.float32)
    keys_word, keys_ent, values, offsets, blocks = split_keys(
        (
            lax.all_gather(key_rows, "seq", axis=1, tiled=True),
            lax.all_gather(key_live, "seq", axis=1, tiled=True),
        ),
        words_dev,
        ents_dev,
        head_count,
    )
    scores = score_block(heads_word, heads_ent, keys_word, keys_ent, offsets)
    new_top = jnp.max(scores, -1)
    factor = jnp.exp(forward_row_top - new_top)
    weights = jnp.exp(scores - new_top[..., None])
    row_total = row_total * factor + jnp.sum(weights, -1)
    weighted = weighted * jnp.transpose(factor, (0, 2, 1))[..., None] + jnp.einsum(
        "shqk,skhd->sqhd", weights.astype(lowered), values, preferred_element_type=jnp.float32
    )
    row_top, row_total, weighted = (new_top, row_total, weighted)
    total_rows = jnp.transpose(row_total, (0, 2, 1))[..., None]
    attn = weighted / total_rows
    attn_low = attn.reshape(batch_rows, rows_dev, model_width).astype(lowered)
    branch = project(attn_low, w_attn[6]) + vecs[5]
    mid, normed_one, rstd_one = layer_norm(input_arrays + branch, vecs[7], vecs[8])
    mid_low = mid.astype(lowered)
    pre = project(mid_low, w_up) + vecs[11:15].reshape(hidden_width)
    act_low = gelu_exact(pre).astype(lowered)
    ffn = project(act_low, w_down) + vecs[6]
    result, normed_two, rstd_two = layer_norm(mid + ffn, vecs[9], vecs[10])
    grad_result = jnp.concatenate([cot_words, cot_ents], 1)
    grad_two, gain_two, shift_two = norm_back(grad_result, normed_two, rstd_two, vecs[9])
    bias_down = jnp.sum(grad_two, axis=(0, 1))
    grad_ffn_low = grad_two.astype(lowered)
    grad_down = weight_grad(act_low, grad_ffn_low)
    grad_act = project_back(grad_ffn_low, w_down)
    unused_value, gelu_pull = jax.vjp(gelu_exact, pre)
    grad_pre = gelu_pull(grad_act)[0]
    bias_up = jnp.sum(grad_pre, axis=(0, 1))
    grad_pre_low = grad_pre.astype(lowered)
    grad_up = weight_grad(mid_low, grad_pre_low)
    grad_mid = grad_two + project_back(grad_pre_low, w_up)
    grad_one, gain_one, shift_one = norm_back(grad_mid, normed_one, rstd_one, vecs[7])
    bias_out = jnp.sum(grad_one, axis=(0, 1))
    grad_branch_low = grad_one.astype(lowered)
    grad_out_proj = weight_grad(attn_low, grad_branch_low)
    grad_attn = project_back(grad_branch_low, w_attn[6]).reshape(
        batch_rows, rows_dev, head_count, head_dim
    )
    grad_unnorm = (grad_attn / total_rows).astype(lowered)
    delta_rows = jnp.transpose(jnp.sum(grad_attn * attn, -1), (0, 2, 1)) / row_total
    keys_word, keys_ent, values, offsets, blocks = split_keys(
        (
            lax.all_gather(key_rows, "seq", axis=1, tiled=True),
            lax.all_gather(key_live, "seq", axis=1, tiled=True),
        ),
        words_dev,
        ents_dev,
        head_count,
    )
    scores = score_block(heads_word, heads_ent, keys_word, keys_ent, offsets)
    weights = jnp.exp(scores - row_top[..., None])
    grad_weights = jnp.einsum(
        "sqhd,skhd->shqk", grad_unnorm, values, preferred_element_type=jnp.float32
    )
    grad_scores = (weights * (grad_weights - delta_rows[..., None])).astype(lowered)
    word_count = keys_word.shape[1]
    scores_word = grad_scores[..., :word_count]
    scores_ent = grad_scores[..., word_count:]
    grad_query_word = jnp.einsum(
        "shqk,skhd->sqhd", scores_word, keys_word, preferred_element_type=jnp.float32
    )
    grad_query_ent = jnp.einsum(
        "shqk,skhd->sqhd", scores_ent, keys_ent, preferred_element_type=jnp.float32
    )
    grad_keys_word = jnp.einsum(
        "shqk,sqhd->skhd", scores_word, heads_word, preferred_element_type=jnp.float32
    )
    grad_keys_ent = jnp.einsum(
        "shqk,sqhd->skhd", scores_ent, heads_ent, preferred_element_type=jnp.float32
    )
    grad_values = jnp.einsum(
        "shqk,sqhd->skhd", weights.astype(lowered), grad_unnorm, preferred_element_type=jnp.float32
    )
    piece_grad = join_rows(grad_keys_word, grad_keys_ent, grad_values, blocks, words_dev, ents_dev)
    grad_rows = piece_grad
    grad_query_word, grad_query_ent, grad_rows = (grad_query_word, grad_query_ent, grad_rows)
    own_rows = lax.psum_scatter(
        grad_rows.astype(jnp.bfloat16), "seq", scatter_dimension=1, tiled=True
    ).astype(jnp.float32)
    grad_keys = own_rows[..., :model_width]
    grad_values = own_rows[..., model_width:]
    bias_values = jnp.sum(grad_values, axis=(0, 1))
    keys_grad_low = grad_keys.astype(lowered)
    values_grad_low = grad_values.astype(lowered)
    grad_key_w = weight_grad(inputs_low, keys_grad_low)
    grad_value_w = weight_grad(inputs_low, values_grad_low)
    inner_word = grad_query_word.reshape(batch_rows, rows_dev, model_width) * 0.125
    inner_ent = grad_query_ent.reshape(batch_rows, rows_dev, model_width) * 0.125
    bias_query = [
        jnp.sum(inner_word[:, :words_dev], axis=(0, 1)),
        jnp.sum(inner_ent[:, :words_dev], axis=(0, 1)),
        jnp.sum(inner_word[:, words_dev:], axis=(0, 1)),
        jnp.sum(inner_ent[:, words_dev:], axis=(0, 1)),
    ]
    inner_word_low = inner_word.astype(lowered)
    inner_ent_low = inner_ent.astype(lowered)
    grad_query_mats = [
        weight_grad(word_low, inner_word_low[:, :words_dev]),
        weight_grad(word_low, inner_ent_low[:, :words_dev]),
        weight_grad(ent_low, inner_word_low[:, words_dev:]),
        weight_grad(ent_low, inner_ent_low[:, words_dev:]),
    ]
    back_keys = project_back(keys_grad_low, w_attn[4]) + project_back(values_grad_low, w_attn[5])
    back_word = project_back(inner_word_low[:, :words_dev], w_attn[0]) + project_back(
        inner_ent_low[:, :words_dev], w_attn[1]
    )
    back_ent = project_back(inner_word_low[:, words_dev:], w_attn[2]) + project_back(
        inner_ent_low[:, words_dev:], w_attn[3]
    )
    grad_inputs = grad_one + back_keys + jnp.concatenate([back_word, back_ent], 1)
    grad_attn_w = jnp.stack(grad_query_mats + [grad_key_w, grad_value_w, grad_out_proj])
    vec_grad = jnp.concatenate(
        [
            jnp.stack(
                bias_query
                + [bias_values, bias_out, bias_down, gain_one, shift_one, gain_two, shift_two]
            ),
            bias_up.reshape(4, model_width),
        ],
        0,
    )
    rows_attn, rows_up, rows_down = (
        lax.psum_scatter(
            grad_attn_w.astype(jnp.bfloat16), "seq", scatter_dimension=1, tiled=True
        ).astype(jnp.float32),
        lax.psum_scatter(
            grad_up.astype(jnp.bfloat16), "seq", scatter_dimension=0, tiled=True
        ).astype(jnp.float32),
        lax.psum_scatter(
            grad_down.astype(jnp.bfloat16), "seq", scatter_dimension=0, tiled=True
        ).astype(jnp.float32),
    )
    attention_full_gradient = rows_attn + err_attn[0]
    full_up = rows_up + err_up[0]
    full_down = rows_down + err_down[0]
    attention_left_factor = jnp.einsum(
        "vcg,vgo->vco", attention_full_gradient, attention_prior_right, precision=HIGH_PRECISION
    )
    left_up = jnp.dot(full_up, qf_up, precision=HIGH_PRECISION)
    left_down = jnp.dot(full_down, qf_down, precision=HIGH_PRECISION)
    count_attn = attention_full_gradient.shape[1]
    count_up = full_up.shape[0]
    count_down = full_down.shape[0]
    placed_attn = lax.dynamic_update_slice_in_dim(
        jnp.zeros((7, count_attn * seq_count, attention_left_factor.shape[2]), jnp.float32),
        attention_left_factor,
        seq_index * count_attn,
        1,
    )
    placed_up = lax.dynamic_update_slice_in_dim(
        jnp.zeros((count_up * seq_count, left_up.shape[1]), jnp.float32),
        left_up,
        seq_index * count_up,
        0,
    )
    placed_down = lax.dynamic_update_slice_in_dim(
        jnp.zeros((count_down * seq_count, left_down.shape[1]), jnp.float32),
        left_down,
        seq_index * count_down,
        0,
    )
    summed_attn, summed_up, summed_down = lax.psum(
        (placed_attn, placed_up, placed_down), ("seq", "rep")
    )
    orth_attn = jax.vmap(orthonormal)(summed_attn / rep_count)
    orth_up = orthonormal(summed_up / rep_count)
    orth_down = orthonormal(summed_down / rep_count)
    attention_local_gradient = lax.dynamic_slice_in_dim(
        orth_attn, seq_index * count_attn, count_attn, 1
    )
    own_up = lax.dynamic_slice_in_dim(orth_up, seq_index * count_up, count_up, 0)
    own_down = lax.dynamic_slice_in_dim(orth_down, seq_index * count_down, count_down, 0)
    right_parts = (
        jnp.einsum(
            "dpl,dpg->dgl",
            attention_local_gradient,
            attention_full_gradient,
            precision=HIGH_PRECISION,
        ),
        jnp.dot(full_up.T, own_up, precision=HIGH_PRECISION),
        jnp.dot(full_down.T, own_down, precision=HIGH_PRECISION),
        vec_grad,
    )
    attention_right_factor, right_up, right_down, vec_total = lax.psum(
        (right_parts[0], right_parts[1], right_parts[2], right_parts[3]), ("seq", "rep")
    )
    attention_right_factor = attention_right_factor / rep_count
    right_up = right_up / rep_count
    right_down = right_down / rep_count
    vec_mean = vec_total / rep_count
    attention_estimate = jnp.einsum(
        "whg,wng->whn", attention_local_gradient, attention_right_factor, precision=HIGH_PRECISION
    )
    approx_up = jnp.dot(own_up, right_up.T, precision=HIGH_PRECISION)
    approx_down = jnp.dot(own_down, right_down.T, precision=HIGH_PRECISION)
    next_err_attn = (attention_full_gradient - attention_estimate)[None]
    next_err_up = (full_up - approx_up)[None]
    next_err_down = (full_down - approx_down)[None]
    cols_attn = attn_w.shape[2]
    cols_up = up_w.shape[1]
    cols_down = down_w.shape[1]
    step_attn = lax.dynamic_slice_in_dim(attention_estimate, rep_index * cols_attn, cols_attn, 2)
    step_up = lax.dynamic_slice_in_dim(approx_up, rep_index * cols_up, cols_up, 1)
    step_down = lax.dynamic_slice_in_dim(approx_down, rep_index * cols_down, cols_down, 1)
    lr_mat = 1.5 * math.sqrt(rep_count / (SEQS * (WORDS + ENTS)))
    lr_vec = 0.2 * math.sqrt(rep_count / (SEQS * (WORDS + ENTS)))
    next_mom_attn = MOMENTUM * mom_attn + step_attn
    next_mom_up = MOMENTUM * mom_up + step_up
    next_mom_down = MOMENTUM * mom_down + step_down
    next_mom_vecs = MOMENTUM * mom_vecs + vec_mean
    new_attn = attn_w - lr_mat * next_mom_attn
    new_up = up_w - lr_mat * next_mom_up
    new_down = down_w - lr_mat * next_mom_down
    new_vecs = vecs - lr_vec * next_mom_vecs
    return (
        result[:, :words_dev],
        result[:, words_dev:],
        grad_inputs[:, :words_dev],
        grad_inputs[:, words_dev:],
        new_attn,
        new_up,
        new_down,
        new_vecs,
        next_mom_attn,
        next_mom_up,
        next_mom_down,
        next_mom_vecs,
        next_err_attn,
        next_err_up,
        next_err_down,
        attention_local_gradient,
        own_up,
        own_down,
        attention_right_factor,
        right_up,
        right_down,
    )


def seq_swap(array, bits):
    size = lax.axis_size("seq")
    return lax.ppermute(array, "seq", [(i, i ^ bits) for i in range(size)])


def rep_swap(array, bits):
    size = lax.axis_size("rep")
    return lax.ppermute(array, "rep", [(i, i ^ bits) for i in range(size)])


def planes_swap(array):
    seqs, reps = lax.axis_size("seq"), lax.axis_size("rep")
    pairs = []
    for s in range(seqs):
        for r in range(reps):
            pairs.append((s * reps + r, (r // 2) * reps + 2 * s + r % 2))
    return lax.ppermute(array, ("seq", "rep"), pairs)


def gather_seq(piece):
    other_chip = seq_swap(piece, 2)
    other_core = seq_swap(piece, 1)
    return [piece, other_core, other_chip, seq_swap(other_chip, 1)]


def ordered(bit, mine, other, axis):
    return jnp.where(
        bit == 0, jnp.stack([mine, other], axis), jnp.stack([other, mine], axis)
    )


def gather_rep(piece):
    rep_index = lax.axis_index("rep")
    side, level, far = rep_index % 2, (rep_index // 2) % 2, rep_index // 4
    pair = ordered(far, piece, rep_swap(piece, 4), 0)
    pair_side = rep_swap(pair, 1)
    next_pair = rep_swap(pair, 2)
    next_side = rep_swap(next_pair, 1)
    mine = ordered(level, pair, next_pair, 1)
    other = ordered(level, pair_side, next_side, 1)
    return ordered(side, mine, other, 2).reshape((4, 2) + piece.shape)


def join_pieces(pieces, words_dev):
    return jnp.concatenate(
        [piece[:words_dev] for piece in pieces] + [piece[words_dev:] for piece in pieces], 0
    )


def scatter_rows(full, words_dev, ents_dev):
    count = 4
    first_ent = count * words_dev

    def rows(k):
        return [
            full[k * words_dev : (k + 1) * words_dev],
            full[first_ent + k * ents_dev : first_ent + (k + 1) * ents_dev],
        ]

    rows_dev = words_dev + ents_dev
    got = seq_swap(jnp.concatenate(rows(1) + rows(3), 0).astype(jnp.bfloat16), 1)
    got = got.astype(jnp.float32)
    mine = jnp.concatenate(rows(0), 0) + got[:rows_dev]
    other = jnp.concatenate(rows(2), 0) + got[rows_dev:]
    return mine + seq_swap(other.astype(jnp.bfloat16), 2).astype(jnp.float32)


def rows_norm(hidden, gain, shift):
    center = hidden - jnp.mean(hidden, -1, keepdims=True)
    rstd = lax.rsqrt(jnp.mean(center * center, -1, keepdims=True) + EPS)
    normed = center * rstd
    return (normed * gain + shift, normed, rstd)


def rows_norm_back(grad, normed, rstd, gain):
    dnormed = grad * gain
    grad_in = rstd * (
        dnormed
        - jnp.mean(dnormed, -1, keepdims=True)
        - normed * jnp.mean(dnormed * normed, -1, keepdims=True)
    )
    return (grad_in, jnp.sum(grad * normed, axis=0), jnp.sum(grad, axis=0))


def mm(left, right, left_dim=1, right_dim=0):
    return lax.dot_general(
        left, right, (((left_dim,), (right_dim,)), ((), ())), preferred_element_type=jnp.float32
    )


def nt_dot(left, right):
    return mm(left, right, 1, 1)


def tn_dot(left, right):
    return mm(left, right, 0, 0)


HEAD_DIM = 64


def attention_kernel(word_count, heads, query_ref, key_ref, offset_ref, attn_ref, low_ref, stat_ref):
    width = heads * HEAD_DIM
    rows = query_ref.shape[0]
    lane = lax.broadcasted_iota(jnp.int32, (rows, 128), 1)
    stats = jnp.zeros((rows, 128), jnp.float32)
    for h in range(heads):
        low, high = h * HEAD_DIM, (h + 1) * HEAD_DIM
        q_word = query_ref[:, low:high]
        q_ent = query_ref[:, width + low : width + high]
        k_word = key_ref[:word_count, 2 * width + low : 2 * width + high]
        k_ent = key_ref[word_count:, 2 * width + low : 2 * width + high]
        s_word = nt_dot(q_word, k_word) + offset_ref[:, :word_count]
        s_ent = nt_dot(q_ent, k_ent) + offset_ref[:, word_count:]
        top = jnp.maximum(
            jnp.max(s_word, -1, keepdims=True), jnp.max(s_ent, -1, keepdims=True)
        )
        w_word = jnp.exp(s_word - top)
        w_ent = jnp.exp(s_ent - top)
        total = jnp.sum(w_word, -1, keepdims=True) + jnp.sum(w_ent, -1, keepdims=True)
        v_word = key_ref[:word_count, 3 * width + low : 3 * width + high]
        v_ent = key_ref[word_count:, 3 * width + low : 3 * width + high]
        unnorm = mm(w_word.astype(jnp.bfloat16), v_word) + mm(w_ent.astype(jnp.bfloat16), v_ent)
        attn = unnorm / total
        attn_ref[:, low:high] = attn
        low_ref[:, low:high] = attn.astype(jnp.bfloat16)
        stats = jnp.where(lane == h, top, stats)
        stats = jnp.where(lane == heads + h, total, stats)
    stat_ref[...] = stats


def attention_forward(packed, offsets, word_count, heads, block):
    count, packed_width = packed.shape
    width = heads * HEAD_DIM
    return pl.pallas_call(
        functools.partial(attention_kernel, word_count, heads),
        grid=(count // block,),
        in_specs=[
            pl.BlockSpec((block, packed_width), lambda i: (i, 0)),
            pl.BlockSpec((count, packed_width), lambda i: (0, 0)),
            pl.BlockSpec((1, count), lambda i: (0, 0)),
        ],
        out_specs=[
            pl.BlockSpec((block, width), lambda i: (i, 0)),
            pl.BlockSpec((block, width), lambda i: (i, 0)),
            pl.BlockSpec((block, 128), lambda i: (i, 0)),
        ],
        out_shape=[
            jax.ShapeDtypeStruct((count, width), jnp.float32),
            jax.ShapeDtypeStruct((count, width), jnp.bfloat16),
            jax.ShapeDtypeStruct((count, 128), jnp.float32),
        ],
        compiler_params=pltpu.CompilerParams(dimension_semantics=("arbitrary",)),
        cost_estimate=pl.CostEstimate(
            flops=4 * count * count * width,
            bytes_accessed=6 * count * packed_width,
            transcendentals=count * count * heads,
        ),
        name="attention",
    )(packed, packed, offsets)


def attention_back_kernel(
    word_count,
    heads,
    query_ref,
    key_ref,
    offset_ref,
    attn_ref,
    stat_ref,
    grad_ref,
    dquery_ref,
    dkey_ref,
    dvalue_ref,
    key_sum,
    value_sum,
):
    width = heads * HEAD_DIM
    step = pl.program_id(0)

    @pl.when(step == 0)
    def _():
        key_sum[...] = jnp.zeros_like(key_sum)
        value_sum[...] = jnp.zeros_like(value_sum)

    for h in range(heads):
        low, high = h * HEAD_DIM, (h + 1) * HEAD_DIM
        q_word = query_ref[:, low:high]
        q_ent = query_ref[:, width + low : width + high]
        k_word = key_ref[:word_count, 2 * width + low : 2 * width + high]
        k_ent = key_ref[word_count:, 2 * width + low : 2 * width + high]
        v_word = key_ref[:word_count, 3 * width + low : 3 * width + high]
        v_ent = key_ref[word_count:, 3 * width + low : 3 * width + high]
        top = stat_ref[:, h : h + 1]
        inverse = 1.0 / stat_ref[:, heads + h : heads + h + 1]
        grad = grad_ref[:, low:high]
        delta = jnp.sum(grad * attn_ref[:, low:high], -1, keepdims=True) * inverse
        grad_low = (grad * inverse).astype(jnp.bfloat16)
        w_word = jnp.exp(nt_dot(q_word, k_word) + offset_ref[:, :word_count] - top)
        w_ent = jnp.exp(nt_dot(q_ent, k_ent) + offset_ref[:, word_count:] - top)
        d_word = (w_word * (nt_dot(grad_low, v_word) - delta)).astype(jnp.bfloat16)
        d_ent = (w_ent * (nt_dot(grad_low, v_ent) - delta)).astype(jnp.bfloat16)
        dquery_ref[:, low:high] = mm(d_word, k_word)
        dquery_ref[:, width + low : width + high] = mm(d_ent, k_ent)
        key_sum[low:high, :word_count] += tn_dot(q_word, d_word)
        key_sum[low:high, word_count:] += tn_dot(q_ent, d_ent)
        value_sum[low:high, :word_count] += tn_dot(grad_low, w_word.astype(jnp.bfloat16))
        value_sum[low:high, word_count:] += tn_dot(grad_low, w_ent.astype(jnp.bfloat16))

    @pl.when(step == pl.num_programs(0) - 1)
    def _():
        dkey_ref[...] = key_sum[...].T
        dvalue_ref[...] = value_sum[...].T


def attention_backward(packed, offsets, attn, stats, grad, word_count, heads, block):
    count, packed_width = packed.shape
    width = heads * HEAD_DIM
    return pl.pallas_call(
        functools.partial(attention_back_kernel, word_count, heads),
        grid=(count // block,),
        in_specs=[
            pl.BlockSpec((block, packed_width), lambda i: (i, 0)),
            pl.BlockSpec((count, packed_width), lambda i: (0, 0)),
            pl.BlockSpec((1, count), lambda i: (0, 0)),
            pl.BlockSpec((block, width), lambda i: (i, 0)),
            pl.BlockSpec((block, 128), lambda i: (i, 0)),
            pl.BlockSpec((block, width), lambda i: (i, 0)),
        ],
        out_specs=[
            pl.BlockSpec((block, 2 * width), lambda i: (i, 0)),
            pl.BlockSpec((count, width), lambda i: (0, 0)),
            pl.BlockSpec((count, width), lambda i: (0, 0)),
        ],
        out_shape=[
            jax.ShapeDtypeStruct((count, 2 * width), jnp.float32),
            jax.ShapeDtypeStruct((count, width), jnp.float32),
            jax.ShapeDtypeStruct((count, width), jnp.float32),
        ],
        scratch_shapes=[
            pltpu.VMEM((width, count), jnp.float32),
            pltpu.VMEM((width, count), jnp.float32),
        ],
        compiler_params=pltpu.CompilerParams(dimension_semantics=("arbitrary",)),
        cost_estimate=pl.CostEstimate(
            flops=10 * count * count * width,
            bytes_accessed=16 * count * packed_width,
            transcendentals=count * count * heads,
        ),
        name="attention_back",
    )(packed, packed, offsets, attn, stats, grad)


def tall(left):
    return jnp.swapaxes(left, -1, -2)


def head_split_device(
    x_words,
    x_ents,
    spans,
    word_mask,
    ent_mask,
    cot_words,
    cot_ents,
    attn_w,
    up_w,
    down_w,
    vecs,
    mom_attn,
    mom_up,
    mom_down,
    mom_vecs,
    err_attn,
    err_up,
    err_down,
    attention_prior_right,
    qf_up,
    qf_down,
):
    low_type = jnp.bfloat16
    words_dev, width = x_words.shape[1:]
    ents_dev = x_ents.shape[1]
    rows_dev = words_dev + ents_dev
    seq_count, rep_count = lax.axis_size("seq"), lax.axis_size("rep")
    seq_index, rep_index = lax.axis_index("seq"), lax.axis_index("rep")
    heads = HEADS // seq_count
    part = width // seq_count
    word_count = words_dev * seq_count
    ent_count = ents_dev * seq_count
    cols = attn_w.shape[2]
    cols_up = up_w.shape[1]
    hidden = cols_up * rep_count
    hidden_part = hidden // seq_count

    project_piece = jnp.swapaxes(attn_w[:6].astype(low_type), 0, 1).reshape(part, 6 * cols)
    project_all = gather_rep(planes_swap(project_piece))
    out_all = gather_rep(attn_w[6].astype(low_type).T)
    up_all = gather_rep(planes_swap(up_w.astype(low_type)))
    down_all = gather_rep(down_w.astype(low_type).T)
    w_project = jnp.transpose(
        project_all.reshape(4, 2, part, 6, cols), (0, 2, 3, 1, 4)
    ).reshape(width, 6, part)
    w_out = out_all.reshape(width, part)
    w_up = jnp.transpose(up_all, (0, 2, 1, 3)).reshape(width, hidden_part)
    w_down = down_all.reshape(width, hidden_part)

    inputs = jnp.concatenate([x_words[0], x_ents[0] + span_mean(spans[0], width)], 0)
    live = jnp.concatenate([word_mask[0], ent_mask[0]], 0).astype(low_type)
    live = jnp.pad(live, (0, 16 * width - rows_dev)).reshape(16, width)
    pieces = gather_seq(jnp.concatenate([inputs.astype(low_type), live], 0))
    rows_low = join_pieces([piece[:rows_dev] for piece in pieces], words_dev)
    lives = [piece[rows_dev:].reshape(-1)[:rows_dev] for piece in pieces]
    offsets = (join_pieces(lives, words_dev).astype(jnp.float32) - 1.0) * MASK_FILL
    offsets = offsets.reshape(1, -1)

    own_vecs = lax.dynamic_slice_in_dim(vecs, seq_index * part, part, 1)
    none = jnp.zeros((part,), jnp.float32)
    scale = jnp.where(jnp.arange(4 * part) < 2 * part, 0.125, 1.0).astype(jnp.float32)
    w_word = jnp.concatenate([w_project[:, j] for j in (0, 1, 4, 5)], -1)
    w_ent = jnp.concatenate([w_project[:, j] for j in (2, 3, 4, 5)], -1)
    bias_word = jnp.concatenate([own_vecs[0], own_vecs[1], none, own_vecs[4]])
    bias_ent = jnp.concatenate([own_vecs[2], own_vecs[3], none, own_vecs[4]])
    packed = jnp.concatenate(
        [
            ((mm(rows_low[:word_count], w_word) + bias_word) * scale).astype(low_type),
            ((mm(rows_low[word_count:], w_ent) + bias_ent) * scale).astype(low_type),
        ],
        0,
    )
    attn, attn_low, stats = attention_forward(packed, offsets, word_count, heads, rows_dev)

    branch = scatter_rows(nt_dot(attn_low, w_out), words_dev, ents_dev) + vecs[5]
    mid, normed_one, rstd_one = rows_norm(inputs + branch, vecs[7], vecs[8])
    mid_low = join_pieces(gather_seq(mid.astype(low_type)), words_dev)
    bias_up = lax.dynamic_slice_in_dim(
        vecs[11:15].reshape(hidden), seq_index * hidden_part, hidden_part, 0
    )
    pre = mm(mid_low, w_up) + bias_up
    act_low = gelu_exact(pre).astype(low_type)
    ffn = scatter_rows(nt_dot(act_low, w_down), words_dev, ents_dev) + vecs[6]
    result, normed_two, rstd_two = rows_norm(mid + ffn, vecs[9], vecs[10])

    grad_result = jnp.concatenate([cot_words[0], cot_ents[0]], 0)
    grad_two, gain_two, shift_two = rows_norm_back(grad_result, normed_two, rstd_two, vecs[9])
    bias_down = jnp.sum(grad_two, 0)
    grad_ffn = join_pieces(gather_seq(grad_two.astype(low_type)), words_dev)
    grad_act = mm(grad_ffn, w_down)
    unused_value, gelu_pull = jax.vjp(gelu_exact, pre)
    grad_pre = gelu_pull(grad_act)[0]
    grad_bias_up = jnp.sum(grad_pre, 0)
    grad_pre_low = grad_pre.astype(low_type)
    grad_mid = grad_two + scatter_rows(nt_dot(grad_pre_low, w_up), words_dev, ents_dev)
    grad_down = tn_dot(act_low, grad_ffn)
    grad_up = tn_dot(mid_low, grad_pre_low).astype(low_type)
    grad_up = lax.all_to_all(grad_up.reshape(seq_count, part, hidden_part), "seq", 0, 0)
    grad_up = jnp.swapaxes(grad_up, 0, 1).reshape(part, hidden).astype(jnp.float32)

    grad_one, gain_one, shift_one = rows_norm_back(grad_mid, normed_one, rstd_one, vecs[7])
    bias_out = jnp.sum(grad_one, 0)
    grad_branch = join_pieces(gather_seq(grad_one.astype(low_type)), words_dev)
    grad_out = tn_dot(attn_low, grad_branch)
    grad_attn = mm(grad_branch, w_out)
    dquery, dkey, dvalue = attention_backward(
        packed, offsets, attn, stats, grad_attn, word_count, heads, rows_dev
    )
    dquery = dquery * 0.125
    dkey_low = dkey.astype(low_type)
    dvalue_low = dvalue.astype(low_type)
    dquery_low = dquery.astype(low_type)
    d_low = jnp.concatenate([dquery_low, dkey_low, dvalue_low], 1)
    grad_inputs = grad_one + scatter_rows(
        jnp.concatenate(
            [nt_dot(d_low[:word_count], w_word), nt_dot(d_low[word_count:], w_ent)], 0
        ),
        words_dev,
        ents_dev,
    )
    rows_word, rows_ent = rows_low[:word_count], rows_low[word_count:]
    grad_project = jnp.concatenate(
        [
            tn_dot(rows_word, dquery_low[:word_count]),
            tn_dot(rows_ent, dquery_low[word_count:]),
            tn_dot(rows_low, jnp.concatenate([dkey_low, dvalue_low], 1)),
        ],
        1,
    ).astype(low_type)
    grad_project = lax.all_to_all(
        grad_project.reshape(seq_count, part, 6 * part), "seq", 0, 0
    )
    grad_project = jnp.transpose(
        grad_project.reshape(seq_count, part, 6, part), (2, 1, 0, 3)
    ).reshape(6, part, width)

    bias_query = jnp.stack(
        [
            jnp.sum(dquery[:word_count, :part], 0),
            jnp.sum(dquery[:word_count, part:], 0),
            jnp.sum(dquery[word_count:, :part], 0),
            jnp.sum(dquery[word_count:, part:], 0),
            jnp.sum(dvalue, 0),
        ]
    )
    vec_grad = jnp.zeros((15, width), jnp.float32)
    vec_grad = lax.dynamic_update_slice(vec_grad, bias_query, (0, seq_index * part))
    vec_grad = lax.dynamic_update_slice(
        vec_grad,
        jnp.stack([bias_out, bias_down, gain_one, shift_one, gain_two, shift_two]),
        (5, 0),
    )
    bias_rows = hidden_part // width
    vec_grad = lax.dynamic_update_slice(
        vec_grad, grad_bias_up.reshape(bias_rows, width), (11 + seq_index * bias_rows, 0)
    )

    full_attn = jnp.concatenate([grad_project.astype(jnp.float32), grad_out[None]], 0) + err_attn[0]
    full_up = grad_up + err_up[0]
    full_down = grad_down + err_down[0]
    left_attn = jnp.einsum(
        "jcg,jgr->jrc", full_attn, attention_prior_right, precision=HIGH_PRECISION
    )
    left_up = jnp.einsum("cg,gr->rc", full_up, qf_up, precision=HIGH_PRECISION)
    left_down = jnp.einsum("cg,gr->rc", full_down, qf_down, precision=HIGH_PRECISION)
    rank = qf_up.shape[1]
    left = jnp.concatenate(
        [jnp.swapaxes(left_attn, 0, 1).reshape(rank, 7 * part), left_up, left_down], 1
    )
    for bits in (1, 2, 4):
        left = left + rep_swap(left, bits)
    left = left / rep_count
    left_attn = jnp.swapaxes(left[:, : 7 * part].reshape(rank, 7, part), 0, 1)
    left_up = left[:, 7 * part : 8 * part]
    left_down = left[:, 8 * part :]
    gram = jnp.concatenate(
        [
            jnp.einsum("jrc,jtc->jrt", left_attn, left_attn, precision=HIGH_PRECISION),
            jnp.einsum("rc,tc->rt", left_up, left_up, precision=HIGH_PRECISION)[None],
            jnp.einsum("rc,tc->rt", left_down, left_down, precision=HIGH_PRECISION)[None],
        ],
        0,
    )
    gram = gram + seq_swap(gram, 1)
    gram = gram + seq_swap(gram, 2)
    lower = jnp.linalg.cholesky(gram)
    inverse = jax.scipy.linalg.solve_triangular(
        lower, jnp.broadcast_to(jnp.eye(rank, dtype=jnp.float32), lower.shape), lower=True
    )
    orth_attn = jnp.einsum("jrt,jtc->jrc", inverse[:7], left_attn, precision=HIGH_PRECISION)
    orth_up = jnp.dot(inverse[7], left_up, precision=HIGH_PRECISION)
    orth_down = jnp.dot(inverse[8], left_down, precision=HIGH_PRECISION)
    right = jnp.concatenate(
        [
            jnp.swapaxes(
                jnp.einsum("jrc,jcg->jrg", orth_attn, full_attn, precision=HIGH_PRECISION), 0, 1
            ).reshape(rank, 7 * width),
            jnp.dot(orth_up, full_up, precision=HIGH_PRECISION),
            jnp.dot(orth_down, full_down, precision=HIGH_PRECISION),
            vec_grad.reshape(rank, -1),
        ],
        1,
    )
    right_size = right.shape[1]
    right = jnp.pad(right, ((0, 0), (0, -right_size % 512)))
    core, chip = seq_index % 2, seq_index // 2
    for bits, bit in ((1, core), (2, chip)):
        half = right.shape[1] // 2
        below, above = right[:, :half], right[:, half:]
        right = jnp.where(bit == 0, below, above) + seq_swap(
            jnp.where(bit == 0, above, below), bits
        )
    for bits in (1, 2, 4):
        right = right + rep_swap(right, bits)
    for bits, bit in ((2, chip), (1, core)):
        right = ordered(bit, right, seq_swap(right, bits), 1).reshape(rank, -1)
    right = right / rep_count
    right_attn = jnp.swapaxes(right[:, : 7 * width].reshape(rank, 7, width), 0, 1)
    right_up = right[:, 7 * width : 7 * width + hidden]
    right_down = right[:, 7 * width + hidden : 8 * width + hidden]
    vec_mean = right[:, 8 * width + hidden : right_size].reshape(15, width)

    approx_attn = jnp.einsum("jrc,jrg->jcg", orth_attn, right_attn, precision=HIGH_PRECISION)
    approx_up = jnp.einsum("rc,rg->cg", orth_up, right_up, precision=HIGH_PRECISION)
    approx_down = jnp.einsum("rc,rg->cg", orth_down, right_down, precision=HIGH_PRECISION)
    step_attn = lax.dynamic_slice_in_dim(approx_attn, rep_index * cols, cols, 2)
    step_up = lax.dynamic_slice_in_dim(approx_up, rep_index * cols_up, cols_up, 1)
    step_down = lax.dynamic_slice_in_dim(approx_down, rep_index * cols, cols, 1)
    lr_mat = 1.5 * math.sqrt(rep_count / (SEQS * (WORDS + ENTS)))
    lr_vec = 0.2 * math.sqrt(rep_count / (SEQS * (WORDS + ENTS)))
    next_mom_attn = MOMENTUM * mom_attn + step_attn
    next_mom_up = MOMENTUM * mom_up + step_up
    next_mom_down = MOMENTUM * mom_down + step_down
    next_mom_vecs = MOMENTUM * mom_vecs + vec_mean
    return (
        result[None, :words_dev],
        result[None, words_dev:],
        grad_inputs[None, :words_dev],
        grad_inputs[None, words_dev:],
        attn_w - lr_mat * next_mom_attn,
        up_w - lr_mat * next_mom_up,
        down_w - lr_mat * next_mom_down,
        vecs - lr_vec * next_mom_vecs,
        next_mom_attn,
        next_mom_up,
        next_mom_down,
        next_mom_vecs,
        (full_attn - approx_attn)[None],
        (full_up - approx_up)[None],
        (full_down - approx_down)[None],
        tall(orth_attn),
        tall(orth_up),
        tall(orth_down),
        tall(right_attn),
        tall(right_up),
        tall(right_down),
    )


def solution(mesh):
    in_specs = (
        P("rep", "seq", None),
        P("rep", "seq", None),
        P("rep", "seq", None),
        P("rep", "seq"),
        P("rep", "seq"),
        P("rep", "seq", None),
        P("rep", "seq", None),
        P(None, "seq", "rep"),
        P("seq", "rep"),
        P("seq", "rep"),
        P(),
        P(None, "seq", "rep"),
        P("seq", "rep"),
        P("seq", "rep"),
        P(),
        P("rep", None, "seq", None),
        P("rep", "seq", None),
        P("rep", "seq", None),
        P(),
        P(),
        P(),
    )
    out_specs = (
        P("rep", "seq", None),
        P("rep", "seq", None),
        P("rep", "seq", None),
        P("rep", "seq", None),
        P(None, "seq", "rep"),
        P("seq", "rep"),
        P("seq", "rep"),
        P(),
        P(None, "seq", "rep"),
        P("seq", "rep"),
        P("seq", "rep"),
        P(),
        P("rep", None, "seq", None),
        P("rep", "seq", None),
        P("rep", "seq", None),
        P(None, "seq", None),
        P("seq", None),
        P("seq", None),
        P(),
        P(),
        P(),
    )
    seqs, reps = mesh.shape["seq"], mesh.shape["rep"]
    split_heads = seqs == 4 and reps == 2 * seqs and HEADS % seqs == 0
    body = head_split_device if split_heads else on_device
    return jax.shard_map(
        body, mesh=mesh, in_specs=in_specs, out_specs=out_specs, check_vma=False
    )
```

```python
import functools
import math

import jax
import jax.numpy as jnp
from jax import lax
from jax.experimental import pallas as pl
from jax.experimental.pallas import tpu as pltpu
from jax.sharding import PartitionSpec as P

HEADS = 12
WORDS = 1024
ENTS = 128
SPAN = 16
SEQS = 1


HIGH_PRECISION = lax.Precision.HIGHEST
EPS = 1e-05
MASK_FILL = 30000.0
MOMENTUM = 0.9


def span_mean(spans, model_width):
    starts = spans[..., 0]
    finals = spans[..., 1]
    lengths = (finals - starts + 1).astype(jnp.float32)
    offsets = jnp.arange(SPAN, dtype=jnp.int32)
    places = (starts[..., None] + offsets).astype(jnp.float32)
    shares = (offsets <= (finals - starts)[..., None]).astype(jnp.float32) / lengths[..., None]
    half_width = model_width // 2
    rates = jnp.exp(
        jnp.arange(half_width).astype(jnp.float32) * (-2.0 * math.log(10000.0) / model_width)
    )
    angles = places[..., None] * rates
    table = jnp.concatenate([jnp.sin(angles), jnp.cos(angles)], -1)
    return jnp.sum(table * shares[..., None], axis=-2)


def span_mean_closed(spans, model_width):
    lengths = (spans[..., 1] - spans[..., 0] + 1).astype(jnp.float32)[..., None]
    middles = (spans[..., 1] + spans[..., 0]).astype(jnp.float32)[..., None]
    half_rates = 0.5 * jnp.exp(
        jnp.arange(model_width // 2).astype(jnp.float32) * (-2.0 * math.log(10000.0) / model_width)
    )
    share = jnp.sin(lengths * half_rates) / (lengths * jnp.sin(half_rates))
    angles = middles * half_rates
    return jnp.concatenate([share * jnp.sin(angles), share * jnp.cos(angles)], -1)


def layer_norm(hidden, gain, shift):
    center = hidden - jnp.mean(hidden, -1, keepdims=True)
    rstd = lax.rsqrt(jnp.mean(center * center, -1, keepdims=True) + EPS)
    normed = center * rstd
    return (normed * gain + shift, normed, rstd)


def norm_back(grad, normed, rstd, gain):
    dnormed = grad * gain
    grad_in = rstd * (
        dnormed
        - jnp.mean(dnormed, -1, keepdims=True)
        - normed * jnp.mean(dnormed * normed, -1, keepdims=True)
    )
    return (grad_in, jnp.sum(grad * normed, axis=(0, 1)), jnp.sum(grad, axis=(0, 1)))


def gelu_exact(value):
    return jax.nn.gelu(value, approximate=False)


def project(row_entries, weight_matrix):
    return jnp.einsum("thq,qo->tho", row_entries, weight_matrix, preferred_element_type=jnp.float32)


def project_back(row_entries, weight_matrix):
    return jnp.einsum("hpf,zf->hpz", row_entries, weight_matrix, preferred_element_type=jnp.float32)


def weight_grad(input_arrays, gradient_list):
    return jnp.einsum(
        "cev,ceg->vg", input_arrays, gradient_list, preferred_element_type=jnp.float32
    )


def split_keys(pieces, words_dev, ents_dev, head_count):
    key_piece, live_piece = pieces
    batch_rows = key_piece.shape[0]
    both = key_piece.shape[2]
    model_width = both // 2
    head_dim = model_width // head_count
    rows_dev = words_dev + ents_dev
    blocks = key_piece.shape[1] // rows_dev
    grouped = key_piece.reshape(batch_rows, blocks, rows_dev, both)
    live_grouped = live_piece.reshape(batch_rows, blocks, rows_dev)
    word_part = grouped[:, :, :words_dev].reshape(batch_rows, blocks * words_dev, both)
    ent_part = grouped[:, :, words_dev:].reshape(batch_rows, blocks * ents_dev, both)
    keys_word = word_part[..., :model_width].reshape(batch_rows, -1, head_count, head_dim)
    keys_ent = ent_part[..., :model_width].reshape(batch_rows, -1, head_count, head_dim)
    values = jnp.concatenate(
        [word_part[..., model_width:], ent_part[..., model_width:]], 1
    ).reshape(batch_rows, -1, head_count, head_dim)
    live = jnp.concatenate(
        [
            live_grouped[:, :, :words_dev].reshape(batch_rows, -1),
            live_grouped[:, :, words_dev:].reshape(batch_rows, -1),
        ],
        1,
    )
    offsets = (live.astype(jnp.float32) - 1.0) * MASK_FILL
    return (keys_word, keys_ent, values, offsets, blocks)


def score_block(query_word, query_ent, keys_word, keys_ent, offsets):
    score_word = jnp.einsum(
        "sqhd,skhd->shqk", query_word, keys_word, preferred_element_type=jnp.float32
    )
    score_ent = jnp.einsum(
        "sqhd,skhd->shqk", query_ent, keys_ent, preferred_element_type=jnp.float32
    )
    return jnp.concatenate([score_word, score_ent], -1) + offsets[:, None, None, :]


def flat_heads(array):
    return array.reshape(array.shape[0], array.shape[1], -1)


def join_rows(grad_keys_word, grad_keys_ent, grad_values, blocks, words_dev, ents_dev):
    batch_rows = grad_keys_word.shape[0]
    word_count = grad_keys_word.shape[1]
    word_rows = jnp.concatenate(
        [flat_heads(grad_keys_word), flat_heads(grad_values[:, :word_count])], -1
    )
    ent_rows = jnp.concatenate(
        [flat_heads(grad_keys_ent), flat_heads(grad_values[:, word_count:])], -1
    )
    word_rows = word_rows.reshape(batch_rows, blocks, words_dev, -1)
    ent_rows = ent_rows.reshape(batch_rows, blocks, ents_dev, -1)
    return jnp.concatenate([word_rows, ent_rows], 2).reshape(
        batch_rows, blocks * (words_dev + ents_dev), -1
    )


def from_gram(left, gram):
    lower = jnp.linalg.cholesky(gram)
    return jax.scipy.linalg.solve_triangular(lower, left.T, lower=True).T


def orthonormal(left):
    return from_gram(left, jnp.dot(left.T, left, precision=HIGH_PRECISION))


def on_device(
    x_words,
    x_ents,
    spans,
    word_mask,
    ent_mask,
    cot_words,
    cot_ents,
    attn_w,
    up_w,
    down_w,
    vecs,
    mom_attn,
    mom_up,
    mom_down,
    mom_vecs,
    err_attn,
    err_up,
    err_down,
    attention_prior_right,
    qf_up,
    qf_down,
):
    batch_rows, words_dev, model_width = x_words.shape
    ents_dev = x_ents.shape[1]
    rows_dev = words_dev + ents_dev
    head_count = HEADS
    head_dim = model_width // head_count
    hidden_width = up_w.shape[1] * lax.axis_size("rep")
    seq_count = lax.axis_size("seq")
    rep_count = lax.axis_size("rep")
    seq_index = lax.axis_index("seq")
    rep_index = lax.axis_index("rep")
    lowered = jnp.bfloat16
    column_parts = (
        lax.all_gather(attn_w.astype(lowered), "rep", axis=2, tiled=True),
        lax.all_gather(up_w.astype(lowered), "rep", axis=1, tiled=True),
        lax.all_gather(down_w.astype(lowered), "rep", axis=1, tiled=True),
    )
    w_attn, w_up, w_down = (
        lax.all_gather(column_parts[0], "seq", axis=1, tiled=True),
        lax.all_gather(column_parts[1], "seq", axis=0, tiled=True),
        lax.all_gather(column_parts[2], "seq", axis=0, tiled=True),
    )
    input_arrays = jnp.concatenate([x_words, x_ents + span_mean(spans, model_width)], 1)
    inputs_low = input_arrays.astype(lowered)
    word_low = inputs_low[:, :words_dev]
    ent_low = inputs_low[:, words_dev:]
    query_word = (
        jnp.concatenate(
            [project(word_low, w_attn[0]) + vecs[0], project(ent_low, w_attn[2]) + vecs[2]], 1
        )
        * 0.125
    ).astype(lowered)
    query_ent = (
        jnp.concatenate(
            [project(word_low, w_attn[1]) + vecs[1], project(ent_low, w_attn[3]) + vecs[3]], 1
        )
        * 0.125
    ).astype(lowered)
    keys_low = project(inputs_low, w_attn[4]).astype(lowered)
    values_low = (project(inputs_low, w_attn[5]) + vecs[4]).astype(lowered)
    key_rows = jnp.concatenate([keys_low, values_low], -1)
    key_live = jnp.concatenate([word_mask, ent_mask], 1).astype(lowered)
    heads_word = query_word.reshape(batch_rows, rows_dev, head_count, head_dim)
    heads_ent = query_ent.reshape(batch_rows, rows_dev, head_count, head_dim)
    forward_row_top = jnp.full((batch_rows, head_count, rows_dev), -jnp.inf, jnp.float32)
    row_total = jnp.zeros((batch_rows, head_count, rows_dev), jnp.float32)
    weighted = jnp.zeros((batch_rows, rows_dev, head_count, head_dim), jnp.float32)
    keys_word, keys_ent, values, offsets, blocks = split_keys(
        (
            lax.all_gather(key_rows, "seq", axis=1, tiled=True),
            lax.all_gather(key_live, "seq", axis=1, tiled=True),
        ),
        words_dev,
        ents_dev,
        head_count,
    )
    scores = score_block(heads_word, heads_ent, keys_word, keys_ent, offsets)
    new_top = jnp.max(scores, -1)
    factor = jnp.exp(forward_row_top - new_top)
    weights = jnp.exp(scores - new_top[..., None])
    row_total = row_total * factor + jnp.sum(weights, -1)
    weighted = weighted * jnp.transpose(factor, (0, 2, 1))[..., None] + jnp.einsum(
        "shqk,skhd->sqhd", weights.astype(lowered), values, preferred_element_type=jnp.float32
    )
    row_top, row_total, weighted = (new_top, row_total, weighted)
    total_rows = jnp.transpose(row_total, (0, 2, 1))[..., None]
    attn = weighted / total_rows
    attn_low = attn.reshape(batch_rows, rows_dev, model_width).astype(lowered)
    branch = project(attn_low, w_attn[6]) + vecs[5]
    mid, normed_one, rstd_one = layer_norm(input_arrays + branch, vecs[7], vecs[8])
    mid_low = mid.astype(lowered)
    pre = project(mid_low, w_up) + vecs[11:15].reshape(hidden_width)
    act_low = gelu_exact(pre).astype(lowered)
    ffn = project(act_low, w_down) + vecs[6]
    result, normed_two, rstd_two = layer_norm(mid + ffn, vecs[9], vecs[10])
    grad_result = jnp.concatenate([cot_words, cot_ents], 1)
    grad_two, gain_two, shift_two = norm_back(grad_result, normed_two, rstd_two, vecs[9])
    bias_down = jnp.sum(grad_two, axis=(0, 1))
    grad_ffn_low = grad_two.astype(lowered)
    grad_down = weight_grad(act_low, grad_ffn_low)
    grad_act = project_back(grad_ffn_low, w_down)
    unused_value, gelu_pull = jax.vjp(gelu_exact, pre)
    grad_pre = gelu_pull(grad_act)[0]
    bias_up = jnp.sum(grad_pre, axis=(0, 1))
    grad_pre_low = grad_pre.astype(lowered)
    grad_up = weight_grad(mid_low, grad_pre_low)
    grad_mid = grad_two + project_back(grad_pre_low, w_up)
    grad_one, gain_one, shift_one = norm_back(grad_mid, normed_one, rstd_one, vecs[7])
    bias_out = jnp.sum(grad_one, axis=(0, 1))
    grad_branch_low = grad_one.astype(lowered)
    grad_out_proj = weight_grad(attn_low, grad_branch_low)
    grad_attn = project_back(grad_branch_low, w_attn[6]).reshape(
        batch_rows, rows_dev, head_count, head_dim
    )
    grad_unnorm = (grad_attn / total_rows).astype(lowered)
    delta_rows = jnp.transpose(jnp.sum(grad_attn * attn, -1), (0, 2, 1)) / row_total
    keys_word, keys_ent, values, offsets, blocks = split_keys(
        (
            lax.all_gather(key_rows, "seq", axis=1, tiled=True),
            lax.all_gather(key_live, "seq", axis=1, tiled=True),
        ),
        words_dev,
        ents_dev,
        head_count,
    )
    scores = score_block(heads_word, heads_ent, keys_word, keys_ent, offsets)
    weights = jnp.exp(scores - row_top[..., None])
    grad_weights = jnp.einsum(
        "sqhd,skhd->shqk", grad_unnorm, values, preferred_element_type=jnp.float32
    )
    grad_scores = (weights * (grad_weights - delta_rows[..., None])).astype(lowered)
    word_count = keys_word.shape[1]
    scores_word = grad_scores[..., :word_count]
    scores_ent = grad_scores[..., word_count:]
    grad_query_word = jnp.einsum(
        "shqk,skhd->sqhd", scores_word, keys_word, preferred_element_type=jnp.float32
    )
    grad_query_ent = jnp.einsum(
        "shqk,skhd->sqhd", scores_ent, keys_ent, preferred_element_type=jnp.float32
    )
    grad_keys_word = jnp.einsum(
        "shqk,sqhd->skhd", scores_word, heads_word, preferred_element_type=jnp.float32
    )
    grad_keys_ent = jnp.einsum(
        "shqk,sqhd->skhd", scores_ent, heads_ent, preferred_element_type=jnp.float32
    )
    grad_values = jnp.einsum(
        "shqk,sqhd->skhd", weights.astype(lowered), grad_unnorm, preferred_element_type=jnp.float32
    )
    piece_grad = join_rows(grad_keys_word, grad_keys_ent, grad_values, blocks, words_dev, ents_dev)
    grad_rows = piece_grad
    grad_query_word, grad_query_ent, grad_rows = (grad_query_word, grad_query_ent, grad_rows)
    own_rows = lax.psum_scatter(
        grad_rows.astype(jnp.bfloat16), "seq", scatter_dimension=1, tiled=True
    ).astype(jnp.float32)
    grad_keys = own_rows[..., :model_width]
    grad_values = own_rows[..., model_width:]
    bias_values = jnp.sum(grad_values, axis=(0, 1))
    keys_grad_low = grad_keys.astype(lowered)
    values_grad_low = grad_values.astype(lowered)
    grad_key_w = weight_grad(inputs_low, keys_grad_low)
    grad_value_w = weight_grad(inputs_low, values_grad_low)
    inner_word = grad_query_word.reshape(batch_rows, rows_dev, model_width) * 0.125
    inner_ent = grad_query_ent.reshape(batch_rows, rows_dev, model_width) * 0.125
    bias_query = [
        jnp.sum(inner_word[:, :words_dev], axis=(0, 1)),
        jnp.sum(inner_ent[:, :words_dev], axis=(0, 1)),
        jnp.sum(inner_word[:, words_dev:], axis=(0, 1)),
        jnp.sum(inner_ent[:, words_dev:], axis=(0, 1)),
    ]
    inner_word_low = inner_word.astype(lowered)
    inner_ent_low = inner_ent.astype(lowered)
    grad_query_mats = [
        weight_grad(word_low, inner_word_low[:, :words_dev]),
        weight_grad(word_low, inner_ent_low[:, :words_dev]),
        weight_grad(ent_low, inner_word_low[:, words_dev:]),
        weight_grad(ent_low, inner_ent_low[:, words_dev:]),
    ]
    back_keys = project_back(keys_grad_low, w_attn[4]) + project_back(values_grad_low, w_attn[5])
    back_word = project_back(inner_word_low[:, :words_dev], w_attn[0]) + project_back(
        inner_ent_low[:, :words_dev], w_attn[1]
    )
    back_ent = project_back(inner_word_low[:, words_dev:], w_attn[2]) + project_back(
        inner_ent_low[:, words_dev:], w_attn[3]
    )
    grad_inputs = grad_one + back_keys + jnp.concatenate([back_word, back_ent], 1)
    grad_attn_w = jnp.stack(grad_query_mats + [grad_key_w, grad_value_w, grad_out_proj])
    vec_grad = jnp.concatenate(
        [
            jnp.stack(
                bias_query
                + [bias_values, bias_out, bias_down, gain_one, shift_one, gain_two, shift_two]
            ),
            bias_up.reshape(4, model_width),
        ],
        0,
    )
    rows_attn, rows_up, rows_down = (
        lax.psum_scatter(
            grad_attn_w.astype(jnp.bfloat16), "seq", scatter_dimension=1, tiled=True
        ).astype(jnp.float32),
        lax.psum_scatter(
            grad_up.astype(jnp.bfloat16), "seq", scatter_dimension=0, tiled=True
        ).astype(jnp.float32),
        lax.psum_scatter(
            grad_down.astype(jnp.bfloat16), "seq", scatter_dimension=0, tiled=True
        ).astype(jnp.float32),
    )
    attention_full_gradient = rows_attn + err_attn[0]
    full_up = rows_up + err_up[0]
    full_down = rows_down + err_down[0]
    attention_left_factor = jnp.einsum(
        "vcg,vgo->vco", attention_full_gradient, attention_prior_right, precision=HIGH_PRECISION
    )
    left_up = jnp.dot(full_up, qf_up, precision=HIGH_PRECISION)
    left_down = jnp.dot(full_down, qf_down, precision=HIGH_PRECISION)
    count_attn = attention_full_gradient.shape[1]
    count_up = full_up.shape[0]
    count_down = full_down.shape[0]
    placed_attn = lax.dynamic_update_slice_in_dim(
        jnp.zeros((7, count_attn * seq_count, attention_left_factor.shape[2]), jnp.float32),
        attention_left_factor,
        seq_index * count_attn,
        1,
    )
    placed_up = lax.dynamic_update_slice_in_dim(
        jnp.zeros((count_up * seq_count, left_up.shape[1]), jnp.float32),
        left_up,
        seq_index * count_up,
        0,
    )
    placed_down = lax.dynamic_update_slice_in_dim(
        jnp.zeros((count_down * seq_count, left_down.shape[1]), jnp.float32),
        left_down,
        seq_index * count_down,
        0,
    )
    summed_attn, summed_up, summed_down = lax.psum(
        (placed_attn, placed_up, placed_down), ("seq", "rep")
    )
    orth_attn = jax.vmap(orthonormal)(summed_attn / rep_count)
    orth_up = orthonormal(summed_up / rep_count)
    orth_down = orthonormal(summed_down / rep_count)
    attention_local_gradient = lax.dynamic_slice_in_dim(
        orth_attn, seq_index * count_attn, count_attn, 1
    )
    own_up = lax.dynamic_slice_in_dim(orth_up, seq_index * count_up, count_up, 0)
    own_down = lax.dynamic_slice_in_dim(orth_down, seq_index * count_down, count_down, 0)
    right_parts = (
        jnp.einsum(
            "dpl,dpg->dgl",
            attention_local_gradient,
            attention_full_gradient,
            precision=HIGH_PRECISION,
        ),
        jnp.dot(full_up.T, own_up, precision=HIGH_PRECISION),
        jnp.dot(full_down.T, own_down, precision=HIGH_PRECISION),
        vec_grad,
    )
    attention_right_factor, right_up, right_down, vec_total = lax.psum(
        (right_parts[0], right_parts[1], right_parts[2], right_parts[3]), ("seq", "rep")
    )
    attention_right_factor = attention_right_factor / rep_count
    right_up = right_up / rep_count
    right_down = right_down / rep_count
    vec_mean = vec_total / rep_count
    attention_estimate = jnp.einsum(
        "whg,wng->whn", attention_local_gradient, attention_right_factor, precision=HIGH_PRECISION
    )
    approx_up = jnp.dot(own_up, right_up.T, precision=HIGH_PRECISION)
    approx_down = jnp.dot(own_down, right_down.T, precision=HIGH_PRECISION)
    next_err_attn = (attention_full_gradient - attention_estimate)[None]
    next_err_up = (full_up - approx_up)[None]
    next_err_down = (full_down - approx_down)[None]
    cols_attn = attn_w.shape[2]
    cols_up = up_w.shape[1]
    cols_down = down_w.shape[1]
    step_attn = lax.dynamic_slice_in_dim(attention_estimate, rep_index * cols_attn, cols_attn, 2)
    step_up = lax.dynamic_slice_in_dim(approx_up, rep_index * cols_up, cols_up, 1)
    step_down = lax.dynamic_slice_in_dim(approx_down, rep_index * cols_down, cols_down, 1)
    lr_mat = 1.5 * math.sqrt(rep_count / (SEQS * (WORDS + ENTS)))
    lr_vec = 0.2 * math.sqrt(rep_count / (SEQS * (WORDS + ENTS)))
    next_mom_attn = MOMENTUM * mom_attn + step_attn
    next_mom_up = MOMENTUM * mom_up + step_up
    next_mom_down = MOMENTUM * mom_down + step_down
    next_mom_vecs = MOMENTUM * mom_vecs + vec_mean
    new_attn = attn_w - lr_mat * next_mom_attn
    new_up = up_w - lr_mat * next_mom_up
    new_down = down_w - lr_mat * next_mom_down
    new_vecs = vecs - lr_vec * next_mom_vecs
    return (
        result[:, :words_dev],
        result[:, words_dev:],
        grad_inputs[:, :words_dev],
        grad_inputs[:, words_dev:],
        new_attn,
        new_up,
        new_down,
        new_vecs,
        next_mom_attn,
        next_mom_up,
        next_mom_down,
        next_mom_vecs,
        next_err_attn,
        next_err_up,
        next_err_down,
        attention_local_gradient,
        own_up,
        own_down,
        attention_right_factor,
        right_up,
        right_down,
    )


def seq_swap(array, bits):
    size = lax.axis_size("seq")
    return lax.ppermute(array, "seq", [(i, i ^ bits) for i in range(size)])


def rep_swap(array, bits):
    size = lax.axis_size("rep")
    return lax.ppermute(array, "rep", [(i, i ^ bits) for i in range(size)])


def planes_swap(array):
    seqs, reps = lax.axis_size("seq"), lax.axis_size("rep")
    pairs = []
    for s in range(seqs):
        for r in range(reps):
            pairs.append((s * reps + r, (r // 2) * reps + 2 * s + r % 2))
    return lax.ppermute(array, ("seq", "rep"), pairs)


def gather_seq(piece):
    other_chip = seq_swap(piece, 2)
    return [seq_swap(piece, 1), seq_swap(other_chip, 1), piece, other_chip]


def gather_direct(piece):
    pieces = [piece] + [rep_swap(piece, 2 * change) for change in (1, 2, 3)]
    return pieces, rep_swap(piece, 1)


def gather_tree(piece):
    own_side = rep_swap(piece, 1)
    far = rep_swap(piece, 4)
    near = rep_swap(jnp.stack([piece, far]), 2)
    far_side = rep_swap(far, 1)
    near_side = rep_swap(near, 1)
    return [piece, own_side, far, far_side, near, near_side]


def tree_pieces(refs):
    own, own_side, far, far_side, near, near_side = refs
    return (
        (0, own[...], own_side[...]),
        (2, far[...], far_side[...]),
        (1, near[0], near_side[0]),
        (3, near[1], near_side[1]),
    )


def project_kernel(
    words_dev, rows_dev, place_ref, bias_word_ref, bias_ent_ref, scale_ref, *refs
):
    trees, row_refs = (refs[:6], refs[6:12]), refs[12:16]
    word_ref, ent_ref, packed_word_ref, packed_ent_ref, rows_word_ref, rows_ent_ref = refs[16:22]
    piece_ref = refs[22]
    ents_dev = rows_dev - words_dev
    z, y = place_ref[0], place_ref[1]
    for half, tree in enumerate(trees):
        for change, own, other in tree_pieces(tree):
            piece_ref[half, z ^ change, y] = own
            piece_ref[half, z ^ change, 1 - y] = other
    rows, both = piece_ref.shape[3:]
    cols = both // 12
    for half in (0, 1):
        for place in range(4):
            left, right = piece_ref[half, place, 0], piece_ref[half, place, 1]
            for upper in (0, 1):
                parts = []
                for j in range(6):
                    low = (upper * 6 + j) * cols
                    parts.append(left[:, low : low + cols])
                    parts.append(right[:, low : low + cols])
                start = (4 * place + 2 * upper + half) * rows
                target = slice(start, start + rows)
                word_ref[target] = jnp.concatenate(parts[:4] + parts[8:], 1)
                ent_ref[target] = jnp.concatenate(parts[4:], 1)

    scale = scale_ref[...]
    word, ent = word_ref[...], ent_ref[...]
    for k, row_ref in enumerate(row_refs):
        words = row_ref[:words_dev]
        at = slice(k * words_dev, (k + 1) * words_dev)
        rows_word_ref[at] = words
        packed_word_ref[at] = ((mm(words, word) + bias_word_ref[...]) * scale).astype(
            jnp.bfloat16
        )
        at = slice(k * ents_dev, (k + 1) * ents_dev)
        rows_ent_ref[at] = row_ref[words_dev:rows_dev]
    packed_ent_ref[...] = ((mm(rows_ent_ref[...], ent) + bias_ent_ref[...]) * scale).astype(
        jnp.bfloat16
    )


def ffn_join_kernel(place_ref, *refs):
    pieces, sides, (up_ref, down_ref) = refs[:4], refs[4:8], refs[8:]
    z, y = place_ref[0], place_ref[1]
    for side in (0, 1):

        @pl.when(y == side)
        def _():
            for change in range(4):
                for y_at, piece in ((side, pieces[change]), (1 - side, sides[change])):
                    rows, both = piece.shape
                    cols = both // 4
                    place = z ^ change
                    for upper in (0, 1):
                        start = pl.multiple_of(place * (2 * rows) + upper * rows, 16)
                        up_ref[pl.ds(start, rows), y_at * cols : (y_at + 1) * cols] = piece[
                            :, upper * cols : (upper + 1) * cols
                        ]
                    start = pl.multiple_of((2 * place + y_at) * rows, 16)
                    down_ref[pl.ds(start, rows), :] = piece[:, 2 * cols :]


def out_join_kernel(place_ref, *refs):
    tree, out_ref = refs[:6], refs[6]
    z, y = place_ref[0], place_ref[1]
    for change, own, other in tree_pieces(tree):
        rows = own.shape[0]
        own_start = pl.multiple_of((2 * (z ^ change) + y) * rows, 16)
        other_start = pl.multiple_of((2 * (z ^ change) + 1 - y) * rows, 16)
        out_ref[pl.ds(own_start, rows), :] = own
        out_ref[pl.ds(other_start, rows), :] = other


def join_call(kernel, place, pieces, shapes, name):
    whole = [pl.BlockSpec(memory_space=pltpu.VMEM)] * len(pieces)
    return pl.pallas_call(
        kernel,
        in_specs=[pl.BlockSpec(memory_space=pltpu.SMEM)] + whole,
        out_specs=[pl.BlockSpec(memory_space=pltpu.VMEM)] * len(shapes),
        out_shape=[jax.ShapeDtypeStruct(shape, jnp.bfloat16) for shape in shapes],
        name=name,
    )(place, *pieces)


def scatter_blocks(rows, dot, weight):
    half = rows.shape[0] // 2
    own = half // 2
    got = seq_swap(dot(rows[:half], weight).astype(jnp.bfloat16), 1).astype(jnp.float32)
    kept = dot(rows[half:], weight) + got
    return kept[:own] + seq_swap(kept[own:].astype(jnp.bfloat16), 2).astype(jnp.float32)


def scatter_parts(words, ents):
    words_dev, ents_dev = words.shape[0] // 4, ents.shape[0] // 4
    half = words_dev + ents_dev

    def rows(first):
        parts = []
        for k in (first, first + 1):
            parts.append(words[k * words_dev : (k + 1) * words_dev])
            parts.append(ents[k * ents_dev : (k + 1) * ents_dev])
        return jnp.concatenate(parts, 0)

    got = seq_swap(rows(0).astype(jnp.bfloat16), 1).astype(jnp.float32)
    kept = rows(2) + got
    return kept[:half] + seq_swap(kept[half:].astype(jnp.bfloat16), 2).astype(jnp.float32)


def rows_norm(hidden, gain, shift):
    center = hidden - jnp.mean(hidden, -1, keepdims=True)
    rstd = lax.rsqrt(jnp.mean(center * center, -1, keepdims=True) + EPS)
    normed = center * rstd
    return (normed * gain + shift, normed, rstd)


def rows_norm_back(grad, normed, rstd, gain):
    dnormed = grad * gain
    grad_in = rstd * (
        dnormed
        - jnp.mean(dnormed, -1, keepdims=True)
        - normed * jnp.mean(dnormed * normed, -1, keepdims=True)
    )
    return (grad_in, jnp.sum(grad * normed, axis=0), jnp.sum(grad, axis=0))


def mm(left, right, left_dim=1, right_dim=0):
    return lax.dot_general(
        left, right, (((left_dim,), (right_dim,)), ((), ())), preferred_element_type=jnp.float32
    )


def nt_dot(left, right):
    return mm(left, right, 1, 1)


def tn_dot(left, right):
    return mm(left, right, 0, 0)


HEAD_DIM = 64


def head_parts(word_ref, ent_ref, low, high):
    return jnp.concatenate([word_ref[:, low:high], ent_ref[:, low:high]], 0)


def attention_kernel(
    heads,
    query_word_ref,
    query_ent_ref,
    key_word_ref,
    key_ent_ref,
    offset_ref,
    attn_ref,
    low_ref,
    high_ref,
    stat_ref,
):
    width = heads * HEAD_DIM
    word_count = key_word_ref.shape[0]
    rows = attn_ref.shape[0]
    lane = lax.broadcasted_iota(jnp.int32, (rows, 128), 1)
    stats = jnp.zeros((rows, 128), jnp.float32)
    for h in range(heads):
        low, high = h * HEAD_DIM, (h + 1) * HEAD_DIM
        q_word = head_parts(query_word_ref, query_ent_ref, low, high)
        q_ent = head_parts(query_word_ref, query_ent_ref, width + low, width + high)
        k_word = key_word_ref[:, 2 * width + low : 2 * width + high]
        k_ent = key_ent_ref[:, 2 * width + low : 2 * width + high]
        s_word = nt_dot(q_word, k_word) + offset_ref[:, :word_count]
        s_ent = nt_dot(q_ent, k_ent) + offset_ref[:, word_count:]
        top = jnp.maximum(
            jnp.max(s_word, -1, keepdims=True), jnp.max(s_ent, -1, keepdims=True)
        )
        w_word = jnp.exp(s_word - top)
        w_ent = jnp.exp(s_ent - top)
        total = jnp.sum(w_word, -1, keepdims=True) + jnp.sum(w_ent, -1, keepdims=True)
        v_word = key_word_ref[:, 3 * width + low : 3 * width + high]
        v_ent = key_ent_ref[:, 3 * width + low : 3 * width + high]
        unnorm = mm(w_word.astype(jnp.bfloat16), v_word) + mm(w_ent.astype(jnp.bfloat16), v_ent)
        attn_ref[:, low:high] = unnorm / total
        stats = jnp.where(lane == h, top, stats)
        stats = jnp.where(lane == heads + h, total, stats)
    stat_ref[...] = stats
    low_ref[...] = attn_ref[: rows // 2].astype(jnp.bfloat16)
    high_ref[...] = attn_ref[rows // 2 :].astype(jnp.bfloat16)


def attention_forward(packed_word, packed_ent, offsets, heads):
    word_count, packed_width = packed_word.shape
    ent_count = packed_ent.shape[0]
    count = word_count + ent_count
    width = heads * HEAD_DIM
    block = count // 4
    return pl.pallas_call(
        functools.partial(attention_kernel, heads),
        grid=(4,),
        in_specs=[
            pl.BlockSpec((word_count // 4, packed_width), lambda i: (i, 0)),
            pl.BlockSpec((ent_count // 4, packed_width), lambda i: (i, 0)),
            pl.BlockSpec((word_count, packed_width), lambda i: (0, 0)),
            pl.BlockSpec((ent_count, packed_width), lambda i: (0, 0)),
            pl.BlockSpec((1, count), lambda i: (0, 0)),
        ],
        out_specs=[
            pl.BlockSpec((block, width), lambda i: (i, 0)),
            pl.BlockSpec((block // 2, width), lambda i: (i, 0)),
            pl.BlockSpec((block // 2, width), lambda i: (i, 0)),
            pl.BlockSpec((block, 128), lambda i: (i, 0)),
        ],
        out_shape=[
            jax.ShapeDtypeStruct((count, width), jnp.float32),
            jax.ShapeDtypeStruct((count // 2, width), jnp.bfloat16),
            jax.ShapeDtypeStruct((count // 2, width), jnp.bfloat16),
            jax.ShapeDtypeStruct((count, 128), jnp.float32),
        ],
        compiler_params=pltpu.CompilerParams(dimension_semantics=("arbitrary",)),
        cost_estimate=pl.CostEstimate(
            flops=4 * count * count * width,
            bytes_accessed=6 * count * packed_width,
            transcendentals=count * count * heads,
        ),
        name="attention",
    )(packed_word, packed_ent, packed_word, packed_ent, offsets)


def attention_back_kernel(
    heads,
    query_word_ref,
    query_ent_ref,
    key_word_ref,
    key_ent_ref,
    offset_ref,
    attn_ref,
    stat_ref,
    grad_low_ref,
    grad_high_ref,
    d_word_ref,
    d_ent_ref,
    sum_ref,
    key_sum,
    value_sum,
):
    width = heads * HEAD_DIM
    word_count = key_word_ref.shape[0]
    words_dev, ents_dev = query_word_ref.shape[0], query_ent_ref.shape[0]
    step = pl.program_id(0)

    @pl.when(step == 0)
    def _():
        key_sum[...] = jnp.zeros_like(key_sum)
        value_sum[...] = jnp.zeros_like(value_sum)
        sum_ref[...] = jnp.zeros_like(sum_ref)

    word_rows = pl.ds(pl.multiple_of(step * words_dev, words_dev), words_dev)
    ent_rows = pl.ds(pl.multiple_of(step * ents_dev, ents_dev), ents_dev)
    for h in range(heads):
        low, high = h * HEAD_DIM, (h + 1) * HEAD_DIM
        q_word = head_parts(query_word_ref, query_ent_ref, low, high)
        q_ent = head_parts(query_word_ref, query_ent_ref, width + low, width + high)
        k_word = key_word_ref[:, 2 * width + low : 2 * width + high]
        k_ent = key_ent_ref[:, 2 * width + low : 2 * width + high]
        v_word = key_word_ref[:, 3 * width + low : 3 * width + high]
        v_ent = key_ent_ref[:, 3 * width + low : 3 * width + high]
        top = stat_ref[:, h : h + 1]
        inverse = 1.0 / stat_ref[:, heads + h : heads + h + 1]
        grad = head_parts(grad_low_ref, grad_high_ref, low, high)
        delta = jnp.sum(grad * attn_ref[:, low:high], -1, keepdims=True) * inverse
        grad_low = (grad * inverse).astype(jnp.bfloat16)
        w_word = jnp.exp(nt_dot(q_word, k_word) + offset_ref[:, :word_count] - top)
        w_ent = jnp.exp(nt_dot(q_ent, k_ent) + offset_ref[:, word_count:] - top)
        d_word = (w_word * (nt_dot(grad_low, v_word) - delta)).astype(jnp.bfloat16)
        d_ent = (w_ent * (nt_dot(grad_low, v_ent) - delta)).astype(jnp.bfloat16)
        for at, dquery in ((low, mm(d_word, k_word)), (width + low, mm(d_ent, k_ent))):
            dquery = dquery * 0.125
            lanes = slice(at, at + HEAD_DIM)
            d_word_ref[word_rows, lanes] = dquery[:words_dev].astype(jnp.bfloat16)
            d_ent_ref[ent_rows, lanes] = dquery[words_dev:].astype(jnp.bfloat16)
            sum_ref[0:1, lanes] += jnp.sum(dquery[:words_dev], 0, keepdims=True)
            sum_ref[1:2, lanes] += jnp.sum(dquery[words_dev:], 0, keepdims=True)
        key_sum[low:high, :word_count] += tn_dot(q_word, d_word)
        key_sum[low:high, word_count:] += tn_dot(q_ent, d_ent)
        value_sum[low:high, :word_count] += tn_dot(grad_low, w_word.astype(jnp.bfloat16))
        value_sum[low:high, word_count:] += tn_dot(grad_low, w_ent.astype(jnp.bfloat16))

    @pl.when(step == pl.num_programs(0) - 1)
    def _():
        dkey = key_sum[...].T
        dvalue = value_sum[...].T
        sum_ref[2:3, :width] = jnp.sum(dvalue, 0, keepdims=True)
        both = jnp.concatenate([dkey, dvalue], 1).astype(jnp.bfloat16)
        d_word_ref[:, 2 * width :] = both[:word_count]
        d_ent_ref[:, 2 * width :] = both[word_count:]


def attention_backward(packed_word, packed_ent, offsets, attn, stats, grads, heads):
    word_count, packed_width = packed_word.shape
    ent_count = packed_ent.shape[0]
    count = word_count + ent_count
    width = heads * HEAD_DIM
    block = count // 4
    return pl.pallas_call(
        functools.partial(attention_back_kernel, heads),
        grid=(4,),
        in_specs=[
            pl.BlockSpec((word_count // 4, packed_width), lambda i: (i, 0)),
            pl.BlockSpec((ent_count // 4, packed_width), lambda i: (i, 0)),
            pl.BlockSpec((word_count, packed_width), lambda i: (0, 0)),
            pl.BlockSpec((ent_count, packed_width), lambda i: (0, 0)),
            pl.BlockSpec((1, count), lambda i: (0, 0)),
            pl.BlockSpec((block, width), lambda i: (i, 0)),
            pl.BlockSpec((block, 128), lambda i: (i, 0)),
            pl.BlockSpec((block // 2, width), lambda i: (i, 0)),
            pl.BlockSpec((block // 2, width), lambda i: (i, 0)),
        ],
        out_specs=[
            pl.BlockSpec((word_count, packed_width), lambda i: (0, 0)),
            pl.BlockSpec((ent_count, packed_width), lambda i: (0, 0)),
            pl.BlockSpec((8, 2 * width), lambda i: (0, 0)),
        ],
        out_shape=[
            jax.ShapeDtypeStruct((word_count, packed_width), jnp.bfloat16),
            jax.ShapeDtypeStruct((ent_count, packed_width), jnp.bfloat16),
            jax.ShapeDtypeStruct((8, 2 * width), jnp.float32),
        ],
        scratch_shapes=[
            pltpu.VMEM((width, count), jnp.float32),
            pltpu.VMEM((width, count), jnp.float32),
        ],
        compiler_params=pltpu.CompilerParams(dimension_semantics=("arbitrary",)),
        cost_estimate=pl.CostEstimate(
            flops=10 * count * count * width,
            bytes_accessed=16 * count * packed_width,
            transcendentals=count * count * heads,
        ),
        name="attention_back",
    )(packed_word, packed_ent, packed_word, packed_ent, offsets, attn, stats, *grads)


def tall(left):
    return jnp.swapaxes(left, -1, -2)


def halves(array):
    high = array.astype(jnp.bfloat16)
    return high, (array - high.astype(jnp.float32)).astype(jnp.bfloat16)


def stacked_halves(array):
    high = array.astype(jnp.bfloat16).astype(jnp.float32)
    return jnp.concatenate([array, array - high], 0).astype(jnp.bfloat16)


def factor(rank_rows, full, dot):
    rank = rank_rows.shape[0]
    both = stacked_halves(rank_rows)
    high, low = halves(full)
    out = dot(both, high) + dot(both, low)
    return out[:rank] + out[rank:]


def left_ffn_kernel(
    got_ref, down_ref, err_up_ref, err_down_ref, q_up_ref, q_down_ref, full_up_ref, full_down_ref, left_ref
):
    step = pl.program_id(0)

    @pl.when(step < 4)
    def _():
        full = got_ref[0].astype(jnp.float32) + err_up_ref[0]
        full_up_ref[...] = full
        part = factor(q_up_ref[...], full, nt_dot)

        @pl.when(step == 0)
        def _():
            left_ref[0] = part

        @pl.when(step > 0)
        def _():
            left_ref[0] += part

    @pl.when(step >= 4)
    def _():
        full = down_ref[...] + err_down_ref[0]
        full_down_ref[...] = full
        left_ref[0] = factor(q_down_ref[...], full, nt_dot)


def left_of_ffn(got_up, grad_down, err_up, err_down, q_up, q_down):
    rows, width = got_up.shape[1:]
    rank = q_up.shape[0]

    def up_at(i):
        return jnp.minimum(i, 3)

    def down_at(i):
        return jnp.maximum(i - 4, 0)

    return pl.pallas_call(
        left_ffn_kernel,
        grid=(8,),
        in_specs=[
            pl.BlockSpec((1, rows, width), lambda i: (up_at(i), 0, 0)),
            pl.BlockSpec((rows, width), lambda i: (down_at(i), 0)),
            pl.BlockSpec((1, rows, width), lambda i: (0, 0, up_at(i))),
            pl.BlockSpec((1, rows, width), lambda i: (0, down_at(i), 0)),
            pl.BlockSpec((rank, width), lambda i: (0, up_at(i))),
            pl.BlockSpec((rank, width), lambda i: (0, 0)),
        ],
        out_specs=[
            pl.BlockSpec((rows, width), lambda i: (0, up_at(i))),
            pl.BlockSpec((rows, width), lambda i: (down_at(i), 0)),
            pl.BlockSpec((1, rank, rows), lambda i: (jnp.maximum(i - 3, 0), 0, 0)),
        ],
        out_shape=[
            jax.ShapeDtypeStruct((rows, 4 * width), jnp.float32),
            jax.ShapeDtypeStruct((4 * rows, width), jnp.float32),
            jax.ShapeDtypeStruct((5, rank, rows), jnp.float32),
        ],
        name="left_ffn",
    )(got_up, grad_down, err_up, err_down, q_up, q_down)


def left_attn_kernel(got_ref, out_ref, err_ref, q_ref, ffn_ref, full_ref, left_ref):
    step = pl.program_id(0)
    rows = full_ref.shape[1]

    @pl.when(step == 0)
    def _():
        left_ref[7:] = ffn_ref[...]

    for j in range(6):

        @pl.when(step == j)
        def _():
            grad = jnp.concatenate(
                [got_ref[s, :, j * rows : (j + 1) * rows] for s in range(4)], 1
            )
            full_ref[0] = grad.astype(jnp.float32) + err_ref[0, 0]

    @pl.when(step == 6)
    def _():
        full_ref[0] = out_ref[...] + err_ref[0, 0]

    left_ref[step] = factor(q_ref[0], full_ref[0], nt_dot)


def left_of_attn(got, grad_out, err_attn, q_attn, left_ffn):
    rows, width = grad_out.shape
    rank = q_attn.shape[1]
    return pl.pallas_call(
        left_attn_kernel,
        grid=(7,),
        in_specs=[
            pl.BlockSpec(got.shape, lambda i: (0, 0, 0)),
            pl.BlockSpec((rows, width), lambda i: (0, 0)),
            pl.BlockSpec((1, 1, rows, width), lambda i: (0, i, 0, 0)),
            pl.BlockSpec((1, rank, width), lambda i: (i, 0, 0)),
            pl.BlockSpec((5, rank, rows), lambda i: (0, 0, 0)),
        ],
        out_specs=[
            pl.BlockSpec((1, rows, width), lambda i: (i, 0, 0)),
            pl.BlockSpec((12, rank, rows), lambda i: (0, 0, 0)),
        ],
        out_shape=[
            jax.ShapeDtypeStruct((7, rows, width), jnp.float32),
            jax.ShapeDtypeStruct((12, rank, rows), jnp.float32),
        ],
        name="left_attn",
    )(got, grad_out, err_attn, q_attn, left_ffn)


MATRIX_BLOCKS = [[j] for j in range(8)] + [[8, 9, 10, 11]]


def gram_kernel(scale, mine_ref, other_ref, left_ref, gram_ref):
    rank = mine_ref.shape[1]
    left = (mine_ref[...] + other_ref[...]) * scale
    left_ref[...] = left
    lane = lax.broadcasted_iota(jnp.int32, (rank, 128), 1)
    row = lax.broadcasted_iota(jnp.int32, (rank, 128), 0)
    for r in range(rank):
        gram = jnp.where((lane >= len(MATRIX_BLOCKS)) & (row == r), 1.0, 0.0)
        for m, blocks in enumerate(MATRIX_BLOCKS):
            product = sum(left[b] * left[b, r : r + 1] for b in blocks)
            gram = jnp.where(lane == m, jnp.sum(product, -1, keepdims=True), gram)
        gram_ref[r] = gram


def gram_of(mine, other, scale):
    rank = mine.shape[1]
    return pl.pallas_call(
        functools.partial(gram_kernel, scale),
        out_shape=[
            jax.ShapeDtypeStruct(mine.shape, jnp.float32),
            jax.ShapeDtypeStruct((rank, rank, 128), jnp.float32),
        ],
        name="gram",
    )(mine, other)


def inverse_factor(columns, rank):
    row = lax.broadcasted_iota(jnp.int32, columns[0].shape, 0)
    columns, lower = list(columns), []
    for k in range(rank):
        column = columns[k] / jnp.sqrt(columns[k][k : k + 1])
        lower.append(column)
        for c in range(k + 1, rank):
            columns[c] = columns[c] - column * column[c : c + 1]
    inverse = []
    for r in range(rank):
        value = jnp.where(row == r, 1.0, 0.0)
        for t in range(r):
            value = value - lower[t][r : r + 1] * inverse[t]
        inverse.append(value / lower[r][r : r + 1])
    return inverse


def right_kernel(
    gram_ref, other_ref, left_ref, attn_ref, up_ref, down_ref, vec_ref, orth_ref, right_ref
):
    step = pl.program_id(0)
    rank, rows = left_ref.shape[1:]

    @pl.when(step == 0)
    def _():
        inverse = inverse_factor([gram_ref[r] + other_ref[r] for r in range(rank)], rank)
        row = lax.broadcasted_iota(jnp.int32, (rank, rows), 0)
        for m, blocks in enumerate(MATRIX_BLOCKS):
            weights = [inverse[r][:, m : m + 1] for r in range(rank)]
            for b in blocks:
                left = left_ref[b]
                orth = jnp.zeros((rank, rows), jnp.float32)
                for r in range(rank):
                    total = jnp.sum(left * weights[r], 0, keepdims=True)
                    orth = jnp.where(row == r, total, orth)
                orth_ref[b] = orth

    @pl.when(step < 7)
    def _():
        right_ref[0] = factor(orth_ref[step], attn_ref[0], mm)

    @pl.when((step >= 7) & (step < 11))
    def _():
        right_ref[0] = factor(orth_ref[7], up_ref[...], mm)

    @pl.when((step >= 11) & (step < 15))
    def _():
        part = factor(orth_ref[step - 3], down_ref[...], mm)

        @pl.when(step == 11)
        def _():
            right_ref[0] = part

        @pl.when(step > 11)
        def _():
            right_ref[0] += part

    @pl.when(step >= 15)
    def _():
        right_ref[0] = vec_ref[0]


def right_of(gram, other, left, full_attn, full_up, full_down, vecs):
    rank, rows = left.shape[1:]
    width = full_attn.shape[2]

    def whole(array):
        return pl.BlockSpec(array.shape, lambda i: (0,) * array.ndim)

    return pl.pallas_call(
        right_kernel,
        grid=(17,),
        in_specs=[
            whole(gram),
            whole(other),
            whole(left),
            pl.BlockSpec((1, rows, width), lambda i: (jnp.minimum(i, 6), 0, 0)),
            pl.BlockSpec((rows, width), lambda i: (0, jnp.clip(i - 7, 0, 3))),
            pl.BlockSpec((rows, width), lambda i: (jnp.clip(i - 11, 0, 3), 0)),
            pl.BlockSpec((1, rank, width), lambda i: (jnp.clip(i - 15, 0, 1), 0, 0)),
        ],
        out_specs=[
            whole(left),
            pl.BlockSpec(
                (1, rank, width),
                lambda i: (jnp.where(i < 15, jnp.minimum(i, 11), i - 3), 0, 0),
            ),
        ],
        out_shape=[
            jax.ShapeDtypeStruct(left.shape, jnp.float32),
            jax.ShapeDtypeStruct((14, rank, width), jnp.float32),
        ],
        name="right",
    )(gram, other, left, full_attn, full_up, full_down, vecs)


def left_stack(orth):
    high = orth.astype(jnp.bfloat16).astype(jnp.float32)
    return jnp.concatenate([orth, orth, orth - high, jnp.zeros_like(orth)], 0).astype(jnp.bfloat16)


def right_stack(right):
    high = right.astype(jnp.bfloat16).astype(jnp.float32)
    return jnp.concatenate([right, right - high, right, jnp.zeros_like(right)], 0).astype(
        jnp.bfloat16
    )


def update_kernel(rate, orth_ref, right_ref, cols_ref, up_cols_ref, *refs):
    full_refs, mom_refs, weight_refs = refs[:3], refs[3:6], refs[6:9]
    err_refs, next_refs, new_refs = refs[9:12], refs[12:15], refs[15:18]
    step = pl.program_id(0)

    def move(change, mom_ref, weight_ref, next_ref, new_ref, at):
        value = MOMENTUM * mom_ref[at] + change
        next_ref[at] = value
        new_ref[at] = weight_ref[at] - rate * value

    @pl.when(step < 7)
    def _():
        left = left_stack(orth_ref[step])
        approx = tn_dot(left, right_stack(right_ref[step]))
        err_refs[0][0, 0] = full_refs[0][0] - approx
        change = tn_dot(left, right_stack(cols_ref[step]))
        move(change, mom_refs[0], weight_refs[0], next_refs[0], new_refs[0], 0)

    @pl.when((step >= 7) & (step < 11))
    def _():
        left = left_stack(orth_ref[7])
        approx = tn_dot(left, right_stack(right_ref[step]))
        err_refs[1][0] = full_refs[1][...] - approx

        @pl.when(step == 7)
        def _():
            change = tn_dot(left, right_stack(up_cols_ref[0]))
            move(change, mom_refs[1], weight_refs[1], next_refs[1], new_refs[1], ...)

    @pl.when(step >= 11)
    def _():
        left = left_stack(orth_ref[step - 3])
        approx = tn_dot(left, right_stack(right_ref[11]))
        err_refs[2][0] = full_refs[2][...] - approx
        change = tn_dot(left, right_stack(cols_ref[11]))
        move(change, mom_refs[2], weight_refs[2], next_refs[2], new_refs[2], ...)


def updates(orth, right, right_cols, up_cols, full, mom, weight, rate):
    rows = orth.shape[2]
    width = right.shape[2]
    cols, cols_up = right_cols.shape[2], up_cols.shape[2]

    def whole(array):
        return pl.BlockSpec(array.shape, lambda i: (0,) * array.ndim)

    def attn_at(i):
        return jnp.minimum(i, 6)

    def up_at(i):
        return jnp.clip(i - 7, 0, 3)

    def down_at(i):
        return jnp.clip(i - 11, 0, 3)

    full_specs = [
        pl.BlockSpec((1, rows, width), lambda i: (attn_at(i), 0, 0)),
        pl.BlockSpec((rows, width), lambda i: (0, up_at(i))),
        pl.BlockSpec((rows, width), lambda i: (down_at(i), 0)),
    ]
    own_specs = [
        pl.BlockSpec((1, rows, cols), lambda i: (attn_at(i), 0, 0)),
        pl.BlockSpec((rows, cols_up), lambda i: (0, 0)),
        pl.BlockSpec((rows, cols), lambda i: (down_at(i), 0)),
    ]
    err_specs = [
        pl.BlockSpec((1, 1, rows, width), lambda i: (0, attn_at(i), 0, 0)),
        pl.BlockSpec((1, rows, width), lambda i: (0, 0, up_at(i))),
        pl.BlockSpec((1, rows, width), lambda i: (0, down_at(i), 0)),
    ]
    err_shapes = [jax.ShapeDtypeStruct((1,) + array.shape, jnp.float32) for array in full]
    own_shapes = [jax.ShapeDtypeStruct(array.shape, jnp.float32) for array in mom]
    outs = pl.pallas_call(
        functools.partial(update_kernel, rate),
        grid=(15,),
        in_specs=[whole(orth), whole(right), whole(right_cols), whole(up_cols)]
        + full_specs
        + own_specs
        + own_specs,
        out_specs=err_specs + own_specs + own_specs,
        out_shape=err_shapes + own_shapes + own_shapes,
        name="updates",
    )(orth, right, right_cols, up_cols, *full, *mom, *weight)
    return outs[:3], outs[3:6], outs[6:]


def head_split_device(
    x_words,
    x_ents,
    spans,
    word_mask,
    ent_mask,
    cot_words,
    cot_ents,
    attn_w,
    up_w,
    down_w,
    vecs,
    mom_attn,
    mom_up,
    mom_down,
    mom_vecs,
    err_attn,
    err_up,
    err_down,
    attention_prior_right,
    qf_up,
    qf_down,
):
    low_type = jnp.bfloat16
    words_dev, width = x_words.shape[1:]
    ents_dev = x_ents.shape[1]
    rows_dev = words_dev + ents_dev
    seq_count, rep_count = lax.axis_size("seq"), lax.axis_size("rep")
    seq_index, rep_index = lax.axis_index("seq"), lax.axis_index("rep")
    heads = HEADS // seq_count
    part = width // seq_count
    word_count = words_dev * seq_count
    ent_count = ents_dev * seq_count
    cols = attn_w.shape[2]
    cols_up = up_w.shape[1]
    hidden = cols_up * rep_count
    hidden_part = hidden // seq_count

    place = jnp.stack([rep_index // 2, rep_index % 2]).astype(jnp.int32)
    block = part // 2
    project_piece = jnp.transpose(
        attn_w[:6].astype(low_type).reshape(6, 2, block, cols), (2, 1, 0, 3)
    ).reshape(block, 12 * cols)
    half = block // 2
    trees = [
        gather_tree(planes_swap(project_piece[:half])),
        gather_tree(planes_swap(project_piece[half:])),
    ]
    (w_out,) = join_call(
        out_join_kernel,
        place,
        gather_tree(attn_w[6].astype(low_type).T),
        [(width, part)],
        "join_out",
    )
    up_piece = jnp.transpose(
        up_w.astype(low_type).reshape(2, block, cols_up), (1, 0, 2)
    ).reshape(block, 2 * cols_up)
    up_piece, unused_near = lax.optimization_barrier((up_piece, trees[1][4]))
    ffn_piece = jnp.concatenate([planes_swap(up_piece), down_w.astype(low_type).T], 1)
    ffn_pieces, ffn_side = gather_direct(ffn_piece)

    spans, unused_piece = lax.optimization_barrier((spans, project_piece))
    inputs = jnp.concatenate([x_words[0], x_ents[0] + span_mean_closed(spans[0], width)], 0)
    live = jnp.concatenate([word_mask[0], ent_mask[0]], 0).astype(low_type)
    live = jnp.pad(live.reshape(1, rows_dev), ((0, 15), (0, width - rows_dev)))
    pieces = gather_seq(jnp.concatenate([inputs.astype(low_type), live], 0))
    lives = [piece[rows_dev, :rows_dev] for piece in pieces]
    lives = [piece[:words_dev] for piece in lives] + [piece[words_dev:] for piece in lives]
    offsets = ((jnp.concatenate(lives).astype(jnp.float32) - 1.0) * MASK_FILL).reshape(1, -1)

    own_vecs = lax.dynamic_slice_in_dim(vecs, seq_index * part, part, 1)
    none = jnp.zeros((part,), jnp.float32)
    scale = jnp.where(jnp.arange(4 * part) < 2 * part, 0.125, 1.0).astype(jnp.float32)
    bias_word = jnp.concatenate([own_vecs[0], own_vecs[1], none, own_vecs[4]])
    bias_ent = jnp.concatenate([own_vecs[2], own_vecs[3], none, own_vecs[4]])
    in_vmem = pl.BlockSpec(memory_space=pltpu.VMEM)
    w_word, w_ent, packed_word, packed_ent, rows_word, rows_ent = pl.pallas_call(
        functools.partial(project_kernel, words_dev, rows_dev),
        in_specs=[pl.BlockSpec(memory_space=pltpu.SMEM)] + [in_vmem] * 19,
        out_specs=[in_vmem] * 6,
        out_shape=[
            jax.ShapeDtypeStruct(shape, low_type)
            for shape in [
                (rows, width)
                for rows in (width, width, word_count, ent_count, word_count, ent_count)
            ]
        ],
        scratch_shapes=[pltpu.VMEM((2, 4, 2, half, 12 * cols), low_type)],
        name="project",
    )(
        place,
        bias_word.reshape(1, -1),
        bias_ent.reshape(1, -1),
        scale.reshape(1, -1),
        *trees[0],
        *trees[1],
        *pieces,
    )
    attn, *attn_low, stats = attention_forward(packed_word, packed_ent, offsets, heads)
    attn_low, ffn_pieces, ffn_side = lax.optimization_barrier((attn_low, ffn_pieces, ffn_side))
    ffn_sides = [ffn_side] + [rep_swap(piece, 1) for piece in ffn_pieces[1:]]
    w_up, w_down = join_call(
        ffn_join_kernel,
        place,
        ffn_pieces + ffn_sides,
        [(width, hidden_part), (width, hidden_part)],
        "join_ffn",
    )

    bias_up = lax.dynamic_slice_in_dim(
        vecs[11:15].reshape(hidden), seq_index * hidden_part, hidden_part, 0
    )
    grad_result = jnp.concatenate([cot_words[0], cot_ents[0]], 0)
    split = rows_dev // 2
    results, grads_one, grads_attn, kept = [], [], [], []
    sums = [0.0] * 7
    for c in (0, 1):
        at = slice(c * split, (c + 1) * split)
        branch = scatter_blocks(attn_low[c], nt_dot, w_out) + vecs[5]
        mid, normed_one, rstd_one = rows_norm(inputs[at] + branch, vecs[7], vecs[8])
        mid_low = jnp.concatenate(gather_seq(mid.astype(low_type)), 0)
        pre = mm(mid_low, w_up) + bias_up
        cdf = 0.5 * (1.0 + lax.erf(pre * math.sqrt(0.5)))
        act_low = (pre * cdf).astype(low_type)
        ffn = scatter_blocks(act_low, nt_dot, w_down) + vecs[6]
        result, normed_two, rstd_two = rows_norm(mid + ffn, vecs[9], vecs[10])
        grad_two, gain_two, shift_two = rows_norm_back(grad_result[at], normed_two, rstd_two, vecs[9])
        grad_ffn = jnp.concatenate(gather_seq(grad_two.astype(low_type)), 0)
        density = jnp.exp(-0.5 * pre * pre) * (1.0 / math.sqrt(2.0 * math.pi))
        grad_pre = mm(grad_ffn, w_down) * (cdf + pre * density)
        grad_pre_low = grad_pre.astype(low_type)
        grad_mid = grad_two + scatter_blocks(grad_pre_low, nt_dot, w_up)
        grad_one, gain_one, shift_one = rows_norm_back(grad_mid, normed_one, rstd_one, vecs[7])
        grad_branch = jnp.concatenate(gather_seq(grad_one.astype(low_type)), 0)
        grads_attn.append(mm(grad_branch, w_out))
        results.append(result)
        grads_one.append(grad_one)
        kept.append((mid_low, act_low, grad_ffn, grad_pre_low, grad_branch))
        parts = (
            jnp.sum(grad_one, 0),
            jnp.sum(grad_two, 0),
            gain_one,
            shift_one,
            gain_two,
            shift_two,
            jnp.sum(grad_pre, 0),
        )
        sums = [total + value for total, value in zip(sums, parts)]
    result = jnp.concatenate(results, 0)
    grad_one = jnp.concatenate(grads_one, 0)
    grad_down = sum(tn_dot(act_low, grad_ffn) for _, act_low, grad_ffn, _, _ in kept)
    grad_up = sum(tn_dot(mid_low, grad_pre_low) for mid_low, _, _, grad_pre_low, _ in kept)
    grad_up, unused_branch = lax.optimization_barrier((grad_up.astype(low_type), kept[1][4]))
    got_up = lax.all_to_all(grad_up.reshape(seq_count, part, hidden_part), "seq", 0, 0)
    full_up, full_down, left_ffn = left_of_ffn(
        got_up, grad_down, err_up, err_down, qf_up.T, qf_down.T
    )
    grad_out = sum(tn_dot(low, parts[4]) for low, parts in zip(attn_low, kept))
    d_word, d_ent, d_sums = attention_backward(
        packed_word, packed_ent, offsets, attn, stats, grads_attn, heads
    )
    grad_word = tn_dot(rows_word, d_word)
    grad_ent = tn_dot(rows_ent, d_ent)
    grad_project = jnp.concatenate(
        [
            grad_word[:, : 2 * part],
            grad_ent[:, : 2 * part],
            grad_word[:, 2 * part :] + grad_ent[:, 2 * part :],
        ],
        1,
    ).astype(low_type)
    got_project = lax.all_to_all(
        grad_project.reshape(seq_count, part, 6 * part), "seq", 0, 0
    )
    grad_inputs = grad_one + scatter_parts(nt_dot(d_word, w_word), nt_dot(d_ent, w_ent))

    vec_grad = jnp.zeros((15, width), jnp.float32)
    bias_query = jnp.concatenate(
        [d_sums[0].reshape(2, part), d_sums[1].reshape(2, part), d_sums[2, :part].reshape(1, part)], 0
    )
    vec_grad = lax.dynamic_update_slice(vec_grad, bias_query, (0, seq_index * part))
    vec_grad = lax.dynamic_update_slice(vec_grad, jnp.stack(sums[:6]), (5, 0))
    bias_rows = hidden_part // width
    vec_grad = lax.dynamic_update_slice(
        vec_grad, sums[6].reshape(bias_rows, width), (11 + seq_index * bias_rows, 0)
    )

    full_attn, left = left_of_attn(
        got_project, grad_out, err_attn, tall(attention_prior_right), left_ffn
    )
    for bits in (1, 2):
        left = left + rep_swap(left, bits)
    left, gram = gram_of(left, rep_swap(left, 4), 1.0 / rep_count)
    gram = gram + seq_swap(gram, 1)
    rows_vec = jnp.pad(vec_grad, ((0, 1), (0, 0))).reshape(2, 8, width)
    orth, right = right_of(
        gram, seq_swap(gram, 2), left, full_attn, full_up, full_down, rows_vec
    )
    core, chip = seq_index % 2, seq_index // 2
    blocks, rank = right.shape[:2]
    lanes, upper = width // 2, blocks // 2
    sent = lax.dynamic_slice_in_dim(right, (1 - core) * lanes, lanes, 2)
    kept = lax.dynamic_slice_in_dim(right, core * lanes, lanes, 2) + seq_swap(sent, 1)
    sent = lax.dynamic_slice_in_dim(kept, (1 - chip) * upper, upper, 0)
    kept = lax.dynamic_slice_in_dim(kept, chip * upper, upper, 0) + seq_swap(sent, 2)
    for bits in (1, 2, 4):
        kept = kept + rep_swap(kept, bits)
    kept = kept / rep_count
    got = seq_swap(kept, 2)
    kept = jnp.where(
        chip == 0, jnp.concatenate([kept, got], 0), jnp.concatenate([got, kept], 0)
    )
    got = seq_swap(kept, 1)
    right = jnp.where(
        core == 0, jnp.concatenate([kept, got], 2), jnp.concatenate([got, kept], 2)
    )
    vec_mean = right[12:].reshape(16, width)[:15]
    lr_mat = 1.5 * math.sqrt(rep_count / (SEQS * (WORDS + ENTS)))
    lr_vec = 0.2 * math.sqrt(rep_count / (SEQS * (WORDS + ENTS)))
    right_cols = lax.dynamic_slice_in_dim(right, rep_index * cols, cols, 2)
    up_cols = lax.dynamic_slice(
        right, (7 + rep_index // 2, 0, (rep_index % 2) * cols_up), (1, rank, cols_up)
    )
    next_err, next_mom, new = updates(
        orth,
        right,
        right_cols,
        up_cols,
        (full_attn, full_up, full_down),
        (mom_attn, mom_up, mom_down),
        (attn_w, up_w, down_w),
        lr_mat,
    )
    next_mom_vecs = MOMENTUM * mom_vecs + vec_mean
    return (
        result[None, :words_dev],
        result[None, words_dev:],
        grad_inputs[None, :words_dev],
        grad_inputs[None, words_dev:],
        new[0],
        new[1],
        new[2],
        vecs - lr_vec * next_mom_vecs,
        next_mom[0],
        next_mom[1],
        next_mom[2],
        next_mom_vecs,
        next_err[0],
        next_err[1],
        next_err[2],
        tall(orth[:7]),
        tall(orth[7]),
        tall(orth[8:]).reshape(4 * part, rank),
        tall(right[:7]),
        tall(right[7:11]).reshape(4 * width, rank),
        tall(right[11]),
    )


def solution(mesh):
    in_specs = (
        P("rep", "seq", None),
        P("rep", "seq", None),
        P("rep", "seq", None),
        P("rep", "seq"),
        P("rep", "seq"),
        P("rep", "seq", None),
        P("rep", "seq", None),
        P(None, "seq", "rep"),
        P("seq", "rep"),
        P("seq", "rep"),
        P(),
        P(None, "seq", "rep"),
        P("seq", "rep"),
        P("seq", "rep"),
        P(),
        P("rep", None, "seq", None),
        P("rep", "seq", None),
        P("rep", "seq", None),
        P(),
        P(),
        P(),
    )
    out_specs = (
        P("rep", "seq", None),
        P("rep", "seq", None),
        P("rep", "seq", None),
        P("rep", "seq", None),
        P(None, "seq", "rep"),
        P("seq", "rep"),
        P("seq", "rep"),
        P(),
        P(None, "seq", "rep"),
        P("seq", "rep"),
        P("seq", "rep"),
        P(),
        P("rep", None, "seq", None),
        P("rep", "seq", None),
        P("rep", "seq", None),
        P(None, "seq", None),
        P("seq", None),
        P("seq", None),
        P(),
        P(),
        P(),
    )
    seqs, reps = mesh.shape["seq"], mesh.shape["rep"]
    split_heads = seqs == 4 and reps == 2 * seqs and HEADS % seqs == 0
    body = head_split_device if split_heads else on_device
    return jax.shard_map(
        body, mesh=mesh, in_specs=in_specs, out_specs=out_specs, check_vma=False
    )
```

```python
import functools
import math

import jax
import jax.numpy as jnp
from jax import lax
from jax.experimental import pallas as pl
from jax.experimental.pallas import tpu as pltpu
from jax.sharding import PartitionSpec as P

HEADS = 12
WORDS = 1024
ENTS = 128
SPAN = 16
SEQS = 1


HIGH_PRECISION = lax.Precision.HIGHEST
EPS = 1e-05
MASK_FILL = 30000.0
MOMENTUM = 0.9


def span_mean(spans, model_width):
    starts = spans[..., 0]
    finals = spans[..., 1]
    lengths = (finals - starts + 1).astype(jnp.float32)
    offsets = jnp.arange(SPAN, dtype=jnp.int32)
    places = (starts[..., None] + offsets).astype(jnp.float32)
    shares = (offsets <= (finals - starts)[..., None]).astype(jnp.float32) / lengths[..., None]
    half_width = model_width // 2
    rates = jnp.exp(
        jnp.arange(half_width).astype(jnp.float32) * (-2.0 * math.log(10000.0) / model_width)
    )
    angles = places[..., None] * rates
    table = jnp.concatenate([jnp.sin(angles), jnp.cos(angles)], -1)
    return jnp.sum(table * shares[..., None], axis=-2)


def span_mean_closed(spans, model_width):
    lengths = (spans[..., 1] - spans[..., 0] + 1).astype(jnp.float32)[..., None]
    middles = (spans[..., 1] + spans[..., 0]).astype(jnp.float32)[..., None]
    half_rates = 0.5 * jnp.exp(
        jnp.arange(model_width // 2).astype(jnp.float32) * (-2.0 * math.log(10000.0) / model_width)
    )
    share = jnp.sin(lengths * half_rates) / (lengths * jnp.sin(half_rates))
    angles = middles * half_rates
    return jnp.concatenate([share * jnp.sin(angles), share * jnp.cos(angles)], -1)


def layer_norm(hidden, gain, shift):
    center = hidden - jnp.mean(hidden, -1, keepdims=True)
    rstd = lax.rsqrt(jnp.mean(center * center, -1, keepdims=True) + EPS)
    normed = center * rstd
    return (normed * gain + shift, normed, rstd)


def norm_back(grad, normed, rstd, gain):
    dnormed = grad * gain
    grad_in = rstd * (
        dnormed
        - jnp.mean(dnormed, -1, keepdims=True)
        - normed * jnp.mean(dnormed * normed, -1, keepdims=True)
    )
    return (grad_in, jnp.sum(grad * normed, axis=(0, 1)), jnp.sum(grad, axis=(0, 1)))


def gelu_exact(value):
    return jax.nn.gelu(value, approximate=False)


def project(row_entries, weight_matrix):
    return jnp.einsum("thq,qo->tho", row_entries, weight_matrix, preferred_element_type=jnp.float32)


def project_back(row_entries, weight_matrix):
    return jnp.einsum("hpf,zf->hpz", row_entries, weight_matrix, preferred_element_type=jnp.float32)


def weight_grad(input_arrays, gradient_list):
    return jnp.einsum(
        "cev,ceg->vg", input_arrays, gradient_list, preferred_element_type=jnp.float32
    )


def split_keys(pieces, words_dev, ents_dev, head_count):
    key_piece, live_piece = pieces
    batch_rows = key_piece.shape[0]
    both = key_piece.shape[2]
    model_width = both // 2
    head_dim = model_width // head_count
    rows_dev = words_dev + ents_dev
    blocks = key_piece.shape[1] // rows_dev
    grouped = key_piece.reshape(batch_rows, blocks, rows_dev, both)
    live_grouped = live_piece.reshape(batch_rows, blocks, rows_dev)
    word_part = grouped[:, :, :words_dev].reshape(batch_rows, blocks * words_dev, both)
    ent_part = grouped[:, :, words_dev:].reshape(batch_rows, blocks * ents_dev, both)
    keys_word = word_part[..., :model_width].reshape(batch_rows, -1, head_count, head_dim)
    keys_ent = ent_part[..., :model_width].reshape(batch_rows, -1, head_count, head_dim)
    values = jnp.concatenate(
        [word_part[..., model_width:], ent_part[..., model_width:]], 1
    ).reshape(batch_rows, -1, head_count, head_dim)
    live = jnp.concatenate(
        [
            live_grouped[:, :, :words_dev].reshape(batch_rows, -1),
            live_grouped[:, :, words_dev:].reshape(batch_rows, -1),
        ],
        1,
    )
    offsets = (live.astype(jnp.float32) - 1.0) * MASK_FILL
    return (keys_word, keys_ent, values, offsets, blocks)


def score_block(query_word, query_ent, keys_word, keys_ent, offsets):
    score_word = jnp.einsum(
        "sqhd,skhd->shqk", query_word, keys_word, preferred_element_type=jnp.float32
    )
    score_ent = jnp.einsum(
        "sqhd,skhd->shqk", query_ent, keys_ent, preferred_element_type=jnp.float32
    )
    return jnp.concatenate([score_word, score_ent], -1) + offsets[:, None, None, :]


def flat_heads(array):
    return array.reshape(array.shape[0], array.shape[1], -1)


def join_rows(grad_keys_word, grad_keys_ent, grad_values, blocks, words_dev, ents_dev):
    batch_rows = grad_keys_word.shape[0]
    word_count = grad_keys_word.shape[1]
    word_rows = jnp.concatenate(
        [flat_heads(grad_keys_word), flat_heads(grad_values[:, :word_count])], -1
    )
    ent_rows = jnp.concatenate(
        [flat_heads(grad_keys_ent), flat_heads(grad_values[:, word_count:])], -1
    )
    word_rows = word_rows.reshape(batch_rows, blocks, words_dev, -1)
    ent_rows = ent_rows.reshape(batch_rows, blocks, ents_dev, -1)
    return jnp.concatenate([word_rows, ent_rows], 2).reshape(
        batch_rows, blocks * (words_dev + ents_dev), -1
    )


def from_gram(left, gram):
    lower = jnp.linalg.cholesky(gram)
    return jax.scipy.linalg.solve_triangular(lower, left.T, lower=True).T


def orthonormal(left):
    return from_gram(left, jnp.dot(left.T, left, precision=HIGH_PRECISION))


def on_device(
    x_words,
    x_ents,
    spans,
    word_mask,
    ent_mask,
    cot_words,
    cot_ents,
    attn_w,
    up_w,
    down_w,
    vecs,
    mom_attn,
    mom_up,
    mom_down,
    mom_vecs,
    err_attn,
    err_up,
    err_down,
    attention_prior_right,
    qf_up,
    qf_down,
):
    batch_rows, words_dev, model_width = x_words.shape
    ents_dev = x_ents.shape[1]
    rows_dev = words_dev + ents_dev
    head_count = HEADS
    head_dim = model_width // head_count
    hidden_width = up_w.shape[1] * lax.axis_size("rep")
    seq_count = lax.axis_size("seq")
    rep_count = lax.axis_size("rep")
    seq_index = lax.axis_index("seq")
    rep_index = lax.axis_index("rep")
    lowered = jnp.bfloat16
    column_parts = (
        lax.all_gather(attn_w.astype(lowered), "rep", axis=2, tiled=True),
        lax.all_gather(up_w.astype(lowered), "rep", axis=1, tiled=True),
        lax.all_gather(down_w.astype(lowered), "rep", axis=1, tiled=True),
    )
    w_attn, w_up, w_down = (
        lax.all_gather(column_parts[0], "seq", axis=1, tiled=True),
        lax.all_gather(column_parts[1], "seq", axis=0, tiled=True),
        lax.all_gather(column_parts[2], "seq", axis=0, tiled=True),
    )
    input_arrays = jnp.concatenate([x_words, x_ents + span_mean(spans, model_width)], 1)
    inputs_low = input_arrays.astype(lowered)
    word_low = inputs_low[:, :words_dev]
    ent_low = inputs_low[:, words_dev:]
    query_word = (
        jnp.concatenate(
            [project(word_low, w_attn[0]) + vecs[0], project(ent_low, w_attn[2]) + vecs[2]], 1
        )
        * 0.125
    ).astype(lowered)
    query_ent = (
        jnp.concatenate(
            [project(word_low, w_attn[1]) + vecs[1], project(ent_low, w_attn[3]) + vecs[3]], 1
        )
        * 0.125
    ).astype(lowered)
    keys_low = project(inputs_low, w_attn[4]).astype(lowered)
    values_low = (project(inputs_low, w_attn[5]) + vecs[4]).astype(lowered)
    key_rows = jnp.concatenate([keys_low, values_low], -1)
    key_live = jnp.concatenate([word_mask, ent_mask], 1).astype(lowered)
    heads_word = query_word.reshape(batch_rows, rows_dev, head_count, head_dim)
    heads_ent = query_ent.reshape(batch_rows, rows_dev, head_count, head_dim)
    forward_row_top = jnp.full((batch_rows, head_count, rows_dev), -jnp.inf, jnp.float32)
    row_total = jnp.zeros((batch_rows, head_count, rows_dev), jnp.float32)
    weighted = jnp.zeros((batch_rows, rows_dev, head_count, head_dim), jnp.float32)
    keys_word, keys_ent, values, offsets, blocks = split_keys(
        (
            lax.all_gather(key_rows, "seq", axis=1, tiled=True),
            lax.all_gather(key_live, "seq", axis=1, tiled=True),
        ),
        words_dev,
        ents_dev,
        head_count,
    )
    scores = score_block(heads_word, heads_ent, keys_word, keys_ent, offsets)
    new_top = jnp.max(scores, -1)
    factor = jnp.exp(forward_row_top - new_top)
    weights = jnp.exp(scores - new_top[..., None])
    row_total = row_total * factor + jnp.sum(weights, -1)
    weighted = weighted * jnp.transpose(factor, (0, 2, 1))[..., None] + jnp.einsum(
        "shqk,skhd->sqhd", weights.astype(lowered), values, preferred_element_type=jnp.float32
    )
    row_top, row_total, weighted = (new_top, row_total, weighted)
    total_rows = jnp.transpose(row_total, (0, 2, 1))[..., None]
    attn = weighted / total_rows
    attn_low = attn.reshape(batch_rows, rows_dev, model_width).astype(lowered)
    branch = project(attn_low, w_attn[6]) + vecs[5]
    mid, normed_one, rstd_one = layer_norm(input_arrays + branch, vecs[7], vecs[8])
    mid_low = mid.astype(lowered)
    pre = project(mid_low, w_up) + vecs[11:15].reshape(hidden_width)
    act_low = gelu_exact(pre).astype(lowered)
    ffn = project(act_low, w_down) + vecs[6]
    result, normed_two, rstd_two = layer_norm(mid + ffn, vecs[9], vecs[10])
    grad_result = jnp.concatenate([cot_words, cot_ents], 1)
    grad_two, gain_two, shift_two = norm_back(grad_result, normed_two, rstd_two, vecs[9])
    bias_down = jnp.sum(grad_two, axis=(0, 1))
    grad_ffn_low = grad_two.astype(lowered)
    grad_down = weight_grad(act_low, grad_ffn_low)
    grad_act = project_back(grad_ffn_low, w_down)
    unused_value, gelu_pull = jax.vjp(gelu_exact, pre)
    grad_pre = gelu_pull(grad_act)[0]
    bias_up = jnp.sum(grad_pre, axis=(0, 1))
    grad_pre_low = grad_pre.astype(lowered)
    grad_up = weight_grad(mid_low, grad_pre_low)
    grad_mid = grad_two + project_back(grad_pre_low, w_up)
    grad_one, gain_one, shift_one = norm_back(grad_mid, normed_one, rstd_one, vecs[7])
    bias_out = jnp.sum(grad_one, axis=(0, 1))
    grad_branch_low = grad_one.astype(lowered)
    grad_out_proj = weight_grad(attn_low, grad_branch_low)
    grad_attn = project_back(grad_branch_low, w_attn[6]).reshape(
        batch_rows, rows_dev, head_count, head_dim
    )
    grad_unnorm = (grad_attn / total_rows).astype(lowered)
    delta_rows = jnp.transpose(jnp.sum(grad_attn * attn, -1), (0, 2, 1)) / row_total
    keys_word, keys_ent, values, offsets, blocks = split_keys(
        (
            lax.all_gather(key_rows, "seq", axis=1, tiled=True),
            lax.all_gather(key_live, "seq", axis=1, tiled=True),
        ),
        words_dev,
        ents_dev,
        head_count,
    )
    scores = score_block(heads_word, heads_ent, keys_word, keys_ent, offsets)
    weights = jnp.exp(scores - row_top[..., None])
    grad_weights = jnp.einsum(
        "sqhd,skhd->shqk", grad_unnorm, values, preferred_element_type=jnp.float32
    )
    grad_scores = (weights * (grad_weights - delta_rows[..., None])).astype(lowered)
    word_count = keys_word.shape[1]
    scores_word = grad_scores[..., :word_count]
    scores_ent = grad_scores[..., word_count:]
    grad_query_word = jnp.einsum(
        "shqk,skhd->sqhd", scores_word, keys_word, preferred_element_type=jnp.float32
    )
    grad_query_ent = jnp.einsum(
        "shqk,skhd->sqhd", scores_ent, keys_ent, preferred_element_type=jnp.float32
    )
    grad_keys_word = jnp.einsum(
        "shqk,sqhd->skhd", scores_word, heads_word, preferred_element_type=jnp.float32
    )
    grad_keys_ent = jnp.einsum(
        "shqk,sqhd->skhd", scores_ent, heads_ent, preferred_element_type=jnp.float32
    )
    grad_values = jnp.einsum(
        "shqk,sqhd->skhd", weights.astype(lowered), grad_unnorm, preferred_element_type=jnp.float32
    )
    piece_grad = join_rows(grad_keys_word, grad_keys_ent, grad_values, blocks, words_dev, ents_dev)
    grad_rows = piece_grad
    grad_query_word, grad_query_ent, grad_rows = (grad_query_word, grad_query_ent, grad_rows)
    own_rows = lax.psum_scatter(
        grad_rows.astype(jnp.bfloat16), "seq", scatter_dimension=1, tiled=True
    ).astype(jnp.float32)
    grad_keys = own_rows[..., :model_width]
    grad_values = own_rows[..., model_width:]
    bias_values = jnp.sum(grad_values, axis=(0, 1))
    keys_grad_low = grad_keys.astype(lowered)
    values_grad_low = grad_values.astype(lowered)
    grad_key_w = weight_grad(inputs_low, keys_grad_low)
    grad_value_w = weight_grad(inputs_low, values_grad_low)
    inner_word = grad_query_word.reshape(batch_rows, rows_dev, model_width) * 0.125
    inner_ent = grad_query_ent.reshape(batch_rows, rows_dev, model_width) * 0.125
    bias_query = [
        jnp.sum(inner_word[:, :words_dev], axis=(0, 1)),
        jnp.sum(inner_ent[:, :words_dev], axis=(0, 1)),
        jnp.sum(inner_word[:, words_dev:], axis=(0, 1)),
        jnp.sum(inner_ent[:, words_dev:], axis=(0, 1)),
    ]
    inner_word_low = inner_word.astype(lowered)
    inner_ent_low = inner_ent.astype(lowered)
    grad_query_mats = [
        weight_grad(word_low, inner_word_low[:, :words_dev]),
        weight_grad(word_low, inner_ent_low[:, :words_dev]),
        weight_grad(ent_low, inner_word_low[:, words_dev:]),
        weight_grad(ent_low, inner_ent_low[:, words_dev:]),
    ]
    back_keys = project_back(keys_grad_low, w_attn[4]) + project_back(values_grad_low, w_attn[5])
    back_word = project_back(inner_word_low[:, :words_dev], w_attn[0]) + project_back(
        inner_ent_low[:, :words_dev], w_attn[1]
    )
    back_ent = project_back(inner_word_low[:, words_dev:], w_attn[2]) + project_back(
        inner_ent_low[:, words_dev:], w_attn[3]
    )
    grad_inputs = grad_one + back_keys + jnp.concatenate([back_word, back_ent], 1)
    grad_attn_w = jnp.stack(grad_query_mats + [grad_key_w, grad_value_w, grad_out_proj])
    vec_grad = jnp.concatenate(
        [
            jnp.stack(
                bias_query
                + [bias_values, bias_out, bias_down, gain_one, shift_one, gain_two, shift_two]
            ),
            bias_up.reshape(4, model_width),
        ],
        0,
    )
    rows_attn, rows_up, rows_down = (
        lax.psum_scatter(
            grad_attn_w.astype(jnp.bfloat16), "seq", scatter_dimension=1, tiled=True
        ).astype(jnp.float32),
        lax.psum_scatter(
            grad_up.astype(jnp.bfloat16), "seq", scatter_dimension=0, tiled=True
        ).astype(jnp.float32),
        lax.psum_scatter(
            grad_down.astype(jnp.bfloat16), "seq", scatter_dimension=0, tiled=True
        ).astype(jnp.float32),
    )
    attention_full_gradient = rows_attn + err_attn[0]
    full_up = rows_up + err_up[0]
    full_down = rows_down + err_down[0]
    attention_left_factor = jnp.einsum(
        "vcg,vgo->vco", attention_full_gradient, attention_prior_right, precision=HIGH_PRECISION
    )
    left_up = jnp.dot(full_up, qf_up, precision=HIGH_PRECISION)
    left_down = jnp.dot(full_down, qf_down, precision=HIGH_PRECISION)
    count_attn = attention_full_gradient.shape[1]
    count_up = full_up.shape[0]
    count_down = full_down.shape[0]
    placed_attn = lax.dynamic_update_slice_in_dim(
        jnp.zeros((7, count_attn * seq_count, attention_left_factor.shape[2]), jnp.float32),
        attention_left_factor,
        seq_index * count_attn,
        1,
    )
    placed_up = lax.dynamic_update_slice_in_dim(
        jnp.zeros((count_up * seq_count, left_up.shape[1]), jnp.float32),
        left_up,
        seq_index * count_up,
        0,
    )
    placed_down = lax.dynamic_update_slice_in_dim(
        jnp.zeros((count_down * seq_count, left_down.shape[1]), jnp.float32),
        left_down,
        seq_index * count_down,
        0,
    )
    summed_attn, summed_up, summed_down = lax.psum(
        (placed_attn, placed_up, placed_down), ("seq", "rep")
    )
    orth_attn = jax.vmap(orthonormal)(summed_attn / rep_count)
    orth_up = orthonormal(summed_up / rep_count)
    orth_down = orthonormal(summed_down / rep_count)
    attention_local_gradient = lax.dynamic_slice_in_dim(
        orth_attn, seq_index * count_attn, count_attn, 1
    )
    own_up = lax.dynamic_slice_in_dim(orth_up, seq_index * count_up, count_up, 0)
    own_down = lax.dynamic_slice_in_dim(orth_down, seq_index * count_down, count_down, 0)
    right_parts = (
        jnp.einsum(
            "dpl,dpg->dgl",
            attention_local_gradient,
            attention_full_gradient,
            precision=HIGH_PRECISION,
        ),
        jnp.dot(full_up.T, own_up, precision=HIGH_PRECISION),
        jnp.dot(full_down.T, own_down, precision=HIGH_PRECISION),
        vec_grad,
    )
    attention_right_factor, right_up, right_down, vec_total = lax.psum(
        (right_parts[0], right_parts[1], right_parts[2], right_parts[3]), ("seq", "rep")
    )
    attention_right_factor = attention_right_factor / rep_count
    right_up = right_up / rep_count
    right_down = right_down / rep_count
    vec_mean = vec_total / rep_count
    attention_estimate = jnp.einsum(
        "whg,wng->whn", attention_local_gradient, attention_right_factor, precision=HIGH_PRECISION
    )
    approx_up = jnp.dot(own_up, right_up.T, precision=HIGH_PRECISION)
    approx_down = jnp.dot(own_down, right_down.T, precision=HIGH_PRECISION)
    next_err_attn = (attention_full_gradient - attention_estimate)[None]
    next_err_up = (full_up - approx_up)[None]
    next_err_down = (full_down - approx_down)[None]
    cols_attn = attn_w.shape[2]
    cols_up = up_w.shape[1]
    cols_down = down_w.shape[1]
    step_attn = lax.dynamic_slice_in_dim(attention_estimate, rep_index * cols_attn, cols_attn, 2)
    step_up = lax.dynamic_slice_in_dim(approx_up, rep_index * cols_up, cols_up, 1)
    step_down = lax.dynamic_slice_in_dim(approx_down, rep_index * cols_down, cols_down, 1)
    lr_mat = 1.5 * math.sqrt(rep_count / (SEQS * (WORDS + ENTS)))
    lr_vec = 0.2 * math.sqrt(rep_count / (SEQS * (WORDS + ENTS)))
    next_mom_attn = MOMENTUM * mom_attn + step_attn
    next_mom_up = MOMENTUM * mom_up + step_up
    next_mom_down = MOMENTUM * mom_down + step_down
    next_mom_vecs = MOMENTUM * mom_vecs + vec_mean
    new_attn = attn_w - lr_mat * next_mom_attn
    new_up = up_w - lr_mat * next_mom_up
    new_down = down_w - lr_mat * next_mom_down
    new_vecs = vecs - lr_vec * next_mom_vecs
    return (
        result[:, :words_dev],
        result[:, words_dev:],
        grad_inputs[:, :words_dev],
        grad_inputs[:, words_dev:],
        new_attn,
        new_up,
        new_down,
        new_vecs,
        next_mom_attn,
        next_mom_up,
        next_mom_down,
        next_mom_vecs,
        next_err_attn,
        next_err_up,
        next_err_down,
        attention_local_gradient,
        own_up,
        own_down,
        attention_right_factor,
        right_up,
        right_down,
    )


def seq_swap(array, bits):
    size = lax.axis_size("seq")
    return lax.ppermute(array, "seq", [(i, i ^ bits) for i in range(size)])


def rep_swap(array, bits):
    size = lax.axis_size("rep")
    return lax.ppermute(array, "rep", [(i, i ^ bits) for i in range(size)])


def planes_swap(array):
    seqs, reps = lax.axis_size("seq"), lax.axis_size("rep")
    pairs = []
    for s in range(seqs):
        for r in range(reps):
            pairs.append((s * reps + r, (r // 2) * reps + 2 * s + r % 2))
    return lax.ppermute(array, ("seq", "rep"), pairs)


def gather_seq(piece):
    other_chip = seq_swap(piece, 2)
    return [seq_swap(piece, 1), seq_swap(other_chip, 1), piece, other_chip]


def gather_direct(piece):
    pieces = [piece] + [rep_swap(piece, 2 * change) for change in (1, 2, 3)]
    return pieces, rep_swap(piece, 1)


def gather_tree(piece):
    own_side = rep_swap(piece, 1)
    far = rep_swap(piece, 4)
    near = rep_swap(jnp.stack([piece, far]), 2)
    far_side = rep_swap(far, 1)
    near_side = rep_swap(near, 1)
    return [piece, own_side, far, far_side, near, near_side]


def tree_pieces(refs):
    own, own_side, far, far_side, near, near_side = refs
    return (
        (0, own[...], own_side[...]),
        (2, far[...], far_side[...]),
        (1, near[0], near_side[0]),
        (3, near[1], near_side[1]),
    )


def project_kernel(
    words_dev, rows_dev, place_ref, bias_word_ref, bias_ent_ref, scale_ref, *refs
):
    trees, row_refs = (refs[:6], refs[6:12]), refs[12:16]
    word_ref, ent_ref, packed_word_ref, packed_ent_ref, rows_word_ref, rows_ent_ref = refs[16:22]
    piece_ref = refs[22]
    ents_dev = rows_dev - words_dev
    z, y = place_ref[0], place_ref[1]
    for half, tree in enumerate(trees):
        for change, own, other in tree_pieces(tree):
            piece_ref[half, z ^ change, y] = own
            piece_ref[half, z ^ change, 1 - y] = other
    rows, both = piece_ref.shape[3:]
    cols = both // 12
    for half in (0, 1):
        for place in range(4):
            left, right = piece_ref[half, place, 0], piece_ref[half, place, 1]
            for upper in (0, 1):
                parts = []
                for j in range(6):
                    low = (upper * 6 + j) * cols
                    parts.append(left[:, low : low + cols])
                    parts.append(right[:, low : low + cols])
                start = (4 * place + 2 * upper + half) * rows
                target = slice(start, start + rows)
                word_ref[target] = jnp.concatenate(parts[:4] + parts[8:], 1)
                ent_ref[target] = jnp.concatenate(parts[4:], 1)

    scale = scale_ref[...]
    word, ent = word_ref[...], ent_ref[...]
    for k, row_ref in enumerate(row_refs):
        words = row_ref[:words_dev]
        at = slice(k * words_dev, (k + 1) * words_dev)
        rows_word_ref[at] = words
        packed_word_ref[at] = ((mm(words, word) + bias_word_ref[...]) * scale).astype(
            jnp.bfloat16
        )
        at = slice(k * ents_dev, (k + 1) * ents_dev)
        rows_ent_ref[at] = row_ref[words_dev:rows_dev]
    packed_ent_ref[...] = ((mm(rows_ent_ref[...], ent) + bias_ent_ref[...]) * scale).astype(
        jnp.bfloat16
    )


def ffn_join_kernel(place_ref, *refs):
    pieces, sides, (up_ref, down_ref) = refs[:4], refs[4:8], refs[8:]
    z, y = place_ref[0], place_ref[1]
    for side in (0, 1):

        @pl.when(y == side)
        def _():
            for change in range(4):
                for y_at, piece in ((side, pieces[change]), (1 - side, sides[change])):
                    rows, both = piece.shape
                    cols = both // 4
                    place = z ^ change
                    for upper in (0, 1):
                        start = pl.multiple_of(place * (2 * rows) + upper * rows, 16)
                        up_ref[pl.ds(start, rows), y_at * cols : (y_at + 1) * cols] = piece[
                            :, upper * cols : (upper + 1) * cols
                        ]
                    start = pl.multiple_of((2 * place + y_at) * rows, 16)
                    down_ref[pl.ds(start, rows), :] = piece[:, 2 * cols :]


def out_join_kernel(place_ref, *refs):
    tree, out_ref = refs[:6], refs[6]
    z, y = place_ref[0], place_ref[1]
    for change, own, other in tree_pieces(tree):
        rows = own.shape[0]
        own_start = pl.multiple_of((2 * (z ^ change) + y) * rows, 16)
        other_start = pl.multiple_of((2 * (z ^ change) + 1 - y) * rows, 16)
        out_ref[pl.ds(own_start, rows), :] = own
        out_ref[pl.ds(other_start, rows), :] = other


def join_call(kernel, place, pieces, shapes, name):
    whole = [pl.BlockSpec(memory_space=pltpu.VMEM)] * len(pieces)
    return pl.pallas_call(
        kernel,
        in_specs=[pl.BlockSpec(memory_space=pltpu.SMEM)] + whole,
        out_specs=[pl.BlockSpec(memory_space=pltpu.VMEM)] * len(shapes),
        out_shape=[jax.ShapeDtypeStruct(shape, jnp.bfloat16) for shape in shapes],
        name=name,
    )(place, *pieces)


def scatter_blocks(rows, dot, weight):
    half = rows.shape[0] // 2
    own = half // 2
    got = seq_swap(dot(rows[:half], weight).astype(jnp.bfloat16), 1).astype(jnp.float32)
    kept = dot(rows[half:], weight) + got
    return kept[:own] + seq_swap(kept[own:].astype(jnp.bfloat16), 2).astype(jnp.float32)


def scatter_parts(words, ents):
    words_dev, ents_dev = words.shape[0] // 4, ents.shape[0] // 4
    half = words_dev + ents_dev

    def rows(first):
        parts = []
        for k in (first, first + 1):
            parts.append(words[k * words_dev : (k + 1) * words_dev])
            parts.append(ents[k * ents_dev : (k + 1) * ents_dev])
        return jnp.concatenate(parts, 0)

    got = seq_swap(rows(0).astype(jnp.bfloat16), 1).astype(jnp.float32)
    kept = rows(2) + got
    return kept[:half] + seq_swap(kept[half:].astype(jnp.bfloat16), 2).astype(jnp.float32)


def rows_norm(hidden, gain, shift):
    center = hidden - jnp.mean(hidden, -1, keepdims=True)
    rstd = lax.rsqrt(jnp.mean(center * center, -1, keepdims=True) + EPS)
    normed = center * rstd
    return (normed * gain + shift, normed, rstd)


def rows_norm_back(grad, normed, rstd, gain):
    dnormed = grad * gain
    grad_in = rstd * (
        dnormed
        - jnp.mean(dnormed, -1, keepdims=True)
        - normed * jnp.mean(dnormed * normed, -1, keepdims=True)
    )
    return (grad_in, jnp.sum(grad * normed, axis=0), jnp.sum(grad, axis=0))


def mm(left, right, left_dim=1, right_dim=0):
    return lax.dot_general(
        left, right, (((left_dim,), (right_dim,)), ((), ())), preferred_element_type=jnp.float32
    )


def nt_dot(left, right):
    return mm(left, right, 1, 1)


def tn_dot(left, right):
    return mm(left, right, 0, 0)


HEAD_DIM = 64


def head_parts(word_ref, ent_ref, low, high):
    return jnp.concatenate([word_ref[:, low:high], ent_ref[:, low:high]], 0)


def attention_kernel(
    heads,
    query_word_ref,
    query_ent_ref,
    key_word_ref,
    key_ent_ref,
    offset_ref,
    attn_ref,
    low_ref,
    high_ref,
    stat_ref,
):
    width = heads * HEAD_DIM
    word_count = key_word_ref.shape[0]
    rows = attn_ref.shape[0]
    lane = lax.broadcasted_iota(jnp.int32, (rows, 128), 1)
    stats = jnp.zeros((rows, 128), jnp.float32)
    for h in range(heads):
        low, high = h * HEAD_DIM, (h + 1) * HEAD_DIM
        q_word = head_parts(query_word_ref, query_ent_ref, low, high)
        q_ent = head_parts(query_word_ref, query_ent_ref, width + low, width + high)
        k_word = key_word_ref[:, 2 * width + low : 2 * width + high]
        k_ent = key_ent_ref[:, 2 * width + low : 2 * width + high]
        s_word = nt_dot(q_word, k_word) + offset_ref[:, :word_count]
        s_ent = nt_dot(q_ent, k_ent) + offset_ref[:, word_count:]
        top = jnp.maximum(
            jnp.max(s_word, -1, keepdims=True), jnp.max(s_ent, -1, keepdims=True)
        )
        w_word = jnp.exp(s_word - top)
        w_ent = jnp.exp(s_ent - top)
        total = jnp.sum(w_word, -1, keepdims=True) + jnp.sum(w_ent, -1, keepdims=True)
        v_word = key_word_ref[:, 3 * width + low : 3 * width + high]
        v_ent = key_ent_ref[:, 3 * width + low : 3 * width + high]
        unnorm = mm(w_word.astype(jnp.bfloat16), v_word) + mm(w_ent.astype(jnp.bfloat16), v_ent)
        attn_ref[:, low:high] = unnorm / total
        stats = jnp.where(lane == h, top, stats)
        stats = jnp.where(lane == heads + h, total, stats)
    stat_ref[...] = stats
    low_ref[...] = attn_ref[: rows // 2].astype(jnp.bfloat16)
    high_ref[...] = attn_ref[rows // 2 :].astype(jnp.bfloat16)


def attention_forward(packed_word, packed_ent, offsets, heads):
    word_count, packed_width = packed_word.shape
    ent_count = packed_ent.shape[0]
    count = word_count + ent_count
    width = heads * HEAD_DIM
    block = count // 4
    return pl.pallas_call(
        functools.partial(attention_kernel, heads),
        grid=(4,),
        in_specs=[
            pl.BlockSpec((word_count // 4, packed_width), lambda i: (i, 0)),
            pl.BlockSpec((ent_count // 4, packed_width), lambda i: (i, 0)),
            pl.BlockSpec((word_count, packed_width), lambda i: (0, 0)),
            pl.BlockSpec((ent_count, packed_width), lambda i: (0, 0)),
            pl.BlockSpec((1, count), lambda i: (0, 0)),
        ],
        out_specs=[
            pl.BlockSpec((block, width), lambda i: (i, 0)),
            pl.BlockSpec((block // 2, width), lambda i: (i, 0)),
            pl.BlockSpec((block // 2, width), lambda i: (i, 0)),
            pl.BlockSpec((block, 128), lambda i: (i, 0)),
        ],
        out_shape=[
            jax.ShapeDtypeStruct((count, width), jnp.float32),
            jax.ShapeDtypeStruct((count // 2, width), jnp.bfloat16),
            jax.ShapeDtypeStruct((count // 2, width), jnp.bfloat16),
            jax.ShapeDtypeStruct((count, 128), jnp.float32),
        ],
        compiler_params=pltpu.CompilerParams(dimension_semantics=("arbitrary",)),
        cost_estimate=pl.CostEstimate(
            flops=4 * count * count * width,
            bytes_accessed=6 * count * packed_width,
            transcendentals=count * count * heads,
        ),
        name="attention",
    )(packed_word, packed_ent, packed_word, packed_ent, offsets)


def attention_back_kernel(
    heads,
    query_word_ref,
    query_ent_ref,
    key_word_ref,
    key_ent_ref,
    offset_ref,
    attn_ref,
    stat_ref,
    grad_low_ref,
    grad_high_ref,
    d_word_ref,
    d_ent_ref,
    sum_ref,
    key_sum,
    value_sum,
):
    width = heads * HEAD_DIM
    word_count = key_word_ref.shape[0]
    words_dev, ents_dev = query_word_ref.shape[0], query_ent_ref.shape[0]
    step = pl.program_id(0)

    @pl.when(step == 0)
    def _():
        key_sum[...] = jnp.zeros_like(key_sum)
        value_sum[...] = jnp.zeros_like(value_sum)
        sum_ref[...] = jnp.zeros_like(sum_ref)

    word_rows = pl.ds(pl.multiple_of(step * words_dev, words_dev), words_dev)
    ent_rows = pl.ds(pl.multiple_of(step * ents_dev, ents_dev), ents_dev)
    for h in range(heads):
        low, high = h * HEAD_DIM, (h + 1) * HEAD_DIM
        q_word = head_parts(query_word_ref, query_ent_ref, low, high)
        q_ent = head_parts(query_word_ref, query_ent_ref, width + low, width + high)
        k_word = key_word_ref[:, 2 * width + low : 2 * width + high]
        k_ent = key_ent_ref[:, 2 * width + low : 2 * width + high]
        v_word = key_word_ref[:, 3 * width + low : 3 * width + high]
        v_ent = key_ent_ref[:, 3 * width + low : 3 * width + high]
        top = stat_ref[:, h : h + 1]
        inverse = 1.0 / stat_ref[:, heads + h : heads + h + 1]
        grad = head_parts(grad_low_ref, grad_high_ref, low, high)
        delta = jnp.sum(grad * attn_ref[:, low:high], -1, keepdims=True) * inverse
        grad_low = (grad * inverse).astype(jnp.bfloat16)
        w_word = jnp.exp(nt_dot(q_word, k_word) + offset_ref[:, :word_count] - top)
        w_ent = jnp.exp(nt_dot(q_ent, k_ent) + offset_ref[:, word_count:] - top)
        d_word = (w_word * (nt_dot(grad_low, v_word) - delta)).astype(jnp.bfloat16)
        d_ent = (w_ent * (nt_dot(grad_low, v_ent) - delta)).astype(jnp.bfloat16)
        for at, dquery in ((low, mm(d_word, k_word)), (width + low, mm(d_ent, k_ent))):
            dquery = dquery * 0.125
            lanes = slice(at, at + HEAD_DIM)
            d_word_ref[word_rows, lanes] = dquery[:words_dev].astype(jnp.bfloat16)
            d_ent_ref[ent_rows, lanes] = dquery[words_dev:].astype(jnp.bfloat16)
            sum_ref[0:1, lanes] += jnp.sum(dquery[:words_dev], 0, keepdims=True)
            sum_ref[1:2, lanes] += jnp.sum(dquery[words_dev:], 0, keepdims=True)
        key_sum[low:high, :word_count] += tn_dot(q_word, d_word)
        key_sum[low:high, word_count:] += tn_dot(q_ent, d_ent)
        value_sum[low:high, :word_count] += tn_dot(grad_low, w_word.astype(jnp.bfloat16))
        value_sum[low:high, word_count:] += tn_dot(grad_low, w_ent.astype(jnp.bfloat16))

    @pl.when(step == pl.num_programs(0) - 1)
    def _():
        dkey = key_sum[...].T
        dvalue = value_sum[...].T
        sum_ref[2:3, :width] = jnp.sum(dvalue, 0, keepdims=True)
        both = jnp.concatenate([dkey, dvalue], 1).astype(jnp.bfloat16)
        d_word_ref[:, 2 * width :] = both[:word_count]
        d_ent_ref[:, 2 * width :] = both[word_count:]


def attention_backward(packed_word, packed_ent, offsets, attn, stats, grads, heads):
    word_count, packed_width = packed_word.shape
    ent_count = packed_ent.shape[0]
    count = word_count + ent_count
    width = heads * HEAD_DIM
    block = count // 4
    return pl.pallas_call(
        functools.partial(attention_back_kernel, heads),
        grid=(4,),
        in_specs=[
            pl.BlockSpec((word_count // 4, packed_width), lambda i: (i, 0)),
            pl.BlockSpec((ent_count // 4, packed_width), lambda i: (i, 0)),
            pl.BlockSpec((word_count, packed_width), lambda i: (0, 0)),
            pl.BlockSpec((ent_count, packed_width), lambda i: (0, 0)),
            pl.BlockSpec((1, count), lambda i: (0, 0)),
            pl.BlockSpec((block, width), lambda i: (i, 0)),
            pl.BlockSpec((block, 128), lambda i: (i, 0)),
            pl.BlockSpec((block // 2, width), lambda i: (i, 0)),
            pl.BlockSpec((block // 2, width), lambda i: (i, 0)),
        ],
        out_specs=[
            pl.BlockSpec((word_count, packed_width), lambda i: (0, 0)),
            pl.BlockSpec((ent_count, packed_width), lambda i: (0, 0)),
            pl.BlockSpec((8, 2 * width), lambda i: (0, 0)),
        ],
        out_shape=[
            jax.ShapeDtypeStruct((word_count, packed_width), jnp.bfloat16),
            jax.ShapeDtypeStruct((ent_count, packed_width), jnp.bfloat16),
            jax.ShapeDtypeStruct((8, 2 * width), jnp.float32),
        ],
        scratch_shapes=[
            pltpu.VMEM((width, count), jnp.float32),
            pltpu.VMEM((width, count), jnp.float32),
        ],
        compiler_params=pltpu.CompilerParams(dimension_semantics=("arbitrary",)),
        cost_estimate=pl.CostEstimate(
            flops=10 * count * count * width,
            bytes_accessed=16 * count * packed_width,
            transcendentals=count * count * heads,
        ),
        name="attention_back",
    )(packed_word, packed_ent, packed_word, packed_ent, offsets, attn, stats, *grads)


def tall(left):
    return jnp.swapaxes(left, -1, -2)


def halves(array):
    high = array.astype(jnp.bfloat16)
    return high, (array - high.astype(jnp.float32)).astype(jnp.bfloat16)


def stacked_halves(array):
    high = array.astype(jnp.bfloat16).astype(jnp.float32)
    return jnp.concatenate([array, array - high], 0).astype(jnp.bfloat16)


def columns_of(rank_rows):
    return jnp.concatenate(
        [rank_rows, rank_rows - rank_rows.astype(jnp.bfloat16).astype(jnp.float32)], 0
    ).T.astype(jnp.bfloat16)


def left_part(full, columns):
    high, low = halves(full)
    return mm(high, columns) + mm(low, columns)


def rank_first(part):
    both = part.T
    rank = both.shape[0] // 2
    return both[:rank] + both[rank:]


def left_ffn_kernel(
    got_ref, down_ref, err_up_ref, err_down_ref, q_up_ref, q_down_ref, full_up_ref, full_down_ref, left_ref
):
    step = pl.program_id(0)
    width = got_ref.shape[2]
    rows = got_ref.shape[1]
    left = 0.0
    for s in range(4):
        lanes = slice(s * width, (s + 1) * width)
        full = got_ref[s].astype(jnp.float32) + err_up_ref[0, :, lanes]
        full_up_ref[:, lanes] = full
        left = left + left_part(full, columns_of(q_up_ref[:, lanes]))
    left = rank_first(left)
    full = down_ref[...] + err_down_ref[0]
    full_down_ref[...] = full
    below = rank_first(left_part(full, columns_of(q_down_ref[...])))
    for side in (0, 1):

        @pl.when(step == side)
        def _():
            left_ref[0, :, side * rows : (side + 1) * rows] = left
            left_ref[1 + 2 * side] = below[:, : 2 * rows]
            left_ref[2 + 2 * side] = below[:, 2 * rows :]


def left_of_ffn(got_up, grad_down, err_up, err_down, q_up, q_down):
    rows, width = got_up.shape[1:]
    rank = q_up.shape[0]
    return pl.pallas_call(
        left_ffn_kernel,
        grid=(2,),
        in_specs=[
            pl.BlockSpec((4, rows // 2, width), lambda i: (0, i, 0)),
            pl.BlockSpec((2 * rows, width), lambda i: (i, 0)),
            pl.BlockSpec((1, rows // 2, 4 * width), lambda i: (0, i, 0)),
            pl.BlockSpec((1, 2 * rows, width), lambda i: (0, i, 0)),
            pl.BlockSpec((rank, 4 * width), lambda i: (0, 0)),
            pl.BlockSpec((rank, width), lambda i: (0, 0)),
        ],
        out_specs=[
            pl.BlockSpec((rows // 2, 4 * width), lambda i: (i, 0)),
            pl.BlockSpec((2 * rows, width), lambda i: (i, 0)),
            pl.BlockSpec((5, rank, rows), lambda i: (0, 0, 0)),
        ],
        out_shape=[
            jax.ShapeDtypeStruct((rows, 4 * width), jnp.float32),
            jax.ShapeDtypeStruct((4 * rows, width), jnp.float32),
            jax.ShapeDtypeStruct((5, rank, rows), jnp.float32),
        ],
        name="left_ffn",
    )(got_up, grad_down, err_up, err_down, q_up, q_down)


def left_attn_kernel(got_ref, out_ref, err_ref, q_ref, ffn_ref, full_ref, left_ref):
    step = pl.program_id(0)
    rows = full_ref.shape[1]
    part = 2 * rows
    lefts = []
    for j in range(7):
        if j < 6:
            lanes = slice(j * part, (j + 1) * part)
            grad = jnp.concatenate([got_ref[s, :, lanes] for s in range(4)], 1)
            full = grad.astype(jnp.float32) + err_ref[0, j]
        else:
            full = out_ref[...] + err_ref[0, j]
        full_ref[j] = full
        lefts.append(rank_first(left_part(full, columns_of(q_ref[j]))))
    for side in (0, 1):

        @pl.when(step == side)
        def _():
            for j in range(7):
                left_ref[j, :, side * rows : (side + 1) * rows] = lefts[j]

    @pl.when(step == 1)
    def _():
        left_ref[7:] = ffn_ref[...]


def left_of_attn(got, grad_out, err_attn, q_attn, left_ffn):
    rows, width = grad_out.shape
    rank = q_attn.shape[1]
    return pl.pallas_call(
        left_attn_kernel,
        grid=(2,),
        in_specs=[
            pl.BlockSpec((4, rows // 2, got.shape[2]), lambda i: (0, i, 0)),
            pl.BlockSpec((rows // 2, width), lambda i: (i, 0)),
            pl.BlockSpec((1, 7, rows // 2, width), lambda i: (0, 0, i, 0)),
            pl.BlockSpec((7, rank, width), lambda i: (0, 0, 0)),
            pl.BlockSpec((5, rank, rows), lambda i: (0, 0, 0)),
        ],
        out_specs=[
            pl.BlockSpec((7, rows // 2, width), lambda i: (0, i, 0)),
            pl.BlockSpec((12, rank, rows), lambda i: (0, 0, 0)),
        ],
        out_shape=[
            jax.ShapeDtypeStruct((7, rows, width), jnp.float32),
            jax.ShapeDtypeStruct((12, rank, rows), jnp.float32),
        ],
        name="left_attn",
    )(got, grad_out, err_attn, q_attn, left_ffn)


MATRIX_BLOCKS = [[j] for j in range(8)] + [[8, 9, 10, 11]]


def gram_kernel(scale, mine_ref, other_ref, left_ref, gram_ref):
    rank = mine_ref.shape[1]
    left = (mine_ref[...] + other_ref[...]) * scale
    left_ref[...] = left
    lane = lax.broadcasted_iota(jnp.int32, (rank, 128), 1)
    row = lax.broadcasted_iota(jnp.int32, (rank, 128), 0)
    for r in range(rank):
        gram = jnp.where((lane >= len(MATRIX_BLOCKS)) & (row == r), 1.0, 0.0)
        for m, blocks in enumerate(MATRIX_BLOCKS):
            product = sum(left[b] * left[b, r : r + 1] for b in blocks)
            gram = jnp.where(lane == m, jnp.sum(product, -1, keepdims=True), gram)
        gram_ref[r] = gram


def gram_of(mine, other, scale):
    rank = mine.shape[1]
    return pl.pallas_call(
        functools.partial(gram_kernel, scale),
        out_shape=[
            jax.ShapeDtypeStruct(mine.shape, jnp.float32),
            jax.ShapeDtypeStruct((rank, rank, 128), jnp.float32),
        ],
        name="gram",
    )(mine, other)


def inverse_factor(columns, rank):
    row = lax.broadcasted_iota(jnp.int32, columns[0].shape, 0)
    columns, lower = list(columns), []
    for k in range(rank):
        column = columns[k] / jnp.sqrt(columns[k][k : k + 1])
        lower.append(column)
        for c in range(k + 1, rank):
            columns[c] = columns[c] - column * column[c : c + 1]
    inverse = []
    for r in range(rank):
        value = jnp.where(row == r, 1.0, 0.0)
        for t in range(r):
            value = value - lower[t][r : r + 1] * inverse[t]
        inverse.append(value / lower[r][r : r + 1])
    return inverse


def right_part(both_ref, blocks, fulls):
    out = 0.0
    for b, full in zip(blocks, fulls):
        high, low = halves(full)
        out = out + mm(both_ref[b], high) + mm(both_ref[b], low)
    rank = out.shape[0] // 2
    return out[:rank] + out[rank:]


def right_kernel(gram_ref, other_ref, left_ref, attn_ref, *refs):
    up_refs, (down_ref, vec_ref, orth_ref, right_ref, both_ref) = refs[:4], refs[4:]
    step = pl.program_id(0)
    rank, rows = left_ref.shape[1:]

    @pl.when(step == 0)
    def _():
        inverse = inverse_factor([gram_ref[r] + other_ref[r] for r in range(rank)], rank)
        row = lax.broadcasted_iota(jnp.int32, (rank, rows), 0)
        for m, blocks in enumerate(MATRIX_BLOCKS):
            weights = [inverse[r][:, m : m + 1] for r in range(rank)]
            for b in blocks:
                left = left_ref[b]
                orth = jnp.zeros((rank, rows), jnp.float32)
                for r in range(rank):
                    total = jnp.sum(left * weights[r], 0, keepdims=True)
                    orth = jnp.where(row == r, total, orth)
                orth_ref[b] = orth
                both_ref[b] = stacked_halves(orth)

    for j in range(7):
        right_ref[j] = right_part(both_ref, [j], [attn_ref[j]])
    for k in range(4):
        right_ref[7 + k] = right_part(both_ref, [7], [up_refs[k][...]])
    right_ref[11] = right_part(
        both_ref, [8, 9, 10, 11], [down_ref[k * rows : (k + 1) * rows] for k in range(4)]
    )
    right_ref[12:] = vec_ref[...]


def right_of(gram, other, left, full_attn, full_up, full_down, vecs):
    rank, rows = left.shape[1:]
    width = full_attn.shape[2]
    lanes = width // 3

    def whole(array):
        return pl.BlockSpec(array.shape, lambda i: (0,) * array.ndim)

    def up_spec(k):
        return pl.BlockSpec((rows, lanes), lambda i: (0, 3 * k + i))

    return pl.pallas_call(
        right_kernel,
        grid=(3,),
        in_specs=[
            whole(gram),
            whole(other),
            whole(left),
            pl.BlockSpec((7, rows, lanes), lambda i: (0, 0, i)),
            up_spec(0),
            up_spec(1),
            up_spec(2),
            up_spec(3),
            pl.BlockSpec((4 * rows, lanes), lambda i: (0, i)),
            pl.BlockSpec((2, rank, lanes), lambda i: (0, 0, i)),
        ],
        out_specs=[whole(left), pl.BlockSpec((14, rank, lanes), lambda i: (0, 0, i))],
        out_shape=[
            jax.ShapeDtypeStruct(left.shape, jnp.float32),
            jax.ShapeDtypeStruct((14, rank, width), jnp.float32),
        ],
        scratch_shapes=[pltpu.VMEM((12, 2 * rank, rows), jnp.bfloat16)],
        name="right",
    )(gram, other, left, full_attn, full_up, full_up, full_up, full_up, full_down, vecs)


def left_stack(orth):
    high = orth.astype(jnp.bfloat16).astype(jnp.float32)
    return jnp.concatenate([orth, orth, orth - high, jnp.zeros_like(orth)], 0)


def right_stack(right):
    high = right.astype(jnp.bfloat16).astype(jnp.float32)
    return jnp.concatenate([right, right - high, right, jnp.zeros_like(right)], 0).astype(
        jnp.bfloat16
    )


def update_kernel(rate, orth_ref, right_ref, cols_ref, up_cols_ref, *refs):
    full_refs, mom_refs, weight_refs = refs[:3], refs[3:6], refs[6:9]
    err_refs, next_refs, new_refs = refs[9:12], refs[12:15], refs[15:18]
    tall_ref, right_rows, cols_rows = refs[18:]
    step = pl.program_id(0)
    rows, width = full_refs[1].shape[0], right_ref.shape[2]
    part = orth_ref.shape[2]

    @pl.when(step == 0)
    def _():
        for b in range(12):
            tall_ref[b] = left_stack(orth_ref[b]).T.astype(jnp.bfloat16)
            right_rows[b] = right_stack(right_ref[b])
        for j in range(7):
            cols_rows[j] = right_stack(cols_ref[j])

    def move(change, mom_ref, weight_ref, next_ref, new_ref, at):
        value = MOMENTUM * mom_ref[at] + change
        next_ref[at] = value
        new_ref[at] = weight_ref[at] - rate * value

    own = pl.ds(pl.multiple_of(step * rows, 16), rows)
    for j in range(7):
        left = tall_ref[j, own]
        err_refs[0][0, j] = full_refs[0][j] - mm(left, right_rows[j])
        change = mm(left, cols_rows[j])
        move(change, mom_refs[0], weight_refs[0], next_refs[0], new_refs[0], j)
    left = tall_ref[7, own]
    for k in range(4):
        lanes = slice(k * width, (k + 1) * width)
        err_refs[1][0, :, lanes] = full_refs[1][:, lanes] - mm(left, right_rows[7 + k])
    change = mm(left, right_stack(up_cols_ref[0]))
    move(change, mom_refs[1], weight_refs[1], next_refs[1], new_refs[1], ...)
    err_refs[2][0] = full_refs[2][...] - mm(tall_ref[8 + step], right_rows[11])

    @pl.when(step == 3)
    def _():
        cols = right_stack(cols_ref[11])
        for k in range(4):
            change = tn_dot(cols, left_stack(orth_ref[8 + k]).astype(jnp.bfloat16))
            at = (slice(None), slice(k * part, (k + 1) * part))
            move(change, mom_refs[2], weight_refs[2], next_refs[2], new_refs[2], at)


def updates(orth, right, right_cols, up_cols, full, mom, weight, rate):
    part = orth.shape[2]
    width = right.shape[2]
    cols, cols_up = right_cols.shape[2], up_cols.shape[2]
    rows = part // 4

    def whole(array):
        return pl.BlockSpec(array.shape, lambda i: (0,) * array.ndim)

    full_specs = [
        pl.BlockSpec((7, rows, width), lambda i: (0, i, 0)),
        pl.BlockSpec((rows, 4 * width), lambda i: (i, 0)),
        pl.BlockSpec((part, width), lambda i: (i, 0)),
    ]
    own_specs = [
        pl.BlockSpec((7, rows, cols), lambda i: (0, i, 0)),
        pl.BlockSpec((rows, cols_up), lambda i: (i, 0)),
        whole(mom[2]),
    ]
    err_specs = [
        pl.BlockSpec((1, 7, rows, width), lambda i: (0, 0, i, 0)),
        pl.BlockSpec((1, rows, 4 * width), lambda i: (0, i, 0)),
        pl.BlockSpec((1, part, width), lambda i: (0, i, 0)),
    ]
    err_shapes = [jax.ShapeDtypeStruct((1,) + array.shape, jnp.float32) for array in full]
    own_shapes = [jax.ShapeDtypeStruct(array.shape, jnp.float32) for array in mom]
    outs = pl.pallas_call(
        functools.partial(update_kernel, rate),
        grid=(4,),
        in_specs=[whole(orth), whole(right), whole(right_cols), whole(up_cols)]
        + full_specs
        + own_specs
        + own_specs,
        out_specs=err_specs + own_specs + own_specs,
        out_shape=err_shapes + own_shapes + own_shapes,
        scratch_shapes=[
            pltpu.VMEM((12, part, 32), jnp.bfloat16),
            pltpu.VMEM((12, 32, width), jnp.bfloat16),
            pltpu.VMEM((7, 32, cols), jnp.bfloat16),
        ],
        name="updates",
    )(orth, right, right_cols, up_cols, *full, *mom, *weight)
    return outs[:3], outs[3:6], outs[6:]


def head_split_device(
    x_words,
    x_ents,
    spans,
    word_mask,
    ent_mask,
    cot_words,
    cot_ents,
    attn_w,
    up_w,
    down_w,
    vecs,
    mom_attn,
    mom_up,
    mom_down,
    mom_vecs,
    err_attn,
    err_up,
    err_down,
    attention_prior_right,
    qf_up,
    qf_down,
):
    low_type = jnp.bfloat16
    words_dev, width = x_words.shape[1:]
    ents_dev = x_ents.shape[1]
    rows_dev = words_dev + ents_dev
    seq_count, rep_count = lax.axis_size("seq"), lax.axis_size("rep")
    seq_index, rep_index = lax.axis_index("seq"), lax.axis_index("rep")
    heads = HEADS // seq_count
    part = width // seq_count
    word_count = words_dev * seq_count
    ent_count = ents_dev * seq_count
    cols = attn_w.shape[2]
    cols_up = up_w.shape[1]
    hidden = cols_up * rep_count
    hidden_part = hidden // seq_count

    place = jnp.stack([rep_index // 2, rep_index % 2]).astype(jnp.int32)
    block = part // 2
    project_piece = jnp.transpose(
        attn_w[:6].astype(low_type).reshape(6, 2, block, cols), (2, 1, 0, 3)
    ).reshape(block, 12 * cols)
    half = block // 2
    trees = [
        gather_tree(planes_swap(project_piece[:half])),
        gather_tree(planes_swap(project_piece[half:])),
    ]
    (w_out,) = join_call(
        out_join_kernel,
        place,
        gather_tree(attn_w[6].astype(low_type).T),
        [(width, part)],
        "join_out",
    )
    up_piece = jnp.transpose(
        up_w.astype(low_type).reshape(2, block, cols_up), (1, 0, 2)
    ).reshape(block, 2 * cols_up)
    up_piece, unused_near = lax.optimization_barrier((up_piece, (trees[0][5], trees[1][5])))
    ffn_piece = jnp.concatenate([planes_swap(up_piece), down_w.astype(low_type).T], 1)
    ffn_pieces, ffn_side = gather_direct(ffn_piece)

    spans, unused_piece = lax.optimization_barrier((spans, project_piece))
    inputs = jnp.concatenate([x_words[0], x_ents[0] + span_mean_closed(spans[0], width)], 0)
    live = jnp.concatenate([word_mask[0], ent_mask[0]], 0).astype(low_type)
    live = jnp.pad(live.reshape(1, rows_dev), ((0, 15), (0, width - rows_dev)))
    pieces = gather_seq(jnp.concatenate([inputs.astype(low_type), live], 0))
    lives = [piece[rows_dev, :rows_dev] for piece in pieces]
    lives = [piece[:words_dev] for piece in lives] + [piece[words_dev:] for piece in lives]
    offsets = ((jnp.concatenate(lives).astype(jnp.float32) - 1.0) * MASK_FILL).reshape(1, -1)

    own_vecs = lax.dynamic_slice_in_dim(vecs, seq_index * part, part, 1)
    none = jnp.zeros((part,), jnp.float32)
    scale = jnp.where(jnp.arange(4 * part) < 2 * part, 0.125, 1.0).astype(jnp.float32)
    bias_word = jnp.concatenate([own_vecs[0], own_vecs[1], none, own_vecs[4]])
    bias_ent = jnp.concatenate([own_vecs[2], own_vecs[3], none, own_vecs[4]])
    in_vmem = pl.BlockSpec(memory_space=pltpu.VMEM)
    w_word, w_ent, packed_word, packed_ent, rows_word, rows_ent = pl.pallas_call(
        functools.partial(project_kernel, words_dev, rows_dev),
        in_specs=[pl.BlockSpec(memory_space=pltpu.SMEM)] + [in_vmem] * 19,
        out_specs=[in_vmem] * 6,
        out_shape=[
            jax.ShapeDtypeStruct(shape, low_type)
            for shape in [
                (rows, width)
                for rows in (width, width, word_count, ent_count, word_count, ent_count)
            ]
        ],
        scratch_shapes=[pltpu.VMEM((2, 4, 2, half, 12 * cols), low_type)],
        name="project",
    )(
        place,
        bias_word.reshape(1, -1),
        bias_ent.reshape(1, -1),
        scale.reshape(1, -1),
        *trees[0],
        *trees[1],
        *pieces,
    )
    attn, *attn_low, stats = attention_forward(packed_word, packed_ent, offsets, heads)
    attn_low, ffn_pieces, ffn_side = lax.optimization_barrier((attn_low, ffn_pieces, ffn_side))
    ffn_sides = [ffn_side] + [rep_swap(piece, 1) for piece in ffn_pieces[1:]]
    w_up, w_down = join_call(
        ffn_join_kernel,
        place,
        ffn_pieces + ffn_sides,
        [(width, hidden_part), (width, hidden_part)],
        "join_ffn",
    )

    bias_up = lax.dynamic_slice_in_dim(
        vecs[11:15].reshape(hidden), seq_index * hidden_part, hidden_part, 0
    )
    grad_result = jnp.concatenate([cot_words[0], cot_ents[0]], 0)
    split = rows_dev // 2
    results, grads_one, grads_attn, kept = [], [], [], []
    sums = [0.0] * 7
    for c in (0, 1):
        at = slice(c * split, (c + 1) * split)
        branch = scatter_blocks(attn_low[c], nt_dot, w_out) + vecs[5]
        mid, normed_one, rstd_one = rows_norm(inputs[at] + branch, vecs[7], vecs[8])
        mid_low = jnp.concatenate(gather_seq(mid.astype(low_type)), 0)
        pre = mm(mid_low, w_up) + bias_up
        cdf = 0.5 * (1.0 + lax.erf(pre * math.sqrt(0.5)))
        act_low = (pre * cdf).astype(low_type)
        ffn = scatter_blocks(act_low, nt_dot, w_down) + vecs[6]
        result, normed_two, rstd_two = rows_norm(mid + ffn, vecs[9], vecs[10])
        grad_two, gain_two, shift_two = rows_norm_back(grad_result[at], normed_two, rstd_two, vecs[9])
        grad_ffn = jnp.concatenate(gather_seq(grad_two.astype(low_type)), 0)
        density = jnp.exp(-0.5 * pre * pre) * (1.0 / math.sqrt(2.0 * math.pi))
        grad_pre = mm(grad_ffn, w_down) * (cdf + pre * density)
        grad_pre_low = grad_pre.astype(low_type)
        grad_mid = grad_two + scatter_blocks(grad_pre_low, nt_dot, w_up)
        grad_one, gain_one, shift_one = rows_norm_back(grad_mid, normed_one, rstd_one, vecs[7])
        grad_branch = jnp.concatenate(gather_seq(grad_one.astype(low_type)), 0)
        grads_attn.append(mm(grad_branch, w_out))
        results.append(result)
        grads_one.append(grad_one)
        kept.append((mid_low, act_low, grad_ffn, grad_pre_low, grad_branch))
        parts = (
            jnp.sum(grad_one, 0),
            jnp.sum(grad_two, 0),
            gain_one,
            shift_one,
            gain_two,
            shift_two,
            jnp.sum(grad_pre, 0),
        )
        sums = [total + value for total, value in zip(sums, parts)]
    result = jnp.concatenate(results, 0)
    grad_one = jnp.concatenate(grads_one, 0)
    grad_down = sum(tn_dot(act_low, grad_ffn) for _, act_low, grad_ffn, _, _ in kept)
    grad_up = sum(tn_dot(mid_low, grad_pre_low) for mid_low, _, _, grad_pre_low, _ in kept)
    grad_up, unused_branch = lax.optimization_barrier((grad_up.astype(low_type), kept[1][4]))
    got_up = lax.all_to_all(grad_up.reshape(seq_count, part, hidden_part), "seq", 0, 0)
    full_up, full_down, left_ffn = left_of_ffn(
        got_up, grad_down, err_up, err_down, qf_up.T, qf_down.T
    )
    grad_out = sum(tn_dot(low, parts[4]) for low, parts in zip(attn_low, kept))
    d_word, d_ent, d_sums = attention_backward(
        packed_word, packed_ent, offsets, attn, stats, grads_attn, heads
    )
    grad_word = tn_dot(rows_word, d_word)
    grad_ent = tn_dot(rows_ent, d_ent)
    grad_project = jnp.concatenate(
        [
            grad_word[:, : 2 * part],
            grad_ent[:, : 2 * part],
            grad_word[:, 2 * part :] + grad_ent[:, 2 * part :],
        ],
        1,
    ).astype(low_type)
    got_project = lax.all_to_all(
        grad_project.reshape(seq_count, part, 6 * part), "seq", 0, 0
    )
    grad_inputs = grad_one + scatter_parts(nt_dot(d_word, w_word), nt_dot(d_ent, w_ent))

    vec_grad = jnp.zeros((15, width), jnp.float32)
    bias_query = jnp.concatenate(
        [d_sums[0].reshape(2, part), d_sums[1].reshape(2, part), d_sums[2, :part].reshape(1, part)], 0
    )
    vec_grad = lax.dynamic_update_slice(vec_grad, bias_query, (0, seq_index * part))
    vec_grad = lax.dynamic_update_slice(vec_grad, jnp.stack(sums[:6]), (5, 0))
    bias_rows = hidden_part // width
    vec_grad = lax.dynamic_update_slice(
        vec_grad, sums[6].reshape(bias_rows, width), (11 + seq_index * bias_rows, 0)
    )

    full_attn, left = left_of_attn(
        got_project, grad_out, err_attn, tall(attention_prior_right), left_ffn
    )
    for bits in (1, 2):
        left = left + rep_swap(left, bits)
    left, gram = gram_of(left, rep_swap(left, 4), 1.0 / rep_count)
    gram = gram + seq_swap(gram, 1)
    rows_vec = jnp.pad(vec_grad, ((0, 1), (0, 0))).reshape(2, 8, width)
    orth, right = right_of(
        gram, seq_swap(gram, 2), left, full_attn, full_up, full_down, rows_vec
    )
    core, chip = seq_index % 2, seq_index // 2
    blocks, rank = right.shape[:2]
    lanes, upper = width // 2, blocks // 2
    sent = lax.dynamic_slice_in_dim(right, (1 - core) * lanes, lanes, 2)
    kept = lax.dynamic_slice_in_dim(right, core * lanes, lanes, 2) + seq_swap(sent, 1)
    sent = lax.dynamic_slice_in_dim(kept, (1 - chip) * upper, upper, 0)
    kept = lax.dynamic_slice_in_dim(kept, chip * upper, upper, 0) + seq_swap(sent, 2)
    for bits in (1, 2, 4):
        kept = kept + rep_swap(kept, bits)
    kept = kept / rep_count
    got = seq_swap(kept, 2)
    kept = jnp.where(
        chip == 0, jnp.concatenate([kept, got], 0), jnp.concatenate([got, kept], 0)
    )
    got = seq_swap(kept, 1)
    right = jnp.where(
        core == 0, jnp.concatenate([kept, got], 2), jnp.concatenate([got, kept], 2)
    )
    vec_mean = right[12:].reshape(16, width)[:15]
    lr_mat = 1.5 * math.sqrt(rep_count / (SEQS * (WORDS + ENTS)))
    lr_vec = 0.2 * math.sqrt(rep_count / (SEQS * (WORDS + ENTS)))
    right_cols = lax.dynamic_slice_in_dim(right, rep_index * cols, cols, 2)
    up_cols = lax.dynamic_slice(
        right, (7 + rep_index // 2, 0, (rep_index % 2) * cols_up), (1, rank, cols_up)
    )
    next_err, next_mom, new = updates(
        orth,
        right,
        right_cols,
        up_cols,
        (full_attn, full_up, full_down),
        (mom_attn, mom_up, mom_down.T),
        (attn_w, up_w, down_w.T),
        lr_mat,
    )
    next_mom_vecs = MOMENTUM * mom_vecs + vec_mean
    return (
        result[None, :words_dev],
        result[None, words_dev:],
        grad_inputs[None, :words_dev],
        grad_inputs[None, words_dev:],
        new[0],
        new[1],
        new[2].T,
        vecs - lr_vec * next_mom_vecs,
        next_mom[0],
        next_mom[1],
        next_mom[2].T,
        next_mom_vecs,
        next_err[0],
        next_err[1],
        next_err[2],
        tall(orth[:7]),
        tall(orth[7]),
        tall(orth[8:]).reshape(4 * part, rank),
        tall(right[:7]),
        tall(right[7:11]).reshape(4 * width, rank),
        tall(right[11]),
    )


def solution(mesh):
    in_specs = (
        P("rep", "seq", None),
        P("rep", "seq", None),
        P("rep", "seq", None),
        P("rep", "seq"),
        P("rep", "seq"),
        P("rep", "seq", None),
        P("rep", "seq", None),
        P(None, "seq", "rep"),
        P("seq", "rep"),
        P("seq", "rep"),
        P(),
        P(None, "seq", "rep"),
        P("seq", "rep"),
        P("seq", "rep"),
        P(),
        P("rep", None, "seq", None),
        P("rep", "seq", None),
        P("rep", "seq", None),
        P(),
        P(),
        P(),
    )
    out_specs = (
        P("rep", "seq", None),
        P("rep", "seq", None),
        P("rep", "seq", None),
        P("rep", "seq", None),
        P(None, "seq", "rep"),
        P("seq", "rep"),
        P("seq", "rep"),
        P(),
        P(None, "seq", "rep"),
        P("seq", "rep"),
        P("seq", "rep"),
        P(),
        P("rep", None, "seq", None),
        P("rep", "seq", None),
        P("rep", "seq", None),
        P(None, "seq", None),
        P("seq", None),
        P("seq", None),
        P(),
        P(),
        P(),
    )
    seqs, reps = mesh.shape["seq"], mesh.shape["rep"]
    split_heads = seqs == 4 and reps == 2 * seqs and HEADS % seqs == 0
    body = head_split_device if split_heads else on_device
    return jax.shard_map(
        body, mesh=mesh, in_specs=in_specs, out_specs=out_specs, check_vma=False
    )
```

```python
import functools
import math

import jax
import jax.numpy as jnp
from jax import lax
from jax.experimental import pallas as pl
from jax.experimental.pallas import tpu as pltpu
from jax.sharding import PartitionSpec as P

HEADS = 12
WORDS = 1024
ENTS = 128
SPAN = 16
SEQS = 1


HIGH_PRECISION = lax.Precision.HIGHEST
EPS = 1e-05
MASK_FILL = 30000.0
MOMENTUM = 0.9


def span_mean(spans, model_width):
    starts = spans[..., 0]
    finals = spans[..., 1]
    lengths = (finals - starts + 1).astype(jnp.float32)
    offsets = jnp.arange(SPAN, dtype=jnp.int32)
    places = (starts[..., None] + offsets).astype(jnp.float32)
    shares = (offsets <= (finals - starts)[..., None]).astype(jnp.float32) / lengths[..., None]
    half_width = model_width // 2
    rates = jnp.exp(
        jnp.arange(half_width).astype(jnp.float32) * (-2.0 * math.log(10000.0) / model_width)
    )
    angles = places[..., None] * rates
    table = jnp.concatenate([jnp.sin(angles), jnp.cos(angles)], -1)
    return jnp.sum(table * shares[..., None], axis=-2)


def span_mean_closed(spans, model_width):
    lengths = (spans[..., 1] - spans[..., 0] + 1).astype(jnp.float32)[..., None]
    middles = (spans[..., 1] + spans[..., 0]).astype(jnp.float32)[..., None]
    half_rates = 0.5 * jnp.exp(
        jnp.arange(model_width // 2).astype(jnp.float32) * (-2.0 * math.log(10000.0) / model_width)
    )
    share = jnp.sin(lengths * half_rates) / (lengths * jnp.sin(half_rates))
    angles = middles * half_rates
    return jnp.concatenate([share * jnp.sin(angles), share * jnp.cos(angles)], -1)


def layer_norm(hidden, gain, shift):
    center = hidden - jnp.mean(hidden, -1, keepdims=True)
    rstd = lax.rsqrt(jnp.mean(center * center, -1, keepdims=True) + EPS)
    normed = center * rstd
    return (normed * gain + shift, normed, rstd)


def norm_back(grad, normed, rstd, gain):
    dnormed = grad * gain
    grad_in = rstd * (
        dnormed
        - jnp.mean(dnormed, -1, keepdims=True)
        - normed * jnp.mean(dnormed * normed, -1, keepdims=True)
    )
    return (grad_in, jnp.sum(grad * normed, axis=(0, 1)), jnp.sum(grad, axis=(0, 1)))


def gelu_exact(value):
    return jax.nn.gelu(value, approximate=False)


def project(row_entries, weight_matrix):
    return jnp.einsum("thq,qo->tho", row_entries, weight_matrix, preferred_element_type=jnp.float32)


def project_back(row_entries, weight_matrix):
    return jnp.einsum("hpf,zf->hpz", row_entries, weight_matrix, preferred_element_type=jnp.float32)


def weight_grad(input_arrays, gradient_list):
    return jnp.einsum(
        "cev,ceg->vg", input_arrays, gradient_list, preferred_element_type=jnp.float32
    )


def split_keys(pieces, words_dev, ents_dev, head_count):
    key_piece, live_piece = pieces
    batch_rows = key_piece.shape[0]
    both = key_piece.shape[2]
    model_width = both // 2
    head_dim = model_width // head_count
    rows_dev = words_dev + ents_dev
    blocks = key_piece.shape[1] // rows_dev
    grouped = key_piece.reshape(batch_rows, blocks, rows_dev, both)
    live_grouped = live_piece.reshape(batch_rows, blocks, rows_dev)
    word_part = grouped[:, :, :words_dev].reshape(batch_rows, blocks * words_dev, both)
    ent_part = grouped[:, :, words_dev:].reshape(batch_rows, blocks * ents_dev, both)
    keys_word = word_part[..., :model_width].reshape(batch_rows, -1, head_count, head_dim)
    keys_ent = ent_part[..., :model_width].reshape(batch_rows, -1, head_count, head_dim)
    values = jnp.concatenate(
        [word_part[..., model_width:], ent_part[..., model_width:]], 1
    ).reshape(batch_rows, -1, head_count, head_dim)
    live = jnp.concatenate(
        [
            live_grouped[:, :, :words_dev].reshape(batch_rows, -1),
            live_grouped[:, :, words_dev:].reshape(batch_rows, -1),
        ],
        1,
    )
    offsets = (live.astype(jnp.float32) - 1.0) * MASK_FILL
    return (keys_word, keys_ent, values, offsets, blocks)


def score_block(query_word, query_ent, keys_word, keys_ent, offsets):
    score_word = jnp.einsum(
        "sqhd,skhd->shqk", query_word, keys_word, preferred_element_type=jnp.float32
    )
    score_ent = jnp.einsum(
        "sqhd,skhd->shqk", query_ent, keys_ent, preferred_element_type=jnp.float32
    )
    return jnp.concatenate([score_word, score_ent], -1) + offsets[:, None, None, :]


def flat_heads(array):
    return array.reshape(array.shape[0], array.shape[1], -1)


def join_rows(grad_keys_word, grad_keys_ent, grad_values, blocks, words_dev, ents_dev):
    batch_rows = grad_keys_word.shape[0]
    word_count = grad_keys_word.shape[1]
    word_rows = jnp.concatenate(
        [flat_heads(grad_keys_word), flat_heads(grad_values[:, :word_count])], -1
    )
    ent_rows = jnp.concatenate(
        [flat_heads(grad_keys_ent), flat_heads(grad_values[:, word_count:])], -1
    )
    word_rows = word_rows.reshape(batch_rows, blocks, words_dev, -1)
    ent_rows = ent_rows.reshape(batch_rows, blocks, ents_dev, -1)
    return jnp.concatenate([word_rows, ent_rows], 2).reshape(
        batch_rows, blocks * (words_dev + ents_dev), -1
    )


def from_gram(left, gram):
    lower = jnp.linalg.cholesky(gram)
    return jax.scipy.linalg.solve_triangular(lower, left.T, lower=True).T


def orthonormal(left):
    return from_gram(left, jnp.dot(left.T, left, precision=HIGH_PRECISION))


def on_device(
    x_words,
    x_ents,
    spans,
    word_mask,
    ent_mask,
    cot_words,
    cot_ents,
    attn_w,
    up_w,
    down_w,
    vecs,
    mom_attn,
    mom_up,
    mom_down,
    mom_vecs,
    err_attn,
    err_up,
    err_down,
    attention_prior_right,
    qf_up,
    qf_down,
):
    batch_rows, words_dev, model_width = x_words.shape
    ents_dev = x_ents.shape[1]
    rows_dev = words_dev + ents_dev
    head_count = HEADS
    head_dim = model_width // head_count
    hidden_width = up_w.shape[1] * lax.axis_size("rep")
    seq_count = lax.axis_size("seq")
    rep_count = lax.axis_size("rep")
    seq_index = lax.axis_index("seq")
    rep_index = lax.axis_index("rep")
    lowered = jnp.bfloat16
    column_parts = (
        lax.all_gather(attn_w.astype(lowered), "rep", axis=2, tiled=True),
        lax.all_gather(up_w.astype(lowered), "rep", axis=1, tiled=True),
        lax.all_gather(down_w.astype(lowered), "rep", axis=1, tiled=True),
    )
    w_attn, w_up, w_down = (
        lax.all_gather(column_parts[0], "seq", axis=1, tiled=True),
        lax.all_gather(column_parts[1], "seq", axis=0, tiled=True),
        lax.all_gather(column_parts[2], "seq", axis=0, tiled=True),
    )
    input_arrays = jnp.concatenate([x_words, x_ents + span_mean(spans, model_width)], 1)
    inputs_low = input_arrays.astype(lowered)
    word_low = inputs_low[:, :words_dev]
    ent_low = inputs_low[:, words_dev:]
    query_word = (
        jnp.concatenate(
            [project(word_low, w_attn[0]) + vecs[0], project(ent_low, w_attn[2]) + vecs[2]], 1
        )
        * 0.125
    ).astype(lowered)
    query_ent = (
        jnp.concatenate(
            [project(word_low, w_attn[1]) + vecs[1], project(ent_low, w_attn[3]) + vecs[3]], 1
        )
        * 0.125
    ).astype(lowered)
    keys_low = project(inputs_low, w_attn[4]).astype(lowered)
    values_low = (project(inputs_low, w_attn[5]) + vecs[4]).astype(lowered)
    key_rows = jnp.concatenate([keys_low, values_low], -1)
    key_live = jnp.concatenate([word_mask, ent_mask], 1).astype(lowered)
    heads_word = query_word.reshape(batch_rows, rows_dev, head_count, head_dim)
    heads_ent = query_ent.reshape(batch_rows, rows_dev, head_count, head_dim)
    forward_row_top = jnp.full((batch_rows, head_count, rows_dev), -jnp.inf, jnp.float32)
    row_total = jnp.zeros((batch_rows, head_count, rows_dev), jnp.float32)
    weighted = jnp.zeros((batch_rows, rows_dev, head_count, head_dim), jnp.float32)
    keys_word, keys_ent, values, offsets, blocks = split_keys(
        (
            lax.all_gather(key_rows, "seq", axis=1, tiled=True),
            lax.all_gather(key_live, "seq", axis=1, tiled=True),
        ),
        words_dev,
        ents_dev,
        head_count,
    )
    scores = score_block(heads_word, heads_ent, keys_word, keys_ent, offsets)
    new_top = jnp.max(scores, -1)
    factor = jnp.exp(forward_row_top - new_top)
    weights = jnp.exp(scores - new_top[..., None])
    row_total = row_total * factor + jnp.sum(weights, -1)
    weighted = weighted * jnp.transpose(factor, (0, 2, 1))[..., None] + jnp.einsum(
        "shqk,skhd->sqhd", weights.astype(lowered), values, preferred_element_type=jnp.float32
    )
    row_top, row_total, weighted = (new_top, row_total, weighted)
    total_rows = jnp.transpose(row_total, (0, 2, 1))[..., None]
    attn = weighted / total_rows
    attn_low = attn.reshape(batch_rows, rows_dev, model_width).astype(lowered)
    branch = project(attn_low, w_attn[6]) + vecs[5]
    mid, normed_one, rstd_one = layer_norm(input_arrays + branch, vecs[7], vecs[8])
    mid_low = mid.astype(lowered)
    pre = project(mid_low, w_up) + vecs[11:15].reshape(hidden_width)
    act_low = gelu_exact(pre).astype(lowered)
    ffn = project(act_low, w_down) + vecs[6]
    result, normed_two, rstd_two = layer_norm(mid + ffn, vecs[9], vecs[10])
    grad_result = jnp.concatenate([cot_words, cot_ents], 1)
    grad_two, gain_two, shift_two = norm_back(grad_result, normed_two, rstd_two, vecs[9])
    bias_down = jnp.sum(grad_two, axis=(0, 1))
    grad_ffn_low = grad_two.astype(lowered)
    grad_down = weight_grad(act_low, grad_ffn_low)
    grad_act = project_back(grad_ffn_low, w_down)
    unused_value, gelu_pull = jax.vjp(gelu_exact, pre)
    grad_pre = gelu_pull(grad_act)[0]
    bias_up = jnp.sum(grad_pre, axis=(0, 1))
    grad_pre_low = grad_pre.astype(lowered)
    grad_up = weight_grad(mid_low, grad_pre_low)
    grad_mid = grad_two + project_back(grad_pre_low, w_up)
    grad_one, gain_one, shift_one = norm_back(grad_mid, normed_one, rstd_one, vecs[7])
    bias_out = jnp.sum(grad_one, axis=(0, 1))
    grad_branch_low = grad_one.astype(lowered)
    grad_out_proj = weight_grad(attn_low, grad_branch_low)
    grad_attn = project_back(grad_branch_low, w_attn[6]).reshape(
        batch_rows, rows_dev, head_count, head_dim
    )
    grad_unnorm = (grad_attn / total_rows).astype(lowered)
    delta_rows = jnp.transpose(jnp.sum(grad_attn * attn, -1), (0, 2, 1)) / row_total
    keys_word, keys_ent, values, offsets, blocks = split_keys(
        (
            lax.all_gather(key_rows, "seq", axis=1, tiled=True),
            lax.all_gather(key_live, "seq", axis=1, tiled=True),
        ),
        words_dev,
        ents_dev,
        head_count,
    )
    scores = score_block(heads_word, heads_ent, keys_word, keys_ent, offsets)
    weights = jnp.exp(scores - row_top[..., None])
    grad_weights = jnp.einsum(
        "sqhd,skhd->shqk", grad_unnorm, values, preferred_element_type=jnp.float32
    )
    grad_scores = (weights * (grad_weights - delta_rows[..., None])).astype(lowered)
    word_count = keys_word.shape[1]
    scores_word = grad_scores[..., :word_count]
    scores_ent = grad_scores[..., word_count:]
    grad_query_word = jnp.einsum(
        "shqk,skhd->sqhd", scores_word, keys_word, preferred_element_type=jnp.float32
    )
    grad_query_ent = jnp.einsum(
        "shqk,skhd->sqhd", scores_ent, keys_ent, preferred_element_type=jnp.float32
    )
    grad_keys_word = jnp.einsum(
        "shqk,sqhd->skhd", scores_word, heads_word, preferred_element_type=jnp.float32
    )
    grad_keys_ent = jnp.einsum(
        "shqk,sqhd->skhd", scores_ent, heads_ent, preferred_element_type=jnp.float32
    )
    grad_values = jnp.einsum(
        "shqk,sqhd->skhd", weights.astype(lowered), grad_unnorm, preferred_element_type=jnp.float32
    )
    piece_grad = join_rows(grad_keys_word, grad_keys_ent, grad_values, blocks, words_dev, ents_dev)
    grad_rows = piece_grad
    grad_query_word, grad_query_ent, grad_rows = (grad_query_word, grad_query_ent, grad_rows)
    own_rows = lax.psum_scatter(
        grad_rows.astype(jnp.bfloat16), "seq", scatter_dimension=1, tiled=True
    ).astype(jnp.float32)
    grad_keys = own_rows[..., :model_width]
    grad_values = own_rows[..., model_width:]
    bias_values = jnp.sum(grad_values, axis=(0, 1))
    keys_grad_low = grad_keys.astype(lowered)
    values_grad_low = grad_values.astype(lowered)
    grad_key_w = weight_grad(inputs_low, keys_grad_low)
    grad_value_w = weight_grad(inputs_low, values_grad_low)
    inner_word = grad_query_word.reshape(batch_rows, rows_dev, model_width) * 0.125
    inner_ent = grad_query_ent.reshape(batch_rows, rows_dev, model_width) * 0.125
    bias_query = [
        jnp.sum(inner_word[:, :words_dev], axis=(0, 1)),
        jnp.sum(inner_ent[:, :words_dev], axis=(0, 1)),
        jnp.sum(inner_word[:, words_dev:], axis=(0, 1)),
        jnp.sum(inner_ent[:, words_dev:], axis=(0, 1)),
    ]
    inner_word_low = inner_word.astype(lowered)
    inner_ent_low = inner_ent.astype(lowered)
    grad_query_mats = [
        weight_grad(word_low, inner_word_low[:, :words_dev]),
        weight_grad(word_low, inner_ent_low[:, :words_dev]),
        weight_grad(ent_low, inner_word_low[:, words_dev:]),
        weight_grad(ent_low, inner_ent_low[:, words_dev:]),
    ]
    back_keys = project_back(keys_grad_low, w_attn[4]) + project_back(values_grad_low, w_attn[5])
    back_word = project_back(inner_word_low[:, :words_dev], w_attn[0]) + project_back(
        inner_ent_low[:, :words_dev], w_attn[1]
    )
    back_ent = project_back(inner_word_low[:, words_dev:], w_attn[2]) + project_back(
        inner_ent_low[:, words_dev:], w_attn[3]
    )
    grad_inputs = grad_one + back_keys + jnp.concatenate([back_word, back_ent], 1)
    grad_attn_w = jnp.stack(grad_query_mats + [grad_key_w, grad_value_w, grad_out_proj])
    vec_grad = jnp.concatenate(
        [
            jnp.stack(
                bias_query
                + [bias_values, bias_out, bias_down, gain_one, shift_one, gain_two, shift_two]
            ),
            bias_up.reshape(4, model_width),
        ],
        0,
    )
    rows_attn, rows_up, rows_down = (
        lax.psum_scatter(
            grad_attn_w.astype(jnp.bfloat16), "seq", scatter_dimension=1, tiled=True
        ).astype(jnp.float32),
        lax.psum_scatter(
            grad_up.astype(jnp.bfloat16), "seq", scatter_dimension=0, tiled=True
        ).astype(jnp.float32),
        lax.psum_scatter(
            grad_down.astype(jnp.bfloat16), "seq", scatter_dimension=0, tiled=True
        ).astype(jnp.float32),
    )
    attention_full_gradient = rows_attn + err_attn[0]
    full_up = rows_up + err_up[0]
    full_down = rows_down + err_down[0]
    attention_left_factor = jnp.einsum(
        "vcg,vgo->vco", attention_full_gradient, attention_prior_right, precision=HIGH_PRECISION
    )
    left_up = jnp.dot(full_up, qf_up, precision=HIGH_PRECISION)
    left_down = jnp.dot(full_down, qf_down, precision=HIGH_PRECISION)
    count_attn = attention_full_gradient.shape[1]
    count_up = full_up.shape[0]
    count_down = full_down.shape[0]
    placed_attn = lax.dynamic_update_slice_in_dim(
        jnp.zeros((7, count_attn * seq_count, attention_left_factor.shape[2]), jnp.float32),
        attention_left_factor,
        seq_index * count_attn,
        1,
    )
    placed_up = lax.dynamic_update_slice_in_dim(
        jnp.zeros((count_up * seq_count, left_up.shape[1]), jnp.float32),
        left_up,
        seq_index * count_up,
        0,
    )
    placed_down = lax.dynamic_update_slice_in_dim(
        jnp.zeros((count_down * seq_count, left_down.shape[1]), jnp.float32),
        left_down,
        seq_index * count_down,
        0,
    )
    summed_attn, summed_up, summed_down = lax.psum(
        (placed_attn, placed_up, placed_down), ("seq", "rep")
    )
    orth_attn = jax.vmap(orthonormal)(summed_attn / rep_count)
    orth_up = orthonormal(summed_up / rep_count)
    orth_down = orthonormal(summed_down / rep_count)
    attention_local_gradient = lax.dynamic_slice_in_dim(
        orth_attn, seq_index * count_attn, count_attn, 1
    )
    own_up = lax.dynamic_slice_in_dim(orth_up, seq_index * count_up, count_up, 0)
    own_down = lax.dynamic_slice_in_dim(orth_down, seq_index * count_down, count_down, 0)
    right_parts = (
        jnp.einsum(
            "dpl,dpg->dgl",
            attention_local_gradient,
            attention_full_gradient,
            precision=HIGH_PRECISION,
        ),
        jnp.dot(full_up.T, own_up, precision=HIGH_PRECISION),
        jnp.dot(full_down.T, own_down, precision=HIGH_PRECISION),
        vec_grad,
    )
    attention_right_factor, right_up, right_down, vec_total = lax.psum(
        (right_parts[0], right_parts[1], right_parts[2], right_parts[3]), ("seq", "rep")
    )
    attention_right_factor = attention_right_factor / rep_count
    right_up = right_up / rep_count
    right_down = right_down / rep_count
    vec_mean = vec_total / rep_count
    attention_estimate = jnp.einsum(
        "whg,wng->whn", attention_local_gradient, attention_right_factor, precision=HIGH_PRECISION
    )
    approx_up = jnp.dot(own_up, right_up.T, precision=HIGH_PRECISION)
    approx_down = jnp.dot(own_down, right_down.T, precision=HIGH_PRECISION)
    next_err_attn = (attention_full_gradient - attention_estimate)[None]
    next_err_up = (full_up - approx_up)[None]
    next_err_down = (full_down - approx_down)[None]
    cols_attn = attn_w.shape[2]
    cols_up = up_w.shape[1]
    cols_down = down_w.shape[1]
    step_attn = lax.dynamic_slice_in_dim(attention_estimate, rep_index * cols_attn, cols_attn, 2)
    step_up = lax.dynamic_slice_in_dim(approx_up, rep_index * cols_up, cols_up, 1)
    step_down = lax.dynamic_slice_in_dim(approx_down, rep_index * cols_down, cols_down, 1)
    lr_mat = 1.5 * math.sqrt(rep_count / (SEQS * (WORDS + ENTS)))
    lr_vec = 0.2 * math.sqrt(rep_count / (SEQS * (WORDS + ENTS)))
    next_mom_attn = MOMENTUM * mom_attn + step_attn
    next_mom_up = MOMENTUM * mom_up + step_up
    next_mom_down = MOMENTUM * mom_down + step_down
    next_mom_vecs = MOMENTUM * mom_vecs + vec_mean
    new_attn = attn_w - lr_mat * next_mom_attn
    new_up = up_w - lr_mat * next_mom_up
    new_down = down_w - lr_mat * next_mom_down
    new_vecs = vecs - lr_vec * next_mom_vecs
    return (
        result[:, :words_dev],
        result[:, words_dev:],
        grad_inputs[:, :words_dev],
        grad_inputs[:, words_dev:],
        new_attn,
        new_up,
        new_down,
        new_vecs,
        next_mom_attn,
        next_mom_up,
        next_mom_down,
        next_mom_vecs,
        next_err_attn,
        next_err_up,
        next_err_down,
        attention_local_gradient,
        own_up,
        own_down,
        attention_right_factor,
        right_up,
        right_down,
    )


def seq_swap(array, bits):
    size = lax.axis_size("seq")
    return lax.ppermute(array, "seq", [(i, i ^ bits) for i in range(size)])


def rep_swap(array, bits):
    size = lax.axis_size("rep")
    return lax.ppermute(array, "rep", [(i, i ^ bits) for i in range(size)])


def planes_swap(array):
    seqs, reps = lax.axis_size("seq"), lax.axis_size("rep")
    pairs = []
    for s in range(seqs):
        for r in range(reps):
            pairs.append((s * reps + r, (r // 2) * reps + 2 * s + r % 2))
    return lax.ppermute(array, ("seq", "rep"), pairs)


def gather_seq(piece):
    other_chip = seq_swap(piece, 2)
    return [seq_swap(piece, 1), seq_swap(other_chip, 1), piece, other_chip]


def gather_direct(piece):
    pieces = [piece] + [rep_swap(piece, 2 * change) for change in (1, 2, 3)]
    return pieces, rep_swap(piece, 1)


def gather_tree(piece):
    own_side = rep_swap(piece, 1)
    far, own_side = lax.optimization_barrier((rep_swap(piece, 4), own_side))
    near = rep_swap(jnp.stack([piece, far]), 2)
    near, far_side = lax.optimization_barrier((near, rep_swap(far, 1)))
    near_side = rep_swap(near, 1)
    return [piece, own_side, far, far_side, near, near_side]


def tree_pieces(refs):
    own, own_side, far, far_side, near, near_side = refs
    return (
        (0, own[...], own_side[...]),
        (2, far[...], far_side[...]),
        (1, near[0], near_side[0]),
        (3, near[1], near_side[1]),
    )


def project_kernel(
    words_dev, rows_dev, place_ref, bias_word_ref, bias_ent_ref, scale_ref, *refs
):
    trees, row_refs = (refs[:6], refs[6:12]), refs[12:16]
    word_ref, ent_ref, packed_word_ref, packed_ent_ref, rows_word_ref, rows_ent_ref = refs[16:22]
    out_ref, piece_ref = refs[22:]
    ents_dev = rows_dev - words_dev
    z, y = place_ref[0], place_ref[1]
    for half, tree in enumerate(trees):
        for change, own, other in tree_pieces(tree):
            piece_ref[half, z ^ change, y] = own
            piece_ref[half, z ^ change, 1 - y] = other
    rows, both = piece_ref.shape[3:]
    cols = both // 14
    for half in (0, 1):
        for place in range(4):
            left, right = piece_ref[half, place, 0], piece_ref[half, place, 1]
            for side, piece in ((0, left), (1, right)):
                start = (4 * place + 2 * side + half) * rows
                out_ref[start : start + rows] = piece[:, 12 * cols :]
            for upper in (0, 1):
                parts = []
                for j in range(6):
                    low = (upper * 6 + j) * cols
                    parts.append(left[:, low : low + cols])
                    parts.append(right[:, low : low + cols])
                start = (4 * place + 2 * upper + half) * rows
                target = slice(start, start + rows)
                word_ref[target] = jnp.concatenate(parts[:4] + parts[8:], 1)
                ent_ref[target] = jnp.concatenate(parts[4:], 1)

    scale = scale_ref[...]
    word, ent = word_ref[...], ent_ref[...]
    for k, row_ref in enumerate(row_refs):
        words = row_ref[:words_dev]
        at = slice(k * words_dev, (k + 1) * words_dev)
        rows_word_ref[at] = words
        packed_word_ref[at] = ((mm(words, word) + bias_word_ref[...]) * scale).astype(
            jnp.bfloat16
        )
        at = slice(k * ents_dev, (k + 1) * ents_dev)
        rows_ent_ref[at] = row_ref[words_dev:rows_dev]
    packed_ent_ref[...] = ((mm(rows_ent_ref[...], ent) + bias_ent_ref[...]) * scale).astype(
        jnp.bfloat16
    )


def ffn_join_kernel(place_ref, *refs):
    pieces, sides, (up_ref, down_ref) = refs[:4], refs[4:8], refs[8:]
    z, y = place_ref[0], place_ref[1]
    for side in (0, 1):

        @pl.when(y == side)
        def _():
            for change in range(4):
                for y_at, piece in ((side, pieces[change]), (1 - side, sides[change])):
                    rows, both = piece.shape
                    cols = both // 4
                    place = z ^ change
                    for upper in (0, 1):
                        start = pl.multiple_of(place * (2 * rows) + upper * rows, 16)
                        up_ref[pl.ds(start, rows), y_at * cols : (y_at + 1) * cols] = piece[
                            :, upper * cols : (upper + 1) * cols
                        ]
                    start = pl.multiple_of((2 * place + y_at) * rows, 16)
                    down_ref[pl.ds(start, rows), :] = piece[:, 2 * cols :]


def join_call(kernel, place, pieces, shapes, name):
    whole = [pl.BlockSpec(memory_space=pltpu.VMEM)] * len(pieces)
    return pl.pallas_call(
        kernel,
        in_specs=[pl.BlockSpec(memory_space=pltpu.SMEM)] + whole,
        out_specs=[pl.BlockSpec(memory_space=pltpu.VMEM)] * len(shapes),
        out_shape=[jax.ShapeDtypeStruct(shape, jnp.bfloat16) for shape in shapes],
        name=name,
    )(place, *pieces)


def scatter_blocks(rows, dot, weight):
    half = rows.shape[0] // 2
    own = half // 2
    got = seq_swap(dot(rows[:half], weight).astype(jnp.bfloat16), 1).astype(jnp.float32)
    kept = dot(rows[half:], weight) + got
    return kept[:own] + seq_swap(kept[own:].astype(jnp.bfloat16), 2).astype(jnp.float32)


def scatter_parts(words, ents):
    words_dev, ents_dev = words.shape[0] // 4, ents.shape[0] // 4
    half = words_dev + ents_dev

    def rows(first):
        parts = []
        for k in (first, first + 1):
            parts.append(words[k * words_dev : (k + 1) * words_dev])
            parts.append(ents[k * ents_dev : (k + 1) * ents_dev])
        return jnp.concatenate(parts, 0)

    got = seq_swap(rows(0).astype(jnp.bfloat16), 1).astype(jnp.float32)
    kept = rows(2) + got
    return kept[:half], kept[half:].astype(jnp.bfloat16)


def rows_norm(hidden, gain, shift):
    center = hidden - jnp.mean(hidden, -1, keepdims=True)
    rstd = lax.rsqrt(jnp.mean(center * center, -1, keepdims=True) + EPS)
    normed = center * rstd
    return (normed * gain + shift, normed, rstd)


def rows_norm_back(grad, normed, rstd, gain):
    dnormed = grad * gain
    grad_in = rstd * (
        dnormed
        - jnp.mean(dnormed, -1, keepdims=True)
        - normed * jnp.mean(dnormed * normed, -1, keepdims=True)
    )
    return (grad_in, jnp.sum(grad * normed, axis=0), jnp.sum(grad, axis=0))


def mm(left, right, left_dim=1, right_dim=0):
    return lax.dot_general(
        left, right, (((left_dim,), (right_dim,)), ((), ())), preferred_element_type=jnp.float32
    )


def nt_dot(left, right):
    return mm(left, right, 1, 1)


def tn_dot(left, right):
    return mm(left, right, 0, 0)


HEAD_DIM = 64


def head_parts(word_ref, ent_ref, low, high):
    return jnp.concatenate([word_ref[:, low:high], ent_ref[:, low:high]], 0)


def attention_kernel(
    heads,
    query_word_ref,
    query_ent_ref,
    key_word_ref,
    key_ent_ref,
    offset_ref,
    attn_ref,
    low_ref,
    high_ref,
    stat_ref,
):
    width = heads * HEAD_DIM
    word_count = key_word_ref.shape[0]
    rows = attn_ref.shape[0]
    lane = lax.broadcasted_iota(jnp.int32, (rows, 128), 1)
    stats = jnp.zeros((rows, 128), jnp.float32)
    for h in range(heads):
        low, high = h * HEAD_DIM, (h + 1) * HEAD_DIM
        q_word = head_parts(query_word_ref, query_ent_ref, low, high)
        q_ent = head_parts(query_word_ref, query_ent_ref, width + low, width + high)
        k_word = key_word_ref[:, 2 * width + low : 2 * width + high]
        k_ent = key_ent_ref[:, 2 * width + low : 2 * width + high]
        s_word = nt_dot(q_word, k_word) + offset_ref[:, :word_count]
        s_ent = nt_dot(q_ent, k_ent) + offset_ref[:, word_count:]
        top = jnp.maximum(
            jnp.max(s_word, -1, keepdims=True), jnp.max(s_ent, -1, keepdims=True)
        )
        w_word = jnp.exp(s_word - top)
        w_ent = jnp.exp(s_ent - top)
        total = jnp.sum(w_word, -1, keepdims=True) + jnp.sum(w_ent, -1, keepdims=True)
        v_word = key_word_ref[:, 3 * width + low : 3 * width + high]
        v_ent = key_ent_ref[:, 3 * width + low : 3 * width + high]
        unnorm = mm(w_word.astype(jnp.bfloat16), v_word) + mm(w_ent.astype(jnp.bfloat16), v_ent)
        attn_ref[:, low:high] = unnorm / total
        stats = jnp.where(lane == h, top, stats)
        stats = jnp.where(lane == heads + h, total, stats)
    stat_ref[...] = stats
    low_ref[...] = attn_ref[: rows // 2].astype(jnp.bfloat16)
    high_ref[...] = attn_ref[rows // 2 :].astype(jnp.bfloat16)


def attention_forward(packed_word, packed_ent, offsets, heads):
    word_count, packed_width = packed_word.shape
    ent_count = packed_ent.shape[0]
    count = word_count + ent_count
    width = heads * HEAD_DIM
    block = count // 4
    return pl.pallas_call(
        functools.partial(attention_kernel, heads),
        grid=(4,),
        in_specs=[
            pl.BlockSpec((word_count // 4, packed_width), lambda i: (i, 0)),
            pl.BlockSpec((ent_count // 4, packed_width), lambda i: (i, 0)),
            pl.BlockSpec((word_count, packed_width), lambda i: (0, 0)),
            pl.BlockSpec((ent_count, packed_width), lambda i: (0, 0)),
            pl.BlockSpec((1, count), lambda i: (0, 0)),
        ],
        out_specs=[
            pl.BlockSpec((block, width), lambda i: (i, 0)),
            pl.BlockSpec((block // 2, width), lambda i: (i, 0)),
            pl.BlockSpec((block // 2, width), lambda i: (i, 0)),
            pl.BlockSpec((block, 128), lambda i: (i, 0)),
        ],
        out_shape=[
            jax.ShapeDtypeStruct((count, width), jnp.float32),
            jax.ShapeDtypeStruct((count // 2, width), jnp.bfloat16),
            jax.ShapeDtypeStruct((count // 2, width), jnp.bfloat16),
            jax.ShapeDtypeStruct((count, 128), jnp.float32),
        ],
        compiler_params=pltpu.CompilerParams(dimension_semantics=("arbitrary",)),
        cost_estimate=pl.CostEstimate(
            flops=4 * count * count * width,
            bytes_accessed=6 * count * packed_width,
            transcendentals=count * count * heads,
        ),
        name="attention",
    )(packed_word, packed_ent, packed_word, packed_ent, offsets)


def attention_back_kernel(
    heads,
    query_word_ref,
    query_ent_ref,
    key_word_ref,
    key_ent_ref,
    offset_ref,
    attn_ref,
    stat_ref,
    grad_low_ref,
    grad_high_ref,
    d_word_ref,
    d_ent_ref,
    sum_ref,
    key_sum,
    value_sum,
):
    width = heads * HEAD_DIM
    word_count = key_word_ref.shape[0]
    words_dev, ents_dev = query_word_ref.shape[0], query_ent_ref.shape[0]
    step = pl.program_id(0)

    @pl.when(step == 0)
    def _():
        key_sum[...] = jnp.zeros_like(key_sum)
        value_sum[...] = jnp.zeros_like(value_sum)
        sum_ref[...] = jnp.zeros_like(sum_ref)

    word_rows = pl.ds(pl.multiple_of(step * words_dev, words_dev), words_dev)
    ent_rows = pl.ds(pl.multiple_of(step * ents_dev, ents_dev), ents_dev)
    for h in range(heads):
        low, high = h * HEAD_DIM, (h + 1) * HEAD_DIM
        q_word = head_parts(query_word_ref, query_ent_ref, low, high)
        q_ent = head_parts(query_word_ref, query_ent_ref, width + low, width + high)
        k_word = key_word_ref[:, 2 * width + low : 2 * width + high]
        k_ent = key_ent_ref[:, 2 * width + low : 2 * width + high]
        v_word = key_word_ref[:, 3 * width + low : 3 * width + high]
        v_ent = key_ent_ref[:, 3 * width + low : 3 * width + high]
        top = stat_ref[:, h : h + 1]
        inverse = 1.0 / stat_ref[:, heads + h : heads + h + 1]
        grad = head_parts(grad_low_ref, grad_high_ref, low, high)
        delta = jnp.sum(grad * attn_ref[:, low:high], -1, keepdims=True) * inverse
        grad_low = (grad * inverse).astype(jnp.bfloat16)
        w_word = jnp.exp(nt_dot(q_word, k_word) + offset_ref[:, :word_count] - top)
        w_ent = jnp.exp(nt_dot(q_ent, k_ent) + offset_ref[:, word_count:] - top)
        d_word = (w_word * (nt_dot(grad_low, v_word) - delta)).astype(jnp.bfloat16)
        d_ent = (w_ent * (nt_dot(grad_low, v_ent) - delta)).astype(jnp.bfloat16)
        for at, dquery in ((low, mm(d_word, k_word)), (width + low, mm(d_ent, k_ent))):
            dquery = dquery * 0.125
            lanes = slice(at, at + HEAD_DIM)
            d_word_ref[word_rows, lanes] = dquery[:words_dev].astype(jnp.bfloat16)
            d_ent_ref[ent_rows, lanes] = dquery[words_dev:].astype(jnp.bfloat16)
            sum_ref[0:1, lanes] += jnp.sum(dquery[:words_dev], 0, keepdims=True)
            sum_ref[1:2, lanes] += jnp.sum(dquery[words_dev:], 0, keepdims=True)
        key_sum[low:high, :word_count] += tn_dot(q_word, d_word)
        key_sum[low:high, word_count:] += tn_dot(q_ent, d_ent)
        value_sum[low:high, :word_count] += tn_dot(grad_low, w_word.astype(jnp.bfloat16))
        value_sum[low:high, word_count:] += tn_dot(grad_low, w_ent.astype(jnp.bfloat16))

    @pl.when(step == pl.num_programs(0) - 1)
    def _():
        dkey = key_sum[...].T
        dvalue = value_sum[...].T
        sum_ref[2:3, :width] = jnp.sum(dvalue, 0, keepdims=True)
        both = jnp.concatenate([dkey, dvalue], 1).astype(jnp.bfloat16)
        d_word_ref[:, 2 * width :] = both[:word_count]
        d_ent_ref[:, 2 * width :] = both[word_count:]


def attention_backward(packed_word, packed_ent, offsets, attn, stats, grads, heads):
    word_count, packed_width = packed_word.shape
    ent_count = packed_ent.shape[0]
    count = word_count + ent_count
    width = heads * HEAD_DIM
    block = count // 4
    return pl.pallas_call(
        functools.partial(attention_back_kernel, heads),
        grid=(4,),
        in_specs=[
            pl.BlockSpec((word_count // 4, packed_width), lambda i: (i, 0)),
            pl.BlockSpec((ent_count // 4, packed_width), lambda i: (i, 0)),
            pl.BlockSpec((word_count, packed_width), lambda i: (0, 0)),
            pl.BlockSpec((ent_count, packed_width), lambda i: (0, 0)),
            pl.BlockSpec((1, count), lambda i: (0, 0)),
            pl.BlockSpec((block, width), lambda i: (i, 0)),
            pl.BlockSpec((block, 128), lambda i: (i, 0)),
            pl.BlockSpec((block // 2, width), lambda i: (i, 0)),
            pl.BlockSpec((block // 2, width), lambda i: (i, 0)),
        ],
        out_specs=[
            pl.BlockSpec((word_count, packed_width), lambda i: (0, 0)),
            pl.BlockSpec((ent_count, packed_width), lambda i: (0, 0)),
            pl.BlockSpec((8, 2 * width), lambda i: (0, 0)),
        ],
        out_shape=[
            jax.ShapeDtypeStruct((word_count, packed_width), jnp.bfloat16),
            jax.ShapeDtypeStruct((ent_count, packed_width), jnp.bfloat16),
            jax.ShapeDtypeStruct((8, 2 * width), jnp.float32),
        ],
        scratch_shapes=[
            pltpu.VMEM((width, count), jnp.float32),
            pltpu.VMEM((width, count), jnp.float32),
        ],
        compiler_params=pltpu.CompilerParams(dimension_semantics=("arbitrary",)),
        cost_estimate=pl.CostEstimate(
            flops=10 * count * count * width,
            bytes_accessed=16 * count * packed_width,
            transcendentals=count * count * heads,
        ),
        name="attention_back",
    )(packed_word, packed_ent, packed_word, packed_ent, offsets, attn, stats, *grads)


def tall(left):
    return jnp.swapaxes(left, -1, -2)


def halves(array):
    high = array.astype(jnp.bfloat16)
    return high, (array - high.astype(jnp.float32)).astype(jnp.bfloat16)


def stacked_halves(array):
    high = array.astype(jnp.bfloat16).astype(jnp.float32)
    return jnp.concatenate([array, array - high], 0).astype(jnp.bfloat16)


def columns_of(rank_rows):
    return jnp.concatenate(
        [rank_rows, rank_rows - rank_rows.astype(jnp.bfloat16).astype(jnp.float32)], 0
    ).T.astype(jnp.bfloat16)


def left_part(full, columns):
    high, low = halves(full)
    return mm(high, columns) + mm(low, columns)


def rank_first(part):
    both = part.T
    rank = both.shape[0] // 2
    return both[:rank] + both[rank:]


def left_ffn_kernel(
    got_ref, down_ref, err_up_ref, err_down_ref, q_up_ref, q_down_ref, full_up_ref, full_down_ref, left_ref
):
    step = pl.program_id(0)
    width = got_ref.shape[2]
    rows = got_ref.shape[1]
    left = 0.0
    for s in range(4):
        lanes = slice(s * width, (s + 1) * width)
        full = got_ref[s].astype(jnp.float32) + err_up_ref[0, :, lanes]
        full_up_ref[:, lanes] = full
        left = left + left_part(full, columns_of(q_up_ref[:, lanes]))
    left = rank_first(left)
    full = down_ref[...] + err_down_ref[0]
    full_down_ref[...] = full
    below = rank_first(left_part(full, columns_of(q_down_ref[...])))
    for side in (0, 1):

        @pl.when(step == side)
        def _():
            left_ref[0, :, side * rows : (side + 1) * rows] = left
            left_ref[1 + 2 * side] = below[:, : 2 * rows]
            left_ref[2 + 2 * side] = below[:, 2 * rows :]


def left_of_ffn(got_up, grad_down, err_up, err_down, q_up, q_down):
    rows, width = got_up.shape[1:]
    rank = q_up.shape[0]
    return pl.pallas_call(
        left_ffn_kernel,
        grid=(2,),
        in_specs=[
            pl.BlockSpec((4, rows // 2, width), lambda i: (0, i, 0)),
            pl.BlockSpec((2 * rows, width), lambda i: (i, 0)),
            pl.BlockSpec((1, rows // 2, 4 * width), lambda i: (0, i, 0)),
            pl.BlockSpec((1, 2 * rows, width), lambda i: (0, i, 0)),
            pl.BlockSpec((rank, 4 * width), lambda i: (0, 0)),
            pl.BlockSpec((rank, width), lambda i: (0, 0)),
        ],
        out_specs=[
            pl.BlockSpec((rows // 2, 4 * width), lambda i: (i, 0)),
            pl.BlockSpec((2 * rows, width), lambda i: (i, 0)),
            pl.BlockSpec((5, rank, rows), lambda i: (0, 0, 0)),
        ],
        out_shape=[
            jax.ShapeDtypeStruct((rows, 4 * width), jnp.float32),
            jax.ShapeDtypeStruct((4 * rows, width), jnp.float32),
            jax.ShapeDtypeStruct((5, rank, rows), jnp.float32),
        ],
        name="left_ffn",
    )(got_up, grad_down, err_up, err_down, q_up, q_down)


def left_attn_kernel(got_ref, out_ref, err_ref, q_ref, ffn_ref, full_ref, left_ref):
    step = pl.program_id(0)
    rows = full_ref.shape[1]
    part = 2 * rows
    lefts = []
    for j in range(7):
        if j < 6:
            lanes = slice(j * part, (j + 1) * part)
            grad = jnp.concatenate([got_ref[s, :, lanes] for s in range(4)], 1)
            full = grad.astype(jnp.float32) + err_ref[0, j]
        else:
            full = out_ref[...] + err_ref[0, j]
        full_ref[j] = full
        lefts.append(rank_first(left_part(full, columns_of(q_ref[j]))))
    for side in (0, 1):

        @pl.when(step == side)
        def _():
            for j in range(7):
                left_ref[j, :, side * rows : (side + 1) * rows] = lefts[j]

    @pl.when(step == 1)
    def _():
        left_ref[7:] = ffn_ref[...]


def left_of_attn(got, grad_out, err_attn, q_attn, left_ffn):
    rows, width = grad_out.shape
    rank = q_attn.shape[1]
    return pl.pallas_call(
        left_attn_kernel,
        grid=(2,),
        in_specs=[
            pl.BlockSpec((4, rows // 2, got.shape[2]), lambda i: (0, i, 0)),
            pl.BlockSpec((rows // 2, width), lambda i: (i, 0)),
            pl.BlockSpec((1, 7, rows // 2, width), lambda i: (0, 0, i, 0)),
            pl.BlockSpec((7, rank, width), lambda i: (0, 0, 0)),
            pl.BlockSpec((5, rank, rows), lambda i: (0, 0, 0)),
        ],
        out_specs=[
            pl.BlockSpec((7, rows // 2, width), lambda i: (0, i, 0)),
            pl.BlockSpec((12, rank, rows), lambda i: (0, 0, 0)),
        ],
        out_shape=[
            jax.ShapeDtypeStruct((7, rows, width), jnp.float32),
            jax.ShapeDtypeStruct((12, rank, rows), jnp.float32),
        ],
        name="left_attn",
    )(got, grad_out, err_attn, q_attn, left_ffn)


MATRIX_BLOCKS = [[j] for j in range(8)] + [[8, 9, 10, 11]]


def gram_kernel(scale, mine_ref, other_ref, left_ref, gram_ref):
    rank = mine_ref.shape[1]
    left = (mine_ref[...] + other_ref[...]) * scale
    left_ref[...] = left
    lane = lax.broadcasted_iota(jnp.int32, (rank, 128), 1)
    row = lax.broadcasted_iota(jnp.int32, (rank, 128), 0)
    for r in range(rank):
        gram = jnp.where((lane >= len(MATRIX_BLOCKS)) & (row == r), 1.0, 0.0)
        for m, blocks in enumerate(MATRIX_BLOCKS):
            product = sum(left[b] * left[b, r : r + 1] for b in blocks)
            gram = jnp.where(lane == m, jnp.sum(product, -1, keepdims=True), gram)
        gram_ref[r] = gram


def gram_of(mine, other, scale):
    rank = mine.shape[1]
    return pl.pallas_call(
        functools.partial(gram_kernel, scale),
        out_shape=[
            jax.ShapeDtypeStruct(mine.shape, jnp.float32),
            jax.ShapeDtypeStruct((rank, rank, 128), jnp.float32),
        ],
        name="gram",
    )(mine, other)


def inverse_factor(columns, rank):
    row = lax.broadcasted_iota(jnp.int32, columns[0].shape, 0)
    columns, lower = list(columns), []
    for k in range(rank):
        column = columns[k] / jnp.sqrt(columns[k][k : k + 1])
        lower.append(column)
        for c in range(k + 1, rank):
            columns[c] = columns[c] - column * column[c : c + 1]
    inverse = []
    for r in range(rank):
        value = jnp.where(row == r, 1.0, 0.0)
        for t in range(r):
            value = value - lower[t][r : r + 1] * inverse[t]
        inverse.append(value / lower[r][r : r + 1])
    return inverse


def right_part(both_ref, blocks, fulls):
    out = 0.0
    for b, full in zip(blocks, fulls):
        high, low = halves(full)
        out = out + mm(both_ref[b], high) + mm(both_ref[b], low)
    rank = out.shape[0] // 2
    return out[:rank] + out[rank:]


def right_kernel(place_ref, gram_ref, other_ref, left_ref, attn_ref, *refs):
    up_refs, (down_ref, vec_ref, orth_ref) = refs[:4], refs[4:7]
    p_attn_ref, p_up_ref, p_down_ref, sent_ref, kept_ref, both_ref = refs[7:]
    step = pl.program_id(0)
    rank, rows = left_ref.shape[1:]
    chip = place_ref[2]

    @pl.when(step == 0)
    def _():
        inverse = inverse_factor([gram_ref[r] + other_ref[r] for r in range(rank)], rank)
        row = lax.broadcasted_iota(jnp.int32, (rank, rows), 0)
        for m, blocks in enumerate(MATRIX_BLOCKS):
            weights = [inverse[r][:, m : m + 1] for r in range(rank)]
            for b in blocks:
                left = left_ref[b]
                orth = jnp.zeros((rank, rows), jnp.float32)
                for r in range(rank):
                    total = jnp.sum(left * weights[r], 0, keepdims=True)
                    orth = jnp.where(row == r, total, orth)
                orth_ref[b] = orth
                both_ref[b] = stacked_halves(orth)
                if b < 7:
                    p_attn_ref[b] = orth
                elif b == 7:
                    p_up_ref[...] = orth
                else:
                    p_down_ref[:, (b - 8) * rows : (b - 7) * rows] = orth

    parts = [right_part(both_ref, [j], [attn_ref[j]]) for j in range(7)]
    parts += [right_part(both_ref, [7], [up_refs[k][...]]) for k in range(4)]
    parts.append(
        right_part(
            both_ref, [8, 9, 10, 11], [down_ref[k * rows : (k + 1) * rows] for k in range(4)]
        )
    )
    parts += [vec_ref[0], vec_ref[1]]
    for at, ref in enumerate((sent_ref, kept_ref)):

        @pl.when(step == at)
        def _():
            for b, part in enumerate(parts):
                ref[(b // 7) ^ chip, b % 7] = part


def right_of(place, gram, other, left, full_attn, full_up, full_down, vecs):
    rank, rows = left.shape[1:]
    width = full_attn.shape[2]
    lanes = width // 2

    def whole(shape):
        return pl.BlockSpec(shape, lambda i, place: (0,) * len(shape))

    def half(i, place):
        return 1 - place[3] + i * (2 * place[3] - 1)

    def up_spec(k):
        return pl.BlockSpec((rows, lanes), lambda i, place: (0, 2 * k + half(i, place)))

    out_shapes = [
        left.shape,
        (7, rank, rows),
        (rank, rows),
        (rank, 4 * rows),
        (2, 7, rank, lanes),
        (2, 7, rank, lanes),
    ]
    return pl.pallas_call(
        right_kernel,
        grid_spec=pltpu.PrefetchScalarGridSpec(
            num_scalar_prefetch=1,
            grid=(2,),
            in_specs=[
                whole(gram.shape),
                whole(other.shape),
                whole(left.shape),
                pl.BlockSpec((7, rows, lanes), lambda i, place: (0, 0, half(i, place))),
                up_spec(0),
                up_spec(1),
                up_spec(2),
                up_spec(3),
                pl.BlockSpec((4 * rows, lanes), lambda i, place: (0, half(i, place))),
                pl.BlockSpec((2, rank, lanes), lambda i, place: (0, 0, half(i, place))),
            ],
            out_specs=[whole(shape) for shape in out_shapes],
            scratch_shapes=[pltpu.VMEM((12, 2 * rank, rows), jnp.bfloat16)],
        ),
        out_shape=[jax.ShapeDtypeStruct(shape, jnp.float32) for shape in out_shapes],
        name="right",
    )(place, gram, other, left, full_attn, full_up, full_up, full_up, full_up, full_down, vecs)


def left_stack(orth):
    high = orth.astype(jnp.bfloat16).astype(jnp.float32)
    return jnp.concatenate([orth, orth, orth - high, jnp.zeros_like(orth)], 0)


def right_stack(right):
    high = right.astype(jnp.bfloat16).astype(jnp.float32)
    return jnp.concatenate([right, right - high, right, jnp.zeros_like(right)], 0).astype(
        jnp.bfloat16
    )


def update_kernel(rate, rate_vecs, place_ref, orth_ref, mine_ref, other_ref, *refs):
    full_refs, mom_refs, weight_refs = refs[:3], refs[3:7], refs[7:11]
    err_refs, next_refs, new_refs = refs[11:14], refs[14:18], refs[18:22]
    q_attn_ref, q_up_ref, q_down_ref, right_ref, tall_ref, right_rows, cols_rows = refs[22:]
    step = pl.program_id(0)
    rows = full_refs[1].shape[0]
    rank, width = right_ref.shape[1:]
    part = orth_ref.shape[2]
    cols = mom_refs[0].shape[2]
    cols_up = mom_refs[1].shape[1]

    def move(change, at, i, rate=rate):
        value = MOMENTUM * mom_refs[i][at] + change
        next_refs[i][at] = value
        new_refs[i][at] = weight_refs[i][at] - rate * value

    @pl.when(step == 0)
    def _():
        lanes = width // 2
        chip, core = place_ref[2], place_ref[3]
        for own in (0, 1):

            @pl.when(core == own)
            def _():
                for half in (0, 1):
                    blocks = pl.ds((chip ^ half) * 7, 7)
                    right_ref[blocks, :, own * lanes : (own + 1) * lanes] = mine_ref[half]
                    right_ref[blocks, :, (1 - own) * lanes : (2 - own) * lanes] = other_ref[half]

        replica = 2 * place_ref[0] + place_ref[1]
        shift = width - replica * cols
        for b in range(12):
            tall_ref[b] = left_stack(orth_ref[b]).T.astype(jnp.bfloat16)
            right = right_ref[b]
            right_rows[b] = right_stack(right)
            if b < 7 or b == 11:
                own = pltpu.roll(right, shift, 1)[:, :cols]
                cols_rows[min(b, 7)] = right_stack(own)
            if b < 7:
                q_attn_ref[b] = right
            elif b < 11:
                q_up_ref[:, (b - 7) * width : (b - 6) * width] = right
            else:
                q_down_ref[...] = right
        move(right_ref[12], slice(0, rank), 3, rate_vecs)
        move(right_ref[13, : rank - 1], slice(rank, 2 * rank - 1), 3, rate_vecs)

    own = pl.ds(pl.multiple_of(step * rows, 16), rows)
    for j in range(7):
        left = tall_ref[j, own]
        err_refs[0][0, j] = full_refs[0][j] - mm(left, right_rows[j])
        move(mm(left, cols_rows[j]), j, 0)
    left = tall_ref[7, own]
    for k in range(4):
        lanes = slice(k * width, (k + 1) * width)
        err_refs[1][0, :, lanes] = full_refs[1][:, lanes] - mm(left, right_rows[7 + k])
    block = right_rows[7 + place_ref[0]]
    low = mm(left, block[:, :cols_up])
    high = mm(left, block[:, cols_up:])
    side = place_ref[1].astype(jnp.float32)
    move(jnp.where(jnp.full(low.shape, side) == 0.0, low, high), ..., 1)
    err_refs[2][0] = full_refs[2][...] - mm(tall_ref[8 + step], right_rows[11])

    @pl.when(step == 3)
    def _():
        for k in range(4):
            change = tn_dot(cols_rows[7], left_stack(orth_ref[8 + k]).astype(jnp.bfloat16))
            move(change, (slice(None), slice(k * part, (k + 1) * part)), 2)


def updates(place, orth, mine, other, full, mom, weight, rate, rate_vecs):
    rank, part = orth.shape[1:]
    width = full[2].shape[1]
    cols, cols_up = mom[0].shape[2], mom[1].shape[1]
    rows = part // 4

    def whole(array):
        return pl.BlockSpec(array.shape, lambda i: (0,) * array.ndim)

    full_specs = [
        pl.BlockSpec((7, rows, width), lambda i: (0, i, 0)),
        pl.BlockSpec((rows, 4 * width), lambda i: (i, 0)),
        pl.BlockSpec((part, width), lambda i: (i, 0)),
    ]
    own_specs = [
        pl.BlockSpec((7, rows, cols), lambda i: (0, i, 0)),
        pl.BlockSpec((rows, cols_up), lambda i: (i, 0)),
        whole(mom[2]),
        whole(mom[3]),
    ]
    err_specs = [
        pl.BlockSpec((1, 7, rows, width), lambda i: (0, 0, i, 0)),
        pl.BlockSpec((1, rows, 4 * width), lambda i: (0, i, 0)),
        pl.BlockSpec((1, part, width), lambda i: (0, i, 0)),
    ]
    err_shapes = [jax.ShapeDtypeStruct((1,) + array.shape, jnp.float32) for array in full]
    own_shapes = [jax.ShapeDtypeStruct(array.shape, jnp.float32) for array in mom]
    q_shapes = [
        jax.ShapeDtypeStruct(shape, jnp.float32)
        for shape in ((7, rank, width), (rank, 4 * width), (rank, width))
    ]
    outs = pl.pallas_call(
        functools.partial(update_kernel, rate, rate_vecs),
        grid=(4,),
        in_specs=[pl.BlockSpec(memory_space=pltpu.SMEM), whole(orth), whole(mine), whole(other)]
        + full_specs
        + own_specs
        + own_specs,
        out_specs=err_specs + own_specs + own_specs + [whole(shape) for shape in q_shapes],
        out_shape=err_shapes + own_shapes + own_shapes + q_shapes,
        scratch_shapes=[
            pltpu.VMEM((14, rank, width), jnp.float32),
            pltpu.VMEM((12, part, 32), jnp.bfloat16),
            pltpu.VMEM((12, 32, width), jnp.bfloat16),
            pltpu.VMEM((8, 32, cols), jnp.bfloat16),
        ],
        name="updates",
    )(place, orth, mine, other, *full, *mom, *weight)
    return outs[:3], outs[3:7], outs[7:11], outs[11:]


def head_split_device(
    x_words,
    x_ents,
    spans,
    word_mask,
    ent_mask,
    cot_words,
    cot_ents,
    attn_w,
    up_w,
    down_w,
    vecs,
    mom_attn,
    mom_up,
    mom_down,
    mom_vecs,
    err_attn,
    err_up,
    err_down,
    attention_prior_right,
    qf_up,
    qf_down,
):
    low_type = jnp.bfloat16
    words_dev, width = x_words.shape[1:]
    ents_dev = x_ents.shape[1]
    rows_dev = words_dev + ents_dev
    seq_count, rep_count = lax.axis_size("seq"), lax.axis_size("rep")
    seq_index, rep_index = lax.axis_index("seq"), lax.axis_index("rep")
    heads = HEADS // seq_count
    part = width // seq_count
    word_count = words_dev * seq_count
    ent_count = ents_dev * seq_count
    cols = attn_w.shape[2]
    cols_up = up_w.shape[1]
    hidden = cols_up * rep_count
    hidden_part = hidden // seq_count

    core, chip = seq_index % 2, seq_index // 2
    place = jnp.stack([rep_index // 2, rep_index % 2, chip, core]).astype(jnp.int32)
    block = part // 2
    project_piece = jnp.transpose(
        attn_w[:6].astype(low_type).reshape(6, 2, block, cols), (2, 1, 0, 3)
    ).reshape(block, 12 * cols)
    out_piece = attn_w[6].astype(low_type).T
    half = block // 2
    first, second = [
        jnp.concatenate([planes_swap(project_piece[rows]), out_piece[rows]], 1)
        for rows in (slice(half), slice(half, block))
    ]
    trees = [gather_tree(first)]
    second, unused_far = lax.optimization_barrier((second, trees[0][2]))
    trees.append(gather_tree(second))
    up_piece = jnp.transpose(
        up_w.astype(low_type).reshape(2, block, cols_up), (1, 0, 2)
    ).reshape(block, 2 * cols_up)
    ffn_piece = jnp.concatenate([planes_swap(up_piece), down_w.astype(low_type).T], 1)
    ffn_piece, unused_near = lax.optimization_barrier((ffn_piece, (trees[0][4], trees[1][4])))
    ffn_pieces, ffn_side = gather_direct(ffn_piece)

    spans, unused_piece = lax.optimization_barrier((spans, project_piece))
    inputs = jnp.concatenate([x_words[0], x_ents[0] + span_mean_closed(spans[0], width)], 0)
    live = jnp.concatenate([word_mask[0], ent_mask[0]], 0).astype(low_type)
    live = jnp.pad(live.reshape(1, rows_dev), ((0, 15), (0, width - rows_dev)))
    pieces = gather_seq(jnp.concatenate([inputs.astype(low_type), live], 0))
    lives = [piece[rows_dev, :rows_dev] for piece in pieces]
    lives = [piece[:words_dev] for piece in lives] + [piece[words_dev:] for piece in lives]
    offsets = ((jnp.concatenate(lives).astype(jnp.float32) - 1.0) * MASK_FILL).reshape(1, -1)

    own_vecs = lax.dynamic_slice_in_dim(vecs, seq_index * part, part, 1)
    none = jnp.zeros((part,), jnp.float32)
    scale = jnp.where(jnp.arange(4 * part) < 2 * part, 0.125, 1.0).astype(jnp.float32)
    bias_word = jnp.concatenate([own_vecs[0], own_vecs[1], none, own_vecs[4]])
    bias_ent = jnp.concatenate([own_vecs[2], own_vecs[3], none, own_vecs[4]])
    in_vmem = pl.BlockSpec(memory_space=pltpu.VMEM)
    w_word, w_ent, packed_word, packed_ent, rows_word, rows_ent, w_out = pl.pallas_call(
        functools.partial(project_kernel, words_dev, rows_dev),
        in_specs=[pl.BlockSpec(memory_space=pltpu.SMEM)] + [in_vmem] * 19,
        out_specs=[in_vmem] * 7,
        out_shape=[
            jax.ShapeDtypeStruct(shape, low_type)
            for shape in [
                (rows, width)
                for rows in (width, width, word_count, ent_count, word_count, ent_count)
            ]
            + [(width, part)]
        ],
        scratch_shapes=[pltpu.VMEM((2, 4, 2, half, 14 * cols), low_type)],
        name="project",
    )(
        place,
        bias_word.reshape(1, -1),
        bias_ent.reshape(1, -1),
        scale.reshape(1, -1),
        *trees[0],
        *trees[1],
        *pieces,
    )
    attn, *attn_low, stats = attention_forward(packed_word, packed_ent, offsets, heads)
    attn_low[1], ffn_pieces, ffn_side = lax.optimization_barrier(
        (attn_low[1], ffn_pieces, ffn_side)
    )
    ffn_sides = [ffn_side] + [rep_swap(piece, 1) for piece in ffn_pieces[1:]]
    w_up, w_down = join_call(
        ffn_join_kernel,
        place,
        ffn_pieces + ffn_sides,
        [(width, hidden_part), (width, hidden_part)],
        "join_ffn",
    )

    bias_up = lax.dynamic_slice_in_dim(
        vecs[11:15].reshape(hidden), seq_index * hidden_part, hidden_part, 0
    )
    grad_result = jnp.concatenate([cot_words[0], cot_ents[0]], 0)
    split = rows_dev // 2
    results, grads_one, grads_attn, kept = [], [], [], []
    sums = [0.0] * 7
    for c in (0, 1):
        at = slice(c * split, (c + 1) * split)
        branch = scatter_blocks(attn_low[c], nt_dot, w_out) + vecs[5]
        mid, normed_one, rstd_one = rows_norm(inputs[at] + branch, vecs[7], vecs[8])
        mid_low = jnp.concatenate(gather_seq(mid.astype(low_type)), 0)
        pre = mm(mid_low, w_up) + bias_up
        cdf = 0.5 * (1.0 + lax.erf(pre * math.sqrt(0.5)))
        act_low = (pre * cdf).astype(low_type)
        ffn = scatter_blocks(act_low, nt_dot, w_down) + vecs[6]
        result, normed_two, rstd_two = rows_norm(mid + ffn, vecs[9], vecs[10])
        grad_two, gain_two, shift_two = rows_norm_back(grad_result[at], normed_two, rstd_two, vecs[9])
        grad_ffn = jnp.concatenate(gather_seq(grad_two.astype(low_type)), 0)
        density = jnp.exp(-0.5 * pre * pre) * (1.0 / math.sqrt(2.0 * math.pi))
        grad_pre = mm(grad_ffn, w_down) * (cdf + pre * density)
        grad_pre_low = grad_pre.astype(low_type)
        grad_mid = grad_two + scatter_blocks(grad_pre_low, nt_dot, w_up)
        grad_one, gain_one, shift_one = rows_norm_back(grad_mid, normed_one, rstd_one, vecs[7])
        grad_branch = jnp.concatenate(gather_seq(grad_one.astype(low_type)), 0)
        grads_attn.append(mm(grad_branch, w_out))
        results.append(result)
        grads_one.append(grad_one)
        kept.append((mid_low, act_low, grad_ffn, grad_pre_low, grad_branch))
        parts = (
            jnp.sum(grad_one, 0),
            jnp.sum(grad_two, 0),
            gain_one,
            shift_one,
            gain_two,
            shift_two,
            jnp.sum(grad_pre, 0),
        )
        sums = [total + value for total, value in zip(sums, parts)]
    result = jnp.concatenate(results, 0)
    grad_one = jnp.concatenate(grads_one, 0)
    grad_down = sum(tn_dot(act_low, grad_ffn) for _, act_low, grad_ffn, _, _ in kept)
    grad_up = sum(tn_dot(mid_low, grad_pre_low) for mid_low, _, _, grad_pre_low, _ in kept)
    grad_up, unused_branch = lax.optimization_barrier((grad_up.astype(low_type), kept[1][4]))
    got_up = lax.all_to_all(grad_up.reshape(seq_count, part, hidden_part), "seq", 0, 0)
    grad_out = sum(tn_dot(low, parts[4]) for low, parts in zip(attn_low, kept))
    d_word, d_ent, d_sums = attention_backward(
        packed_word, packed_ent, offsets, attn, stats, grads_attn, heads
    )
    d_word, got_up = lax.optimization_barrier((d_word, got_up))
    grad_word = tn_dot(rows_word, d_word)
    grad_ent = tn_dot(rows_ent, d_ent)
    grad_project = jnp.concatenate(
        [
            grad_word[:, : 2 * part],
            grad_ent[:, : 2 * part],
            grad_word[:, 2 * part :] + grad_ent[:, 2 * part :],
        ],
        1,
    ).astype(low_type)
    d_word, d_ent, grad_project = lax.optimization_barrier((d_word, d_ent, grad_project))
    got_project = lax.all_to_all(
        grad_project.reshape(seq_count, part, 6 * part), "seq", 0, 0
    )
    full_up, full_down, left_ffn = left_of_ffn(
        got_up, grad_down, err_up, err_down, qf_up.T, qf_down.T
    )
    own_inputs, sent_inputs = scatter_parts(nt_dot(d_word, w_word), nt_dot(d_ent, w_ent))

    vec_grad = jnp.zeros((15, width), jnp.float32)
    bias_query = jnp.concatenate(
        [d_sums[0].reshape(2, part), d_sums[1].reshape(2, part), d_sums[2, :part].reshape(1, part)], 0
    )
    vec_grad = lax.dynamic_update_slice(vec_grad, bias_query, (0, seq_index * part))
    vec_grad = lax.dynamic_update_slice(vec_grad, jnp.stack(sums[:6]), (5, 0))
    bias_rows = hidden_part // width
    vec_grad = lax.dynamic_update_slice(
        vec_grad, sums[6].reshape(bias_rows, width), (11 + seq_index * bias_rows, 0)
    )

    full_attn, left = left_of_attn(
        got_project, grad_out, err_attn, tall(attention_prior_right), left_ffn
    )
    left, sent_inputs = lax.optimization_barrier((left, sent_inputs))
    got_inputs = seq_swap(sent_inputs, 2)
    for bits in (1, 2):
        left = left + rep_swap(left, bits)
    left, got_inputs = lax.optimization_barrier((left, got_inputs))
    left, gram = gram_of(left, rep_swap(left, 4), 1.0 / rep_count)
    gram = gram + seq_swap(gram, 1)
    rows_vec = jnp.pad(vec_grad, ((0, 1), (0, 0))).reshape(2, 8, width)
    orth, p_attn, p_up, p_down, sent, kept = right_of(
        place, gram, seq_swap(gram, 2), left, full_attn, full_up, full_down, rows_vec
    )
    got_inputs, unused_orth = lax.optimization_barrier((got_inputs, orth))
    grad_inputs = grad_one + (own_inputs + got_inputs.astype(jnp.float32))
    kept = kept + seq_swap(sent, 1)
    kept = kept[0] + seq_swap(kept[1], 2)
    for bits in (1, 2, 4):
        kept = kept + rep_swap(kept, bits)
    kept = kept / rep_count
    kept = jnp.stack([kept, seq_swap(kept, 2)])
    lr_mat = 1.5 * math.sqrt(rep_count / (SEQS * (WORDS + ENTS)))
    lr_vec = 0.2 * math.sqrt(rep_count / (SEQS * (WORDS + ENTS)))
    next_err, next_mom, new, (q_attn, q_up, q_down) = updates(
        place,
        orth,
        kept,
        seq_swap(kept, 1),
        (full_attn, full_up, full_down),
        (mom_attn, mom_up, mom_down.T, mom_vecs),
        (attn_w, up_w, down_w.T, vecs),
        lr_mat,
        lr_vec,
    )
    return (
        result[None, :words_dev],
        result[None, words_dev:],
        grad_inputs[None, :words_dev],
        grad_inputs[None, words_dev:],
        new[0],
        new[1],
        new[2].T,
        new[3],
        next_mom[0],
        next_mom[1],
        next_mom[2].T,
        next_mom[3],
        next_err[0],
        next_err[1],
        next_err[2],
        tall(p_attn),
        tall(p_up),
        tall(p_down),
        tall(q_attn),
        tall(q_up),
        tall(q_down),
    )


def solution(mesh):
    in_specs = (
        P("rep", "seq", None),
        P("rep", "seq", None),
        P("rep", "seq", None),
        P("rep", "seq"),
        P("rep", "seq"),
        P("rep", "seq", None),
        P("rep", "seq", None),
        P(None, "seq", "rep"),
        P("seq", "rep"),
        P("seq", "rep"),
        P(),
        P(None, "seq", "rep"),
        P("seq", "rep"),
        P("seq", "rep"),
        P(),
        P("rep", None, "seq", None),
        P("rep", "seq", None),
        P("rep", "seq", None),
        P(),
        P(),
        P(),
    )
    out_specs = (
        P("rep", "seq", None),
        P("rep", "seq", None),
        P("rep", "seq", None),
        P("rep", "seq", None),
        P(None, "seq", "rep"),
        P("seq", "rep"),
        P("seq", "rep"),
        P(),
        P(None, "seq", "rep"),
        P("seq", "rep"),
        P("seq", "rep"),
        P(),
        P("rep", None, "seq", None),
        P("rep", "seq", None),
        P("rep", "seq", None),
        P(None, "seq", None),
        P("seq", None),
        P("seq", None),
        P(),
        P(),
        P(),
    )
    seqs, reps = mesh.shape["seq"], mesh.shape["rep"]
    split_heads = seqs == 4 and reps == 2 * seqs and HEADS % seqs == 0
    body = head_split_device if split_heads else on_device
    return jax.shard_map(
        body, mesh=mesh, in_specs=in_specs, out_specs=out_specs, check_vma=False
    )
```

```python
import functools
import math

import jax
import jax.numpy as jnp
from jax import lax
from jax.experimental import pallas as pl
from jax.experimental.pallas import tpu as pltpu
from jax.sharding import PartitionSpec as P

HEADS = 12
WORDS = 1024
ENTS = 128
SPAN = 16
SEQS = 1


HIGH_PRECISION = lax.Precision.HIGHEST
EPS = 1e-05
MASK_FILL = 30000.0
MOMENTUM = 0.9


def span_mean(spans, model_width):
    starts = spans[..., 0]
    finals = spans[..., 1]
    lengths = (finals - starts + 1).astype(jnp.float32)
    offsets = jnp.arange(SPAN, dtype=jnp.int32)
    places = (starts[..., None] + offsets).astype(jnp.float32)
    shares = (offsets <= (finals - starts)[..., None]).astype(jnp.float32) / lengths[..., None]
    half_width = model_width // 2
    rates = jnp.exp(
        jnp.arange(half_width).astype(jnp.float32) * (-2.0 * math.log(10000.0) / model_width)
    )
    angles = places[..., None] * rates
    table = jnp.concatenate([jnp.sin(angles), jnp.cos(angles)], -1)
    return jnp.sum(table * shares[..., None], axis=-2)


def span_mean_closed(spans, model_width):
    lengths = (spans[..., 1] - spans[..., 0] + 1).astype(jnp.float32)[..., None]
    middles = (spans[..., 1] + spans[..., 0]).astype(jnp.float32)[..., None]
    half_rates = 0.5 * jnp.exp(
        jnp.arange(model_width // 2).astype(jnp.float32) * (-2.0 * math.log(10000.0) / model_width)
    )
    share = jnp.sin(lengths * half_rates) / (lengths * jnp.sin(half_rates))
    angles = middles * half_rates
    return jnp.concatenate([share * jnp.sin(angles), share * jnp.cos(angles)], -1)


def layer_norm(hidden, gain, shift):
    center = hidden - jnp.mean(hidden, -1, keepdims=True)
    rstd = lax.rsqrt(jnp.mean(center * center, -1, keepdims=True) + EPS)
    normed = center * rstd
    return (normed * gain + shift, normed, rstd)


def norm_back(grad, normed, rstd, gain):
    dnormed = grad * gain
    grad_in = rstd * (
        dnormed
        - jnp.mean(dnormed, -1, keepdims=True)
        - normed * jnp.mean(dnormed * normed, -1, keepdims=True)
    )
    return (grad_in, jnp.sum(grad * normed, axis=(0, 1)), jnp.sum(grad, axis=(0, 1)))


def gelu_exact(value):
    return jax.nn.gelu(value, approximate=False)


def project(row_entries, weight_matrix):
    return jnp.einsum("thq,qo->tho", row_entries, weight_matrix, preferred_element_type=jnp.float32)


def project_back(row_entries, weight_matrix):
    return jnp.einsum("hpf,zf->hpz", row_entries, weight_matrix, preferred_element_type=jnp.float32)


def weight_grad(input_arrays, gradient_list):
    return jnp.einsum(
        "cev,ceg->vg", input_arrays, gradient_list, preferred_element_type=jnp.float32
    )


def split_keys(pieces, words_dev, ents_dev, head_count):
    key_piece, live_piece = pieces
    batch_rows = key_piece.shape[0]
    both = key_piece.shape[2]
    model_width = both // 2
    head_dim = model_width // head_count
    rows_dev = words_dev + ents_dev
    blocks = key_piece.shape[1] // rows_dev
    grouped = key_piece.reshape(batch_rows, blocks, rows_dev, both)
    live_grouped = live_piece.reshape(batch_rows, blocks, rows_dev)
    word_part = grouped[:, :, :words_dev].reshape(batch_rows, blocks * words_dev, both)
    ent_part = grouped[:, :, words_dev:].reshape(batch_rows, blocks * ents_dev, both)
    keys_word = word_part[..., :model_width].reshape(batch_rows, -1, head_count, head_dim)
    keys_ent = ent_part[..., :model_width].reshape(batch_rows, -1, head_count, head_dim)
    values = jnp.concatenate(
        [word_part[..., model_width:], ent_part[..., model_width:]], 1
    ).reshape(batch_rows, -1, head_count, head_dim)
    live = jnp.concatenate(
        [
            live_grouped[:, :, :words_dev].reshape(batch_rows, -1),
            live_grouped[:, :, words_dev:].reshape(batch_rows, -1),
        ],
        1,
    )
    offsets = (live.astype(jnp.float32) - 1.0) * MASK_FILL
    return (keys_word, keys_ent, values, offsets, blocks)


def score_block(query_word, query_ent, keys_word, keys_ent, offsets):
    score_word = jnp.einsum(
        "sqhd,skhd->shqk", query_word, keys_word, preferred_element_type=jnp.float32
    )
    score_ent = jnp.einsum(
        "sqhd,skhd->shqk", query_ent, keys_ent, preferred_element_type=jnp.float32
    )
    return jnp.concatenate([score_word, score_ent], -1) + offsets[:, None, None, :]


def flat_heads(array):
    return array.reshape(array.shape[0], array.shape[1], -1)


def join_rows(grad_keys_word, grad_keys_ent, grad_values, blocks, words_dev, ents_dev):
    batch_rows = grad_keys_word.shape[0]
    word_count = grad_keys_word.shape[1]
    word_rows = jnp.concatenate(
        [flat_heads(grad_keys_word), flat_heads(grad_values[:, :word_count])], -1
    )
    ent_rows = jnp.concatenate(
        [flat_heads(grad_keys_ent), flat_heads(grad_values[:, word_count:])], -1
    )
    word_rows = word_rows.reshape(batch_rows, blocks, words_dev, -1)
    ent_rows = ent_rows.reshape(batch_rows, blocks, ents_dev, -1)
    return jnp.concatenate([word_rows, ent_rows], 2).reshape(
        batch_rows, blocks * (words_dev + ents_dev), -1
    )


def from_gram(left, gram):
    lower = jnp.linalg.cholesky(gram)
    return jax.scipy.linalg.solve_triangular(lower, left.T, lower=True).T


def orthonormal(left):
    return from_gram(left, jnp.dot(left.T, left, precision=HIGH_PRECISION))


def on_device(
    x_words,
    x_ents,
    spans,
    word_mask,
    ent_mask,
    cot_words,
    cot_ents,
    attn_w,
    up_w,
    down_w,
    vecs,
    mom_attn,
    mom_up,
    mom_down,
    mom_vecs,
    err_attn,
    err_up,
    err_down,
    attention_prior_right,
    qf_up,
    qf_down,
):
    batch_rows, words_dev, model_width = x_words.shape
    ents_dev = x_ents.shape[1]
    rows_dev = words_dev + ents_dev
    head_count = HEADS
    head_dim = model_width // head_count
    hidden_width = up_w.shape[1] * lax.axis_size("rep")
    seq_count = lax.axis_size("seq")
    rep_count = lax.axis_size("rep")
    seq_index = lax.axis_index("seq")
    rep_index = lax.axis_index("rep")
    lowered = jnp.bfloat16
    column_parts = (
        lax.all_gather(attn_w.astype(lowered), "rep", axis=2, tiled=True),
        lax.all_gather(up_w.astype(lowered), "rep", axis=1, tiled=True),
        lax.all_gather(down_w.astype(lowered), "rep", axis=1, tiled=True),
    )
    w_attn, w_up, w_down = (
        lax.all_gather(column_parts[0], "seq", axis=1, tiled=True),
        lax.all_gather(column_parts[1], "seq", axis=0, tiled=True),
        lax.all_gather(column_parts[2], "seq", axis=0, tiled=True),
    )
    input_arrays = jnp.concatenate([x_words, x_ents + span_mean(spans, model_width)], 1)
    inputs_low = input_arrays.astype(lowered)
    word_low = inputs_low[:, :words_dev]
    ent_low = inputs_low[:, words_dev:]
    query_word = (
        jnp.concatenate(
            [project(word_low, w_attn[0]) + vecs[0], project(ent_low, w_attn[2]) + vecs[2]], 1
        )
        * 0.125
    ).astype(lowered)
    query_ent = (
        jnp.concatenate(
            [project(word_low, w_attn[1]) + vecs[1], project(ent_low, w_attn[3]) + vecs[3]], 1
        )
        * 0.125
    ).astype(lowered)
    keys_low = project(inputs_low, w_attn[4]).astype(lowered)
    values_low = (project(inputs_low, w_attn[5]) + vecs[4]).astype(lowered)
    key_rows = jnp.concatenate([keys_low, values_low], -1)
    key_live = jnp.concatenate([word_mask, ent_mask], 1).astype(lowered)
    heads_word = query_word.reshape(batch_rows, rows_dev, head_count, head_dim)
    heads_ent = query_ent.reshape(batch_rows, rows_dev, head_count, head_dim)
    forward_row_top = jnp.full((batch_rows, head_count, rows_dev), -jnp.inf, jnp.float32)
    row_total = jnp.zeros((batch_rows, head_count, rows_dev), jnp.float32)
    weighted = jnp.zeros((batch_rows, rows_dev, head_count, head_dim), jnp.float32)
    keys_word, keys_ent, values, offsets, blocks = split_keys(
        (
            lax.all_gather(key_rows, "seq", axis=1, tiled=True),
            lax.all_gather(key_live, "seq", axis=1, tiled=True),
        ),
        words_dev,
        ents_dev,
        head_count,
    )
    scores = score_block(heads_word, heads_ent, keys_word, keys_ent, offsets)
    new_top = jnp.max(scores, -1)
    factor = jnp.exp(forward_row_top - new_top)
    weights = jnp.exp(scores - new_top[..., None])
    row_total = row_total * factor + jnp.sum(weights, -1)
    weighted = weighted * jnp.transpose(factor, (0, 2, 1))[..., None] + jnp.einsum(
        "shqk,skhd->sqhd", weights.astype(lowered), values, preferred_element_type=jnp.float32
    )
    row_top, row_total, weighted = (new_top, row_total, weighted)
    total_rows = jnp.transpose(row_total, (0, 2, 1))[..., None]
    attn = weighted / total_rows
    attn_low = attn.reshape(batch_rows, rows_dev, model_width).astype(lowered)
    branch = project(attn_low, w_attn[6]) + vecs[5]
    mid, normed_one, rstd_one = layer_norm(input_arrays + branch, vecs[7], vecs[8])
    mid_low = mid.astype(lowered)
    pre = project(mid_low, w_up) + vecs[11:15].reshape(hidden_width)
    act_low = gelu_exact(pre).astype(lowered)
    ffn = project(act_low, w_down) + vecs[6]
    result, normed_two, rstd_two = layer_norm(mid + ffn, vecs[9], vecs[10])
    grad_result = jnp.concatenate([cot_words, cot_ents], 1)
    grad_two, gain_two, shift_two = norm_back(grad_result, normed_two, rstd_two, vecs[9])
    bias_down = jnp.sum(grad_two, axis=(0, 1))
    grad_ffn_low = grad_two.astype(lowered)
    grad_down = weight_grad(act_low, grad_ffn_low)
    grad_act = project_back(grad_ffn_low, w_down)
    unused_value, gelu_pull = jax.vjp(gelu_exact, pre)
    grad_pre = gelu_pull(grad_act)[0]
    bias_up = jnp.sum(grad_pre, axis=(0, 1))
    grad_pre_low = grad_pre.astype(lowered)
    grad_up = weight_grad(mid_low, grad_pre_low)
    grad_mid = grad_two + project_back(grad_pre_low, w_up)
    grad_one, gain_one, shift_one = norm_back(grad_mid, normed_one, rstd_one, vecs[7])
    bias_out = jnp.sum(grad_one, axis=(0, 1))
    grad_branch_low = grad_one.astype(lowered)
    grad_out_proj = weight_grad(attn_low, grad_branch_low)
    grad_attn = project_back(grad_branch_low, w_attn[6]).reshape(
        batch_rows, rows_dev, head_count, head_dim
    )
    grad_unnorm = (grad_attn / total_rows).astype(lowered)
    delta_rows = jnp.transpose(jnp.sum(grad_attn * attn, -1), (0, 2, 1)) / row_total
    keys_word, keys_ent, values, offsets, blocks = split_keys(
        (
            lax.all_gather(key_rows, "seq", axis=1, tiled=True),
            lax.all_gather(key_live, "seq", axis=1, tiled=True),
        ),
        words_dev,
        ents_dev,
        head_count,
    )
    scores = score_block(heads_word, heads_ent, keys_word, keys_ent, offsets)
    weights = jnp.exp(scores - row_top[..., None])
    grad_weights = jnp.einsum(
        "sqhd,skhd->shqk", grad_unnorm, values, preferred_element_type=jnp.float32
    )
    grad_scores = (weights * (grad_weights - delta_rows[..., None])).astype(lowered)
    word_count = keys_word.shape[1]
    scores_word = grad_scores[..., :word_count]
    scores_ent = grad_scores[..., word_count:]
    grad_query_word = jnp.einsum(
        "shqk,skhd->sqhd", scores_word, keys_word, preferred_element_type=jnp.float32
    )
    grad_query_ent = jnp.einsum(
        "shqk,skhd->sqhd", scores_ent, keys_ent, preferred_element_type=jnp.float32
    )
    grad_keys_word = jnp.einsum(
        "shqk,sqhd->skhd", scores_word, heads_word, preferred_element_type=jnp.float32
    )
    grad_keys_ent = jnp.einsum(
        "shqk,sqhd->skhd", scores_ent, heads_ent, preferred_element_type=jnp.float32
    )
    grad_values = jnp.einsum(
        "shqk,sqhd->skhd", weights.astype(lowered), grad_unnorm, preferred_element_type=jnp.float32
    )
    piece_grad = join_rows(grad_keys_word, grad_keys_ent, grad_values, blocks, words_dev, ents_dev)
    grad_rows = piece_grad
    grad_query_word, grad_query_ent, grad_rows = (grad_query_word, grad_query_ent, grad_rows)
    own_rows = lax.psum_scatter(
        grad_rows.astype(jnp.bfloat16), "seq", scatter_dimension=1, tiled=True
    ).astype(jnp.float32)
    grad_keys = own_rows[..., :model_width]
    grad_values = own_rows[..., model_width:]
    bias_values = jnp.sum(grad_values, axis=(0, 1))
    keys_grad_low = grad_keys.astype(lowered)
    values_grad_low = grad_values.astype(lowered)
    grad_key_w = weight_grad(inputs_low, keys_grad_low)
    grad_value_w = weight_grad(inputs_low, values_grad_low)
    inner_word = grad_query_word.reshape(batch_rows, rows_dev, model_width) * 0.125
    inner_ent = grad_query_ent.reshape(batch_rows, rows_dev, model_width) * 0.125
    bias_query = [
        jnp.sum(inner_word[:, :words_dev], axis=(0, 1)),
        jnp.sum(inner_ent[:, :words_dev], axis=(0, 1)),
        jnp.sum(inner_word[:, words_dev:], axis=(0, 1)),
        jnp.sum(inner_ent[:, words_dev:], axis=(0, 1)),
    ]
    inner_word_low = inner_word.astype(lowered)
    inner_ent_low = inner_ent.astype(lowered)
    grad_query_mats = [
        weight_grad(word_low, inner_word_low[:, :words_dev]),
        weight_grad(word_low, inner_ent_low[:, :words_dev]),
        weight_grad(ent_low, inner_word_low[:, words_dev:]),
        weight_grad(ent_low, inner_ent_low[:, words_dev:]),
    ]
    back_keys = project_back(keys_grad_low, w_attn[4]) + project_back(values_grad_low, w_attn[5])
    back_word = project_back(inner_word_low[:, :words_dev], w_attn[0]) + project_back(
        inner_ent_low[:, :words_dev], w_attn[1]
    )
    back_ent = project_back(inner_word_low[:, words_dev:], w_attn[2]) + project_back(
        inner_ent_low[:, words_dev:], w_attn[3]
    )
    grad_inputs = grad_one + back_keys + jnp.concatenate([back_word, back_ent], 1)
    grad_attn_w = jnp.stack(grad_query_mats + [grad_key_w, grad_value_w, grad_out_proj])
    vec_grad = jnp.concatenate(
        [
            jnp.stack(
                bias_query
                + [bias_values, bias_out, bias_down, gain_one, shift_one, gain_two, shift_two]
            ),
            bias_up.reshape(4, model_width),
        ],
        0,
    )
    rows_attn, rows_up, rows_down = (
        lax.psum_scatter(
            grad_attn_w.astype(jnp.bfloat16), "seq", scatter_dimension=1, tiled=True
        ).astype(jnp.float32),
        lax.psum_scatter(
            grad_up.astype(jnp.bfloat16), "seq", scatter_dimension=0, tiled=True
        ).astype(jnp.float32),
        lax.psum_scatter(
            grad_down.astype(jnp.bfloat16), "seq", scatter_dimension=0, tiled=True
        ).astype(jnp.float32),
    )
    attention_full_gradient = rows_attn + err_attn[0]
    full_up = rows_up + err_up[0]
    full_down = rows_down + err_down[0]
    attention_left_factor = jnp.einsum(
        "vcg,vgo->vco", attention_full_gradient, attention_prior_right, precision=HIGH_PRECISION
    )
    left_up = jnp.dot(full_up, qf_up, precision=HIGH_PRECISION)
    left_down = jnp.dot(full_down, qf_down, precision=HIGH_PRECISION)
    count_attn = attention_full_gradient.shape[1]
    count_up = full_up.shape[0]
    count_down = full_down.shape[0]
    placed_attn = lax.dynamic_update_slice_in_dim(
        jnp.zeros((7, count_attn * seq_count, attention_left_factor.shape[2]), jnp.float32),
        attention_left_factor,
        seq_index * count_attn,
        1,
    )
    placed_up = lax.dynamic_update_slice_in_dim(
        jnp.zeros((count_up * seq_count, left_up.shape[1]), jnp.float32),
        left_up,
        seq_index * count_up,
        0,
    )
    placed_down = lax.dynamic_update_slice_in_dim(
        jnp.zeros((count_down * seq_count, left_down.shape[1]), jnp.float32),
        left_down,
        seq_index * count_down,
        0,
    )
    summed_attn, summed_up, summed_down = lax.psum(
        (placed_attn, placed_up, placed_down), ("seq", "rep")
    )
    orth_attn = jax.vmap(orthonormal)(summed_attn / rep_count)
    orth_up = orthonormal(summed_up / rep_count)
    orth_down = orthonormal(summed_down / rep_count)
    attention_local_gradient = lax.dynamic_slice_in_dim(
        orth_attn, seq_index * count_attn, count_attn, 1
    )
    own_up = lax.dynamic_slice_in_dim(orth_up, seq_index * count_up, count_up, 0)
    own_down = lax.dynamic_slice_in_dim(orth_down, seq_index * count_down, count_down, 0)
    right_parts = (
        jnp.einsum(
            "dpl,dpg->dgl",
            attention_local_gradient,
            attention_full_gradient,
            precision=HIGH_PRECISION,
        ),
        jnp.dot(full_up.T, own_up, precision=HIGH_PRECISION),
        jnp.dot(full_down.T, own_down, precision=HIGH_PRECISION),
        vec_grad,
    )
    attention_right_factor, right_up, right_down, vec_total = lax.psum(
        (right_parts[0], right_parts[1], right_parts[2], right_parts[3]), ("seq", "rep")
    )
    attention_right_factor = attention_right_factor / rep_count
    right_up = right_up / rep_count
    right_down = right_down / rep_count
    vec_mean = vec_total / rep_count
    attention_estimate = jnp.einsum(
        "whg,wng->whn", attention_local_gradient, attention_right_factor, precision=HIGH_PRECISION
    )
    approx_up = jnp.dot(own_up, right_up.T, precision=HIGH_PRECISION)
    approx_down = jnp.dot(own_down, right_down.T, precision=HIGH_PRECISION)
    next_err_attn = (attention_full_gradient - attention_estimate)[None]
    next_err_up = (full_up - approx_up)[None]
    next_err_down = (full_down - approx_down)[None]
    cols_attn = attn_w.shape[2]
    cols_up = up_w.shape[1]
    cols_down = down_w.shape[1]
    step_attn = lax.dynamic_slice_in_dim(attention_estimate, rep_index * cols_attn, cols_attn, 2)
    step_up = lax.dynamic_slice_in_dim(approx_up, rep_index * cols_up, cols_up, 1)
    step_down = lax.dynamic_slice_in_dim(approx_down, rep_index * cols_down, cols_down, 1)
    lr_mat = 1.5 * math.sqrt(rep_count / (SEQS * (WORDS + ENTS)))
    lr_vec = 0.2 * math.sqrt(rep_count / (SEQS * (WORDS + ENTS)))
    next_mom_attn = MOMENTUM * mom_attn + step_attn
    next_mom_up = MOMENTUM * mom_up + step_up
    next_mom_down = MOMENTUM * mom_down + step_down
    next_mom_vecs = MOMENTUM * mom_vecs + vec_mean
    new_attn = attn_w - lr_mat * next_mom_attn
    new_up = up_w - lr_mat * next_mom_up
    new_down = down_w - lr_mat * next_mom_down
    new_vecs = vecs - lr_vec * next_mom_vecs
    return (
        result[:, :words_dev],
        result[:, words_dev:],
        grad_inputs[:, :words_dev],
        grad_inputs[:, words_dev:],
        new_attn,
        new_up,
        new_down,
        new_vecs,
        next_mom_attn,
        next_mom_up,
        next_mom_down,
        next_mom_vecs,
        next_err_attn,
        next_err_up,
        next_err_down,
        attention_local_gradient,
        own_up,
        own_down,
        attention_right_factor,
        right_up,
        right_down,
    )


def seq_swap(array, bits):
    size = lax.axis_size("seq")
    return lax.ppermute(array, "seq", [(i, i ^ bits) for i in range(size)])


def rep_swap(array, bits):
    size = lax.axis_size("rep")
    return lax.ppermute(array, "rep", [(i, i ^ bits) for i in range(size)])


def planes_swap(array):
    seqs, reps = lax.axis_size("seq"), lax.axis_size("rep")
    pairs = []
    for s in range(seqs):
        for r in range(reps):
            pairs.append((s * reps + r, (r // 2) * reps + 2 * s + r % 2))
    return lax.ppermute(array, ("seq", "rep"), pairs)


def gather_seq(piece):
    other_chip = seq_swap(piece, 2)
    return [seq_swap(piece, 1), seq_swap(other_chip, 1), piece, other_chip]


def gather_direct(piece):
    pieces = [piece] + [rep_swap(piece, 2 * change) for change in (1, 2, 3)]
    return pieces, rep_swap(piece, 1)


def gather_tree(piece):
    own_side = rep_swap(piece, 1)
    far, own_side = lax.optimization_barrier((rep_swap(piece, 4), own_side))
    near = rep_swap(jnp.stack([piece, far]), 2)
    near, far_side = lax.optimization_barrier((near, rep_swap(far, 1)))
    near_side = rep_swap(near, 1)
    return [piece, own_side, far, far_side, near, near_side]


def tree_pieces(refs):
    own, own_side, far, far_side, near, near_side = refs
    return (
        (0, own[...], own_side[...]),
        (2, far[...], far_side[...]),
        (1, near[0], near_side[0]),
        (3, near[1], near_side[1]),
    )


def project_kernel(
    words_dev, rows_dev, place_ref, bias_word_ref, bias_ent_ref, scale_ref, *refs
):
    trees, row_refs = (refs[:6], refs[6:12]), refs[12:16]
    word_ref, ent_ref, packed_word_ref, packed_ent_ref, rows_ref, out_ref, piece_ref = refs[16:]
    word_count = packed_word_ref.shape[0]
    ents_dev = rows_dev - words_dev
    z, y = place_ref[0], place_ref[1]
    for half, tree in enumerate(trees):
        for change, own, other in tree_pieces(tree):
            piece_ref[half, z ^ change, y] = own
            piece_ref[half, z ^ change, 1 - y] = other
    rows, both = piece_ref.shape[3:]
    cols = both // 14
    for half in (0, 1):
        for place in range(4):
            left, right = piece_ref[half, place, 0], piece_ref[half, place, 1]
            for side, piece in ((0, left), (1, right)):
                start = (4 * place + 2 * side + half) * rows
                out_ref[start : start + rows] = piece[:, 12 * cols :]
            for upper in (0, 1):
                parts = []
                for j in range(6):
                    low = (upper * 6 + j) * cols
                    parts.append(left[:, low : low + cols])
                    parts.append(right[:, low : low + cols])
                start = (4 * place + 2 * upper + half) * rows
                target = slice(start, start + rows)
                word_ref[target] = jnp.concatenate(parts[:4] + parts[8:], 1)
                ent_ref[target] = jnp.concatenate(parts[4:], 1)

    scale = scale_ref[...]
    word, ent = word_ref[...], ent_ref[...]
    for k, row_ref in enumerate(row_refs):
        words = row_ref[:words_dev]
        at = slice(k * words_dev, (k + 1) * words_dev)
        rows_ref[at] = words
        packed_word_ref[at] = ((mm(words, word) + bias_word_ref[...]) * scale).astype(
            jnp.bfloat16
        )
        start = word_count + k * ents_dev
        rows_ref[start : start + ents_dev] = row_ref[words_dev:rows_dev]
    packed_ent_ref[...] = ((mm(rows_ref[word_count:], ent) + bias_ent_ref[...]) * scale).astype(
        jnp.bfloat16
    )


def ffn_join_kernel(place_ref, *refs):
    pieces, sides, (up_ref, down_ref) = refs[:4], refs[4:8], refs[8:]
    z, y = place_ref[0], place_ref[1]
    for side in (0, 1):

        @pl.when(y == side)
        def _():
            for change in range(4):
                for y_at, piece in ((side, pieces[change]), (1 - side, sides[change])):
                    rows, both = piece.shape
                    cols = both // 4
                    place = z ^ change
                    for upper in (0, 1):
                        start = pl.multiple_of(place * (2 * rows) + upper * rows, 16)
                        up_ref[pl.ds(start, rows), y_at * cols : (y_at + 1) * cols] = piece[
                            :, upper * cols : (upper + 1) * cols
                        ]
                    start = pl.multiple_of((2 * place + y_at) * rows, 16)
                    down_ref[pl.ds(start, rows), :] = piece[:, 2 * cols :]


def join_call(kernel, place, pieces, shapes, name):
    whole = [pl.BlockSpec(memory_space=pltpu.VMEM)] * len(pieces)
    return pl.pallas_call(
        kernel,
        in_specs=[pl.BlockSpec(memory_space=pltpu.SMEM)] + whole,
        out_specs=[pl.BlockSpec(memory_space=pltpu.VMEM)] * len(shapes),
        out_shape=[jax.ShapeDtypeStruct(shape, jnp.bfloat16) for shape in shapes],
        name=name,
    )(place, *pieces)


def tie(value, mark):
    return lax.optimization_barrier((value, mark))[0]


def scatter_blocks(rows, dot, weight):
    half = rows.shape[0] // 2
    own = half // 2
    sent = dot(rows[:half], weight).astype(jnp.bfloat16)
    kept = dot(rows[half:], weight) + seq_swap(sent, 1).astype(jnp.float32)
    return sent, kept[:own], seq_swap(kept[own:].astype(jnp.bfloat16), 2)


def rows_norm(hidden, gain, shift):
    center = hidden - jnp.mean(hidden, -1, keepdims=True)
    rstd = lax.rsqrt(jnp.mean(center * center, -1, keepdims=True) + EPS)
    normed = center * rstd
    return (normed * gain + shift, normed, rstd)


def rows_norm_back(grad, normed, rstd, gain):
    dnormed = grad * gain
    grad_in = rstd * (
        dnormed
        - jnp.mean(dnormed, -1, keepdims=True)
        - normed * jnp.mean(dnormed * normed, -1, keepdims=True)
    )
    return (grad_in, jnp.sum(grad * normed, axis=0), jnp.sum(grad, axis=0))


def mm(left, right, left_dim=1, right_dim=0):
    return lax.dot_general(
        left, right, (((left_dim,), (right_dim,)), ((), ())), preferred_element_type=jnp.float32
    )


def nt_dot(left, right):
    return mm(left, right, 1, 1)


def tn_dot(left, right):
    return mm(left, right, 0, 0)


HEAD_DIM = 64


def head_parts(word_ref, ent_ref, low, high):
    return jnp.concatenate([word_ref[:, low:high], ent_ref[:, low:high]], 0)


def attention_kernel(
    heads,
    query_word_ref,
    query_ent_ref,
    key_word_ref,
    key_ent_ref,
    offset_ref,
    attn_ref,
    low_ref,
    high_ref,
    stat_ref,
):
    width = heads * HEAD_DIM
    word_count = key_word_ref.shape[0]
    rows = attn_ref.shape[0]
    lane = lax.broadcasted_iota(jnp.int32, (rows, 128), 1)
    stats = jnp.zeros((rows, 128), jnp.float32)
    for h in range(heads):
        low, high = h * HEAD_DIM, (h + 1) * HEAD_DIM
        q_word = head_parts(query_word_ref, query_ent_ref, low, high)
        q_ent = head_parts(query_word_ref, query_ent_ref, width + low, width + high)
        k_word = key_word_ref[:, 2 * width + low : 2 * width + high]
        k_ent = key_ent_ref[:, 2 * width + low : 2 * width + high]
        s_word = nt_dot(q_word, k_word) + offset_ref[:, :word_count]
        s_ent = nt_dot(q_ent, k_ent) + offset_ref[:, word_count:]
        top = jnp.maximum(
            jnp.max(s_word, -1, keepdims=True), jnp.max(s_ent, -1, keepdims=True)
        )
        w_word = jnp.exp(s_word - top)
        w_ent = jnp.exp(s_ent - top)
        total = jnp.sum(w_word, -1, keepdims=True) + jnp.sum(w_ent, -1, keepdims=True)
        v_word = key_word_ref[:, 3 * width + low : 3 * width + high]
        v_ent = key_ent_ref[:, 3 * width + low : 3 * width + high]
        unnorm = mm(w_word.astype(jnp.bfloat16), v_word) + mm(w_ent.astype(jnp.bfloat16), v_ent)
        attn_ref[:, low:high] = unnorm / total
        stats = jnp.where(lane == h, top, stats)
        stats = jnp.where(lane == heads + h, total, stats)
    stat_ref[...] = stats
    low_ref[...] = attn_ref[: rows // 2].astype(jnp.bfloat16)
    high_ref[...] = attn_ref[rows // 2 :].astype(jnp.bfloat16)


def attention_forward(packed_word, packed_ent, offsets, heads):
    word_count, packed_width = packed_word.shape
    ent_count = packed_ent.shape[0]
    count = word_count + ent_count
    width = heads * HEAD_DIM
    block = count // 4
    return pl.pallas_call(
        functools.partial(attention_kernel, heads),
        grid=(4,),
        in_specs=[
            pl.BlockSpec((word_count // 4, packed_width), lambda i: (i, 0)),
            pl.BlockSpec((ent_count // 4, packed_width), lambda i: (i, 0)),
            pl.BlockSpec((word_count, packed_width), lambda i: (0, 0)),
            pl.BlockSpec((ent_count, packed_width), lambda i: (0, 0)),
            pl.BlockSpec((1, count), lambda i: (0, 0)),
        ],
        out_specs=[
            pl.BlockSpec((block, width), lambda i: (i, 0)),
            pl.BlockSpec((block // 2, width), lambda i: (i, 0)),
            pl.BlockSpec((block // 2, width), lambda i: (i, 0)),
            pl.BlockSpec((block, 128), lambda i: (i, 0)),
        ],
        out_shape=[
            jax.ShapeDtypeStruct((count, width), jnp.float32),
            jax.ShapeDtypeStruct((count // 2, width), jnp.bfloat16),
            jax.ShapeDtypeStruct((count // 2, width), jnp.bfloat16),
            jax.ShapeDtypeStruct((count, 128), jnp.float32),
        ],
        compiler_params=pltpu.CompilerParams(dimension_semantics=("arbitrary",)),
        cost_estimate=pl.CostEstimate(
            flops=4 * count * count * width,
            bytes_accessed=6 * count * packed_width,
            transcendentals=count * count * heads,
        ),
        name="attention",
    )(packed_word, packed_ent, packed_word, packed_ent, offsets)


def attention_back_kernel(
    heads,
    query_word_ref,
    query_ent_ref,
    key_word_ref,
    key_ent_ref,
    offset_ref,
    attn_ref,
    stat_ref,
    grad_low_ref,
    grad_high_ref,
    d_query_ref,
    d_key_ref,
    sum_ref,
    key_sum,
    value_sum,
):
    width = heads * HEAD_DIM
    word_count = key_word_ref.shape[0]
    words_dev, ents_dev = query_word_ref.shape[0], query_ent_ref.shape[0]
    step = pl.program_id(0)

    @pl.when(step == 0)
    def _():
        key_sum[...] = jnp.zeros_like(key_sum)
        value_sum[...] = jnp.zeros_like(value_sum)
        sum_ref[...] = jnp.zeros_like(sum_ref)

    word_rows = pl.ds(pl.multiple_of(step * words_dev, words_dev), words_dev)
    ent_rows = pl.ds(pl.multiple_of(word_count + step * ents_dev, ents_dev), ents_dev)
    for h in range(heads):
        low, high = h * HEAD_DIM, (h + 1) * HEAD_DIM
        q_word = head_parts(query_word_ref, query_ent_ref, low, high)
        q_ent = head_parts(query_word_ref, query_ent_ref, width + low, width + high)
        k_word = key_word_ref[:, 2 * width + low : 2 * width + high]
        k_ent = key_ent_ref[:, 2 * width + low : 2 * width + high]
        v_word = key_word_ref[:, 3 * width + low : 3 * width + high]
        v_ent = key_ent_ref[:, 3 * width + low : 3 * width + high]
        top = stat_ref[:, h : h + 1]
        inverse = 1.0 / stat_ref[:, heads + h : heads + h + 1]
        grad = head_parts(grad_low_ref, grad_high_ref, low, high)
        delta = jnp.sum(grad * attn_ref[:, low:high], -1, keepdims=True) * inverse
        grad_low = (grad * inverse).astype(jnp.bfloat16)
        w_word = jnp.exp(nt_dot(q_word, k_word) + offset_ref[:, :word_count] - top)
        w_ent = jnp.exp(nt_dot(q_ent, k_ent) + offset_ref[:, word_count:] - top)
        d_word = (w_word * (nt_dot(grad_low, v_word) - delta)).astype(jnp.bfloat16)
        d_ent = (w_ent * (nt_dot(grad_low, v_ent) - delta)).astype(jnp.bfloat16)
        for at, dquery in ((low, mm(d_word, k_word)), (width + low, mm(d_ent, k_ent))):
            dquery = dquery * 0.125
            lanes = slice(at, at + HEAD_DIM)
            d_query_ref[word_rows, lanes] = dquery[:words_dev].astype(jnp.bfloat16)
            d_query_ref[ent_rows, lanes] = dquery[words_dev:].astype(jnp.bfloat16)
            sum_ref[0:1, lanes] += jnp.sum(dquery[:words_dev], 0, keepdims=True)
            sum_ref[1:2, lanes] += jnp.sum(dquery[words_dev:], 0, keepdims=True)
        key_sum[low:high, :word_count] += tn_dot(q_word, d_word)
        key_sum[low:high, word_count:] += tn_dot(q_ent, d_ent)
        value_sum[low:high, :word_count] += tn_dot(grad_low, w_word.astype(jnp.bfloat16))
        value_sum[low:high, word_count:] += tn_dot(grad_low, w_ent.astype(jnp.bfloat16))

    @pl.when(step == pl.num_programs(0) - 1)
    def _():
        dkey = key_sum[...].T
        dvalue = value_sum[...].T
        sum_ref[2:3, :width] = jnp.sum(dvalue, 0, keepdims=True)
        d_key_ref[...] = jnp.concatenate([dkey, dvalue], 1).astype(jnp.bfloat16)


def attention_backward(packed_word, packed_ent, offsets, attn, stats, grads, heads):
    word_count, packed_width = packed_word.shape
    ent_count = packed_ent.shape[0]
    count = word_count + ent_count
    width = heads * HEAD_DIM
    block = count // 4
    return pl.pallas_call(
        functools.partial(attention_back_kernel, heads),
        grid=(4,),
        in_specs=[
            pl.BlockSpec((word_count // 4, packed_width), lambda i: (i, 0)),
            pl.BlockSpec((ent_count // 4, packed_width), lambda i: (i, 0)),
            pl.BlockSpec((word_count, packed_width), lambda i: (0, 0)),
            pl.BlockSpec((ent_count, packed_width), lambda i: (0, 0)),
            pl.BlockSpec((1, count), lambda i: (0, 0)),
            pl.BlockSpec((block, width), lambda i: (i, 0)),
            pl.BlockSpec((block, 128), lambda i: (i, 0)),
            pl.BlockSpec((block // 2, width), lambda i: (i, 0)),
            pl.BlockSpec((block // 2, width), lambda i: (i, 0)),
        ],
        out_specs=[
            pl.BlockSpec((count, 2 * width), lambda i: (0, 0)),
            pl.BlockSpec((count, 2 * width), lambda i: (0, 0)),
            pl.BlockSpec((8, 2 * width), lambda i: (0, 0)),
        ],
        out_shape=[
            jax.ShapeDtypeStruct((count, 2 * width), jnp.bfloat16),
            jax.ShapeDtypeStruct((count, 2 * width), jnp.bfloat16),
            jax.ShapeDtypeStruct((8, 2 * width), jnp.float32),
        ],
        scratch_shapes=[
            pltpu.VMEM((width, count), jnp.float32),
            pltpu.VMEM((width, count), jnp.float32),
        ],
        compiler_params=pltpu.CompilerParams(dimension_semantics=("arbitrary",)),
        cost_estimate=pl.CostEstimate(
            flops=10 * count * count * width,
            bytes_accessed=16 * count * packed_width,
            transcendentals=count * count * heads,
        ),
        name="attention_back",
    )(packed_word, packed_ent, packed_word, packed_ent, offsets, attn, stats, *grads)


def project_grad_kernel(word_count, rows_ref, query_ref, key_ref, grad_ref):
    width = query_ref.shape[1]
    words, ents = rows_ref[:word_count], rows_ref[word_count:]
    for at, value in (
        (0, tn_dot(words, query_ref[:word_count])),
        (width, tn_dot(ents, query_ref[word_count:])),
        (2 * width, tn_dot(words, key_ref[:word_count]) + tn_dot(ents, key_ref[word_count:])),
    ):
        grad_ref[:, at : at + width] = value.astype(jnp.bfloat16)


def project_grad(rows, d_query, d_key, word_count):
    count, model_width = rows.shape
    width = d_query.shape[1]
    lanes = model_width // 3
    return pl.pallas_call(
        functools.partial(project_grad_kernel, word_count),
        grid=(3,),
        in_specs=[
            pl.BlockSpec((count, lanes), lambda i: (0, i)),
            pl.BlockSpec((count, width), lambda i: (0, 0)),
            pl.BlockSpec((count, width), lambda i: (0, 0)),
        ],
        out_specs=pl.BlockSpec((lanes, 3 * width), lambda i: (i, 0)),
        out_shape=jax.ShapeDtypeStruct((model_width, 3 * width), jnp.bfloat16),
        name="project_grad",
    )(rows, d_query, d_key)


def input_grad_kernel(
    query_word_ref, query_ent_ref, key_word_ref, key_ent_ref, word_ref, ent_ref, sent_ref, kept_ref
):
    step = pl.program_id(0)
    width = query_word_ref.shape[1]

    def rows(query_ref, key_ref, weight_ref):
        return nt_dot(query_ref[...], weight_ref[:, :width]) + nt_dot(
            key_ref[...], weight_ref[:, width:]
        )

    words = rows(query_word_ref, key_word_ref, word_ref)
    ents = rows(query_ent_ref, key_ent_ref, ent_ref)
    words_dev = words.shape[0]

    @pl.when(step < 2)
    def _():
        sent_ref[:words_dev] = words.astype(jnp.bfloat16)
        sent_ref[words_dev:] = ents.astype(jnp.bfloat16)

    @pl.when(step >= 2)
    def _():
        kept_ref[:words_dev] = words
        kept_ref[words_dev:] = ents


def input_grad(d_query, d_key, w_word, w_ent, word_count):
    count, width = d_query.shape
    model_width = w_word.shape[0]
    words_dev, ents_dev = word_count // 4, (count - word_count) // 4
    block = words_dev + ents_dev
    first_ent = word_count // ents_dev
    word_spec = pl.BlockSpec((words_dev, width), lambda i: (i, 0))
    ent_spec = pl.BlockSpec((ents_dev, width), lambda i: (first_ent + i, 0))
    weight_spec = pl.BlockSpec(w_word.shape, lambda i: (0, 0))
    return pl.pallas_call(
        input_grad_kernel,
        grid=(4,),
        in_specs=[word_spec, ent_spec, word_spec, ent_spec, weight_spec, weight_spec],
        out_specs=[
            pl.BlockSpec((block, model_width), lambda i: (jnp.minimum(i, 1), 0)),
            pl.BlockSpec((block, model_width), lambda i: (jnp.maximum(i - 2, 0), 0)),
        ],
        out_shape=[
            jax.ShapeDtypeStruct((2 * block, model_width), jnp.bfloat16),
            jax.ShapeDtypeStruct((2 * block, model_width), jnp.float32),
        ],
        name="input_grad",
    )(d_query, d_query, d_key, d_key, w_word, w_ent)


def tall(left):
    return jnp.swapaxes(left, -1, -2)


def halves(array):
    high = array.astype(jnp.bfloat16)
    return high, (array - high.astype(jnp.float32)).astype(jnp.bfloat16)


def stacked_halves(array):
    high = array.astype(jnp.bfloat16).astype(jnp.float32)
    return jnp.concatenate([array, array - high], 0).astype(jnp.bfloat16)


def columns_of(rank_rows):
    return jnp.concatenate(
        [rank_rows, rank_rows - rank_rows.astype(jnp.bfloat16).astype(jnp.float32)], 0
    ).T.astype(jnp.bfloat16)


def left_part(full, columns):
    high, low = halves(full)
    return mm(high, columns) + mm(low, columns)


def rank_first(part):
    both = part.T
    rank = both.shape[0] // 2
    return both[:rank] + both[rank:]


def left_ffn_kernel(
    got_ref, down_ref, err_up_ref, err_down_ref, q_up_ref, q_down_ref, full_up_ref, full_down_ref, left_ref
):
    step = pl.program_id(0)
    width = got_ref.shape[2]
    rows = got_ref.shape[1]
    left = 0.0
    for s in range(4):
        lanes = slice(s * width, (s + 1) * width)
        full = got_ref[s].astype(jnp.float32) + err_up_ref[0, :, lanes]
        full_up_ref[:, lanes] = full
        left = left + left_part(full, columns_of(q_up_ref[:, lanes]))
    left = rank_first(left)
    full = down_ref[...] + err_down_ref[0]
    full_down_ref[...] = full
    below = rank_first(left_part(full, columns_of(q_down_ref[...])))
    for side in (0, 1):

        @pl.when(step == side)
        def _():
            left_ref[0, :, side * rows : (side + 1) * rows] = left
            left_ref[1 + 2 * side] = below[:, : 2 * rows]
            left_ref[2 + 2 * side] = below[:, 2 * rows :]


def left_of_ffn(got_up, grad_down, err_up, err_down, q_up, q_down):
    rows, width = got_up.shape[1:]
    rank = q_up.shape[0]
    return pl.pallas_call(
        left_ffn_kernel,
        grid=(2,),
        in_specs=[
            pl.BlockSpec((4, rows // 2, width), lambda i: (0, i, 0)),
            pl.BlockSpec((2 * rows, width), lambda i: (i, 0)),
            pl.BlockSpec((1, rows // 2, 4 * width), lambda i: (0, i, 0)),
            pl.BlockSpec((1, 2 * rows, width), lambda i: (0, i, 0)),
            pl.BlockSpec((rank, 4 * width), lambda i: (0, 0)),
            pl.BlockSpec((rank, width), lambda i: (0, 0)),
        ],
        out_specs=[
            pl.BlockSpec((rows // 2, 4 * width), lambda i: (i, 0)),
            pl.BlockSpec((2 * rows, width), lambda i: (i, 0)),
            pl.BlockSpec((5, rank, rows), lambda i: (0, 0, 0)),
        ],
        out_shape=[
            jax.ShapeDtypeStruct((rows, 4 * width), jnp.float32),
            jax.ShapeDtypeStruct((4 * rows, width), jnp.float32),
            jax.ShapeDtypeStruct((5, rank, rows), jnp.float32),
        ],
        name="left_ffn",
    )(got_up, grad_down, err_up, err_down, q_up, q_down)


def left_attn_kernel(got_ref, out_ref, err_ref, q_ref, ffn_ref, full_ref, left_ref):
    step = pl.program_id(0)
    rows = full_ref.shape[1]
    part = 2 * rows
    lefts = []
    for j in range(7):
        if j < 6:
            lanes = slice(j * part, (j + 1) * part)
            grad = jnp.concatenate([got_ref[s, :, lanes] for s in range(4)], 1)
            full = grad.astype(jnp.float32) + err_ref[0, j]
        else:
            full = out_ref[...] + err_ref[0, j]
        full_ref[j] = full
        lefts.append(rank_first(left_part(full, columns_of(q_ref[j]))))
    for side in (0, 1):

        @pl.when(step == side)
        def _():
            for j in range(7):
                left_ref[j, :, side * rows : (side + 1) * rows] = lefts[j]

    @pl.when(step == 1)
    def _():
        left_ref[7:] = ffn_ref[...]


def left_of_attn(got, grad_out, err_attn, q_attn, left_ffn):
    rows, width = grad_out.shape
    rank = q_attn.shape[1]
    return pl.pallas_call(
        left_attn_kernel,
        grid=(2,),
        in_specs=[
            pl.BlockSpec((4, rows // 2, got.shape[2]), lambda i: (0, i, 0)),
            pl.BlockSpec((rows // 2, width), lambda i: (i, 0)),
            pl.BlockSpec((1, 7, rows // 2, width), lambda i: (0, 0, i, 0)),
            pl.BlockSpec((7, rank, width), lambda i: (0, 0, 0)),
            pl.BlockSpec((5, rank, rows), lambda i: (0, 0, 0)),
        ],
        out_specs=[
            pl.BlockSpec((7, rows // 2, width), lambda i: (0, i, 0)),
            pl.BlockSpec((12, rank, rows), lambda i: (0, 0, 0)),
        ],
        out_shape=[
            jax.ShapeDtypeStruct((7, rows, width), jnp.float32),
            jax.ShapeDtypeStruct((12, rank, rows), jnp.float32),
        ],
        name="left_attn",
    )(got, grad_out, err_attn, q_attn, left_ffn)


MATRIX_BLOCKS = [[j] for j in range(8)] + [[8, 9, 10, 11]]


def gram_kernel(scale, mine_ref, other_ref, left_ref, gram_ref):
    rank = mine_ref.shape[1]
    left = (mine_ref[...] + other_ref[...]) * scale
    left_ref[...] = left
    lane = lax.broadcasted_iota(jnp.int32, (rank, 128), 1)
    row = lax.broadcasted_iota(jnp.int32, (rank, 128), 0)
    for r in range(rank):
        gram = jnp.where((lane >= len(MATRIX_BLOCKS)) & (row == r), 1.0, 0.0)
        for m, blocks in enumerate(MATRIX_BLOCKS):
            product = sum(left[b] * left[b, r : r + 1] for b in blocks)
            gram = jnp.where(lane == m, jnp.sum(product, -1, keepdims=True), gram)
        gram_ref[r] = gram


def gram_of(mine, other, scale):
    rank = mine.shape[1]
    return pl.pallas_call(
        functools.partial(gram_kernel, scale),
        out_shape=[
            jax.ShapeDtypeStruct(mine.shape, jnp.float32),
            jax.ShapeDtypeStruct((rank, rank, 128), jnp.float32),
        ],
        name="gram",
    )(mine, other)


def inverse_factor(columns, rank):
    row = lax.broadcasted_iota(jnp.int32, columns[0].shape, 0)
    columns, lower = list(columns), []
    for k in range(rank):
        column = columns[k] / jnp.sqrt(columns[k][k : k + 1])
        lower.append(column)
        for c in range(k + 1, rank):
            columns[c] = columns[c] - column * column[c : c + 1]
    inverse = []
    for r in range(rank):
        value = jnp.where(row == r, 1.0, 0.0)
        for t in range(r):
            value = value - lower[t][r : r + 1] * inverse[t]
        inverse.append(value / lower[r][r : r + 1])
    return inverse


def right_part(both_ref, blocks, fulls):
    out = 0.0
    for b, full in zip(blocks, fulls):
        high, low = halves(full)
        out = out + mm(both_ref[b], high) + mm(both_ref[b], low)
    rank = out.shape[0] // 2
    return out[:rank] + out[rank:]


def right_kernel(place_ref, gram_ref, other_ref, left_ref, attn_ref, *refs):
    up_refs, (down_ref, vec_ref, orth_ref) = refs[:4], refs[4:7]
    p_attn_ref, p_up_ref, p_down_ref, sent_ref, kept_ref, both_ref = refs[7:]
    step = pl.program_id(0)
    rank, rows = left_ref.shape[1:]
    chip = place_ref[2]

    @pl.when(step == 0)
    def _():
        inverse = inverse_factor([gram_ref[r] + other_ref[r] for r in range(rank)], rank)
        row = lax.broadcasted_iota(jnp.int32, (rank, rows), 0)
        for m, blocks in enumerate(MATRIX_BLOCKS):
            weights = [inverse[r][:, m : m + 1] for r in range(rank)]
            for b in blocks:
                left = left_ref[b]
                orth = jnp.zeros((rank, rows), jnp.float32)
                for r in range(rank):
                    total = jnp.sum(left * weights[r], 0, keepdims=True)
                    orth = jnp.where(row == r, total, orth)
                orth_ref[b] = orth
                both_ref[b] = stacked_halves(orth)
                if b < 7:
                    p_attn_ref[b] = orth
                elif b == 7:
                    p_up_ref[...] = orth
                else:
                    p_down_ref[:, (b - 8) * rows : (b - 7) * rows] = orth

    parts = [right_part(both_ref, [j], [attn_ref[j]]) for j in range(7)]
    parts += [right_part(both_ref, [7], [up_refs[k][...]]) for k in range(4)]
    parts.append(
        right_part(
            both_ref, [8, 9, 10, 11], [down_ref[k * rows : (k + 1) * rows] for k in range(4)]
        )
    )
    parts += [vec_ref[0], vec_ref[1]]
    for at, ref in enumerate((sent_ref, kept_ref)):

        @pl.when(step == at)
        def _():
            for b, part in enumerate(parts):
                ref[(b // 7) ^ chip, b % 7] = part


def right_of(place, gram, other, left, full_attn, full_up, full_down, vecs):
    rank, rows = left.shape[1:]
    width = full_attn.shape[2]
    lanes = width // 2

    def whole(shape):
        return pl.BlockSpec(shape, lambda i, place: (0,) * len(shape))

    def half(i, place):
        return 1 - place[3] + i * (2 * place[3] - 1)

    def up_spec(k):
        return pl.BlockSpec((rows, lanes), lambda i, place: (0, 2 * k + half(i, place)))

    out_shapes = [
        left.shape,
        (7, rank, rows),
        (rank, rows),
        (rank, 4 * rows),
        (2, 7, rank, lanes),
        (2, 7, rank, lanes),
    ]
    return pl.pallas_call(
        right_kernel,
        grid_spec=pltpu.PrefetchScalarGridSpec(
            num_scalar_prefetch=1,
            grid=(2,),
            in_specs=[
                whole(gram.shape),
                whole(other.shape),
                whole(left.shape),
                pl.BlockSpec((7, rows, lanes), lambda i, place: (0, 0, half(i, place))),
                up_spec(0),
                up_spec(1),
                up_spec(2),
                up_spec(3),
                pl.BlockSpec((4 * rows, lanes), lambda i, place: (0, half(i, place))),
                pl.BlockSpec((2, rank, lanes), lambda i, place: (0, 0, half(i, place))),
            ],
            out_specs=[whole(shape) for shape in out_shapes],
            scratch_shapes=[pltpu.VMEM((12, 2 * rank, rows), jnp.bfloat16)],
        ),
        out_shape=[jax.ShapeDtypeStruct(shape, jnp.float32) for shape in out_shapes],
        name="right",
    )(place, gram, other, left, full_attn, full_up, full_up, full_up, full_up, full_down, vecs)


def left_stack(orth):
    high = orth.astype(jnp.bfloat16).astype(jnp.float32)
    return jnp.concatenate([orth, orth, orth - high, jnp.zeros_like(orth)], 0)


def right_stack(right):
    high = right.astype(jnp.bfloat16).astype(jnp.float32)
    return jnp.concatenate([right, right - high, right, jnp.zeros_like(right)], 0).astype(
        jnp.bfloat16
    )


def update_kernel(rate, rate_vecs, place_ref, orth_ref, mine_ref, other_ref, *refs):
    full_refs, mom_refs, weight_refs = refs[:3], refs[3:7], refs[7:11]
    err_refs, next_refs, new_refs = refs[11:14], refs[14:18], refs[18:22]
    q_attn_ref, q_up_ref, q_down_ref, right_ref, tall_ref, right_rows, cols_rows = refs[22:]
    step = pl.program_id(0)
    rows = full_refs[1].shape[0]
    rank, width = right_ref.shape[1:]
    part = orth_ref.shape[2]
    cols = mom_refs[0].shape[2]
    cols_up = mom_refs[1].shape[1]

    def move(change, at, i, rate=rate):
        value = MOMENTUM * mom_refs[i][at] + change
        next_refs[i][at] = value
        new_refs[i][at] = weight_refs[i][at] - rate * value

    @pl.when(step == 0)
    def _():
        lanes = width // 2
        chip, core = place_ref[2], place_ref[3]
        for own in (0, 1):

            @pl.when(core == own)
            def _():
                for half in (0, 1):
                    blocks = pl.ds((chip ^ half) * 7, 7)
                    right_ref[blocks, :, own * lanes : (own + 1) * lanes] = mine_ref[half]
                    right_ref[blocks, :, (1 - own) * lanes : (2 - own) * lanes] = other_ref[half]

        replica = 2 * place_ref[0] + place_ref[1]
        shift = width - replica * cols
        for b in range(12):
            tall_ref[b] = left_stack(orth_ref[b]).T.astype(jnp.bfloat16)
            right = right_ref[b]
            right_rows[b] = right_stack(right)
            if b < 7 or b == 11:
                own = pltpu.roll(right, shift, 1)[:, :cols]
                cols_rows[min(b, 7)] = right_stack(own)
            if b < 7:
                q_attn_ref[b] = right
            elif b < 11:
                q_up_ref[:, (b - 7) * width : (b - 6) * width] = right
            else:
                q_down_ref[...] = right
        move(right_ref[12], slice(0, rank), 3, rate_vecs)
        move(right_ref[13, : rank - 1], slice(rank, 2 * rank - 1), 3, rate_vecs)

    own = pl.ds(pl.multiple_of(step * rows, 16), rows)
    for j in range(7):
        left = tall_ref[j, own]
        err_refs[0][0, j] = full_refs[0][j] - mm(left, right_rows[j])
        move(mm(left, cols_rows[j]), j, 0)
    left = tall_ref[7, own]
    for k in range(4):
        lanes = slice(k * width, (k + 1) * width)
        err_refs[1][0, :, lanes] = full_refs[1][:, lanes] - mm(left, right_rows[7 + k])
    block = right_rows[7 + place_ref[0]]
    low = mm(left, block[:, :cols_up])
    high = mm(left, block[:, cols_up:])
    side = place_ref[1].astype(jnp.float32)
    move(jnp.where(jnp.full(low.shape, side) == 0.0, low, high), ..., 1)
    err_refs[2][0] = full_refs[2][...] - mm(tall_ref[8 + step], right_rows[11])

    @pl.when(step == 3)
    def _():
        for k in range(4):
            change = tn_dot(cols_rows[7], left_stack(orth_ref[8 + k]).astype(jnp.bfloat16))
            move(change, (slice(None), slice(k * part, (k + 1) * part)), 2)


def updates(place, orth, mine, other, full, mom, weight, rate, rate_vecs):
    rank, part = orth.shape[1:]
    width = full[2].shape[1]
    cols, cols_up = mom[0].shape[2], mom[1].shape[1]
    rows = part // 4

    def whole(array):
        return pl.BlockSpec(array.shape, lambda i: (0,) * array.ndim)

    full_specs = [
        pl.BlockSpec((7, rows, width), lambda i: (0, i, 0)),
        pl.BlockSpec((rows, 4 * width), lambda i: (i, 0)),
        pl.BlockSpec((part, width), lambda i: (i, 0)),
    ]
    own_specs = [
        pl.BlockSpec((7, rows, cols), lambda i: (0, i, 0)),
        pl.BlockSpec((rows, cols_up), lambda i: (i, 0)),
        whole(mom[2]),
        whole(mom[3]),
    ]
    err_specs = [
        pl.BlockSpec((1, 7, rows, width), lambda i: (0, 0, i, 0)),
        pl.BlockSpec((1, rows, 4 * width), lambda i: (0, i, 0)),
        pl.BlockSpec((1, part, width), lambda i: (0, i, 0)),
    ]
    err_shapes = [jax.ShapeDtypeStruct((1,) + array.shape, jnp.float32) for array in full]
    own_shapes = [jax.ShapeDtypeStruct(array.shape, jnp.float32) for array in mom]
    q_shapes = [
        jax.ShapeDtypeStruct(shape, jnp.float32)
        for shape in ((7, rank, width), (rank, 4 * width), (rank, width))
    ]
    outs = pl.pallas_call(
        functools.partial(update_kernel, rate, rate_vecs),
        grid=(4,),
        in_specs=[pl.BlockSpec(memory_space=pltpu.SMEM), whole(orth), whole(mine), whole(other)]
        + full_specs
        + own_specs
        + own_specs,
        out_specs=err_specs + own_specs + own_specs + [whole(shape) for shape in q_shapes],
        out_shape=err_shapes + own_shapes + own_shapes + q_shapes,
        scratch_shapes=[
            pltpu.VMEM((14, rank, width), jnp.float32),
            pltpu.VMEM((12, part, 32), jnp.bfloat16),
            pltpu.VMEM((12, 32, width), jnp.bfloat16),
            pltpu.VMEM((8, 32, cols), jnp.bfloat16),
        ],
        name="updates",
    )(place, orth, mine, other, *full, *mom, *weight)
    return outs[:3], outs[3:7], outs[7:11], outs[11:]


def head_split_device(
    x_words,
    x_ents,
    spans,
    word_mask,
    ent_mask,
    cot_words,
    cot_ents,
    attn_w,
    up_w,
    down_w,
    vecs,
    mom_attn,
    mom_up,
    mom_down,
    mom_vecs,
    err_attn,
    err_up,
    err_down,
    attention_prior_right,
    qf_up,
    qf_down,
):
    low_type = jnp.bfloat16
    words_dev, width = x_words.shape[1:]
    ents_dev = x_ents.shape[1]
    rows_dev = words_dev + ents_dev
    seq_count, rep_count = lax.axis_size("seq"), lax.axis_size("rep")
    seq_index, rep_index = lax.axis_index("seq"), lax.axis_index("rep")
    heads = HEADS // seq_count
    part = width // seq_count
    word_count = words_dev * seq_count
    ent_count = ents_dev * seq_count
    cols = attn_w.shape[2]
    cols_up = up_w.shape[1]
    hidden = cols_up * rep_count
    hidden_part = hidden // seq_count

    core, chip = seq_index % 2, seq_index // 2
    place = jnp.stack([rep_index // 2, rep_index % 2, chip, core]).astype(jnp.int32)
    block = part // 2
    project_piece = jnp.transpose(
        attn_w[:6].astype(low_type).reshape(6, 2, block, cols), (2, 1, 0, 3)
    ).reshape(block, 12 * cols)
    out_piece = attn_w[6].astype(low_type).T
    half = block // 2
    first, second = [
        jnp.concatenate([planes_swap(project_piece[rows]), out_piece[rows]], 1)
        for rows in (slice(half), slice(half, block))
    ]
    trees = [gather_tree(first)]
    second, unused_far = lax.optimization_barrier((second, trees[0][2]))
    trees.append(gather_tree(second))
    up_piece = jnp.transpose(
        up_w.astype(low_type).reshape(2, block, cols_up), (1, 0, 2)
    ).reshape(block, 2 * cols_up)
    ffn_piece = jnp.concatenate([planes_swap(up_piece), down_w.astype(low_type).T], 1)
    ffn_piece, unused_near = lax.optimization_barrier((ffn_piece, (trees[0][4], trees[1][4])))
    ffn_pieces, ffn_side = gather_direct(ffn_piece)

    spans, unused_piece = lax.optimization_barrier((spans, project_piece))
    inputs = jnp.concatenate([x_words[0], x_ents[0] + span_mean_closed(spans[0], width)], 0)
    live = jnp.concatenate([word_mask[0], ent_mask[0]], 0).astype(low_type)
    live = jnp.pad(live.reshape(1, rows_dev), ((0, 15), (0, width - rows_dev)))
    pieces = gather_seq(jnp.concatenate([inputs.astype(low_type), live], 0))
    lives = [piece[rows_dev, :rows_dev] for piece in pieces]
    lives = [piece[:words_dev] for piece in lives] + [piece[words_dev:] for piece in lives]
    offsets = ((jnp.concatenate(lives).astype(jnp.float32) - 1.0) * MASK_FILL).reshape(1, -1)

    own_vecs = lax.dynamic_slice_in_dim(vecs, seq_index * part, part, 1)
    none = jnp.zeros((part,), jnp.float32)
    scale = jnp.where(jnp.arange(4 * part) < 2 * part, 0.125, 1.0).astype(jnp.float32)
    bias_word = jnp.concatenate([own_vecs[0], own_vecs[1], none, own_vecs[4]])
    bias_ent = jnp.concatenate([own_vecs[2], own_vecs[3], none, own_vecs[4]])
    in_vmem = pl.BlockSpec(memory_space=pltpu.VMEM)
    w_word, w_ent, packed_word, packed_ent, rows_low, w_out = pl.pallas_call(
        functools.partial(project_kernel, words_dev, rows_dev),
        in_specs=[pl.BlockSpec(memory_space=pltpu.SMEM)] + [in_vmem] * 19,
        out_specs=[in_vmem] * 6,
        out_shape=[
            jax.ShapeDtypeStruct(shape, low_type)
            for shape in [
                (rows, width)
                for rows in (width, width, word_count, ent_count, word_count + ent_count)
            ]
            + [(width, part)]
        ],
        scratch_shapes=[pltpu.VMEM((2, 4, 2, half, 14 * cols), low_type)],
        name="project",
    )(
        place,
        bias_word.reshape(1, -1),
        bias_ent.reshape(1, -1),
        scale.reshape(1, -1),
        *trees[0],
        *trees[1],
        *pieces,
    )
    attn, *attn_low, stats = attention_forward(packed_word, packed_ent, offsets, heads)
    attn_low[1], ffn_pieces, ffn_side = lax.optimization_barrier(
        (attn_low[1], ffn_pieces, ffn_side)
    )
    ffn_sides = [ffn_side] + [rep_swap(piece, 1) for piece in ffn_pieces[1:]]
    w_up, w_down = join_call(
        ffn_join_kernel,
        place,
        ffn_pieces + ffn_sides,
        [(width, hidden_part), (width, hidden_part)],
        "join_ffn",
    )

    bias_up = lax.dynamic_slice_in_dim(
        vecs[11:15].reshape(hidden), seq_index * hidden_part, hidden_part, 0
    )
    grad_result = jnp.concatenate([cot_words[0], cot_ents[0]], 0)
    split = rows_dev // 2
    ats = [slice(c * split, (c + 1) * split) for c in (0, 1)]
    parts = [{}, {}]

    def gather(part, rows):
        part["own"] = rows.astype(low_type)
        part["core"], part["far"] = seq_swap(part["own"], 1), seq_swap(part["own"], 2)
        return part["own"]

    def gathered(part, mark):
        far = tie(part["far"], mark)
        return jnp.concatenate([part["core"], seq_swap(far, 1), part["own"], far], 0)

    def scatter(part, rows, weight):
        sent, part["own"], part["far"] = scatter_blocks(rows, nt_dot, weight)
        return sent

    def scattered(part, mark):
        return part["own"] + tie(part["far"], mark).astype(jnp.float32)

    def out_stage(part, c, mark):
        rows = attn_low[c] if mark is None else tie(attn_low[c], mark)
        return scatter(part, rows, w_out)

    def mid_stage(part, c, mark):
        branch = scattered(part, mark) + vecs[5]
        part["mid"], *part["one"] = rows_norm(inputs[ats[c]] + branch, vecs[7], vecs[8])
        return gather(part, part["mid"])

    def up_stage(part, c, mark):
        part["mid_low"] = gathered(part, mark)
        part["pre"] = mm(part["mid_low"], w_up) + bias_up
        part["cdf"] = 0.5 * (1.0 + lax.erf(part["pre"] * math.sqrt(0.5)))
        part["act"] = (part["pre"] * part["cdf"]).astype(low_type)
        return scatter(part, part["act"], w_down)

    def result_stage(part, c, mark):
        ffn = scattered(part, mark) + vecs[6]
        part["result"], *two = rows_norm(part["mid"] + ffn, vecs[9], vecs[10])
        grad, *part["sums_two"] = rows_norm_back(grad_result[ats[c]], *two, vecs[9])
        part["grad_two"] = grad
        return gather(part, grad)

    def down_stage(part, c, mark):
        part["grad_ffn"] = gathered(part, mark)
        pre = part["pre"]
        density = jnp.exp(-0.5 * pre * pre) * (1.0 / math.sqrt(2.0 * math.pi))
        part["grad_pre"] = mm(part["grad_ffn"], w_down) * (part["cdf"] + pre * density)
        part["grad_pre_low"] = part["grad_pre"].astype(low_type)
        return scatter(part, part["grad_pre_low"], w_up)

    def norm_stage(part, c, mark):
        grad = part["grad_two"] + scattered(part, mark)
        part["grad_one"], *part["sums_one"] = rows_norm_back(grad, *part["one"], vecs[7])
        return gather(part, part["grad_one"])

    def branch_stage(part, c, mark):
        part["grad_branch"] = gathered(part, mark)
        part["grad_attn"] = mm(part["grad_branch"], w_out)
        return part["grad_branch"]

    mark = None
    for stage in (
        out_stage,
        mid_stage,
        up_stage,
        result_stage,
        down_stage,
        norm_stage,
        branch_stage,
    ):
        for c, chunk in enumerate(parts):
            mark = stage(chunk, c, mark)
    results, grads_one, grads_attn = [
        [part[name] for part in parts] for name in ("result", "grad_one", "grad_attn")
    ]
    kept = [
        [part[name] for name in ("mid_low", "act", "grad_ffn", "grad_pre_low", "grad_branch")]
        for part in parts
    ]
    sums = [
        sum(values)
        for values in zip(
            *[
                [jnp.sum(part["grad_one"], 0), jnp.sum(part["grad_two"], 0)]
                + part["sums_one"]
                + part["sums_two"]
                + [jnp.sum(part["grad_pre"], 0)]
                for part in parts
            ]
        )
    ]
    result = jnp.concatenate(results, 0)
    grad_one = jnp.concatenate(grads_one, 0)
    grad_up = sum(tn_dot(mid_low, grad_pre_low) for mid_low, _, _, grad_pre_low, _ in kept)
    grad_up, unused_branch = lax.optimization_barrier((grad_up.astype(low_type), kept[1][4]))
    got_up = lax.all_to_all(grad_up.reshape(seq_count, part, hidden_part), "seq", 0, 0)
    grad_out = sum(tn_dot(low, parts[4]) for low, parts in zip(attn_low, kept))
    d_query, d_key, d_sums = attention_backward(
        packed_word, packed_ent, offsets, attn, stats, grads_attn, heads
    )
    d_query, got_up = lax.optimization_barrier((d_query, got_up))
    grad_down = sum(
        tn_dot(act_low, tie(grad_ffn, d_sums)) for _, act_low, grad_ffn, _, _ in kept
    )
    grad_project = project_grad(rows_low, d_query, d_key, word_count)
    got_project = lax.all_to_all(
        grad_project.reshape(seq_count, part, 6 * part), "seq", 0, 0
    )
    full_up, full_down, left_ffn = left_of_ffn(
        got_up, grad_down, err_up, err_down, qf_up.T, qf_down.T
    )
    sent_inputs, own_inputs = input_grad(
        d_query, tie(d_key, grad_project[:16, :128]), w_word, w_ent, word_count
    )
    own_inputs = own_inputs + seq_swap(sent_inputs, 1).astype(jnp.float32)
    own_inputs, sent_inputs = own_inputs[:rows_dev], own_inputs[rows_dev:].astype(low_type)

    vec_grad = jnp.zeros((15, width), jnp.float32)
    bias_query = jnp.concatenate(
        [d_sums[0].reshape(2, part), d_sums[1].reshape(2, part), d_sums[2, :part].reshape(1, part)], 0
    )
    vec_grad = lax.dynamic_update_slice(vec_grad, bias_query, (0, seq_index * part))
    vec_grad = lax.dynamic_update_slice(vec_grad, jnp.stack(sums[:6]), (5, 0))
    bias_rows = hidden_part // width
    vec_grad = lax.dynamic_update_slice(
        vec_grad, sums[6].reshape(bias_rows, width), (11 + seq_index * bias_rows, 0)
    )

    full_attn, left = left_of_attn(
        got_project, grad_out, err_attn, tall(attention_prior_right), left_ffn
    )
    left, sent_inputs = lax.optimization_barrier((left, sent_inputs))
    got_inputs = seq_swap(sent_inputs, 2)
    for bits in (1, 2):
        left = left + rep_swap(left, bits)
    left, got_inputs = lax.optimization_barrier((left, got_inputs))
    left, gram = gram_of(left, rep_swap(left, 4), 1.0 / rep_count)
    gram = gram + seq_swap(gram, 1)
    rows_vec = jnp.pad(vec_grad, ((0, 1), (0, 0))).reshape(2, 8, width)
    orth, p_attn, p_up, p_down, sent, kept = right_of(
        place, gram, seq_swap(gram, 2), left, full_attn, full_up, full_down, rows_vec
    )
    got_inputs, unused_orth = lax.optimization_barrier((got_inputs, orth))
    grad_inputs = grad_one + (own_inputs + got_inputs.astype(jnp.float32))
    kept = kept + seq_swap(sent, 1)
    kept = kept[0] + seq_swap(kept[1], 2)
    for bits in (1, 2, 4):
        kept = kept + rep_swap(kept, bits)
    kept = kept / rep_count
    kept = jnp.stack([kept, seq_swap(kept, 2)])
    lr_mat = 1.5 * math.sqrt(rep_count / (SEQS * (WORDS + ENTS)))
    lr_vec = 0.2 * math.sqrt(rep_count / (SEQS * (WORDS + ENTS)))
    next_err, next_mom, new, (q_attn, q_up, q_down) = updates(
        place,
        orth,
        kept,
        seq_swap(kept, 1),
        (full_attn, full_up, full_down),
        (mom_attn, mom_up, mom_down.T, mom_vecs),
        (attn_w, up_w, down_w.T, vecs),
        lr_mat,
        lr_vec,
    )
    return (
        result[None, :words_dev],
        result[None, words_dev:],
        grad_inputs[None, :words_dev],
        grad_inputs[None, words_dev:],
        new[0],
        new[1],
        new[2].T,
        new[3],
        next_mom[0],
        next_mom[1],
        next_mom[2].T,
        next_mom[3],
        next_err[0],
        next_err[1],
        next_err[2],
        tall(p_attn),
        tall(p_up),
        tall(p_down),
        tall(q_attn),
        tall(q_up),
        tall(q_down),
    )


def solution(mesh):
    in_specs = (
        P("rep", "seq", None),
        P("rep", "seq", None),
        P("rep", "seq", None),
        P("rep", "seq"),
        P("rep", "seq"),
        P("rep", "seq", None),
        P("rep", "seq", None),
        P(None, "seq", "rep"),
        P("seq", "rep"),
        P("seq", "rep"),
        P(),
        P(None, "seq", "rep"),
        P("seq", "rep"),
        P("seq", "rep"),
        P(),
        P("rep", None, "seq", None),
        P("rep", "seq", None),
        P("rep", "seq", None),
        P(),
        P(),
        P(),
    )
    out_specs = (
        P("rep", "seq", None),
        P("rep", "seq", None),
        P("rep", "seq", None),
        P("rep", "seq", None),
        P(None, "seq", "rep"),
        P("seq", "rep"),
        P("seq", "rep"),
        P(),
        P(None, "seq", "rep"),
        P("seq", "rep"),
        P("seq", "rep"),
        P(),
        P("rep", None, "seq", None),
        P("rep", "seq", None),
        P("rep", "seq", None),
        P(None, "seq", None),
        P("seq", None),
        P("seq", None),
        P(),
        P(),
        P(),
    )
    seqs, reps = mesh.shape["seq"], mesh.shape["rep"]
    split_heads = seqs == 4 and reps == 2 * seqs and HEADS % seqs == 0
    body = head_split_device if split_heads else on_device
    return jax.shard_map(
        body, mesh=mesh, in_specs=in_specs, out_specs=out_specs, check_vma=False
    )
```

```python
import functools
import math

import jax
import jax.numpy as jnp
from jax import lax
from jax.experimental import pallas as pl
from jax.experimental.pallas import tpu as pltpu
from jax.sharding import PartitionSpec as P

HEADS = 12
WORDS = 1024
ENTS = 128
SPAN = 16
SEQS = 1


HIGH_PRECISION = lax.Precision.HIGHEST
EPS = 1e-05
MASK_FILL = 30000.0
MOMENTUM = 0.9


def span_mean(spans, model_width):
    starts = spans[..., 0]
    finals = spans[..., 1]
    lengths = (finals - starts + 1).astype(jnp.float32)
    offsets = jnp.arange(SPAN, dtype=jnp.int32)
    places = (starts[..., None] + offsets).astype(jnp.float32)
    shares = (offsets <= (finals - starts)[..., None]).astype(jnp.float32) / lengths[..., None]
    half_width = model_width // 2
    rates = jnp.exp(
        jnp.arange(half_width).astype(jnp.float32) * (-2.0 * math.log(10000.0) / model_width)
    )
    angles = places[..., None] * rates
    table = jnp.concatenate([jnp.sin(angles), jnp.cos(angles)], -1)
    return jnp.sum(table * shares[..., None], axis=-2)


def span_mean_closed(spans, model_width):
    lengths = (spans[..., 1] - spans[..., 0] + 1).astype(jnp.float32)[..., None]
    middles = (spans[..., 1] + spans[..., 0]).astype(jnp.float32)[..., None]
    half_rates = 0.5 * jnp.exp(
        jnp.arange(model_width // 2).astype(jnp.float32) * (-2.0 * math.log(10000.0) / model_width)
    )
    share = jnp.sin(lengths * half_rates) / (lengths * jnp.sin(half_rates))
    angles = middles * half_rates
    return jnp.concatenate([share * jnp.sin(angles), share * jnp.cos(angles)], -1)


def layer_norm(hidden, gain, shift):
    center = hidden - jnp.mean(hidden, -1, keepdims=True)
    rstd = lax.rsqrt(jnp.mean(center * center, -1, keepdims=True) + EPS)
    normed = center * rstd
    return (normed * gain + shift, normed, rstd)


def norm_back(grad, normed, rstd, gain):
    dnormed = grad * gain
    grad_in = rstd * (
        dnormed
        - jnp.mean(dnormed, -1, keepdims=True)
        - normed * jnp.mean(dnormed * normed, -1, keepdims=True)
    )
    return (grad_in, jnp.sum(grad * normed, axis=(0, 1)), jnp.sum(grad, axis=(0, 1)))


def gelu_exact(value):
    return jax.nn.gelu(value, approximate=False)


def project(row_entries, weight_matrix):
    return jnp.einsum("thq,qo->tho", row_entries, weight_matrix, preferred_element_type=jnp.float32)


def project_back(row_entries, weight_matrix):
    return jnp.einsum("hpf,zf->hpz", row_entries, weight_matrix, preferred_element_type=jnp.float32)


def weight_grad(input_arrays, gradient_list):
    return jnp.einsum(
        "cev,ceg->vg", input_arrays, gradient_list, preferred_element_type=jnp.float32
    )


def split_keys(pieces, words_dev, ents_dev, head_count):
    key_piece, live_piece = pieces
    batch_rows = key_piece.shape[0]
    both = key_piece.shape[2]
    model_width = both // 2
    head_dim = model_width // head_count
    rows_dev = words_dev + ents_dev
    blocks = key_piece.shape[1] // rows_dev
    grouped = key_piece.reshape(batch_rows, blocks, rows_dev, both)
    live_grouped = live_piece.reshape(batch_rows, blocks, rows_dev)
    word_part = grouped[:, :, :words_dev].reshape(batch_rows, blocks * words_dev, both)
    ent_part = grouped[:, :, words_dev:].reshape(batch_rows, blocks * ents_dev, both)
    keys_word = word_part[..., :model_width].reshape(batch_rows, -1, head_count, head_dim)
    keys_ent = ent_part[..., :model_width].reshape(batch_rows, -1, head_count, head_dim)
    values = jnp.concatenate(
        [word_part[..., model_width:], ent_part[..., model_width:]], 1
    ).reshape(batch_rows, -1, head_count, head_dim)
    live = jnp.concatenate(
        [
            live_grouped[:, :, :words_dev].reshape(batch_rows, -1),
            live_grouped[:, :, words_dev:].reshape(batch_rows, -1),
        ],
        1,
    )
    offsets = (live.astype(jnp.float32) - 1.0) * MASK_FILL
    return (keys_word, keys_ent, values, offsets, blocks)


def score_block(query_word, query_ent, keys_word, keys_ent, offsets):
    score_word = jnp.einsum(
        "sqhd,skhd->shqk", query_word, keys_word, preferred_element_type=jnp.float32
    )
    score_ent = jnp.einsum(
        "sqhd,skhd->shqk", query_ent, keys_ent, preferred_element_type=jnp.float32
    )
    return jnp.concatenate([score_word, score_ent], -1) + offsets[:, None, None, :]


def flat_heads(array):
    return array.reshape(array.shape[0], array.shape[1], -1)


def join_rows(grad_keys_word, grad_keys_ent, grad_values, blocks, words_dev, ents_dev):
    batch_rows = grad_keys_word.shape[0]
    word_count = grad_keys_word.shape[1]
    word_rows = jnp.concatenate(
        [flat_heads(grad_keys_word), flat_heads(grad_values[:, :word_count])], -1
    )
    ent_rows = jnp.concatenate(
        [flat_heads(grad_keys_ent), flat_heads(grad_values[:, word_count:])], -1
    )
    word_rows = word_rows.reshape(batch_rows, blocks, words_dev, -1)
    ent_rows = ent_rows.reshape(batch_rows, blocks, ents_dev, -1)
    return jnp.concatenate([word_rows, ent_rows], 2).reshape(
        batch_rows, blocks * (words_dev + ents_dev), -1
    )


def from_gram(left, gram):
    lower = jnp.linalg.cholesky(gram)
    return jax.scipy.linalg.solve_triangular(lower, left.T, lower=True).T


def orthonormal(left):
    return from_gram(left, jnp.dot(left.T, left, precision=HIGH_PRECISION))


def on_device(
    x_words,
    x_ents,
    spans,
    word_mask,
    ent_mask,
    cot_words,
    cot_ents,
    attn_w,
    up_w,
    down_w,
    vecs,
    mom_attn,
    mom_up,
    mom_down,
    mom_vecs,
    err_attn,
    err_up,
    err_down,
    attention_prior_right,
    qf_up,
    qf_down,
):
    batch_rows, words_dev, model_width = x_words.shape
    ents_dev = x_ents.shape[1]
    rows_dev = words_dev + ents_dev
    head_count = HEADS
    head_dim = model_width // head_count
    hidden_width = up_w.shape[1] * lax.axis_size("rep")
    seq_count = lax.axis_size("seq")
    rep_count = lax.axis_size("rep")
    seq_index = lax.axis_index("seq")
    rep_index = lax.axis_index("rep")
    lowered = jnp.bfloat16
    column_parts = (
        lax.all_gather(attn_w.astype(lowered), "rep", axis=2, tiled=True),
        lax.all_gather(up_w.astype(lowered), "rep", axis=1, tiled=True),
        lax.all_gather(down_w.astype(lowered), "rep", axis=1, tiled=True),
    )
    w_attn, w_up, w_down = (
        lax.all_gather(column_parts[0], "seq", axis=1, tiled=True),
        lax.all_gather(column_parts[1], "seq", axis=0, tiled=True),
        lax.all_gather(column_parts[2], "seq", axis=0, tiled=True),
    )
    input_arrays = jnp.concatenate([x_words, x_ents + span_mean(spans, model_width)], 1)
    inputs_low = input_arrays.astype(lowered)
    word_low = inputs_low[:, :words_dev]
    ent_low = inputs_low[:, words_dev:]
    query_word = (
        jnp.concatenate(
            [project(word_low, w_attn[0]) + vecs[0], project(ent_low, w_attn[2]) + vecs[2]], 1
        )
        * 0.125
    ).astype(lowered)
    query_ent = (
        jnp.concatenate(
            [project(word_low, w_attn[1]) + vecs[1], project(ent_low, w_attn[3]) + vecs[3]], 1
        )
        * 0.125
    ).astype(lowered)
    keys_low = project(inputs_low, w_attn[4]).astype(lowered)
    values_low = (project(inputs_low, w_attn[5]) + vecs[4]).astype(lowered)
    key_rows = jnp.concatenate([keys_low, values_low], -1)
    key_live = jnp.concatenate([word_mask, ent_mask], 1).astype(lowered)
    heads_word = query_word.reshape(batch_rows, rows_dev, head_count, head_dim)
    heads_ent = query_ent.reshape(batch_rows, rows_dev, head_count, head_dim)
    forward_row_top = jnp.full((batch_rows, head_count, rows_dev), -jnp.inf, jnp.float32)
    row_total = jnp.zeros((batch_rows, head_count, rows_dev), jnp.float32)
    weighted = jnp.zeros((batch_rows, rows_dev, head_count, head_dim), jnp.float32)
    keys_word, keys_ent, values, offsets, blocks = split_keys(
        (
            lax.all_gather(key_rows, "seq", axis=1, tiled=True),
            lax.all_gather(key_live, "seq", axis=1, tiled=True),
        ),
        words_dev,
        ents_dev,
        head_count,
    )
    scores = score_block(heads_word, heads_ent, keys_word, keys_ent, offsets)
    new_top = jnp.max(scores, -1)
    factor = jnp.exp(forward_row_top - new_top)
    weights = jnp.exp(scores - new_top[..., None])
    row_total = row_total * factor + jnp.sum(weights, -1)
    weighted = weighted * jnp.transpose(factor, (0, 2, 1))[..., None] + jnp.einsum(
        "shqk,skhd->sqhd", weights.astype(lowered), values, preferred_element_type=jnp.float32
    )
    row_top, row_total, weighted = (new_top, row_total, weighted)
    total_rows = jnp.transpose(row_total, (0, 2, 1))[..., None]
    attn = weighted / total_rows
    attn_low = attn.reshape(batch_rows, rows_dev, model_width).astype(lowered)
    branch = project(attn_low, w_attn[6]) + vecs[5]
    mid, normed_one, rstd_one = layer_norm(input_arrays + branch, vecs[7], vecs[8])
    mid_low = mid.astype(lowered)
    pre = project(mid_low, w_up) + vecs[11:15].reshape(hidden_width)
    act_low = gelu_exact(pre).astype(lowered)
    ffn = project(act_low, w_down) + vecs[6]
    result, normed_two, rstd_two = layer_norm(mid + ffn, vecs[9], vecs[10])
    grad_result = jnp.concatenate([cot_words, cot_ents], 1)
    grad_two, gain_two, shift_two = norm_back(grad_result, normed_two, rstd_two, vecs[9])
    bias_down = jnp.sum(grad_two, axis=(0, 1))
    grad_ffn_low = grad_two.astype(lowered)
    grad_down = weight_grad(act_low, grad_ffn_low)
    grad_act = project_back(grad_ffn_low, w_down)
    unused_value, gelu_pull = jax.vjp(gelu_exact, pre)
    grad_pre = gelu_pull(grad_act)[0]
    bias_up = jnp.sum(grad_pre, axis=(0, 1))
    grad_pre_low = grad_pre.astype(lowered)
    grad_up = weight_grad(mid_low, grad_pre_low)
    grad_mid = grad_two + project_back(grad_pre_low, w_up)
    grad_one, gain_one, shift_one = norm_back(grad_mid, normed_one, rstd_one, vecs[7])
    bias_out = jnp.sum(grad_one, axis=(0, 1))
    grad_branch_low = grad_one.astype(lowered)
    grad_out_proj = weight_grad(attn_low, grad_branch_low)
    grad_attn = project_back(grad_branch_low, w_attn[6]).reshape(
        batch_rows, rows_dev, head_count, head_dim
    )
    grad_unnorm = (grad_attn / total_rows).astype(lowered)
    delta_rows = jnp.transpose(jnp.sum(grad_attn * attn, -1), (0, 2, 1)) / row_total
    keys_word, keys_ent, values, offsets, blocks = split_keys(
        (
            lax.all_gather(key_rows, "seq", axis=1, tiled=True),
            lax.all_gather(key_live, "seq", axis=1, tiled=True),
        ),
        words_dev,
        ents_dev,
        head_count,
    )
    scores = score_block(heads_word, heads_ent, keys_word, keys_ent, offsets)
    weights = jnp.exp(scores - row_top[..., None])
    grad_weights = jnp.einsum(
        "sqhd,skhd->shqk", grad_unnorm, values, preferred_element_type=jnp.float32
    )
    grad_scores = (weights * (grad_weights - delta_rows[..., None])).astype(lowered)
    word_count = keys_word.shape[1]
    scores_word = grad_scores[..., :word_count]
    scores_ent = grad_scores[..., word_count:]
    grad_query_word = jnp.einsum(
        "shqk,skhd->sqhd", scores_word, keys_word, preferred_element_type=jnp.float32
    )
    grad_query_ent = jnp.einsum(
        "shqk,skhd->sqhd", scores_ent, keys_ent, preferred_element_type=jnp.float32
    )
    grad_keys_word = jnp.einsum(
        "shqk,sqhd->skhd", scores_word, heads_word, preferred_element_type=jnp.float32
    )
    grad_keys_ent = jnp.einsum(
        "shqk,sqhd->skhd", scores_ent, heads_ent, preferred_element_type=jnp.float32
    )
    grad_values = jnp.einsum(
        "shqk,sqhd->skhd", weights.astype(lowered), grad_unnorm, preferred_element_type=jnp.float32
    )
    piece_grad = join_rows(grad_keys_word, grad_keys_ent, grad_values, blocks, words_dev, ents_dev)
    grad_rows = piece_grad
    grad_query_word, grad_query_ent, grad_rows = (grad_query_word, grad_query_ent, grad_rows)
    own_rows = lax.psum_scatter(
        grad_rows.astype(jnp.bfloat16), "seq", scatter_dimension=1, tiled=True
    ).astype(jnp.float32)
    grad_keys = own_rows[..., :model_width]
    grad_values = own_rows[..., model_width:]
    bias_values = jnp.sum(grad_values, axis=(0, 1))
    keys_grad_low = grad_keys.astype(lowered)
    values_grad_low = grad_values.astype(lowered)
    grad_key_w = weight_grad(inputs_low, keys_grad_low)
    grad_value_w = weight_grad(inputs_low, values_grad_low)
    inner_word = grad_query_word.reshape(batch_rows, rows_dev, model_width) * 0.125
    inner_ent = grad_query_ent.reshape(batch_rows, rows_dev, model_width) * 0.125
    bias_query = [
        jnp.sum(inner_word[:, :words_dev], axis=(0, 1)),
        jnp.sum(inner_ent[:, :words_dev], axis=(0, 1)),
        jnp.sum(inner_word[:, words_dev:], axis=(0, 1)),
        jnp.sum(inner_ent[:, words_dev:], axis=(0, 1)),
    ]
    inner_word_low = inner_word.astype(lowered)
    inner_ent_low = inner_ent.astype(lowered)
    grad_query_mats = [
        weight_grad(word_low, inner_word_low[:, :words_dev]),
        weight_grad(word_low, inner_ent_low[:, :words_dev]),
        weight_grad(ent_low, inner_word_low[:, words_dev:]),
        weight_grad(ent_low, inner_ent_low[:, words_dev:]),
    ]
    back_keys = project_back(keys_grad_low, w_attn[4]) + project_back(values_grad_low, w_attn[5])
    back_word = project_back(inner_word_low[:, :words_dev], w_attn[0]) + project_back(
        inner_ent_low[:, :words_dev], w_attn[1]
    )
    back_ent = project_back(inner_word_low[:, words_dev:], w_attn[2]) + project_back(
        inner_ent_low[:, words_dev:], w_attn[3]
    )
    grad_inputs = grad_one + back_keys + jnp.concatenate([back_word, back_ent], 1)
    grad_attn_w = jnp.stack(grad_query_mats + [grad_key_w, grad_value_w, grad_out_proj])
    vec_grad = jnp.concatenate(
        [
            jnp.stack(
                bias_query
                + [bias_values, bias_out, bias_down, gain_one, shift_one, gain_two, shift_two]
            ),
            bias_up.reshape(4, model_width),
        ],
        0,
    )
    rows_attn, rows_up, rows_down = (
        lax.psum_scatter(
            grad_attn_w.astype(jnp.bfloat16), "seq", scatter_dimension=1, tiled=True
        ).astype(jnp.float32),
        lax.psum_scatter(
            grad_up.astype(jnp.bfloat16), "seq", scatter_dimension=0, tiled=True
        ).astype(jnp.float32),
        lax.psum_scatter(
            grad_down.astype(jnp.bfloat16), "seq", scatter_dimension=0, tiled=True
        ).astype(jnp.float32),
    )
    attention_full_gradient = rows_attn + err_attn[0]
    full_up = rows_up + err_up[0]
    full_down = rows_down + err_down[0]
    attention_left_factor = jnp.einsum(
        "vcg,vgo->vco", attention_full_gradient, attention_prior_right, precision=HIGH_PRECISION
    )
    left_up = jnp.dot(full_up, qf_up, precision=HIGH_PRECISION)
    left_down = jnp.dot(full_down, qf_down, precision=HIGH_PRECISION)
    count_attn = attention_full_gradient.shape[1]
    count_up = full_up.shape[0]
    count_down = full_down.shape[0]
    placed_attn = lax.dynamic_update_slice_in_dim(
        jnp.zeros((7, count_attn * seq_count, attention_left_factor.shape[2]), jnp.float32),
        attention_left_factor,
        seq_index * count_attn,
        1,
    )
    placed_up = lax.dynamic_update_slice_in_dim(
        jnp.zeros((count_up * seq_count, left_up.shape[1]), jnp.float32),
        left_up,
        seq_index * count_up,
        0,
    )
    placed_down = lax.dynamic_update_slice_in_dim(
        jnp.zeros((count_down * seq_count, left_down.shape[1]), jnp.float32),
        left_down,
        seq_index * count_down,
        0,
    )
    summed_attn, summed_up, summed_down = lax.psum(
        (placed_attn, placed_up, placed_down), ("seq", "rep")
    )
    orth_attn = jax.vmap(orthonormal)(summed_attn / rep_count)
    orth_up = orthonormal(summed_up / rep_count)
    orth_down = orthonormal(summed_down / rep_count)
    attention_local_gradient = lax.dynamic_slice_in_dim(
        orth_attn, seq_index * count_attn, count_attn, 1
    )
    own_up = lax.dynamic_slice_in_dim(orth_up, seq_index * count_up, count_up, 0)
    own_down = lax.dynamic_slice_in_dim(orth_down, seq_index * count_down, count_down, 0)
    right_parts = (
        jnp.einsum(
            "dpl,dpg->dgl",
            attention_local_gradient,
            attention_full_gradient,
            precision=HIGH_PRECISION,
        ),
        jnp.dot(full_up.T, own_up, precision=HIGH_PRECISION),
        jnp.dot(full_down.T, own_down, precision=HIGH_PRECISION),
        vec_grad,
    )
    attention_right_factor, right_up, right_down, vec_total = lax.psum(
        (right_parts[0], right_parts[1], right_parts[2], right_parts[3]), ("seq", "rep")
    )
    attention_right_factor = attention_right_factor / rep_count
    right_up = right_up / rep_count
    right_down = right_down / rep_count
    vec_mean = vec_total / rep_count
    attention_estimate = jnp.einsum(
        "whg,wng->whn", attention_local_gradient, attention_right_factor, precision=HIGH_PRECISION
    )
    approx_up = jnp.dot(own_up, right_up.T, precision=HIGH_PRECISION)
    approx_down = jnp.dot(own_down, right_down.T, precision=HIGH_PRECISION)
    next_err_attn = (attention_full_gradient - attention_estimate)[None]
    next_err_up = (full_up - approx_up)[None]
    next_err_down = (full_down - approx_down)[None]
    cols_attn = attn_w.shape[2]
    cols_up = up_w.shape[1]
    cols_down = down_w.shape[1]
    step_attn = lax.dynamic_slice_in_dim(attention_estimate, rep_index * cols_attn, cols_attn, 2)
    step_up = lax.dynamic_slice_in_dim(approx_up, rep_index * cols_up, cols_up, 1)
    step_down = lax.dynamic_slice_in_dim(approx_down, rep_index * cols_down, cols_down, 1)
    lr_mat = 1.5 * math.sqrt(rep_count / (SEQS * (WORDS + ENTS)))
    lr_vec = 0.2 * math.sqrt(rep_count / (SEQS * (WORDS + ENTS)))
    next_mom_attn = MOMENTUM * mom_attn + step_attn
    next_mom_up = MOMENTUM * mom_up + step_up
    next_mom_down = MOMENTUM * mom_down + step_down
    next_mom_vecs = MOMENTUM * mom_vecs + vec_mean
    new_attn = attn_w - lr_mat * next_mom_attn
    new_up = up_w - lr_mat * next_mom_up
    new_down = down_w - lr_mat * next_mom_down
    new_vecs = vecs - lr_vec * next_mom_vecs
    return (
        result[:, :words_dev],
        result[:, words_dev:],
        grad_inputs[:, :words_dev],
        grad_inputs[:, words_dev:],
        new_attn,
        new_up,
        new_down,
        new_vecs,
        next_mom_attn,
        next_mom_up,
        next_mom_down,
        next_mom_vecs,
        next_err_attn,
        next_err_up,
        next_err_down,
        attention_local_gradient,
        own_up,
        own_down,
        attention_right_factor,
        right_up,
        right_down,
    )


def seq_swap(array, bits):
    size = lax.axis_size("seq")
    return lax.ppermute(array, "seq", [(i, i ^ bits) for i in range(size)])


def rep_swap(array, bits):
    size = lax.axis_size("rep")
    return lax.ppermute(array, "rep", [(i, i ^ bits) for i in range(size)])


def planes_swap(array):
    seqs, reps = lax.axis_size("seq"), lax.axis_size("rep")
    pairs = []
    for s in range(seqs):
        for r in range(reps):
            pairs.append((s * reps + r, (r // 2) * reps + 2 * s + r % 2))
    return lax.ppermute(array, ("seq", "rep"), pairs)


def gather_seq(piece):
    other_chip = seq_swap(piece, 2)
    return [seq_swap(piece, 1), seq_swap(other_chip, 1), piece, other_chip]


def gather_direct(piece):
    pieces = [piece] + [rep_swap(piece, 2 * change) for change in (1, 2, 3)]
    return pieces, rep_swap(piece, 1)


def gather_tree(piece):
    own_side = rep_swap(piece, 1)
    far, own_side = lax.optimization_barrier((rep_swap(piece, 4), own_side))
    near = rep_swap(jnp.stack([piece, far]), 2)
    near, far_side = lax.optimization_barrier((near, rep_swap(far, 1)))
    near_side = rep_swap(near, 1)
    return [piece, own_side, far, far_side, near, near_side]


def tree_pieces(refs):
    own, own_side, far, far_side, near, near_side = refs
    return (
        (0, own[...], own_side[...]),
        (2, far[...], far_side[...]),
        (1, near[0], near_side[0]),
        (3, near[1], near_side[1]),
    )


def project_kernel(
    words_dev, rows_dev, place_ref, bias_word_ref, bias_ent_ref, scale_ref, *refs
):
    trees, row_refs = (refs[:6], refs[6:12]), refs[12:16]
    word_ref, ent_ref, packed_word_ref, packed_ent_ref, rows_ref, out_ref, piece_ref = refs[16:]
    word_count = packed_word_ref.shape[0]
    ents_dev = rows_dev - words_dev
    z, y = place_ref[0], place_ref[1]
    for half, tree in enumerate(trees):
        for change, own, other in tree_pieces(tree):
            piece_ref[half, z ^ change, y] = own
            piece_ref[half, z ^ change, 1 - y] = other
    rows, both = piece_ref.shape[3:]
    cols = both // 14
    for half in (0, 1):
        for place in range(4):
            left, right = piece_ref[half, place, 0], piece_ref[half, place, 1]
            for side, piece in ((0, left), (1, right)):
                start = (4 * place + 2 * side + half) * rows
                out_ref[start : start + rows] = piece[:, 12 * cols :]
            for upper in (0, 1):
                parts = []
                for j in range(6):
                    low = (upper * 6 + j) * cols
                    parts.append(left[:, low : low + cols])
                    parts.append(right[:, low : low + cols])
                start = (4 * place + 2 * upper + half) * rows
                target = slice(start, start + rows)
                word_ref[target] = jnp.concatenate(parts[:4] + parts[8:], 1)
                ent_ref[target] = jnp.concatenate(parts[4:], 1)

    scale = scale_ref[...]
    word, ent = word_ref[...], ent_ref[...]
    for k, row_ref in enumerate(row_refs):
        words = row_ref[:words_dev]
        at = slice(k * words_dev, (k + 1) * words_dev)
        rows_ref[at] = words
        packed_word_ref[at] = ((mm(words, word) + bias_word_ref[...]) * scale).astype(
            jnp.bfloat16
        )
        start = word_count + k * ents_dev
        rows_ref[start : start + ents_dev] = row_ref[words_dev:rows_dev]
    packed_ent_ref[...] = ((mm(rows_ref[word_count:], ent) + bias_ent_ref[...]) * scale).astype(
        jnp.bfloat16
    )


def ffn_join_kernel(place_ref, *refs):
    pieces, sides, (up_ref, down_ref) = refs[:4], refs[4:8], refs[8:]
    z, y = place_ref[0], place_ref[1]
    for side in (0, 1):

        @pl.when(y == side)
        def _():
            for change in range(4):
                for y_at, piece in ((side, pieces[change]), (1 - side, sides[change])):
                    rows, both = piece.shape
                    cols = both // 4
                    place = z ^ change
                    for upper in (0, 1):
                        start = pl.multiple_of(place * (2 * rows) + upper * rows, 16)
                        up_ref[pl.ds(start, rows), y_at * cols : (y_at + 1) * cols] = piece[
                            :, upper * cols : (upper + 1) * cols
                        ]
                    start = pl.multiple_of((2 * place + y_at) * rows, 16)
                    down_ref[pl.ds(start, rows), :] = piece[:, 2 * cols :]


def join_call(kernel, place, pieces, shapes, name):
    whole = [pl.BlockSpec(memory_space=pltpu.VMEM)] * len(pieces)
    return pl.pallas_call(
        kernel,
        in_specs=[pl.BlockSpec(memory_space=pltpu.SMEM)] + whole,
        out_specs=[pl.BlockSpec(memory_space=pltpu.VMEM)] * len(shapes),
        out_shape=[jax.ShapeDtypeStruct(shape, jnp.bfloat16) for shape in shapes],
        name=name,
    )(place, *pieces)


def tie(value, mark):
    return lax.optimization_barrier((value, mark))[0]


def scatter_blocks(rows, dot, weight):
    half = rows.shape[0] // 2
    own = half // 2
    sent = dot(rows[:half], weight).astype(jnp.bfloat16)
    kept = dot(rows[half:], weight) + seq_swap(sent, 1).astype(jnp.float32)
    return sent, kept[:own], seq_swap(kept[own:].astype(jnp.bfloat16), 2)


def rows_norm(hidden, gain, shift):
    center = hidden - jnp.mean(hidden, -1, keepdims=True)
    rstd = lax.rsqrt(jnp.mean(center * center, -1, keepdims=True) + EPS)
    normed = center * rstd
    return (normed * gain + shift, normed, rstd)


def rows_norm_back(grad, normed, rstd, gain):
    dnormed = grad * gain
    grad_in = rstd * (
        dnormed
        - jnp.mean(dnormed, -1, keepdims=True)
        - normed * jnp.mean(dnormed * normed, -1, keepdims=True)
    )
    return (grad_in, jnp.sum(grad * normed, axis=0), jnp.sum(grad, axis=0))


def mm(left, right, left_dim=1, right_dim=0):
    return lax.dot_general(
        left, right, (((left_dim,), (right_dim,)), ((), ())), preferred_element_type=jnp.float32
    )


def nt_dot(left, right):
    return mm(left, right, 1, 1)


def tn_dot(left, right):
    return mm(left, right, 0, 0)


HEAD_DIM = 64


def head_parts(word_ref, ent_ref, low, high):
    return jnp.concatenate([word_ref[:, low:high], ent_ref[:, low:high]], 0)


def attention_kernel(
    heads,
    query_word_ref,
    query_ent_ref,
    key_word_ref,
    key_ent_ref,
    offset_ref,
    attn_ref,
    low_ref,
    high_ref,
    stat_ref,
):
    width = heads * HEAD_DIM
    word_count = key_word_ref.shape[0]
    rows = attn_ref.shape[0]
    lane = lax.broadcasted_iota(jnp.int32, (rows, 128), 1)
    stats = jnp.zeros((rows, 128), jnp.float32)
    for h in range(heads):
        low, high = h * HEAD_DIM, (h + 1) * HEAD_DIM
        q_word = head_parts(query_word_ref, query_ent_ref, low, high)
        q_ent = head_parts(query_word_ref, query_ent_ref, width + low, width + high)
        k_word = key_word_ref[:, 2 * width + low : 2 * width + high]
        k_ent = key_ent_ref[:, 2 * width + low : 2 * width + high]
        s_word = nt_dot(q_word, k_word) + offset_ref[:, :word_count]
        s_ent = nt_dot(q_ent, k_ent) + offset_ref[:, word_count:]
        top = jnp.maximum(
            jnp.max(s_word, -1, keepdims=True), jnp.max(s_ent, -1, keepdims=True)
        )
        w_word = jnp.exp(s_word - top)
        w_ent = jnp.exp(s_ent - top)
        total = jnp.sum(w_word, -1, keepdims=True) + jnp.sum(w_ent, -1, keepdims=True)
        v_word = key_word_ref[:, 3 * width + low : 3 * width + high]
        v_ent = key_ent_ref[:, 3 * width + low : 3 * width + high]
        unnorm = mm(w_word.astype(jnp.bfloat16), v_word) + mm(w_ent.astype(jnp.bfloat16), v_ent)
        attn_ref[:, low:high] = unnorm / total
        stats = jnp.where(lane == h, top, stats)
        stats = jnp.where(lane == heads + h, total, stats)
    stat_ref[...] = stats
    low_ref[...] = attn_ref[: rows // 2].astype(jnp.bfloat16)
    high_ref[...] = attn_ref[rows // 2 :].astype(jnp.bfloat16)


def attention_forward(packed_word, packed_ent, offsets, heads):
    word_count, packed_width = packed_word.shape
    ent_count = packed_ent.shape[0]
    count = word_count + ent_count
    width = heads * HEAD_DIM
    block = count // 4
    return pl.pallas_call(
        functools.partial(attention_kernel, heads),
        grid=(4,),
        in_specs=[
            pl.BlockSpec((word_count // 4, packed_width), lambda i: (i, 0)),
            pl.BlockSpec((ent_count // 4, packed_width), lambda i: (i, 0)),
            pl.BlockSpec((word_count, packed_width), lambda i: (0, 0)),
            pl.BlockSpec((ent_count, packed_width), lambda i: (0, 0)),
            pl.BlockSpec((1, count), lambda i: (0, 0)),
        ],
        out_specs=[
            pl.BlockSpec((block, width), lambda i: (i, 0)),
            pl.BlockSpec((block // 2, width), lambda i: (i, 0)),
            pl.BlockSpec((block // 2, width), lambda i: (i, 0)),
            pl.BlockSpec((block, 128), lambda i: (i, 0)),
        ],
        out_shape=[
            jax.ShapeDtypeStruct((count, width), jnp.float32),
            jax.ShapeDtypeStruct((count // 2, width), jnp.bfloat16),
            jax.ShapeDtypeStruct((count // 2, width), jnp.bfloat16),
            jax.ShapeDtypeStruct((count, 128), jnp.float32),
        ],
        compiler_params=pltpu.CompilerParams(dimension_semantics=("arbitrary",)),
        cost_estimate=pl.CostEstimate(
            flops=4 * count * count * width,
            bytes_accessed=6 * count * packed_width,
            transcendentals=count * count * heads,
        ),
        name="attention",
    )(packed_word, packed_ent, packed_word, packed_ent, offsets)


def attention_back_kernel(
    heads,
    query_word_ref,
    query_ent_ref,
    key_word_ref,
    key_ent_ref,
    offset_ref,
    attn_ref,
    stat_ref,
    grad_low_ref,
    grad_high_ref,
    d_query_ref,
    d_key_ref,
    sum_ref,
    key_sum,
    value_sum,
):
    width = heads * HEAD_DIM
    word_count = key_word_ref.shape[0]
    words_dev, ents_dev = query_word_ref.shape[0], query_ent_ref.shape[0]
    step = pl.program_id(0)

    @pl.when(step == 0)
    def _():
        key_sum[...] = jnp.zeros_like(key_sum)
        value_sum[...] = jnp.zeros_like(value_sum)
        sum_ref[...] = jnp.zeros_like(sum_ref)

    word_rows = pl.ds(pl.multiple_of(step * words_dev, words_dev), words_dev)
    ent_rows = pl.ds(pl.multiple_of(word_count + step * ents_dev, ents_dev), ents_dev)
    for h in range(heads):
        low, high = h * HEAD_DIM, (h + 1) * HEAD_DIM
        q_word = head_parts(query_word_ref, query_ent_ref, low, high)
        q_ent = head_parts(query_word_ref, query_ent_ref, width + low, width + high)
        k_word = key_word_ref[:, 2 * width + low : 2 * width + high]
        k_ent = key_ent_ref[:, 2 * width + low : 2 * width + high]
        v_word = key_word_ref[:, 3 * width + low : 3 * width + high]
        v_ent = key_ent_ref[:, 3 * width + low : 3 * width + high]
        top = stat_ref[:, h : h + 1]
        inverse = 1.0 / stat_ref[:, heads + h : heads + h + 1]
        grad = head_parts(grad_low_ref, grad_high_ref, low, high)
        delta = jnp.sum(grad * attn_ref[:, low:high], -1, keepdims=True) * inverse
        grad_low = (grad * inverse).astype(jnp.bfloat16)
        w_word = jnp.exp(nt_dot(q_word, k_word) + offset_ref[:, :word_count] - top)
        w_ent = jnp.exp(nt_dot(q_ent, k_ent) + offset_ref[:, word_count:] - top)
        d_word = (w_word * (nt_dot(grad_low, v_word) - delta)).astype(jnp.bfloat16)
        d_ent = (w_ent * (nt_dot(grad_low, v_ent) - delta)).astype(jnp.bfloat16)
        for at, dquery in ((low, mm(d_word, k_word)), (width + low, mm(d_ent, k_ent))):
            dquery = dquery * 0.125
            lanes = slice(at, at + HEAD_DIM)
            d_query_ref[word_rows, lanes] = dquery[:words_dev].astype(jnp.bfloat16)
            d_query_ref[ent_rows, lanes] = dquery[words_dev:].astype(jnp.bfloat16)
            sum_ref[0:1, lanes] += jnp.sum(dquery[:words_dev], 0, keepdims=True)
            sum_ref[1:2, lanes] += jnp.sum(dquery[words_dev:], 0, keepdims=True)
        key_sum[low:high, :word_count] += tn_dot(q_word, d_word)
        key_sum[low:high, word_count:] += tn_dot(q_ent, d_ent)
        value_sum[low:high, :word_count] += tn_dot(grad_low, w_word.astype(jnp.bfloat16))
        value_sum[low:high, word_count:] += tn_dot(grad_low, w_ent.astype(jnp.bfloat16))

    @pl.when(step == pl.num_programs(0) - 1)
    def _():
        dkey = key_sum[...].T
        dvalue = value_sum[...].T
        sum_ref[2:3, :width] = jnp.sum(dvalue, 0, keepdims=True)
        d_key_ref[...] = jnp.concatenate([dkey, dvalue], 1).astype(jnp.bfloat16)


def attention_backward(packed_word, packed_ent, offsets, attn, stats, grads, heads):
    word_count, packed_width = packed_word.shape
    ent_count = packed_ent.shape[0]
    count = word_count + ent_count
    width = heads * HEAD_DIM
    block = count // 4
    return pl.pallas_call(
        functools.partial(attention_back_kernel, heads),
        grid=(4,),
        in_specs=[
            pl.BlockSpec((word_count // 4, packed_width), lambda i: (i, 0)),
            pl.BlockSpec((ent_count // 4, packed_width), lambda i: (i, 0)),
            pl.BlockSpec((word_count, packed_width), lambda i: (0, 0)),
            pl.BlockSpec((ent_count, packed_width), lambda i: (0, 0)),
            pl.BlockSpec((1, count), lambda i: (0, 0)),
            pl.BlockSpec((block, width), lambda i: (i, 0)),
            pl.BlockSpec((block, 128), lambda i: (i, 0)),
            pl.BlockSpec((block // 2, width), lambda i: (i, 0)),
            pl.BlockSpec((block // 2, width), lambda i: (i, 0)),
        ],
        out_specs=[
            pl.BlockSpec((count, 2 * width), lambda i: (0, 0)),
            pl.BlockSpec((count, 2 * width), lambda i: (0, 0)),
            pl.BlockSpec((8, 2 * width), lambda i: (0, 0)),
        ],
        out_shape=[
            jax.ShapeDtypeStruct((count, 2 * width), jnp.bfloat16),
            jax.ShapeDtypeStruct((count, 2 * width), jnp.bfloat16),
            jax.ShapeDtypeStruct((8, 2 * width), jnp.float32),
        ],
        scratch_shapes=[
            pltpu.VMEM((width, count), jnp.float32),
            pltpu.VMEM((width, count), jnp.float32),
        ],
        compiler_params=pltpu.CompilerParams(dimension_semantics=("arbitrary",)),
        cost_estimate=pl.CostEstimate(
            flops=10 * count * count * width,
            bytes_accessed=16 * count * packed_width,
            transcendentals=count * count * heads,
        ),
        name="attention_back",
    )(packed_word, packed_ent, packed_word, packed_ent, offsets, attn, stats, *grads)


def project_grad_kernel(word_count, rows_ref, query_ref, key_ref, grad_ref):
    width = query_ref.shape[1]
    words, ents = rows_ref[:word_count], rows_ref[word_count:]
    for at, value in (
        (0, tn_dot(words, query_ref[:word_count])),
        (width, tn_dot(ents, query_ref[word_count:])),
        (2 * width, tn_dot(words, key_ref[:word_count]) + tn_dot(ents, key_ref[word_count:])),
    ):
        grad_ref[:, at : at + width] = value.astype(jnp.bfloat16)


def project_grad(rows, d_query, d_key, word_count):
    count, model_width = rows.shape
    width = d_query.shape[1]
    lanes = model_width // 3
    return pl.pallas_call(
        functools.partial(project_grad_kernel, word_count),
        grid=(3,),
        in_specs=[
            pl.BlockSpec((count, lanes), lambda i: (0, i)),
            pl.BlockSpec((count, width), lambda i: (0, 0)),
            pl.BlockSpec((count, width), lambda i: (0, 0)),
        ],
        out_specs=pl.BlockSpec((lanes, 3 * width), lambda i: (i, 0)),
        out_shape=jax.ShapeDtypeStruct((model_width, 3 * width), jnp.bfloat16),
        name="project_grad",
    )(rows, d_query, d_key)


def input_grad_kernel(
    query_word_ref, query_ent_ref, key_word_ref, key_ent_ref, word_ref, ent_ref, sent_ref, kept_ref
):
    step = pl.program_id(0)
    width = query_word_ref.shape[1]

    def rows(query_ref, key_ref, weight_ref):
        return nt_dot(query_ref[...], weight_ref[:, :width]) + nt_dot(
            key_ref[...], weight_ref[:, width:]
        )

    words = rows(query_word_ref, key_word_ref, word_ref)
    ents = rows(query_ent_ref, key_ent_ref, ent_ref)
    words_dev = words.shape[0]

    @pl.when(step < 2)
    def _():
        sent_ref[:words_dev] = words.astype(jnp.bfloat16)
        sent_ref[words_dev:] = ents.astype(jnp.bfloat16)

    @pl.when(step >= 2)
    def _():
        kept_ref[:words_dev] = words
        kept_ref[words_dev:] = ents


def input_grad(d_query, d_key, w_word, w_ent, word_count):
    count, width = d_query.shape
    model_width = w_word.shape[0]
    words_dev, ents_dev = word_count // 4, (count - word_count) // 4
    block = words_dev + ents_dev
    first_ent = word_count // ents_dev
    word_spec = pl.BlockSpec((words_dev, width), lambda i: (i, 0))
    ent_spec = pl.BlockSpec((ents_dev, width), lambda i: (first_ent + i, 0))
    weight_spec = pl.BlockSpec(w_word.shape, lambda i: (0, 0))
    return pl.pallas_call(
        input_grad_kernel,
        grid=(4,),
        in_specs=[word_spec, ent_spec, word_spec, ent_spec, weight_spec, weight_spec],
        out_specs=[
            pl.BlockSpec((block, model_width), lambda i: (jnp.minimum(i, 1), 0)),
            pl.BlockSpec((block, model_width), lambda i: (jnp.maximum(i - 2, 0), 0)),
        ],
        out_shape=[
            jax.ShapeDtypeStruct((2 * block, model_width), jnp.bfloat16),
            jax.ShapeDtypeStruct((2 * block, model_width), jnp.float32),
        ],
        name="input_grad",
    )(d_query, d_query, d_key, d_key, w_word, w_ent)


def tall(left):
    return jnp.swapaxes(left, -1, -2)


def halves(array):
    high = array.astype(jnp.bfloat16)
    return high, (array - high.astype(jnp.float32)).astype(jnp.bfloat16)


def stacked_halves(array):
    high = array.astype(jnp.bfloat16).astype(jnp.float32)
    return jnp.concatenate([array, array - high], 0).astype(jnp.bfloat16)


def columns_of(rank_rows):
    return jnp.concatenate(
        [rank_rows, rank_rows - rank_rows.astype(jnp.bfloat16).astype(jnp.float32)], 0
    ).T.astype(jnp.bfloat16)


def left_part(full, columns):
    high, low = halves(full)
    return mm(high, columns) + mm(low, columns)


def rank_first(part):
    both = part.T
    rank = both.shape[0] // 2
    return both[:rank] + both[rank:]


def left_ffn_kernel(
    got_ref, down_ref, err_up_ref, err_down_ref, q_up_ref, q_down_ref, full_up_ref, full_down_ref, left_ref
):
    step = pl.program_id(0)
    width = got_ref.shape[2]
    rows = got_ref.shape[1]
    left = 0.0
    for s in range(4):
        lanes = slice(s * width, (s + 1) * width)
        full = got_ref[s].astype(jnp.float32) + err_up_ref[0, :, lanes]
        full_up_ref[:, lanes] = full
        left = left + left_part(full, columns_of(q_up_ref[:, lanes]))
    left = rank_first(left)
    full = down_ref[...] + err_down_ref[0]
    full_down_ref[...] = full
    below = rank_first(left_part(full, columns_of(q_down_ref[...])))
    for side in (0, 1):

        @pl.when(step == side)
        def _():
            left_ref[0, :, side * rows : (side + 1) * rows] = left
            left_ref[1 + 2 * side] = below[:, : 2 * rows]
            left_ref[2 + 2 * side] = below[:, 2 * rows :]


def left_of_ffn(got_up, grad_down, err_up, err_down, q_up, q_down):
    rows, width = got_up.shape[1:]
    rank = q_up.shape[0]
    return pl.pallas_call(
        left_ffn_kernel,
        grid=(2,),
        in_specs=[
            pl.BlockSpec((4, rows // 2, width), lambda i: (0, i, 0)),
            pl.BlockSpec((2 * rows, width), lambda i: (i, 0)),
            pl.BlockSpec((1, rows // 2, 4 * width), lambda i: (0, i, 0)),
            pl.BlockSpec((1, 2 * rows, width), lambda i: (0, i, 0)),
            pl.BlockSpec((rank, 4 * width), lambda i: (0, 0)),
            pl.BlockSpec((rank, width), lambda i: (0, 0)),
        ],
        out_specs=[
            pl.BlockSpec((rows // 2, 4 * width), lambda i: (i, 0)),
            pl.BlockSpec((2 * rows, width), lambda i: (i, 0)),
            pl.BlockSpec((5, rank, rows), lambda i: (0, 0, 0)),
        ],
        out_shape=[
            jax.ShapeDtypeStruct((rows, 4 * width), jnp.float32),
            jax.ShapeDtypeStruct((4 * rows, width), jnp.float32),
            jax.ShapeDtypeStruct((5, rank, rows), jnp.float32),
        ],
        name="left_ffn",
    )(got_up, grad_down, err_up, err_down, q_up, q_down)


def left_attn_kernel(got_ref, out_ref, err_ref, q_ref, ffn_ref, full_ref, left_ref):
    step = pl.program_id(0)
    rows = full_ref.shape[1]
    part = 2 * rows
    lefts = []
    for j in range(7):
        if j < 6:
            lanes = slice(j * part, (j + 1) * part)
            grad = jnp.concatenate([got_ref[s, :, lanes] for s in range(4)], 1)
            full = grad.astype(jnp.float32) + err_ref[0, j]
        else:
            full = out_ref[...] + err_ref[0, j]
        full_ref[j] = full
        lefts.append(rank_first(left_part(full, columns_of(q_ref[j]))))
    for side in (0, 1):

        @pl.when(step == side)
        def _():
            for j in range(7):
                left_ref[j, :, side * rows : (side + 1) * rows] = lefts[j]

    @pl.when(step == 1)
    def _():
        left_ref[7:] = ffn_ref[...]


def left_of_attn(got, grad_out, err_attn, q_attn, left_ffn):
    rows, width = grad_out.shape
    rank = q_attn.shape[1]
    return pl.pallas_call(
        left_attn_kernel,
        grid=(2,),
        in_specs=[
            pl.BlockSpec((4, rows // 2, got.shape[2]), lambda i: (0, i, 0)),
            pl.BlockSpec((rows // 2, width), lambda i: (i, 0)),
            pl.BlockSpec((1, 7, rows // 2, width), lambda i: (0, 0, i, 0)),
            pl.BlockSpec((7, rank, width), lambda i: (0, 0, 0)),
            pl.BlockSpec((5, rank, rows), lambda i: (0, 0, 0)),
        ],
        out_specs=[
            pl.BlockSpec((7, rows // 2, width), lambda i: (0, i, 0)),
            pl.BlockSpec((12, rank, rows), lambda i: (0, 0, 0)),
        ],
        out_shape=[
            jax.ShapeDtypeStruct((7, rows, width), jnp.float32),
            jax.ShapeDtypeStruct((12, rank, rows), jnp.float32),
        ],
        name="left_attn",
    )(got, grad_out, err_attn, q_attn, left_ffn)


MATRIX_BLOCKS = [[j] for j in range(8)] + [[8, 9, 10, 11]]


def gram_kernel(scale, mine_ref, other_ref, left_ref, gram_ref):
    rank = mine_ref.shape[1]
    left = (mine_ref[...] + other_ref[...]) * scale
    left_ref[...] = left
    lane = lax.broadcasted_iota(jnp.int32, (rank, 128), 1)
    row = lax.broadcasted_iota(jnp.int32, (rank, 128), 0)
    for r in range(rank):
        gram = jnp.where((lane >= len(MATRIX_BLOCKS)) & (row == r), 1.0, 0.0)
        for m, blocks in enumerate(MATRIX_BLOCKS):
            product = sum(left[b] * left[b, r : r + 1] for b in blocks)
            gram = jnp.where(lane == m, jnp.sum(product, -1, keepdims=True), gram)
        gram_ref[r] = gram


def gram_of(mine, other, scale):
    rank = mine.shape[1]
    return pl.pallas_call(
        functools.partial(gram_kernel, scale),
        out_shape=[
            jax.ShapeDtypeStruct(mine.shape, jnp.float32),
            jax.ShapeDtypeStruct((rank, rank, 128), jnp.float32),
        ],
        name="gram",
    )(mine, other)


def inverse_factor(columns, rank):
    row = lax.broadcasted_iota(jnp.int32, columns[0].shape, 0)
    columns, lower = list(columns), []
    for k in range(rank):
        column = columns[k] / jnp.sqrt(columns[k][k : k + 1])
        lower.append(column)
        for c in range(k + 1, rank):
            columns[c] = columns[c] - column * column[c : c + 1]
    inverse = []
    for r in range(rank):
        value = jnp.where(row == r, 1.0, 0.0)
        for t in range(r):
            value = value - lower[t][r : r + 1] * inverse[t]
        inverse.append(value / lower[r][r : r + 1])
    return inverse


def right_part(both_ref, blocks, fulls):
    out = 0.0
    for b, full in zip(blocks, fulls):
        high, low = halves(full)
        out = out + mm(both_ref[b], high) + mm(both_ref[b], low)
    rank = out.shape[0] // 2
    return out[:rank] + out[rank:]


def right_kernel(place_ref, gram_ref, other_ref, left_ref, attn_ref, *refs):
    up_refs, (down_ref, vec_ref, orth_ref) = refs[:4], refs[4:7]
    p_attn_ref, p_up_ref, p_down_ref, sent_ref, kept_ref, both_ref = refs[7:]
    step = pl.program_id(0)
    rank, rows = left_ref.shape[1:]
    chip = place_ref[2]

    @pl.when(step == 0)
    def _():
        inverse = inverse_factor([gram_ref[r] + other_ref[r] for r in range(rank)], rank)
        row = lax.broadcasted_iota(jnp.int32, (rank, rows), 0)
        for m, blocks in enumerate(MATRIX_BLOCKS):
            weights = [inverse[r][:, m : m + 1] for r in range(rank)]
            for b in blocks:
                left = left_ref[b]
                orth = jnp.zeros((rank, rows), jnp.float32)
                for r in range(rank):
                    total = jnp.sum(left * weights[r], 0, keepdims=True)
                    orth = jnp.where(row == r, total, orth)
                orth_ref[b] = orth
                both_ref[b] = stacked_halves(orth)
                if b < 7:
                    p_attn_ref[b] = orth
                elif b == 7:
                    p_up_ref[...] = orth
                else:
                    p_down_ref[:, (b - 8) * rows : (b - 7) * rows] = orth

    parts = [right_part(both_ref, [j], [attn_ref[j]]) for j in range(7)]
    parts += [right_part(both_ref, [7], [up_refs[k][...]]) for k in range(4)]
    parts.append(
        right_part(
            both_ref, [8, 9, 10, 11], [down_ref[k * rows : (k + 1) * rows] for k in range(4)]
        )
    )
    parts += [vec_ref[0], vec_ref[1]]
    for at, ref in enumerate((sent_ref, kept_ref)):

        @pl.when(step == at)
        def _():
            for b, part in enumerate(parts):
                ref[(b // 7) ^ chip, b % 7] = part


def right_of(place, gram, other, left, full_attn, full_up, full_down, vecs):
    rank, rows = left.shape[1:]
    width = full_attn.shape[2]
    lanes = width // 2

    def whole(shape):
        return pl.BlockSpec(shape, lambda i, place: (0,) * len(shape))

    def half(i, place):
        return 1 - place[3] + i * (2 * place[3] - 1)

    def up_spec(k):
        return pl.BlockSpec((rows, lanes), lambda i, place: (0, 2 * k + half(i, place)))

    out_shapes = [
        left.shape,
        (7, rank, rows),
        (rank, rows),
        (rank, 4 * rows),
        (2, 7, rank, lanes),
        (2, 7, rank, lanes),
    ]
    return pl.pallas_call(
        right_kernel,
        grid_spec=pltpu.PrefetchScalarGridSpec(
            num_scalar_prefetch=1,
            grid=(2,),
            in_specs=[
                whole(gram.shape),
                whole(other.shape),
                whole(left.shape),
                pl.BlockSpec((7, rows, lanes), lambda i, place: (0, 0, half(i, place))),
                up_spec(0),
                up_spec(1),
                up_spec(2),
                up_spec(3),
                pl.BlockSpec((4 * rows, lanes), lambda i, place: (0, half(i, place))),
                pl.BlockSpec((2, rank, lanes), lambda i, place: (0, 0, half(i, place))),
            ],
            out_specs=[whole(shape) for shape in out_shapes],
            scratch_shapes=[pltpu.VMEM((12, 2 * rank, rows), jnp.bfloat16)],
        ),
        out_shape=[jax.ShapeDtypeStruct(shape, jnp.float32) for shape in out_shapes],
        name="right",
    )(place, gram, other, left, full_attn, full_up, full_up, full_up, full_up, full_down, vecs)


def left_stack(orth):
    high = orth.astype(jnp.bfloat16).astype(jnp.float32)
    return jnp.concatenate([orth, orth, orth - high, jnp.zeros_like(orth)], 0)


def right_stack(right):
    high = right.astype(jnp.bfloat16).astype(jnp.float32)
    return jnp.concatenate([right, right - high, right, jnp.zeros_like(right)], 0).astype(
        jnp.bfloat16
    )


def update_kernel(rate, rate_vecs, place_ref, orth_ref, mine_ref, other_ref, *refs):
    full_refs, mom_refs, weight_refs = refs[:3], refs[3:7], refs[7:11]
    err_refs, next_refs, new_refs = refs[11:14], refs[14:18], refs[18:22]
    q_attn_ref, q_up_ref, q_down_ref, right_ref, tall_ref, right_rows, cols_rows = refs[22:]
    step = pl.program_id(0)
    rows = full_refs[1].shape[0]
    rank, width = right_ref.shape[1:]
    part = orth_ref.shape[2]
    cols = mom_refs[0].shape[2]
    cols_up = mom_refs[1].shape[1]

    def move(change, at, i, rate=rate):
        value = MOMENTUM * mom_refs[i][at] + change
        next_refs[i][at] = value
        new_refs[i][at] = weight_refs[i][at] - rate * value

    @pl.when(step == 0)
    def _():
        lanes = width // 2
        chip, core = place_ref[2], place_ref[3]
        for own in (0, 1):

            @pl.when(core == own)
            def _():
                for half in (0, 1):
                    blocks = pl.ds((chip ^ half) * 7, 7)
                    right_ref[blocks, :, own * lanes : (own + 1) * lanes] = mine_ref[half]
                    right_ref[blocks, :, (1 - own) * lanes : (2 - own) * lanes] = other_ref[half]

        replica = 2 * place_ref[0] + place_ref[1]
        shift = width - replica * cols
        for b in range(12):
            tall_ref[b] = left_stack(orth_ref[b]).T.astype(jnp.bfloat16)
            right = right_ref[b]
            right_rows[b] = right_stack(right)
            if b < 7 or b == 11:
                own = pltpu.roll(right, shift, 1)[:, :cols]
                cols_rows[min(b, 7)] = right_stack(own)
            if b < 7:
                q_attn_ref[b] = right
            elif b < 11:
                q_up_ref[:, (b - 7) * width : (b - 6) * width] = right
            else:
                q_down_ref[...] = right
        move(right_ref[12], slice(0, rank), 3, rate_vecs)
        move(right_ref[13, : rank - 1], slice(rank, 2 * rank - 1), 3, rate_vecs)

    own = pl.ds(pl.multiple_of(step * rows, 16), rows)
    for j in range(7):
        left = tall_ref[j, own]
        err_refs[0][0, j] = full_refs[0][j] - mm(left, right_rows[j])
        move(mm(left, cols_rows[j]), j, 0)
    left = tall_ref[7, own]
    for k in range(4):
        lanes = slice(k * width, (k + 1) * width)
        err_refs[1][0, :, lanes] = full_refs[1][:, lanes] - mm(left, right_rows[7 + k])
    block = right_rows[7 + place_ref[0]]
    low = mm(left, block[:, :cols_up])
    high = mm(left, block[:, cols_up:])
    side = place_ref[1].astype(jnp.float32)
    move(jnp.where(jnp.full(low.shape, side) == 0.0, low, high), ..., 1)
    err_refs[2][0] = full_refs[2][...] - mm(tall_ref[8 + step], right_rows[11])

    @pl.when(step == 3)
    def _():
        for k in range(4):
            change = tn_dot(cols_rows[7], left_stack(orth_ref[8 + k]).astype(jnp.bfloat16))
            move(change, (slice(None), slice(k * part, (k + 1) * part)), 2)


def updates(place, orth, mine, other, full, mom, weight, rate, rate_vecs):
    rank, part = orth.shape[1:]
    width = full[2].shape[1]
    cols, cols_up = mom[0].shape[2], mom[1].shape[1]
    rows = part // 4

    def whole(array):
        return pl.BlockSpec(array.shape, lambda i: (0,) * array.ndim)

    full_specs = [
        pl.BlockSpec((7, rows, width), lambda i: (0, i, 0)),
        pl.BlockSpec((rows, 4 * width), lambda i: (i, 0)),
        pl.BlockSpec((part, width), lambda i: (i, 0)),
    ]
    own_specs = [
        pl.BlockSpec((7, rows, cols), lambda i: (0, i, 0)),
        pl.BlockSpec((rows, cols_up), lambda i: (i, 0)),
        whole(mom[2]),
        whole(mom[3]),
    ]
    err_specs = [
        pl.BlockSpec((1, 7, rows, width), lambda i: (0, 0, i, 0)),
        pl.BlockSpec((1, rows, 4 * width), lambda i: (0, i, 0)),
        pl.BlockSpec((1, part, width), lambda i: (0, i, 0)),
    ]
    err_shapes = [jax.ShapeDtypeStruct((1,) + array.shape, jnp.float32) for array in full]
    own_shapes = [jax.ShapeDtypeStruct(array.shape, jnp.float32) for array in mom]
    q_shapes = [
        jax.ShapeDtypeStruct(shape, jnp.float32)
        for shape in ((7, rank, width), (rank, 4 * width), (rank, width))
    ]
    outs = pl.pallas_call(
        functools.partial(update_kernel, rate, rate_vecs),
        grid=(4,),
        in_specs=[pl.BlockSpec(memory_space=pltpu.SMEM), whole(orth), whole(mine), whole(other)]
        + full_specs
        + own_specs
        + own_specs,
        out_specs=err_specs + own_specs + own_specs + [whole(shape) for shape in q_shapes],
        out_shape=err_shapes + own_shapes + own_shapes + q_shapes,
        scratch_shapes=[
            pltpu.VMEM((14, rank, width), jnp.float32),
            pltpu.VMEM((12, part, 32), jnp.bfloat16),
            pltpu.VMEM((12, 32, width), jnp.bfloat16),
            pltpu.VMEM((8, 32, cols), jnp.bfloat16),
        ],
        name="updates",
    )(place, orth, mine, other, *full, *mom, *weight)
    return outs[:3], outs[3:7], outs[7:11], outs[11:]


def head_split_device(
    x_words,
    x_ents,
    spans,
    word_mask,
    ent_mask,
    cot_words,
    cot_ents,
    attn_w,
    up_w,
    down_w,
    vecs,
    mom_attn,
    mom_up,
    mom_down,
    mom_vecs,
    err_attn,
    err_up,
    err_down,
    attention_prior_right,
    qf_up,
    qf_down,
):
    low_type = jnp.bfloat16
    words_dev, width = x_words.shape[1:]
    ents_dev = x_ents.shape[1]
    rows_dev = words_dev + ents_dev
    seq_count, rep_count = lax.axis_size("seq"), lax.axis_size("rep")
    seq_index, rep_index = lax.axis_index("seq"), lax.axis_index("rep")
    heads = HEADS // seq_count
    part = width // seq_count
    word_count = words_dev * seq_count
    ent_count = ents_dev * seq_count
    cols = attn_w.shape[2]
    cols_up = up_w.shape[1]
    hidden = cols_up * rep_count
    hidden_part = hidden // seq_count

    core, chip = seq_index % 2, seq_index // 2
    place = jnp.stack([rep_index // 2, rep_index % 2, chip, core]).astype(jnp.int32)
    block = part // 2
    project_piece = jnp.transpose(
        attn_w[:6].astype(low_type).reshape(6, 2, block, cols), (2, 1, 0, 3)
    ).reshape(block, 12 * cols)
    out_piece = attn_w[6].astype(low_type).T
    half = block // 2
    first, second = [
        jnp.concatenate([planes_swap(project_piece[rows]), out_piece[rows]], 1)
        for rows in (slice(half), slice(half, block))
    ]
    trees = [gather_tree(first)]
    second, unused_far = lax.optimization_barrier((second, trees[0][2]))
    trees.append(gather_tree(second))
    up_piece = jnp.transpose(
        up_w.astype(low_type).reshape(2, block, cols_up), (1, 0, 2)
    ).reshape(block, 2 * cols_up)
    up_piece = tie(up_piece, trees[0][2])
    ffn_piece = jnp.concatenate([planes_swap(up_piece), down_w.astype(low_type).T], 1)
    ffn_piece, unused_near = lax.optimization_barrier((ffn_piece, (trees[0][4], trees[1][4])))
    ffn_pieces, ffn_side = gather_direct(ffn_piece)

    spans, unused_piece = lax.optimization_barrier((spans, project_piece))
    inputs = jnp.concatenate([x_words[0], x_ents[0] + span_mean_closed(spans[0], width)], 0)
    live = jnp.concatenate([word_mask[0], ent_mask[0]], 0).astype(low_type)
    live = jnp.pad(live.reshape(1, rows_dev), ((0, 15), (0, width - rows_dev)))
    pieces = gather_seq(jnp.concatenate([inputs.astype(low_type), live], 0))
    lives = [piece[rows_dev, :rows_dev] for piece in pieces]
    lives = [piece[:words_dev] for piece in lives] + [piece[words_dev:] for piece in lives]
    offsets = ((jnp.concatenate(lives).astype(jnp.float32) - 1.0) * MASK_FILL).reshape(1, -1)

    own_vecs = lax.dynamic_slice_in_dim(vecs, seq_index * part, part, 1)
    none = jnp.zeros((part,), jnp.float32)
    scale = jnp.where(jnp.arange(4 * part) < 2 * part, 0.125, 1.0).astype(jnp.float32)
    bias_word = jnp.concatenate([own_vecs[0], own_vecs[1], none, own_vecs[4]])
    bias_ent = jnp.concatenate([own_vecs[2], own_vecs[3], none, own_vecs[4]])
    in_vmem = pl.BlockSpec(memory_space=pltpu.VMEM)
    w_word, w_ent, packed_word, packed_ent, rows_low, w_out = pl.pallas_call(
        functools.partial(project_kernel, words_dev, rows_dev),
        in_specs=[pl.BlockSpec(memory_space=pltpu.SMEM)] + [in_vmem] * 19,
        out_specs=[in_vmem] * 6,
        out_shape=[
            jax.ShapeDtypeStruct(shape, low_type)
            for shape in [
                (rows, width)
                for rows in (width, width, word_count, ent_count, word_count + ent_count)
            ]
            + [(width, part)]
        ],
        scratch_shapes=[pltpu.VMEM((2, 4, 2, half, 14 * cols), low_type)],
        name="project",
    )(
        place,
        bias_word.reshape(1, -1),
        bias_ent.reshape(1, -1),
        scale.reshape(1, -1),
        *trees[0],
        *trees[1],
        *pieces,
    )
    attn, *attn_low, stats = attention_forward(packed_word, packed_ent, offsets, heads)
    attn_low[1], ffn_pieces, ffn_side = lax.optimization_barrier(
        (attn_low[1], ffn_pieces, ffn_side)
    )
    ffn_sides = [ffn_side] + [rep_swap(piece, 1) for piece in ffn_pieces[1:]]
    w_up, w_down = join_call(
        ffn_join_kernel,
        place,
        ffn_pieces + ffn_sides,
        [(width, hidden_part), (width, hidden_part)],
        "join_ffn",
    )

    bias_up = lax.dynamic_slice_in_dim(
        vecs[11:15].reshape(hidden), seq_index * hidden_part, hidden_part, 0
    )
    grad_result = jnp.concatenate([cot_words[0], cot_ents[0]], 0)
    split = rows_dev // 2
    ats = [slice(c * split, (c + 1) * split) for c in (0, 1)]
    parts = [{}, {}]

    def gather(part, rows):
        part["own"] = rows.astype(low_type)
        part["core"], part["far"] = seq_swap(part["own"], 1), seq_swap(part["own"], 2)
        return part["own"]

    def gathered(part, mark):
        far = tie(part["far"], mark)
        return jnp.concatenate([part["core"], seq_swap(far, 1), part["own"], far], 0)

    def scatter(part, rows, weight):
        sent, part["own"], part["far"] = scatter_blocks(rows, nt_dot, weight)
        return sent

    def scattered(part, mark):
        return part["own"] + tie(part["far"], mark).astype(jnp.float32)

    def out_stage(part, c, mark):
        rows = attn_low[c] if mark is None else tie(attn_low[c], mark)
        return scatter(part, rows, w_out)

    def mid_stage(part, c, mark):
        branch = scattered(part, mark) + vecs[5]
        part["mid"], *part["one"] = rows_norm(inputs[ats[c]] + branch, vecs[7], vecs[8])
        return gather(part, part["mid"])

    def up_stage(part, c, mark):
        part["mid_low"] = gathered(part, mark)
        part["pre"] = mm(part["mid_low"], w_up) + bias_up
        part["cdf"] = 0.5 * (1.0 + lax.erf(part["pre"] * math.sqrt(0.5)))
        part["act"] = (part["pre"] * part["cdf"]).astype(low_type)
        return scatter(part, part["act"], w_down)

    def result_stage(part, c, mark):
        ffn = scattered(part, mark) + vecs[6]
        part["result"], *two = rows_norm(part["mid"] + ffn, vecs[9], vecs[10])
        grad, *part["sums_two"] = rows_norm_back(grad_result[ats[c]], *two, vecs[9])
        part["grad_two"] = grad
        return gather(part, grad)

    def down_stage(part, c, mark):
        part["grad_ffn"] = gathered(part, mark)
        pre = part["pre"]
        density = jnp.exp(-0.5 * pre * pre) * (1.0 / math.sqrt(2.0 * math.pi))
        part["grad_pre"] = mm(part["grad_ffn"], w_down) * (part["cdf"] + pre * density)
        part["grad_pre_low"] = part["grad_pre"].astype(low_type)
        return scatter(part, part["grad_pre_low"], w_up)

    def norm_stage(part, c, mark):
        grad = part["grad_two"] + scattered(part, mark)
        part["grad_one"], *part["sums_one"] = rows_norm_back(grad, *part["one"], vecs[7])
        return gather(part, part["grad_one"])

    def branch_stage(part, c, mark):
        part["grad_branch"] = gathered(part, mark)
        part["grad_attn"] = mm(part["grad_branch"], w_out)
        return part["grad_branch"]

    mark = None
    for stage in (
        out_stage,
        mid_stage,
        up_stage,
        result_stage,
        down_stage,
        norm_stage,
        branch_stage,
    ):
        for c, chunk in enumerate(parts):
            mark = stage(chunk, c, mark)
    results, grads_one, grads_attn = [
        [part[name] for part in parts] for name in ("result", "grad_one", "grad_attn")
    ]
    kept = [
        [part[name] for name in ("mid_low", "act", "grad_ffn", "grad_pre_low", "grad_branch")]
        for part in parts
    ]
    sums = [
        sum(values)
        for values in zip(
            *[
                [jnp.sum(part["grad_one"], 0), jnp.sum(part["grad_two"], 0)]
                + part["sums_one"]
                + part["sums_two"]
                + [jnp.sum(part["grad_pre"], 0)]
                for part in parts
            ]
        )
    ]
    result = jnp.concatenate(results, 0)
    grad_one = jnp.concatenate(grads_one, 0)
    grad_up = sum(tn_dot(mid_low, grad_pre_low) for mid_low, _, _, grad_pre_low, _ in kept)
    grad_up, unused_branch = lax.optimization_barrier((grad_up.astype(low_type), kept[1][4]))
    got_up = lax.all_to_all(grad_up.reshape(seq_count, part, hidden_part), "seq", 0, 0)
    grad_out = sum(tn_dot(low, parts[4]) for low, parts in zip(attn_low, kept))
    d_query, d_key, d_sums = attention_backward(
        packed_word, packed_ent, offsets, attn, stats, grads_attn, heads
    )
    d_query, got_up = lax.optimization_barrier((d_query, got_up))
    grad_down = sum(
        tn_dot(act_low, tie(grad_ffn, d_sums)) for _, act_low, grad_ffn, _, _ in kept
    )
    grad_project = project_grad(rows_low, d_query, d_key, word_count)
    got_project = lax.all_to_all(
        grad_project.reshape(seq_count, part, 6 * part), "seq", 0, 0
    )
    full_up, full_down, left_ffn = left_of_ffn(
        got_up, grad_down, err_up, err_down, qf_up.T, qf_down.T
    )
    sent_inputs, own_inputs = input_grad(
        d_query, tie(d_key, grad_project[:16, :128]), w_word, w_ent, word_count
    )
    own_inputs = own_inputs + seq_swap(sent_inputs, 1).astype(jnp.float32)
    own_inputs, sent_inputs = own_inputs[:rows_dev], own_inputs[rows_dev:].astype(low_type)

    vec_grad = jnp.zeros((15, width), jnp.float32)
    bias_query = jnp.concatenate(
        [d_sums[0].reshape(2, part), d_sums[1].reshape(2, part), d_sums[2, :part].reshape(1, part)], 0
    )
    vec_grad = lax.dynamic_update_slice(vec_grad, bias_query, (0, seq_index * part))
    vec_grad = lax.dynamic_update_slice(vec_grad, jnp.stack(sums[:6]), (5, 0))
    bias_rows = hidden_part // width
    vec_grad = lax.dynamic_update_slice(
        vec_grad, sums[6].reshape(bias_rows, width), (11 + seq_index * bias_rows, 0)
    )

    full_attn, left = left_of_attn(
        got_project, grad_out, err_attn, tall(attention_prior_right), left_ffn
    )
    left, sent_inputs = lax.optimization_barrier((left, sent_inputs))
    got_inputs = seq_swap(sent_inputs, 2)
    for bits in (1, 2):
        left = left + rep_swap(left, bits)
    left, got_inputs = lax.optimization_barrier((left, got_inputs))
    left, gram = gram_of(left, rep_swap(left, 4), 1.0 / rep_count)
    gram = gram + seq_swap(gram, 1)
    rows_vec = jnp.pad(vec_grad, ((0, 1), (0, 0))).reshape(2, 8, width)
    orth, p_attn, p_up, p_down, sent, kept = right_of(
        place, gram, seq_swap(gram, 2), left, full_attn, full_up, full_down, rows_vec
    )
    got_inputs, unused_orth = lax.optimization_barrier((got_inputs, orth))
    grad_inputs = grad_one + (own_inputs + got_inputs.astype(jnp.float32))
    kept = kept + seq_swap(sent, 1)
    kept = kept[0] + seq_swap(kept[1], 2)
    for bits in (1, 2, 4):
        kept = kept + rep_swap(kept, bits)
    kept = kept / rep_count
    kept = jnp.stack([kept, seq_swap(kept, 2)])
    lr_mat = 1.5 * math.sqrt(rep_count / (SEQS * (WORDS + ENTS)))
    lr_vec = 0.2 * math.sqrt(rep_count / (SEQS * (WORDS + ENTS)))
    next_err, next_mom, new, (q_attn, q_up, q_down) = updates(
        place,
        orth,
        kept,
        seq_swap(kept, 1),
        (full_attn, full_up, full_down),
        (mom_attn, mom_up, mom_down.T, mom_vecs),
        (attn_w, up_w, down_w.T, vecs),
        lr_mat,
        lr_vec,
    )
    return (
        result[None, :words_dev],
        result[None, words_dev:],
        grad_inputs[None, :words_dev],
        grad_inputs[None, words_dev:],
        new[0],
        new[1],
        new[2].T,
        new[3],
        next_mom[0],
        next_mom[1],
        next_mom[2].T,
        next_mom[3],
        next_err[0],
        next_err[1],
        next_err[2],
        tall(p_attn),
        tall(p_up),
        tall(p_down),
        tall(q_attn),
        tall(q_up),
        tall(q_down),
    )


def solution(mesh):
    in_specs = (
        P("rep", "seq", None),
        P("rep", "seq", None),
        P("rep", "seq", None),
        P("rep", "seq"),
        P("rep", "seq"),
        P("rep", "seq", None),
        P("rep", "seq", None),
        P(None, "seq", "rep"),
        P("seq", "rep"),
        P("seq", "rep"),
        P(),
        P(None, "seq", "rep"),
        P("seq", "rep"),
        P("seq", "rep"),
        P(),
        P("rep", None, "seq", None),
        P("rep", "seq", None),
        P("rep", "seq", None),
        P(),
        P(),
        P(),
    )
    out_specs = (
        P("rep", "seq", None),
        P("rep", "seq", None),
        P("rep", "seq", None),
        P("rep", "seq", None),
        P(None, "seq", "rep"),
        P("seq", "rep"),
        P("seq", "rep"),
        P(),
        P(None, "seq", "rep"),
        P("seq", "rep"),
        P("seq", "rep"),
        P(),
        P("rep", None, "seq", None),
        P("rep", "seq", None),
        P("rep", "seq", None),
        P(None, "seq", None),
        P("seq", None),
        P("seq", None),
        P(),
        P(),
        P(),
    )
    seqs, reps = mesh.shape["seq"], mesh.shape["rep"]
    split_heads = seqs == 4 and reps == 2 * seqs and HEADS % seqs == 0
    body = head_split_device if split_heads else on_device
    return jax.shard_map(
        body, mesh=mesh, in_specs=in_specs, out_specs=out_specs, check_vma=False
    )
```

```python
import functools
import math

import jax
import jax.numpy as jnp
from jax import lax
from jax.experimental import pallas as pl
from jax.experimental.pallas import tpu as pltpu
from jax.sharding import PartitionSpec as P

HEADS = 12
WORDS = 1024
ENTS = 128
SPAN = 16
SEQS = 1


HIGH_PRECISION = lax.Precision.HIGHEST
EPS = 1e-05
MASK_FILL = 30000.0
MOMENTUM = 0.9


def span_mean(spans, model_width):
    starts = spans[..., 0]
    finals = spans[..., 1]
    lengths = (finals - starts + 1).astype(jnp.float32)
    offsets = jnp.arange(SPAN, dtype=jnp.int32)
    places = (starts[..., None] + offsets).astype(jnp.float32)
    shares = (offsets <= (finals - starts)[..., None]).astype(jnp.float32) / lengths[..., None]
    half_width = model_width // 2
    rates = jnp.exp(
        jnp.arange(half_width).astype(jnp.float32) * (-2.0 * math.log(10000.0) / model_width)
    )
    angles = places[..., None] * rates
    table = jnp.concatenate([jnp.sin(angles), jnp.cos(angles)], -1)
    return jnp.sum(table * shares[..., None], axis=-2)


def span_mean_closed(spans, model_width):
    lengths = (spans[..., 1] - spans[..., 0] + 1).astype(jnp.float32)[..., None]
    middles = (spans[..., 1] + spans[..., 0]).astype(jnp.float32)[..., None]
    half_rates = 0.5 * jnp.exp(
        jnp.arange(model_width // 2).astype(jnp.float32) * (-2.0 * math.log(10000.0) / model_width)
    )
    share = jnp.sin(lengths * half_rates) / (lengths * jnp.sin(half_rates))
    angles = middles * half_rates
    return jnp.concatenate([share * jnp.sin(angles), share * jnp.cos(angles)], -1)


def layer_norm(hidden, gain, shift):
    center = hidden - jnp.mean(hidden, -1, keepdims=True)
    rstd = lax.rsqrt(jnp.mean(center * center, -1, keepdims=True) + EPS)
    normed = center * rstd
    return (normed * gain + shift, normed, rstd)


def norm_back(grad, normed, rstd, gain):
    dnormed = grad * gain
    grad_in = rstd * (
        dnormed
        - jnp.mean(dnormed, -1, keepdims=True)
        - normed * jnp.mean(dnormed * normed, -1, keepdims=True)
    )
    return (grad_in, jnp.sum(grad * normed, axis=(0, 1)), jnp.sum(grad, axis=(0, 1)))


def gelu_exact(value):
    return jax.nn.gelu(value, approximate=False)


def project(row_entries, weight_matrix):
    return jnp.einsum("thq,qo->tho", row_entries, weight_matrix, preferred_element_type=jnp.float32)


def project_back(row_entries, weight_matrix):
    return jnp.einsum("hpf,zf->hpz", row_entries, weight_matrix, preferred_element_type=jnp.float32)


def weight_grad(input_arrays, gradient_list):
    return jnp.einsum(
        "cev,ceg->vg", input_arrays, gradient_list, preferred_element_type=jnp.float32
    )


def split_keys(pieces, words_dev, ents_dev, head_count):
    key_piece, live_piece = pieces
    batch_rows = key_piece.shape[0]
    both = key_piece.shape[2]
    model_width = both // 2
    head_dim = model_width // head_count
    rows_dev = words_dev + ents_dev
    blocks = key_piece.shape[1] // rows_dev
    grouped = key_piece.reshape(batch_rows, blocks, rows_dev, both)
    live_grouped = live_piece.reshape(batch_rows, blocks, rows_dev)
    word_part = grouped[:, :, :words_dev].reshape(batch_rows, blocks * words_dev, both)
    ent_part = grouped[:, :, words_dev:].reshape(batch_rows, blocks * ents_dev, both)
    keys_word = word_part[..., :model_width].reshape(batch_rows, -1, head_count, head_dim)
    keys_ent = ent_part[..., :model_width].reshape(batch_rows, -1, head_count, head_dim)
    values = jnp.concatenate(
        [word_part[..., model_width:], ent_part[..., model_width:]], 1
    ).reshape(batch_rows, -1, head_count, head_dim)
    live = jnp.concatenate(
        [
            live_grouped[:, :, :words_dev].reshape(batch_rows, -1),
            live_grouped[:, :, words_dev:].reshape(batch_rows, -1),
        ],
        1,
    )
    offsets = (live.astype(jnp.float32) - 1.0) * MASK_FILL
    return (keys_word, keys_ent, values, offsets, blocks)


def score_block(query_word, query_ent, keys_word, keys_ent, offsets):
    score_word = jnp.einsum(
        "sqhd,skhd->shqk", query_word, keys_word, preferred_element_type=jnp.float32
    )
    score_ent = jnp.einsum(
        "sqhd,skhd->shqk", query_ent, keys_ent, preferred_element_type=jnp.float32
    )
    return jnp.concatenate([score_word, score_ent], -1) + offsets[:, None, None, :]


def flat_heads(array):
    return array.reshape(array.shape[0], array.shape[1], -1)


def join_rows(grad_keys_word, grad_keys_ent, grad_values, blocks, words_dev, ents_dev):
    batch_rows = grad_keys_word.shape[0]
    word_count = grad_keys_word.shape[1]
    word_rows = jnp.concatenate(
        [flat_heads(grad_keys_word), flat_heads(grad_values[:, :word_count])], -1
    )
    ent_rows = jnp.concatenate(
        [flat_heads(grad_keys_ent), flat_heads(grad_values[:, word_count:])], -1
    )
    word_rows = word_rows.reshape(batch_rows, blocks, words_dev, -1)
    ent_rows = ent_rows.reshape(batch_rows, blocks, ents_dev, -1)
    return jnp.concatenate([word_rows, ent_rows], 2).reshape(
        batch_rows, blocks * (words_dev + ents_dev), -1
    )


def from_gram(left, gram):
    lower = jnp.linalg.cholesky(gram)
    return jax.scipy.linalg.solve_triangular(lower, left.T, lower=True).T


def orthonormal(left):
    return from_gram(left, jnp.dot(left.T, left, precision=HIGH_PRECISION))


def on_device(
    x_words,
    x_ents,
    spans,
    word_mask,
    ent_mask,
    cot_words,
    cot_ents,
    attn_w,
    up_w,
    down_w,
    vecs,
    mom_attn,
    mom_up,
    mom_down,
    mom_vecs,
    err_attn,
    err_up,
    err_down,
    attention_prior_right,
    qf_up,
    qf_down,
):
    batch_rows, words_dev, model_width = x_words.shape
    ents_dev = x_ents.shape[1]
    rows_dev = words_dev + ents_dev
    head_count = HEADS
    head_dim = model_width // head_count
    hidden_width = up_w.shape[1] * lax.axis_size("rep")
    seq_count = lax.axis_size("seq")
    rep_count = lax.axis_size("rep")
    seq_index = lax.axis_index("seq")
    rep_index = lax.axis_index("rep")
    lowered = jnp.bfloat16
    column_parts = (
        lax.all_gather(attn_w.astype(lowered), "rep", axis=2, tiled=True),
        lax.all_gather(up_w.astype(lowered), "rep", axis=1, tiled=True),
        lax.all_gather(down_w.astype(lowered), "rep", axis=1, tiled=True),
    )
    w_attn, w_up, w_down = (
        lax.all_gather(column_parts[0], "seq", axis=1, tiled=True),
        lax.all_gather(column_parts[1], "seq", axis=0, tiled=True),
        lax.all_gather(column_parts[2], "seq", axis=0, tiled=True),
    )
    input_arrays = jnp.concatenate([x_words, x_ents + span_mean(spans, model_width)], 1)
    inputs_low = input_arrays.astype(lowered)
    word_low = inputs_low[:, :words_dev]
    ent_low = inputs_low[:, words_dev:]
    query_word = (
        jnp.concatenate(
            [project(word_low, w_attn[0]) + vecs[0], project(ent_low, w_attn[2]) + vecs[2]], 1
        )
        * 0.125
    ).astype(lowered)
    query_ent = (
        jnp.concatenate(
            [project(word_low, w_attn[1]) + vecs[1], project(ent_low, w_attn[3]) + vecs[3]], 1
        )
        * 0.125
    ).astype(lowered)
    keys_low = project(inputs_low, w_attn[4]).astype(lowered)
    values_low = (project(inputs_low, w_attn[5]) + vecs[4]).astype(lowered)
    key_rows = jnp.concatenate([keys_low, values_low], -1)
    key_live = jnp.concatenate([word_mask, ent_mask], 1).astype(lowered)
    heads_word = query_word.reshape(batch_rows, rows_dev, head_count, head_dim)
    heads_ent = query_ent.reshape(batch_rows, rows_dev, head_count, head_dim)
    forward_row_top = jnp.full((batch_rows, head_count, rows_dev), -jnp.inf, jnp.float32)
    row_total = jnp.zeros((batch_rows, head_count, rows_dev), jnp.float32)
    weighted = jnp.zeros((batch_rows, rows_dev, head_count, head_dim), jnp.float32)
    keys_word, keys_ent, values, offsets, blocks = split_keys(
        (
            lax.all_gather(key_rows, "seq", axis=1, tiled=True),
            lax.all_gather(key_live, "seq", axis=1, tiled=True),
        ),
        words_dev,
        ents_dev,
        head_count,
    )
    scores = score_block(heads_word, heads_ent, keys_word, keys_ent, offsets)
    new_top = jnp.max(scores, -1)
    factor = jnp.exp(forward_row_top - new_top)
    weights = jnp.exp(scores - new_top[..., None])
    row_total = row_total * factor + jnp.sum(weights, -1)
    weighted = weighted * jnp.transpose(factor, (0, 2, 1))[..., None] + jnp.einsum(
        "shqk,skhd->sqhd", weights.astype(lowered), values, preferred_element_type=jnp.float32
    )
    row_top, row_total, weighted = (new_top, row_total, weighted)
    total_rows = jnp.transpose(row_total, (0, 2, 1))[..., None]
    attn = weighted / total_rows
    attn_low = attn.reshape(batch_rows, rows_dev, model_width).astype(lowered)
    branch = project(attn_low, w_attn[6]) + vecs[5]
    mid, normed_one, rstd_one = layer_norm(input_arrays + branch, vecs[7], vecs[8])
    mid_low = mid.astype(lowered)
    pre = project(mid_low, w_up) + vecs[11:15].reshape(hidden_width)
    act_low = gelu_exact(pre).astype(lowered)
    ffn = project(act_low, w_down) + vecs[6]
    result, normed_two, rstd_two = layer_norm(mid + ffn, vecs[9], vecs[10])
    grad_result = jnp.concatenate([cot_words, cot_ents], 1)
    grad_two, gain_two, shift_two = norm_back(grad_result, normed_two, rstd_two, vecs[9])
    bias_down = jnp.sum(grad_two, axis=(0, 1))
    grad_ffn_low = grad_two.astype(lowered)
    grad_down = weight_grad(act_low, grad_ffn_low)
    grad_act = project_back(grad_ffn_low, w_down)
    unused_value, gelu_pull = jax.vjp(gelu_exact, pre)
    grad_pre = gelu_pull(grad_act)[0]
    bias_up = jnp.sum(grad_pre, axis=(0, 1))
    grad_pre_low = grad_pre.astype(lowered)
    grad_up = weight_grad(mid_low, grad_pre_low)
    grad_mid = grad_two + project_back(grad_pre_low, w_up)
    grad_one, gain_one, shift_one = norm_back(grad_mid, normed_one, rstd_one, vecs[7])
    bias_out = jnp.sum(grad_one, axis=(0, 1))
    grad_branch_low = grad_one.astype(lowered)
    grad_out_proj = weight_grad(attn_low, grad_branch_low)
    grad_attn = project_back(grad_branch_low, w_attn[6]).reshape(
        batch_rows, rows_dev, head_count, head_dim
    )
    grad_unnorm = (grad_attn / total_rows).astype(lowered)
    delta_rows = jnp.transpose(jnp.sum(grad_attn * attn, -1), (0, 2, 1)) / row_total
    keys_word, keys_ent, values, offsets, blocks = split_keys(
        (
            lax.all_gather(key_rows, "seq", axis=1, tiled=True),
            lax.all_gather(key_live, "seq", axis=1, tiled=True),
        ),
        words_dev,
        ents_dev,
        head_count,
    )
    scores = score_block(heads_word, heads_ent, keys_word, keys_ent, offsets)
    weights = jnp.exp(scores - row_top[..., None])
    grad_weights = jnp.einsum(
        "sqhd,skhd->shqk", grad_unnorm, values, preferred_element_type=jnp.float32
    )
    grad_scores = (weights * (grad_weights - delta_rows[..., None])).astype(lowered)
    word_count = keys_word.shape[1]
    scores_word = grad_scores[..., :word_count]
    scores_ent = grad_scores[..., word_count:]
    grad_query_word = jnp.einsum(
        "shqk,skhd->sqhd", scores_word, keys_word, preferred_element_type=jnp.float32
    )
    grad_query_ent = jnp.einsum(
        "shqk,skhd->sqhd", scores_ent, keys_ent, preferred_element_type=jnp.float32
    )
    grad_keys_word = jnp.einsum(
        "shqk,sqhd->skhd", scores_word, heads_word, preferred_element_type=jnp.float32
    )
    grad_keys_ent = jnp.einsum(
        "shqk,sqhd->skhd", scores_ent, heads_ent, preferred_element_type=jnp.float32
    )
    grad_values = jnp.einsum(
        "shqk,sqhd->skhd", weights.astype(lowered), grad_unnorm, preferred_element_type=jnp.float32
    )
    piece_grad = join_rows(grad_keys_word, grad_keys_ent, grad_values, blocks, words_dev, ents_dev)
    grad_rows = piece_grad
    grad_query_word, grad_query_ent, grad_rows = (grad_query_word, grad_query_ent, grad_rows)
    own_rows = lax.psum_scatter(
        grad_rows.astype(jnp.bfloat16), "seq", scatter_dimension=1, tiled=True
    ).astype(jnp.float32)
    grad_keys = own_rows[..., :model_width]
    grad_values = own_rows[..., model_width:]
    bias_values = jnp.sum(grad_values, axis=(0, 1))
    keys_grad_low = grad_keys.astype(lowered)
    values_grad_low = grad_values.astype(lowered)
    grad_key_w = weight_grad(inputs_low, keys_grad_low)
    grad_value_w = weight_grad(inputs_low, values_grad_low)
    inner_word = grad_query_word.reshape(batch_rows, rows_dev, model_width) * 0.125
    inner_ent = grad_query_ent.reshape(batch_rows, rows_dev, model_width) * 0.125
    bias_query = [
        jnp.sum(inner_word[:, :words_dev], axis=(0, 1)),
        jnp.sum(inner_ent[:, :words_dev], axis=(0, 1)),
        jnp.sum(inner_word[:, words_dev:], axis=(0, 1)),
        jnp.sum(inner_ent[:, words_dev:], axis=(0, 1)),
    ]
    inner_word_low = inner_word.astype(lowered)
    inner_ent_low = inner_ent.astype(lowered)
    grad_query_mats = [
        weight_grad(word_low, inner_word_low[:, :words_dev]),
        weight_grad(word_low, inner_ent_low[:, :words_dev]),
        weight_grad(ent_low, inner_word_low[:, words_dev:]),
        weight_grad(ent_low, inner_ent_low[:, words_dev:]),
    ]
    back_keys = project_back(keys_grad_low, w_attn[4]) + project_back(values_grad_low, w_attn[5])
    back_word = project_back(inner_word_low[:, :words_dev], w_attn[0]) + project_back(
        inner_ent_low[:, :words_dev], w_attn[1]
    )
    back_ent = project_back(inner_word_low[:, words_dev:], w_attn[2]) + project_back(
        inner_ent_low[:, words_dev:], w_attn[3]
    )
    grad_inputs = grad_one + back_keys + jnp.concatenate([back_word, back_ent], 1)
    grad_attn_w = jnp.stack(grad_query_mats + [grad_key_w, grad_value_w, grad_out_proj])
    vec_grad = jnp.concatenate(
        [
            jnp.stack(
                bias_query
                + [bias_values, bias_out, bias_down, gain_one, shift_one, gain_two, shift_two]
            ),
            bias_up.reshape(4, model_width),
        ],
        0,
    )
    rows_attn, rows_up, rows_down = (
        lax.psum_scatter(
            grad_attn_w.astype(jnp.bfloat16), "seq", scatter_dimension=1, tiled=True
        ).astype(jnp.float32),
        lax.psum_scatter(
            grad_up.astype(jnp.bfloat16), "seq", scatter_dimension=0, tiled=True
        ).astype(jnp.float32),
        lax.psum_scatter(
            grad_down.astype(jnp.bfloat16), "seq", scatter_dimension=0, tiled=True
        ).astype(jnp.float32),
    )
    attention_full_gradient = rows_attn + err_attn[0]
    full_up = rows_up + err_up[0]
    full_down = rows_down + err_down[0]
    attention_left_factor = jnp.einsum(
        "vcg,vgo->vco", attention_full_gradient, attention_prior_right, precision=HIGH_PRECISION
    )
    left_up = jnp.dot(full_up, qf_up, precision=HIGH_PRECISION)
    left_down = jnp.dot(full_down, qf_down, precision=HIGH_PRECISION)
    count_attn = attention_full_gradient.shape[1]
    count_up = full_up.shape[0]
    count_down = full_down.shape[0]
    placed_attn = lax.dynamic_update_slice_in_dim(
        jnp.zeros((7, count_attn * seq_count, attention_left_factor.shape[2]), jnp.float32),
        attention_left_factor,
        seq_index * count_attn,
        1,
    )
    placed_up = lax.dynamic_update_slice_in_dim(
        jnp.zeros((count_up * seq_count, left_up.shape[1]), jnp.float32),
        left_up,
        seq_index * count_up,
        0,
    )
    placed_down = lax.dynamic_update_slice_in_dim(
        jnp.zeros((count_down * seq_count, left_down.shape[1]), jnp.float32),
        left_down,
        seq_index * count_down,
        0,
    )
    summed_attn, summed_up, summed_down = lax.psum(
        (placed_attn, placed_up, placed_down), ("seq", "rep")
    )
    orth_attn = jax.vmap(orthonormal)(summed_attn / rep_count)
    orth_up = orthonormal(summed_up / rep_count)
    orth_down = orthonormal(summed_down / rep_count)
    attention_local_gradient = lax.dynamic_slice_in_dim(
        orth_attn, seq_index * count_attn, count_attn, 1
    )
    own_up = lax.dynamic_slice_in_dim(orth_up, seq_index * count_up, count_up, 0)
    own_down = lax.dynamic_slice_in_dim(orth_down, seq_index * count_down, count_down, 0)
    right_parts = (
        jnp.einsum(
            "dpl,dpg->dgl",
            attention_local_gradient,
            attention_full_gradient,
            precision=HIGH_PRECISION,
        ),
        jnp.dot(full_up.T, own_up, precision=HIGH_PRECISION),
        jnp.dot(full_down.T, own_down, precision=HIGH_PRECISION),
        vec_grad,
    )
    attention_right_factor, right_up, right_down, vec_total = lax.psum(
        (right_parts[0], right_parts[1], right_parts[2], right_parts[3]), ("seq", "rep")
    )
    attention_right_factor = attention_right_factor / rep_count
    right_up = right_up / rep_count
    right_down = right_down / rep_count
    vec_mean = vec_total / rep_count
    attention_estimate = jnp.einsum(
        "whg,wng->whn", attention_local_gradient, attention_right_factor, precision=HIGH_PRECISION
    )
    approx_up = jnp.dot(own_up, right_up.T, precision=HIGH_PRECISION)
    approx_down = jnp.dot(own_down, right_down.T, precision=HIGH_PRECISION)
    next_err_attn = (attention_full_gradient - attention_estimate)[None]
    next_err_up = (full_up - approx_up)[None]
    next_err_down = (full_down - approx_down)[None]
    cols_attn = attn_w.shape[2]
    cols_up = up_w.shape[1]
    cols_down = down_w.shape[1]
    step_attn = lax.dynamic_slice_in_dim(attention_estimate, rep_index * cols_attn, cols_attn, 2)
    step_up = lax.dynamic_slice_in_dim(approx_up, rep_index * cols_up, cols_up, 1)
    step_down = lax.dynamic_slice_in_dim(approx_down, rep_index * cols_down, cols_down, 1)
    lr_mat = 1.5 * math.sqrt(rep_count / (SEQS * (WORDS + ENTS)))
    lr_vec = 0.2 * math.sqrt(rep_count / (SEQS * (WORDS + ENTS)))
    next_mom_attn = MOMENTUM * mom_attn + step_attn
    next_mom_up = MOMENTUM * mom_up + step_up
    next_mom_down = MOMENTUM * mom_down + step_down
    next_mom_vecs = MOMENTUM * mom_vecs + vec_mean
    new_attn = attn_w - lr_mat * next_mom_attn
    new_up = up_w - lr_mat * next_mom_up
    new_down = down_w - lr_mat * next_mom_down
    new_vecs = vecs - lr_vec * next_mom_vecs
    return (
        result[:, :words_dev],
        result[:, words_dev:],
        grad_inputs[:, :words_dev],
        grad_inputs[:, words_dev:],
        new_attn,
        new_up,
        new_down,
        new_vecs,
        next_mom_attn,
        next_mom_up,
        next_mom_down,
        next_mom_vecs,
        next_err_attn,
        next_err_up,
        next_err_down,
        attention_local_gradient,
        own_up,
        own_down,
        attention_right_factor,
        right_up,
        right_down,
    )


def seq_swap(array, bits):
    size = lax.axis_size("seq")
    return lax.ppermute(array, "seq", [(i, i ^ bits) for i in range(size)])


def rep_swap(array, bits):
    size = lax.axis_size("rep")
    return lax.ppermute(array, "rep", [(i, i ^ bits) for i in range(size)])


def planes_swap(array):
    seqs, reps = lax.axis_size("seq"), lax.axis_size("rep")
    pairs = []
    for s in range(seqs):
        for r in range(reps):
            pairs.append((s * reps + r, (r // 2) * reps + 2 * s + r % 2))
    return lax.ppermute(array, ("seq", "rep"), pairs)


def gather_seq(piece):
    other_chip = seq_swap(piece, 2)
    return [seq_swap(piece, 1), seq_swap(other_chip, 1), piece, other_chip]


def gather_direct(piece):
    pieces = [piece] + [rep_swap(piece, 2 * change) for change in (1, 2, 3)]
    return pieces, rep_swap(piece, 1)


def gather_tree(piece):
    own_side = rep_swap(piece, 1)
    far, own_side = lax.optimization_barrier((rep_swap(piece, 4), own_side))
    near = rep_swap(jnp.stack([piece, far]), 2)
    near, far_side = lax.optimization_barrier((near, rep_swap(far, 1)))
    near_side = rep_swap(near, 1)
    return [piece, own_side, far, far_side, near, near_side]


def tree_pieces(refs):
    own, own_side, far, far_side, near, near_side = refs
    return (
        (0, own[...], own_side[...]),
        (2, far[...], far_side[...]),
        (1, near[0], near_side[0]),
        (3, near[1], near_side[1]),
    )


def project_kernel(
    words_dev, rows_dev, place_ref, bias_word_ref, bias_ent_ref, scale_ref, *refs
):
    trees, row_refs = (refs[:6], refs[6:12]), refs[12:16]
    word_ref, ent_ref, packed_word_ref, packed_ent_ref, rows_ref, out_ref, piece_ref = refs[16:]
    word_count = packed_word_ref.shape[0]
    ents_dev = rows_dev - words_dev
    z, y = place_ref[0], place_ref[1]
    for half, tree in enumerate(trees):
        for change, own, other in tree_pieces(tree):
            piece_ref[half, z ^ change, y] = own
            piece_ref[half, z ^ change, 1 - y] = other
    rows, both = piece_ref.shape[3:]
    cols = both // 14
    for half in (0, 1):
        for place in range(4):
            left, right = piece_ref[half, place, 0], piece_ref[half, place, 1]
            for side, piece in ((0, left), (1, right)):
                start = (4 * place + 2 * side + half) * rows
                out_ref[start : start + rows] = piece[:, 12 * cols :]
            for upper in (0, 1):
                parts = []
                for j in range(6):
                    low = (upper * 6 + j) * cols
                    parts.append(left[:, low : low + cols])
                    parts.append(right[:, low : low + cols])
                start = (4 * place + 2 * upper + half) * rows
                target = slice(start, start + rows)
                word_ref[target] = jnp.concatenate(parts[:4] + parts[8:], 1)
                ent_ref[target] = jnp.concatenate(parts[4:], 1)

    scale = scale_ref[...]
    word, ent = word_ref[...], ent_ref[...]
    for k, row_ref in enumerate(row_refs):
        words = row_ref[:words_dev]
        at = slice(k * words_dev, (k + 1) * words_dev)
        rows_ref[at] = words
        packed_word_ref[at] = ((mm(words, word) + bias_word_ref[...]) * scale).astype(
            jnp.bfloat16
        )
        start = word_count + k * ents_dev
        rows_ref[start : start + ents_dev] = row_ref[words_dev:rows_dev]
    packed_ent_ref[...] = ((mm(rows_ref[word_count:], ent) + bias_ent_ref[...]) * scale).astype(
        jnp.bfloat16
    )


def ffn_join_kernel(place_ref, *refs):
    pieces, sides, (up_ref, down_ref) = refs[:4], refs[4:8], refs[8:]
    z, y = place_ref[0], place_ref[1]
    for side in (0, 1):

        @pl.when(y == side)
        def _():
            for change in range(4):
                for y_at, piece in ((side, pieces[change]), (1 - side, sides[change])):
                    rows, both = piece.shape
                    cols = both // 4
                    place = z ^ change
                    for upper in (0, 1):
                        start = pl.multiple_of(place * (2 * rows) + upper * rows, 16)
                        up_ref[pl.ds(start, rows), y_at * cols : (y_at + 1) * cols] = piece[
                            :, upper * cols : (upper + 1) * cols
                        ]
                    start = pl.multiple_of((2 * place + y_at) * rows, 16)
                    down_ref[pl.ds(start, rows), :] = piece[:, 2 * cols :]


def join_call(kernel, place, pieces, shapes, name):
    whole = [pl.BlockSpec(memory_space=pltpu.VMEM)] * len(pieces)
    return pl.pallas_call(
        kernel,
        in_specs=[pl.BlockSpec(memory_space=pltpu.SMEM)] + whole,
        out_specs=[pl.BlockSpec(memory_space=pltpu.VMEM)] * len(shapes),
        out_shape=[jax.ShapeDtypeStruct(shape, jnp.bfloat16) for shape in shapes],
        name=name,
    )(place, *pieces)


def tie(value, mark):
    return lax.optimization_barrier((value, mark))[0]


def scatter_blocks(rows, dot, weight):
    half = rows.shape[0] // 2
    own = half // 2
    sent = dot(rows[:half], weight).astype(jnp.bfloat16)
    kept = dot(rows[half:], weight) + seq_swap(sent, 1).astype(jnp.float32)
    return sent, kept[:own], seq_swap(kept[own:].astype(jnp.bfloat16), 2)


def rows_norm(hidden, gain, shift):
    center = hidden - jnp.mean(hidden, -1, keepdims=True)
    rstd = lax.rsqrt(jnp.mean(center * center, -1, keepdims=True) + EPS)
    normed = center * rstd
    return (normed * gain + shift, normed, rstd)


def rows_norm_back(grad, normed, rstd, gain):
    dnormed = grad * gain
    grad_in = rstd * (
        dnormed
        - jnp.mean(dnormed, -1, keepdims=True)
        - normed * jnp.mean(dnormed * normed, -1, keepdims=True)
    )
    return (grad_in, jnp.sum(grad * normed, axis=0), jnp.sum(grad, axis=0))


def mm(left, right, left_dim=1, right_dim=0):
    return lax.dot_general(
        left, right, (((left_dim,), (right_dim,)), ((), ())), preferred_element_type=jnp.float32
    )


def nt_dot(left, right):
    return mm(left, right, 1, 1)


def tn_dot(left, right):
    return mm(left, right, 0, 0)


HEAD_DIM = 64


def head_parts(word_ref, ent_ref, low, high):
    return jnp.concatenate([word_ref[:, low:high], ent_ref[:, low:high]], 0)


def attention_kernel(
    heads,
    query_word_ref,
    query_ent_ref,
    key_word_ref,
    key_ent_ref,
    offset_ref,
    attn_ref,
    low_ref,
    high_ref,
    stat_ref,
):
    width = heads * HEAD_DIM
    word_count = key_word_ref.shape[0]
    rows = attn_ref.shape[0]
    lane = lax.broadcasted_iota(jnp.int32, (rows, 128), 1)
    stats = jnp.zeros((rows, 128), jnp.float32)
    for h in range(heads):
        low, high = h * HEAD_DIM, (h + 1) * HEAD_DIM
        q_word = head_parts(query_word_ref, query_ent_ref, low, high)
        q_ent = head_parts(query_word_ref, query_ent_ref, width + low, width + high)
        k_word = key_word_ref[:, 2 * width + low : 2 * width + high]
        k_ent = key_ent_ref[:, 2 * width + low : 2 * width + high]
        s_word = nt_dot(q_word, k_word) + offset_ref[:, :word_count]
        s_ent = nt_dot(q_ent, k_ent) + offset_ref[:, word_count:]
        top = jnp.maximum(
            jnp.max(s_word, -1, keepdims=True), jnp.max(s_ent, -1, keepdims=True)
        )
        w_word = jnp.exp(s_word - top)
        w_ent = jnp.exp(s_ent - top)
        total = jnp.sum(w_word, -1, keepdims=True) + jnp.sum(w_ent, -1, keepdims=True)
        v_word = key_word_ref[:, 3 * width + low : 3 * width + high]
        v_ent = key_ent_ref[:, 3 * width + low : 3 * width + high]
        unnorm = mm(w_word.astype(jnp.bfloat16), v_word) + mm(w_ent.astype(jnp.bfloat16), v_ent)
        attn_ref[:, low:high] = unnorm / total
        stats = jnp.where(lane == h, top, stats)
        stats = jnp.where(lane == heads + h, total, stats)
    stat_ref[...] = stats
    low_ref[...] = attn_ref[: rows // 2].astype(jnp.bfloat16)
    high_ref[...] = attn_ref[rows // 2 :].astype(jnp.bfloat16)


def attention_forward(packed_word, packed_ent, offsets, heads):
    word_count, packed_width = packed_word.shape
    ent_count = packed_ent.shape[0]
    count = word_count + ent_count
    width = heads * HEAD_DIM
    block = count // 4
    return pl.pallas_call(
        functools.partial(attention_kernel, heads),
        grid=(4,),
        in_specs=[
            pl.BlockSpec((word_count // 4, packed_width), lambda i: (i, 0)),
            pl.BlockSpec((ent_count // 4, packed_width), lambda i: (i, 0)),
            pl.BlockSpec((word_count, packed_width), lambda i: (0, 0)),
            pl.BlockSpec((ent_count, packed_width), lambda i: (0, 0)),
            pl.BlockSpec((1, count), lambda i: (0, 0)),
        ],
        out_specs=[
            pl.BlockSpec((block, width), lambda i: (i, 0)),
            pl.BlockSpec((block // 2, width), lambda i: (i, 0)),
            pl.BlockSpec((block // 2, width), lambda i: (i, 0)),
            pl.BlockSpec((block, 128), lambda i: (i, 0)),
        ],
        out_shape=[
            jax.ShapeDtypeStruct((count, width), jnp.float32),
            jax.ShapeDtypeStruct((count // 2, width), jnp.bfloat16),
            jax.ShapeDtypeStruct((count // 2, width), jnp.bfloat16),
            jax.ShapeDtypeStruct((count, 128), jnp.float32),
        ],
        compiler_params=pltpu.CompilerParams(dimension_semantics=("arbitrary",)),
        cost_estimate=pl.CostEstimate(
            flops=4 * count * count * width,
            bytes_accessed=6 * count * packed_width,
            transcendentals=count * count * heads,
        ),
        name="attention",
    )(packed_word, packed_ent, packed_word, packed_ent, offsets)


def attention_back_kernel(
    heads,
    query_word_ref,
    query_ent_ref,
    key_word_ref,
    key_ent_ref,
    offset_ref,
    attn_ref,
    stat_ref,
    grad_low_ref,
    grad_high_ref,
    d_query_ref,
    d_key_ref,
    sum_ref,
    key_sum,
    value_sum,
):
    width = heads * HEAD_DIM
    word_count = key_word_ref.shape[0]
    words_dev, ents_dev = query_word_ref.shape[0], query_ent_ref.shape[0]
    step = pl.program_id(0)

    @pl.when(step == 0)
    def _():
        key_sum[...] = jnp.zeros_like(key_sum)
        value_sum[...] = jnp.zeros_like(value_sum)
        sum_ref[...] = jnp.zeros_like(sum_ref)

    word_rows = pl.ds(pl.multiple_of(step * words_dev, words_dev), words_dev)
    ent_rows = pl.ds(pl.multiple_of(word_count + step * ents_dev, ents_dev), ents_dev)
    for h in range(heads):
        low, high = h * HEAD_DIM, (h + 1) * HEAD_DIM
        q_word = head_parts(query_word_ref, query_ent_ref, low, high)
        q_ent = head_parts(query_word_ref, query_ent_ref, width + low, width + high)
        k_word = key_word_ref[:, 2 * width + low : 2 * width + high]
        k_ent = key_ent_ref[:, 2 * width + low : 2 * width + high]
        v_word = key_word_ref[:, 3 * width + low : 3 * width + high]
        v_ent = key_ent_ref[:, 3 * width + low : 3 * width + high]
        top = stat_ref[:, h : h + 1]
        inverse = 1.0 / stat_ref[:, heads + h : heads + h + 1]
        grad = head_parts(grad_low_ref, grad_high_ref, low, high)
        delta = jnp.sum(grad * attn_ref[:, low:high], -1, keepdims=True) * inverse
        grad_low = (grad * inverse).astype(jnp.bfloat16)
        w_word = jnp.exp(nt_dot(q_word, k_word) + offset_ref[:, :word_count] - top)
        w_ent = jnp.exp(nt_dot(q_ent, k_ent) + offset_ref[:, word_count:] - top)
        d_word = (w_word * (nt_dot(grad_low, v_word) - delta)).astype(jnp.bfloat16)
        d_ent = (w_ent * (nt_dot(grad_low, v_ent) - delta)).astype(jnp.bfloat16)
        for at, dquery in ((low, mm(d_word, k_word)), (width + low, mm(d_ent, k_ent))):
            dquery = dquery * 0.125
            lanes = slice(at, at + HEAD_DIM)
            d_query_ref[word_rows, lanes] = dquery[:words_dev].astype(jnp.bfloat16)
            d_query_ref[ent_rows, lanes] = dquery[words_dev:].astype(jnp.bfloat16)
            sum_ref[0:1, lanes] += jnp.sum(dquery[:words_dev], 0, keepdims=True)
            sum_ref[1:2, lanes] += jnp.sum(dquery[words_dev:], 0, keepdims=True)
        key_sum[low:high, :word_count] += tn_dot(q_word, d_word)
        key_sum[low:high, word_count:] += tn_dot(q_ent, d_ent)
        value_sum[low:high, :word_count] += tn_dot(grad_low, w_word.astype(jnp.bfloat16))
        value_sum[low:high, word_count:] += tn_dot(grad_low, w_ent.astype(jnp.bfloat16))

    @pl.when(step == pl.num_programs(0) - 1)
    def _():
        dkey = key_sum[...].T
        dvalue = value_sum[...].T
        sum_ref[2:3, :width] = jnp.sum(dvalue, 0, keepdims=True)
        d_key_ref[...] = jnp.concatenate([dkey, dvalue], 1).astype(jnp.bfloat16)


def attention_backward(packed_word, packed_ent, offsets, attn, stats, grads, heads):
    word_count, packed_width = packed_word.shape
    ent_count = packed_ent.shape[0]
    count = word_count + ent_count
    width = heads * HEAD_DIM
    block = count // 4
    return pl.pallas_call(
        functools.partial(attention_back_kernel, heads),
        grid=(4,),
        in_specs=[
            pl.BlockSpec((word_count // 4, packed_width), lambda i: (i, 0)),
            pl.BlockSpec((ent_count // 4, packed_width), lambda i: (i, 0)),
            pl.BlockSpec((word_count, packed_width), lambda i: (0, 0)),
            pl.BlockSpec((ent_count, packed_width), lambda i: (0, 0)),
            pl.BlockSpec((1, count), lambda i: (0, 0)),
            pl.BlockSpec((block, width), lambda i: (i, 0)),
            pl.BlockSpec((block, 128), lambda i: (i, 0)),
            pl.BlockSpec((block // 2, width), lambda i: (i, 0)),
            pl.BlockSpec((block // 2, width), lambda i: (i, 0)),
        ],
        out_specs=[
            pl.BlockSpec((count, 2 * width), lambda i: (0, 0)),
            pl.BlockSpec((count, 2 * width), lambda i: (0, 0)),
            pl.BlockSpec((8, 2 * width), lambda i: (0, 0)),
        ],
        out_shape=[
            jax.ShapeDtypeStruct((count, 2 * width), jnp.bfloat16),
            jax.ShapeDtypeStruct((count, 2 * width), jnp.bfloat16),
            jax.ShapeDtypeStruct((8, 2 * width), jnp.float32),
        ],
        scratch_shapes=[
            pltpu.VMEM((width, count), jnp.float32),
            pltpu.VMEM((width, count), jnp.float32),
        ],
        compiler_params=pltpu.CompilerParams(dimension_semantics=("arbitrary",)),
        cost_estimate=pl.CostEstimate(
            flops=10 * count * count * width,
            bytes_accessed=16 * count * packed_width,
            transcendentals=count * count * heads,
        ),
        name="attention_back",
    )(packed_word, packed_ent, packed_word, packed_ent, offsets, attn, stats, *grads)


def project_grad_kernel(word_count, rows_ref, query_ref, key_ref, grad_ref):
    width = query_ref.shape[1]
    words, ents = rows_ref[:word_count], rows_ref[word_count:]
    for at, value in (
        (0, tn_dot(words, query_ref[:word_count])),
        (width, tn_dot(ents, query_ref[word_count:])),
        (2 * width, tn_dot(words, key_ref[:word_count]) + tn_dot(ents, key_ref[word_count:])),
    ):
        grad_ref[:, at : at + width] = value.astype(jnp.bfloat16)


def project_grad(rows, d_query, d_key, word_count):
    count, model_width = rows.shape
    width = d_query.shape[1]
    lanes = model_width // 3
    return pl.pallas_call(
        functools.partial(project_grad_kernel, word_count),
        grid=(3,),
        in_specs=[
            pl.BlockSpec((count, lanes), lambda i: (0, i)),
            pl.BlockSpec((count, width), lambda i: (0, 0)),
            pl.BlockSpec((count, width), lambda i: (0, 0)),
        ],
        out_specs=pl.BlockSpec((lanes, 3 * width), lambda i: (i, 0)),
        out_shape=jax.ShapeDtypeStruct((model_width, 3 * width), jnp.bfloat16),
        name="project_grad",
    )(rows, d_query, d_key)


def input_grad_kernel(
    query_word_ref, query_ent_ref, key_word_ref, key_ent_ref, word_ref, ent_ref, sent_ref, kept_ref
):
    step = pl.program_id(0)
    width = query_word_ref.shape[1]

    def rows(query_ref, key_ref, weight_ref):
        return nt_dot(query_ref[...], weight_ref[:, :width]) + nt_dot(
            key_ref[...], weight_ref[:, width:]
        )

    words = rows(query_word_ref, key_word_ref, word_ref)
    ents = rows(query_ent_ref, key_ent_ref, ent_ref)
    words_dev, ents_dev = words.shape[0] // 2, ents.shape[0] // 2
    block = words_dev + ents_dev
    for at, ref in enumerate((sent_ref, kept_ref)):

        @pl.when(step == at)
        def _():
            for k in (0, 1):
                first, last = k * block, (k + 1) * block
                part = words[k * words_dev : (k + 1) * words_dev]
                ref[first : first + words_dev] = part.astype(ref.dtype)
                part = ents[k * ents_dev : (k + 1) * ents_dev]
                ref[first + words_dev : last] = part.astype(ref.dtype)


def input_grad(d_query, d_key, w_word, w_ent, word_count):
    count, width = d_query.shape
    model_width = w_word.shape[0]
    words, ents = word_count // 2, (count - word_count) // 2
    first_ent = word_count // ents
    word_spec = pl.BlockSpec((words, width), lambda i: (i, 0))
    ent_spec = pl.BlockSpec((ents, width), lambda i: (first_ent + i, 0))
    half = (words + ents, model_width)
    weight_spec = pl.BlockSpec(w_word.shape, lambda i: (0, 0))
    return pl.pallas_call(
        input_grad_kernel,
        grid=(2,),
        in_specs=[word_spec, ent_spec, word_spec, ent_spec, weight_spec, weight_spec],
        out_specs=[
            pl.BlockSpec(half, lambda i: (0, 0)),
            pl.BlockSpec(half, lambda i: (0, 0)),
        ],
        out_shape=[
            jax.ShapeDtypeStruct(half, jnp.bfloat16),
            jax.ShapeDtypeStruct(half, jnp.float32),
        ],
        name="input_grad",
    )(d_query, d_query, d_key, d_key, w_word, w_ent)


def tall(left):
    return jnp.swapaxes(left, -1, -2)


def halves(array):
    high = array.astype(jnp.bfloat16)
    return high, (array - high.astype(jnp.float32)).astype(jnp.bfloat16)


def stacked_halves(array):
    high = array.astype(jnp.bfloat16).astype(jnp.float32)
    return jnp.concatenate([array, array - high], 0).astype(jnp.bfloat16)


def columns_of(rank_rows):
    return jnp.concatenate(
        [rank_rows, rank_rows - rank_rows.astype(jnp.bfloat16).astype(jnp.float32)], 0
    ).T.astype(jnp.bfloat16)


def left_part(full, columns):
    high, low = halves(full)
    return mm(high, columns) + mm(low, columns)


def rank_first(part):
    both = part.T
    rank = both.shape[0] // 2
    return both[:rank] + both[rank:]


def left_ffn_kernel(
    got_ref, down_ref, err_up_ref, err_down_ref, q_up_ref, q_down_ref, full_up_ref, full_down_ref, left_ref
):
    step = pl.program_id(0)
    width = got_ref.shape[2]
    rows = got_ref.shape[1]
    left = 0.0
    for s in range(4):
        lanes = slice(s * width, (s + 1) * width)
        full = got_ref[s].astype(jnp.float32) + err_up_ref[0, :, lanes]
        full_up_ref[:, lanes] = full
        left = left + left_part(full, columns_of(q_up_ref[:, lanes]))
    left = rank_first(left)
    full = down_ref[...] + err_down_ref[0]
    full_down_ref[...] = full
    below = rank_first(left_part(full, columns_of(q_down_ref[...])))
    for side in (0, 1):

        @pl.when(step == side)
        def _():
            left_ref[0, :, side * rows : (side + 1) * rows] = left
            left_ref[1 + 2 * side] = below[:, : 2 * rows]
            left_ref[2 + 2 * side] = below[:, 2 * rows :]


def left_of_ffn(got_up, grad_down, err_up, err_down, q_up, q_down):
    rows, width = got_up.shape[1:]
    rank = q_up.shape[0]
    return pl.pallas_call(
        left_ffn_kernel,
        grid=(2,),
        in_specs=[
            pl.BlockSpec((4, rows // 2, width), lambda i: (0, i, 0)),
            pl.BlockSpec((2 * rows, width), lambda i: (i, 0)),
            pl.BlockSpec((1, rows // 2, 4 * width), lambda i: (0, i, 0)),
            pl.BlockSpec((1, 2 * rows, width), lambda i: (0, i, 0)),
            pl.BlockSpec((rank, 4 * width), lambda i: (0, 0)),
            pl.BlockSpec((rank, width), lambda i: (0, 0)),
        ],
        out_specs=[
            pl.BlockSpec((rows // 2, 4 * width), lambda i: (i, 0)),
            pl.BlockSpec((2 * rows, width), lambda i: (i, 0)),
            pl.BlockSpec((5, rank, rows), lambda i: (0, 0, 0)),
        ],
        out_shape=[
            jax.ShapeDtypeStruct((rows, 4 * width), jnp.float32),
            jax.ShapeDtypeStruct((4 * rows, width), jnp.float32),
            jax.ShapeDtypeStruct((5, rank, rows), jnp.float32),
        ],
        name="left_ffn",
    )(got_up, grad_down, err_up, err_down, q_up, q_down)


def left_attn_kernel(got_ref, out_ref, err_ref, q_ref, ffn_ref, full_ref, left_ref):
    step = pl.program_id(0)
    rows = full_ref.shape[1]
    part = 2 * rows
    lefts = []
    for j in range(7):
        if j < 6:
            lanes = slice(j * part, (j + 1) * part)
            grad = jnp.concatenate([got_ref[s, :, lanes] for s in range(4)], 1)
            full = grad.astype(jnp.float32) + err_ref[0, j]
        else:
            full = out_ref[...] + err_ref[0, j]
        full_ref[j] = full
        lefts.append(rank_first(left_part(full, columns_of(q_ref[j]))))
    for side in (0, 1):

        @pl.when(step == side)
        def _():
            for j in range(7):
                left_ref[j, :, side * rows : (side + 1) * rows] = lefts[j]

    @pl.when(step == 1)
    def _():
        left_ref[7:] = ffn_ref[...]


def left_of_attn(got, grad_out, err_attn, q_attn, left_ffn):
    rows, width = grad_out.shape
    rank = q_attn.shape[1]
    return pl.pallas_call(
        left_attn_kernel,
        grid=(2,),
        in_specs=[
            pl.BlockSpec((4, rows // 2, got.shape[2]), lambda i: (0, i, 0)),
            pl.BlockSpec((rows // 2, width), lambda i: (i, 0)),
            pl.BlockSpec((1, 7, rows // 2, width), lambda i: (0, 0, i, 0)),
            pl.BlockSpec((7, rank, width), lambda i: (0, 0, 0)),
            pl.BlockSpec((5, rank, rows), lambda i: (0, 0, 0)),
        ],
        out_specs=[
            pl.BlockSpec((7, rows // 2, width), lambda i: (0, i, 0)),
            pl.BlockSpec((12, rank, rows), lambda i: (0, 0, 0)),
        ],
        out_shape=[
            jax.ShapeDtypeStruct((7, rows, width), jnp.float32),
            jax.ShapeDtypeStruct((12, rank, rows), jnp.float32),
        ],
        name="left_attn",
    )(got, grad_out, err_attn, q_attn, left_ffn)


MATRIX_BLOCKS = [[j] for j in range(8)] + [[8, 9, 10, 11]]


def gram_kernel(scale, mine_ref, other_ref, left_ref, gram_ref):
    rank = mine_ref.shape[1]
    left = (mine_ref[...] + other_ref[...]) * scale
    left_ref[...] = left
    lane = lax.broadcasted_iota(jnp.int32, (rank, 128), 1)
    row = lax.broadcasted_iota(jnp.int32, (rank, 128), 0)
    for r in range(rank):
        gram = jnp.where((lane >= len(MATRIX_BLOCKS)) & (row == r), 1.0, 0.0)
        for m, blocks in enumerate(MATRIX_BLOCKS):
            product = sum(left[b] * left[b, r : r + 1] for b in blocks)
            gram = jnp.where(lane == m, jnp.sum(product, -1, keepdims=True), gram)
        gram_ref[r] = gram


def gram_of(mine, other, scale):
    rank = mine.shape[1]
    return pl.pallas_call(
        functools.partial(gram_kernel, scale),
        out_shape=[
            jax.ShapeDtypeStruct(mine.shape, jnp.float32),
            jax.ShapeDtypeStruct((rank, rank, 128), jnp.float32),
        ],
        name="gram",
    )(mine, other)


def inverse_factor(columns, rank):
    row = lax.broadcasted_iota(jnp.int32, columns[0].shape, 0)
    columns, lower = list(columns), []
    for k in range(rank):
        column = columns[k] / jnp.sqrt(columns[k][k : k + 1])
        lower.append(column)
        for c in range(k + 1, rank):
            columns[c] = columns[c] - column * column[c : c + 1]
    inverse = []
    for r in range(rank):
        value = jnp.where(row == r, 1.0, 0.0)
        for t in range(r):
            value = value - lower[t][r : r + 1] * inverse[t]
        inverse.append(value / lower[r][r : r + 1])
    return inverse


def right_part(both_ref, blocks, fulls):
    out = 0.0
    for b, full in zip(blocks, fulls):
        high, low = halves(full)
        out = out + mm(both_ref[b], high) + mm(both_ref[b], low)
    rank = out.shape[0] // 2
    return out[:rank] + out[rank:]


def right_kernel(place_ref, gram_ref, other_ref, left_ref, attn_ref, *refs):
    up_refs, (down_ref, vec_ref, orth_ref) = refs[:4], refs[4:7]
    p_attn_ref, p_up_ref, p_down_ref, sent_ref, kept_ref, both_ref = refs[7:]
    step = pl.program_id(0)
    rank, rows = left_ref.shape[1:]
    chip = place_ref[2]

    @pl.when(step == 0)
    def _():
        inverse = inverse_factor([gram_ref[r] + other_ref[r] for r in range(rank)], rank)
        row = lax.broadcasted_iota(jnp.int32, (rank, rows), 0)
        for m, blocks in enumerate(MATRIX_BLOCKS):
            weights = [inverse[r][:, m : m + 1] for r in range(rank)]
            for b in blocks:
                left = left_ref[b]
                orth = jnp.zeros((rank, rows), jnp.float32)
                for r in range(rank):
                    total = jnp.sum(left * weights[r], 0, keepdims=True)
                    orth = jnp.where(row == r, total, orth)
                orth_ref[b] = orth
                both_ref[b] = stacked_halves(orth)
                if b < 7:
                    p_attn_ref[b] = orth
                elif b == 7:
                    p_up_ref[...] = orth
                else:
                    p_down_ref[:, (b - 8) * rows : (b - 7) * rows] = orth

    parts = [right_part(both_ref, [j], [attn_ref[j]]) for j in range(7)]
    parts += [right_part(both_ref, [7], [up_refs[k][...]]) for k in range(4)]
    parts.append(
        right_part(
            both_ref, [8, 9, 10, 11], [down_ref[k * rows : (k + 1) * rows] for k in range(4)]
        )
    )
    parts += [vec_ref[0], vec_ref[1]]
    for at, ref in enumerate((sent_ref, kept_ref)):

        @pl.when(step == at)
        def _():
            for b, part in enumerate(parts):
                ref[(b // 7) ^ chip, b % 7] = part


def right_of(place, gram, other, left, full_attn, full_up, full_down, vecs):
    rank, rows = left.shape[1:]
    width = full_attn.shape[2]
    lanes = width // 2

    def whole(shape):
        return pl.BlockSpec(shape, lambda i, place: (0,) * len(shape))

    def half(i, place):
        return 1 - place[3] + i * (2 * place[3] - 1)

    def up_spec(k):
        return pl.BlockSpec((rows, lanes), lambda i, place: (0, 2 * k + half(i, place)))

    out_shapes = [
        left.shape,
        (7, rank, rows),
        (rank, rows),
        (rank, 4 * rows),
        (2, 7, rank, lanes),
        (2, 7, rank, lanes),
    ]
    return pl.pallas_call(
        right_kernel,
        grid_spec=pltpu.PrefetchScalarGridSpec(
            num_scalar_prefetch=1,
            grid=(2,),
            in_specs=[
                whole(gram.shape),
                whole(other.shape),
                whole(left.shape),
                pl.BlockSpec((7, rows, lanes), lambda i, place: (0, 0, half(i, place))),
                up_spec(0),
                up_spec(1),
                up_spec(2),
                up_spec(3),
                pl.BlockSpec((4 * rows, lanes), lambda i, place: (0, half(i, place))),
                pl.BlockSpec((2, rank, lanes), lambda i, place: (0, 0, half(i, place))),
            ],
            out_specs=[whole(shape) for shape in out_shapes],
            scratch_shapes=[pltpu.VMEM((12, 2 * rank, rows), jnp.bfloat16)],
        ),
        out_shape=[jax.ShapeDtypeStruct(shape, jnp.float32) for shape in out_shapes],
        name="right",
    )(place, gram, other, left, full_attn, full_up, full_up, full_up, full_up, full_down, vecs)


def left_stack(orth):
    high = orth.astype(jnp.bfloat16).astype(jnp.float32)
    return jnp.concatenate([orth, orth, orth - high, jnp.zeros_like(orth)], 0)


def right_stack(right):
    high = right.astype(jnp.bfloat16).astype(jnp.float32)
    return jnp.concatenate([right, right - high, right, jnp.zeros_like(right)], 0).astype(
        jnp.bfloat16
    )


def update_kernel(rate, rate_vecs, place_ref, orth_ref, mine_ref, other_ref, *refs):
    full_refs, mom_refs, weight_refs = refs[:3], refs[3:7], refs[7:11]
    err_refs, next_refs, new_refs = refs[11:14], refs[14:18], refs[18:22]
    q_attn_ref, q_up_ref, q_down_ref, right_ref, tall_ref, right_rows, cols_rows = refs[22:]
    step = pl.program_id(0)
    rows = full_refs[1].shape[0]
    rank, width = right_ref.shape[1:]
    part = orth_ref.shape[2]
    cols = mom_refs[0].shape[2]
    cols_up = mom_refs[1].shape[1]

    def move(change, at, i, rate=rate):
        value = MOMENTUM * mom_refs[i][at] + change
        next_refs[i][at] = value
        new_refs[i][at] = weight_refs[i][at] - rate * value

    @pl.when(step == 0)
    def _():
        lanes = width // 2
        chip, core = place_ref[2], place_ref[3]
        for own in (0, 1):

            @pl.when(core == own)
            def _():
                for half in (0, 1):
                    blocks = pl.ds((chip ^ half) * 7, 7)
                    right_ref[blocks, :, own * lanes : (own + 1) * lanes] = mine_ref[half]
                    right_ref[blocks, :, (1 - own) * lanes : (2 - own) * lanes] = other_ref[half]

        replica = 2 * place_ref[0] + place_ref[1]
        shift = width - replica * cols
        for b in range(12):
            tall_ref[b] = left_stack(orth_ref[b]).T.astype(jnp.bfloat16)
            right = right_ref[b]
            right_rows[b] = right_stack(right)
            if b < 7 or b == 11:
                own = pltpu.roll(right, shift, 1)[:, :cols]
                cols_rows[min(b, 7)] = right_stack(own)
            if b < 7:
                q_attn_ref[b] = right
            elif b < 11:
                q_up_ref[:, (b - 7) * width : (b - 6) * width] = right
            else:
                q_down_ref[...] = right
        move(right_ref[12], slice(0, rank), 3, rate_vecs)
        move(right_ref[13, : rank - 1], slice(rank, 2 * rank - 1), 3, rate_vecs)

    own = pl.ds(pl.multiple_of(step * rows, 16), rows)
    for j in range(7):
        left = tall_ref[j, own]
        err_refs[0][0, j] = full_refs[0][j] - mm(left, right_rows[j])
        move(mm(left, cols_rows[j]), j, 0)
    left = tall_ref[7, own]
    for k in range(4):
        lanes = slice(k * width, (k + 1) * width)
        err_refs[1][0, :, lanes] = full_refs[1][:, lanes] - mm(left, right_rows[7 + k])
    block = right_rows[7 + place_ref[0]]
    low = mm(left, block[:, :cols_up])
    high = mm(left, block[:, cols_up:])
    side = place_ref[1].astype(jnp.float32)
    move(jnp.where(jnp.full(low.shape, side) == 0.0, low, high), ..., 1)
    err_refs[2][0] = full_refs[2][...] - mm(tall_ref[8 + step], right_rows[11])

    @pl.when(step == 3)
    def _():
        for k in range(4):
            change = tn_dot(cols_rows[7], left_stack(orth_ref[8 + k]).astype(jnp.bfloat16))
            move(change, (slice(None), slice(k * part, (k + 1) * part)), 2)


def updates(place, orth, mine, other, full, mom, weight, rate, rate_vecs):
    rank, part = orth.shape[1:]
    width = full[2].shape[1]
    cols, cols_up = mom[0].shape[2], mom[1].shape[1]
    rows = part // 4

    def whole(array):
        return pl.BlockSpec(array.shape, lambda i: (0,) * array.ndim)

    full_specs = [
        pl.BlockSpec((7, rows, width), lambda i: (0, i, 0)),
        pl.BlockSpec((rows, 4 * width), lambda i: (i, 0)),
        pl.BlockSpec((part, width), lambda i: (i, 0)),
    ]
    own_specs = [
        pl.BlockSpec((7, rows, cols), lambda i: (0, i, 0)),
        pl.BlockSpec((rows, cols_up), lambda i: (i, 0)),
        whole(mom[2]),
        whole(mom[3]),
    ]
    err_specs = [
        pl.BlockSpec((1, 7, rows, width), lambda i: (0, 0, i, 0)),
        pl.BlockSpec((1, rows, 4 * width), lambda i: (0, i, 0)),
        pl.BlockSpec((1, part, width), lambda i: (0, i, 0)),
    ]
    err_shapes = [jax.ShapeDtypeStruct((1,) + array.shape, jnp.float32) for array in full]
    own_shapes = [jax.ShapeDtypeStruct(array.shape, jnp.float32) for array in mom]
    q_shapes = [
        jax.ShapeDtypeStruct(shape, jnp.float32)
        for shape in ((7, rank, width), (rank, 4 * width), (rank, width))
    ]
    outs = pl.pallas_call(
        functools.partial(update_kernel, rate, rate_vecs),
        grid=(4,),
        in_specs=[pl.BlockSpec(memory_space=pltpu.SMEM), whole(orth), whole(mine), whole(other)]
        + full_specs
        + own_specs
        + own_specs,
        out_specs=err_specs + own_specs + own_specs + [whole(shape) for shape in q_shapes],
        out_shape=err_shapes + own_shapes + own_shapes + q_shapes,
        scratch_shapes=[
            pltpu.VMEM((14, rank, width), jnp.float32),
            pltpu.VMEM((12, part, 32), jnp.bfloat16),
            pltpu.VMEM((12, 32, width), jnp.bfloat16),
            pltpu.VMEM((8, 32, cols), jnp.bfloat16),
        ],
        name="updates",
    )(place, orth, mine, other, *full, *mom, *weight)
    return outs[:3], outs[3:7], outs[7:11], outs[11:]


def head_split_device(
    x_words,
    x_ents,
    spans,
    word_mask,
    ent_mask,
    cot_words,
    cot_ents,
    attn_w,
    up_w,
    down_w,
    vecs,
    mom_attn,
    mom_up,
    mom_down,
    mom_vecs,
    err_attn,
    err_up,
    err_down,
    attention_prior_right,
    qf_up,
    qf_down,
):
    low_type = jnp.bfloat16
    words_dev, width = x_words.shape[1:]
    ents_dev = x_ents.shape[1]
    rows_dev = words_dev + ents_dev
    seq_count, rep_count = lax.axis_size("seq"), lax.axis_size("rep")
    seq_index, rep_index = lax.axis_index("seq"), lax.axis_index("rep")
    heads = HEADS // seq_count
    part = width // seq_count
    word_count = words_dev * seq_count
    ent_count = ents_dev * seq_count
    cols = attn_w.shape[2]
    cols_up = up_w.shape[1]
    hidden = cols_up * rep_count
    hidden_part = hidden // seq_count

    core, chip = seq_index % 2, seq_index // 2
    place = jnp.stack([rep_index // 2, rep_index % 2, chip, core]).astype(jnp.int32)
    block = part // 2
    project_piece = jnp.transpose(
        attn_w[:6].astype(low_type).reshape(6, 2, block, cols), (2, 1, 0, 3)
    ).reshape(block, 12 * cols)
    out_piece = attn_w[6].astype(low_type).T
    half = block // 2
    first, second = [
        jnp.concatenate([planes_swap(project_piece[rows]), out_piece[rows]], 1)
        for rows in (slice(half), slice(half, block))
    ]
    trees = [gather_tree(first)]
    second, unused_far = lax.optimization_barrier((second, trees[0][2]))
    trees.append(gather_tree(second))
    up_piece = jnp.transpose(
        up_w.astype(low_type).reshape(2, block, cols_up), (1, 0, 2)
    ).reshape(block, 2 * cols_up)
    up_piece = tie(up_piece, trees[0][2])
    ffn_piece = jnp.concatenate([planes_swap(up_piece), down_w.astype(low_type).T], 1)
    ffn_piece, unused_near = lax.optimization_barrier((ffn_piece, (trees[0][4], trees[1][4])))
    ffn_pieces, ffn_side = gather_direct(ffn_piece)

    spans, unused_piece = lax.optimization_barrier((spans, project_piece))
    inputs = jnp.concatenate([x_words[0], x_ents[0] + span_mean_closed(spans[0], width)], 0)
    live = jnp.concatenate([word_mask[0], ent_mask[0]], 0).astype(low_type)
    live = jnp.pad(live.reshape(1, rows_dev), ((0, 15), (0, width - rows_dev)))
    pieces = gather_seq(jnp.concatenate([inputs.astype(low_type), live], 0))
    lives = [piece[rows_dev, :rows_dev] for piece in pieces]
    lives = [piece[:words_dev] for piece in lives] + [piece[words_dev:] for piece in lives]
    offsets = ((jnp.concatenate(lives).astype(jnp.float32) - 1.0) * MASK_FILL).reshape(1, -1)

    own_vecs = lax.dynamic_slice_in_dim(vecs, seq_index * part, part, 1)
    none = jnp.zeros((part,), jnp.float32)
    scale = jnp.where(jnp.arange(4 * part) < 2 * part, 0.125, 1.0).astype(jnp.float32)
    bias_word = jnp.concatenate([own_vecs[0], own_vecs[1], none, own_vecs[4]])
    bias_ent = jnp.concatenate([own_vecs[2], own_vecs[3], none, own_vecs[4]])
    in_vmem = pl.BlockSpec(memory_space=pltpu.VMEM)
    w_word, w_ent, packed_word, packed_ent, rows_low, w_out = pl.pallas_call(
        functools.partial(project_kernel, words_dev, rows_dev),
        in_specs=[pl.BlockSpec(memory_space=pltpu.SMEM)] + [in_vmem] * 19,
        out_specs=[in_vmem] * 6,
        out_shape=[
            jax.ShapeDtypeStruct(shape, low_type)
            for shape in [
                (rows, width)
                for rows in (width, width, word_count, ent_count, word_count + ent_count)
            ]
            + [(width, part)]
        ],
        scratch_shapes=[pltpu.VMEM((2, 4, 2, half, 14 * cols), low_type)],
        name="project",
    )(
        place,
        bias_word.reshape(1, -1),
        bias_ent.reshape(1, -1),
        scale.reshape(1, -1),
        *trees[0],
        *trees[1],
        *pieces,
    )
    attn, *attn_low, stats = attention_forward(packed_word, packed_ent, offsets, heads)
    attn_low[1], ffn_pieces, ffn_side = lax.optimization_barrier(
        (attn_low[1], ffn_pieces, ffn_side)
    )
    ffn_sides = [ffn_side] + [rep_swap(piece, 1) for piece in ffn_pieces[1:]]
    w_up, w_down = join_call(
        ffn_join_kernel,
        place,
        ffn_pieces + ffn_sides,
        [(width, hidden_part), (width, hidden_part)],
        "join_ffn",
    )

    bias_up = lax.dynamic_slice_in_dim(
        vecs[11:15].reshape(hidden), seq_index * hidden_part, hidden_part, 0
    )
    grad_result = jnp.concatenate([cot_words[0], cot_ents[0]], 0)
    split = rows_dev // 2
    ats = [slice(c * split, (c + 1) * split) for c in (0, 1)]
    parts = [{}, {}]

    def gather(part, rows):
        part["own"] = rows.astype(low_type)
        part["core"], part["far"] = seq_swap(part["own"], 1), seq_swap(part["own"], 2)
        return part["own"]

    def gathered(part, mark):
        far = tie(part["far"], mark)
        return jnp.concatenate([part["core"], seq_swap(far, 1), part["own"], far], 0)

    def scatter(part, rows, weight):
        sent, part["own"], part["far"] = scatter_blocks(rows, nt_dot, weight)
        return sent

    def scattered(part, mark):
        return part["own"] + tie(part["far"], mark).astype(jnp.float32)

    def out_stage(part, c, mark):
        rows = attn_low[c] if mark is None else tie(attn_low[c], mark)
        return scatter(part, rows, w_out)

    def mid_stage(part, c, mark):
        branch = scattered(part, mark) + vecs[5]
        part["mid"], *part["one"] = rows_norm(inputs[ats[c]] + branch, vecs[7], vecs[8])
        return gather(part, part["mid"])

    def up_stage(part, c, mark):
        part["mid_low"] = gathered(part, mark)
        part["pre"] = mm(part["mid_low"], w_up) + bias_up
        part["cdf"] = 0.5 * (1.0 + lax.erf(part["pre"] * math.sqrt(0.5)))
        part["act"] = (part["pre"] * part["cdf"]).astype(low_type)
        return scatter(part, part["act"], w_down)

    def result_stage(part, c, mark):
        ffn = scattered(part, mark) + vecs[6]
        part["result"], *two = rows_norm(part["mid"] + ffn, vecs[9], vecs[10])
        grad, *part["sums_two"] = rows_norm_back(grad_result[ats[c]], *two, vecs[9])
        part["grad_two"] = grad
        return gather(part, grad)

    def down_stage(part, c, mark):
        part["grad_ffn"] = gathered(part, mark)
        pre = part["pre"]
        density = jnp.exp(-0.5 * pre * pre) * (1.0 / math.sqrt(2.0 * math.pi))
        part["grad_pre"] = mm(part["grad_ffn"], w_down) * (part["cdf"] + pre * density)
        part["grad_pre_low"] = part["grad_pre"].astype(low_type)
        return scatter(part, part["grad_pre_low"], w_up)

    def norm_stage(part, c, mark):
        grad = part["grad_two"] + scattered(part, mark)
        part["grad_one"], *part["sums_one"] = rows_norm_back(grad, *part["one"], vecs[7])
        return gather(part, part["grad_one"])

    def branch_stage(part, c, mark):
        part["grad_branch"] = gathered(part, mark)
        part["grad_attn"] = mm(part["grad_branch"], w_out)
        return part["grad_branch"]

    mark = None
    for stage in (
        out_stage,
        mid_stage,
        up_stage,
        result_stage,
        down_stage,
        norm_stage,
        branch_stage,
    ):
        for c, chunk in enumerate(parts):
            mark = stage(chunk, c, mark)
    results, grads_one, grads_attn = [
        [part[name] for part in parts] for name in ("result", "grad_one", "grad_attn")
    ]
    kept = [
        [part[name] for name in ("mid_low", "act", "grad_ffn", "grad_pre_low", "grad_branch")]
        for part in parts
    ]
    sums = [
        sum(values)
        for values in zip(
            *[
                [jnp.sum(part["grad_one"], 0), jnp.sum(part["grad_two"], 0)]
                + part["sums_one"]
                + part["sums_two"]
                + [jnp.sum(part["grad_pre"], 0)]
                for part in parts
            ]
        )
    ]
    result = jnp.concatenate(results, 0)
    grad_one = jnp.concatenate(grads_one, 0)
    grad_up = sum(tn_dot(mid_low, grad_pre_low) for mid_low, _, _, grad_pre_low, _ in kept)
    grad_up, unused_branch = lax.optimization_barrier((grad_up.astype(low_type), kept[1][4]))
    got_up = lax.all_to_all(grad_up.reshape(seq_count, part, hidden_part), "seq", 0, 0)
    grad_out = sum(tn_dot(low, parts[4]) for low, parts in zip(attn_low, kept))
    d_query, d_key, d_sums = attention_backward(
        packed_word, packed_ent, offsets, attn, stats, grads_attn, heads
    )
    d_query, got_up = lax.optimization_barrier((d_query, got_up))
    grad_down = sum(
        tn_dot(act_low, tie(grad_ffn, d_sums)) for _, act_low, grad_ffn, _, _ in kept
    )
    grad_project = project_grad(rows_low, d_query, d_key, word_count)
    got_project = lax.all_to_all(
        grad_project.reshape(seq_count, part, 6 * part), "seq", 0, 0
    )
    full_up, full_down, left_ffn = left_of_ffn(
        got_up, grad_down, err_up, err_down, qf_up.T, qf_down.T
    )
    sent_inputs, own_inputs = input_grad(
        d_query, tie(d_key, grad_project[:16, :128]), w_word, w_ent, word_count
    )
    own_inputs = own_inputs + seq_swap(sent_inputs, 1).astype(jnp.float32)
    own_inputs, sent_inputs = own_inputs[:rows_dev], own_inputs[rows_dev:].astype(low_type)

    vec_grad = jnp.zeros((15, width), jnp.float32)
    bias_query = jnp.concatenate(
        [d_sums[0].reshape(2, part), d_sums[1].reshape(2, part), d_sums[2, :part].reshape(1, part)], 0
    )
    vec_grad = lax.dynamic_update_slice(vec_grad, bias_query, (0, seq_index * part))
    vec_grad = lax.dynamic_update_slice(vec_grad, jnp.stack(sums[:6]), (5, 0))
    bias_rows = hidden_part // width
    vec_grad = lax.dynamic_update_slice(
        vec_grad, sums[6].reshape(bias_rows, width), (11 + seq_index * bias_rows, 0)
    )

    full_attn, left = left_of_attn(
        got_project, grad_out, err_attn, tall(attention_prior_right), left_ffn
    )
    left, sent_inputs = lax.optimization_barrier((left, sent_inputs))
    got_inputs = seq_swap(sent_inputs, 2)
    for bits in (1, 2):
        left = left + rep_swap(left, bits)
    left, got_inputs = lax.optimization_barrier((left, got_inputs))
    left, gram = gram_of(left, rep_swap(left, 4), 1.0 / rep_count)
    gram = gram + seq_swap(gram, 1)
    rows_vec = jnp.pad(vec_grad, ((0, 1), (0, 0))).reshape(2, 8, width)
    orth, p_attn, p_up, p_down, sent, kept = right_of(
        place, gram, seq_swap(gram, 2), left, full_attn, full_up, full_down, rows_vec
    )
    got_inputs, unused_orth = lax.optimization_barrier((got_inputs, orth))
    grad_inputs = grad_one + (own_inputs + got_inputs.astype(jnp.float32))
    kept = kept + seq_swap(sent, 1)
    kept = kept[0] + seq_swap(kept[1], 2)
    for bits in (1, 2, 4):
        kept = kept + rep_swap(kept, bits)
    kept = kept / rep_count
    kept = jnp.stack([kept, seq_swap(kept, 2)])
    lr_mat = 1.5 * math.sqrt(rep_count / (SEQS * (WORDS + ENTS)))
    lr_vec = 0.2 * math.sqrt(rep_count / (SEQS * (WORDS + ENTS)))
    next_err, next_mom, new, (q_attn, q_up, q_down) = updates(
        place,
        orth,
        kept,
        seq_swap(kept, 1),
        (full_attn, full_up, full_down),
        (mom_attn, mom_up, mom_down.T, mom_vecs),
        (attn_w, up_w, down_w.T, vecs),
        lr_mat,
        lr_vec,
    )
    return (
        result[None, :words_dev],
        result[None, words_dev:],
        grad_inputs[None, :words_dev],
        grad_inputs[None, words_dev:],
        new[0],
        new[1],
        new[2].T,
        new[3],
        next_mom[0],
        next_mom[1],
        next_mom[2].T,
        next_mom[3],
        next_err[0],
        next_err[1],
        next_err[2],
        tall(p_attn),
        tall(p_up),
        tall(p_down),
        tall(q_attn),
        tall(q_up),
        tall(q_down),
    )


def solution(mesh):
    in_specs = (
        P("rep", "seq", None),
        P("rep", "seq", None),
        P("rep", "seq", None),
        P("rep", "seq"),
        P("rep", "seq"),
        P("rep", "seq", None),
        P("rep", "seq", None),
        P(None, "seq", "rep"),
        P("seq", "rep"),
        P("seq", "rep"),
        P(),
        P(None, "seq", "rep"),
        P("seq", "rep"),
        P("seq", "rep"),
        P(),
        P("rep", None, "seq", None),
        P("rep", "seq", None),
        P("rep", "seq", None),
        P(),
        P(),
        P(),
    )
    out_specs = (
        P("rep", "seq", None),
        P("rep", "seq", None),
        P("rep", "seq", None),
        P("rep", "seq", None),
        P(None, "seq", "rep"),
        P("seq", "rep"),
        P("seq", "rep"),
        P(),
        P(None, "seq", "rep"),
        P("seq", "rep"),
        P("seq", "rep"),
        P(),
        P("rep", None, "seq", None),
        P("rep", "seq", None),
        P("rep", "seq", None),
        P(None, "seq", None),
        P("seq", None),
        P("seq", None),
        P(),
        P(),
        P(),
    )
    seqs, reps = mesh.shape["seq"], mesh.shape["rep"]
    split_heads = seqs == 4 and reps == 2 * seqs and HEADS % seqs == 0
    body = head_split_device if split_heads else on_device
    return jax.shard_map(
        body, mesh=mesh, in_specs=in_specs, out_specs=out_specs, check_vma=False
    )
```
